32 devices in a mesh: fsdp: 4 (over y, x), ctx: 8 (over z, core).
Axes of the slice: x: 2, y: 2, z: 4, core: 2. Of those that a mesh axis runs over, the one named last changes fastest.
Arguments:
- tokens: bfloat16 [4, 1024, 2048], P('fsdp', 'ctx'), may hold values from -6 to 6
- cotangent: bfloat16 [4, 1024, 2048], P('fsdp', 'ctx'), may hold values from -6 to 6
- lengths: int32 [4], P('fsdp'), may hold values from 256 to 1024, as said below
- attn_gain: bfloat16 [2048], P('fsdp'), may hold values from 0.5 to 1.5
- w_query: bfloat16 [2048, 2048], P('fsdp'), may hold values from -0.125 to 0.125
- w_key: bfloat16 [2048, 256], P('fsdp'), may hold values from -0.125 to 0.125
- w_value: bfloat16 [2048, 256], P('fsdp'), may hold values from -0.125 to 0.125
- w_out: bfloat16 [2048, 2048], P('fsdp'), may hold values from -1 to 1
- mlp_gain: bfloat16 [2048], P('fsdp'), may hold values from 0.5 to 1.5
- w_gate: bfloat16 [2048, 5632], P('fsdp'), may hold values from -0.125 to 0.125
- w_up: bfloat16 [2048, 5632], P('fsdp'), may hold values from -0.125 to 0.125
- w_down: bfloat16 [5632, 2048], P('fsdp'), may hold values from -0.078125 to 0.078125
Outputs:
- outputs: float32 [4, 1024, 2048], P('fsdp', 'ctx')
- input_grad: float32 [4, 1024, 2048], P('fsdp', 'ctx')
- attn_gain_grad: float32 [2048], P('fsdp')
- query_grad: float32 [2048, 2048], P('fsdp')
- key_grad: float32 [2048, 256], P('fsdp')
- value_grad: float32 [2048, 256], P('fsdp')
- out_grad: float32 [2048, 2048], P('fsdp')
- mlp_gain_grad: float32 [2048], P('fsdp')
- gate_grad: float32 [2048, 5632], P('fsdp')
- up_grad: float32 [2048, 5632], P('fsdp')
- down_grad: float32 [5632, 2048], P('fsdp')
The draws below stay inside these ranges and needn't reach their ends.
Inputs may be any that keep to these rules, and one draw needn't show every extreme that they name: Each slot holds 256 to 1024 valid positions, which lie at the slot's end (rows 1024 - lengths to 1023); the rows before them are padding. One slot is full and one holds exactly 256.
All inputs are finite; a program needn't handle non-finite values.
Results may differ from the reference program's by a relative error of at most 0.024.
Values may be sent and summed in bfloat16 or wider, within the bound.
A program may use at most 512 MiB of HBM per device.

```python
import math
import jax
import jax.numpy as jnp
from jax import lax

D = 2048
HEADS = 32
KV_HEADS = 4
HEAD_DIM = 64
FF = 5632
SLOT = 1024
SEQS = 4


def draw_lengths(key, part):
    first_key, second_key = jax.random.split(jax.random.fold_in(key, 11))
    drawn = jax.random.randint(first_key, (SEQS,), SLOT // 4, SLOT + 1)
    order = jax.random.permutation(second_key, SEQS)
    drawn = jnp.where(jnp.arange(SEQS) == order[0], SLOT, drawn)
    drawn = jnp.where(jnp.arange(SEQS) == order[1], SLOT // 4, drawn)
    return drawn.astype(jnp.int32)


def steps_of(key, dims, shards, smallest, top_value):
    factor_of = 1.0
    for dim, parts in shards:
        draws = jax.random.uniform(jax.random.fold_in(jax.random.fold_in(key, 6), dim), (parts,), jnp.float32, smallest / len(shards), top_value / len(shards))
        factor_of = factor_of * jnp.repeat(jnp.exp(draws), dims[dim] // parts).reshape((-1,) + (1,) * (len(dims) - 1 - dim))
    return factor_of


def gaussian(own_key, extent, width, reach, cuts=(), kind=jnp.bfloat16):
    factor_of = steps_of(own_key, extent, cuts, -0.22, 0.18) if cuts else 1.0
    result = jax.random.normal(own_key, extent, jnp.float32) * width * factor_of
    return jnp.minimum(jnp.maximum(result, -reach), reach).astype(kind)


def setup_inputs(seed: int = 0) -> dict:
    streams_of = jax.random.split(jax.random.key(seed), 13)
    return {
        "tokens": gaussian(streams_of[0], (SEQS, SLOT, D), 1.0, 6.0, ((0, 4), (1, 8))),
        "cotangent": gaussian(streams_of[1], (SEQS, SLOT, D), 1.0, 6.0, ((0, 4), (1, 8))),
        "lengths": draw_lengths(jax.random.fold_in(streams_of[12], 71), 0),
        "attn_gain": jnp.clip(1.0 + 0.1 * jax.random.normal(streams_of[3], (D,), jnp.float32), 0.5, 1.5).astype(jnp.bfloat16),
        "w_query": gaussian(streams_of[4], (D, D), D ** -0.5, 0.125, ((0, 4),)),
        "w_key": gaussian(streams_of[5], (D, KV_HEADS * HEAD_DIM), D ** -0.5, 0.125, ((0, 4),)),
        "w_value": gaussian(streams_of[6], (D, KV_HEADS * HEAD_DIM), D ** -0.5, 0.125, ((0, 4),)),
        "w_out": gaussian(streams_of[7], (D, D), (D // 64) ** -0.5, 1.0, ((0, 4),)),
        "mlp_gain": jnp.clip(1.0 + 0.1 * jax.random.normal(streams_of[8], (D,), jnp.float32), 0.5, 1.5).astype(jnp.bfloat16),
        "w_gate": gaussian(streams_of[9], (D, FF), D ** -0.5, 0.125, ((0, 4),)),
        "w_up": gaussian(streams_of[10], (D, FF), D ** -0.5, 0.125, ((0, 4),)),
        "w_down": gaussian(streams_of[11], (FF, D), FF ** -0.5, 0.078125, ((0, 4),)),
    }


EPSILON = 1e-05
ROPE_BASE = 10000.0
MASKED = -1e+30

@jax.custom_vjp
def low(v):
    return lax.optimization_barrier(v.astype(jnp.bfloat16)).astype(jnp.float32)

@jax.custom_vjp
def low_back(v):
    return v

def low_keep(v):
    return (low(v), None)

def low_pass(kept, grad):
    return (grad,)

def back_keep(v):
    return (v, None)

def back_low(kept, grad):
    return (low(grad),)
low.defvjp(low_keep, low_pass)
low_back.defvjp(back_keep, back_low)

def product(left, right):
    return jnp.dot(left, right, precision=lax.Precision.HIGHEST, preferred_element_type=jnp.float32)

def rope_tables(positions, head_dim):
    half_dim = head_dim // 2
    frequency = jnp.power(ROPE_BASE, jnp.arange(half_dim, dtype=jnp.float32) * (-2.0 / head_dim))
    angles = positions.astype(jnp.float32)[:, None] * frequency[None, :]
    return (jnp.cos(angles), jnp.sin(angles))

def rotate(tensor, cosine, sine_table):
    half_dim = tensor.shape[-1] // 2
    leading = tensor[..., :half_dim]
    trailing = tensor[..., half_dim:]
    cosine = cosine[:, None, :]
    sine_table = sine_table[:, None, :]
    return jnp.concatenate([leading * cosine - trailing * sine_table, trailing * cosine + leading * sine_table], axis=-1)

def normalize(row_block, gain_vec):
    inverse = lax.rsqrt(lax.optimization_barrier(jnp.mean(row_block * row_block, axis=1, keepdims=True)) + EPSILON)
    return row_block * inverse * gain_vec

def layer(inputs, length, positions, cosine, sine_table, attn_gain, w_query, w_key, w_value, w_out, mlp_gain, w_gate, w_up, w_down):
    seq_len = inputs.shape[0]
    group_size = HEADS // KV_HEADS
    normed_one = low(normalize(inputs, attn_gain))
    queries = low_back(product(normed_one, w_query)).reshape(seq_len, HEADS, HEAD_DIM)
    key_rows = low_back(product(normed_one, w_key)).reshape(seq_len, KV_HEADS, HEAD_DIM)
    value_rows = low(low_back(product(normed_one, w_value))).reshape(seq_len, KV_HEADS, HEAD_DIM)
    queries = low(rotate(queries, cosine, sine_table))
    key_rows = low(rotate(key_rows, cosine, sine_table))
    block_len = math.gcd(seq_len, 512)
    query_blocks = queries.reshape(seq_len // block_len, block_len, KV_HEADS, group_size, HEAD_DIM)
    pos_blocks = positions.reshape(seq_len // block_len, block_len)

    def one_block(pair_in):
        block_queries, block_pos = pair_in
        scores = jnp.einsum('qkgd,tkd->kgqt', block_queries, key_rows, precision=lax.Precision.HIGHEST) * HEAD_DIM ** (-0.5)
        scores = low_back(scores)
        allowed = (positions[None, :] <= block_pos[:, None]) & (positions[None, :] < length)
        scores = jnp.where(allowed[None, None], scores, MASKED)
        weights = low(jax.nn.softmax(scores, axis=-1))
        return jnp.einsum('kgqt,tkd->qkgd', weights, value_rows, precision=lax.Precision.HIGHEST)
    attended = lax.map(jax.checkpoint(one_block), (query_blocks, pos_blocks))
    attended = low(low_back(attended.reshape(seq_len, HEADS * HEAD_DIM)))
    mixed = inputs + low_back(product(attended, w_out))
    normed_two = low(normalize(mixed, mlp_gain))
    gate = low_back(product(normed_two, w_gate))
    up_proj = low_back(product(normed_two, w_up))
    hidden = low(jax.nn.silu(gate) * up_proj)
    return mixed + low_back(product(hidden, w_down))

def reference(tokens, cotangent, lengths, attn_gain, w_query, w_key, w_value, w_out, mlp_gain, w_gate, w_up, w_down):
    params = tuple((weight.astype(jnp.float32) for weight in (attn_gain, w_query, w_key, w_value, w_out, mlp_gain, w_gate, w_up, w_down)))
    positions = (SLOT - 1 - jnp.arange(SLOT, dtype=jnp.int32)).astype(jnp.int32)
    cosine, sine_table = rope_tables(positions, HEAD_DIM)

    def one_sequence(totals, item):
        seq_tokens, seq_cotangent, length = item
        inputs = seq_tokens.astype(jnp.float32)
        valid = (positions < length).astype(jnp.float32)[:, None]

        def forward(layer_in, *weights):
            return layer(layer_in, length, positions, cosine, sine_table, *weights)
        outputs, pullback = jax.vjp(forward, inputs, *params)
        grads = pullback(seq_cotangent.astype(jnp.float32) * valid)
        totals = tuple((total + gradient for total, gradient in zip(totals, grads[1:])))
        return (totals, (outputs, grads[0]))
    zeros = tuple((jnp.zeros_like(weight) for weight in params))
    totals, (all_outputs, all_grads) = lax.scan(one_sequence, zeros, (tokens, cotangent, lengths))
    return (all_outputs, all_grads) + totals
```

```python
import jax
import jax.numpy as jnp
from jax import lax
from jax.experimental import pallas as pl
from jax.experimental.pallas import tpu as pltpu
from jax.sharding import Mesh
from jax.sharding import PartitionSpec as P

HEADS = 32
KV_HEADS = 4
HEAD_DIM = 64
EPSILON = 1e-05
ROPE_BASE = 10000.0
MASKED = -1e30
FAR = 1 << 30
BF = jnp.bfloat16
F32 = jnp.float32
VMEM_BYTES = 56 * 1024 * 1024


def params(**kw):
    return pltpu.CompilerParams(vmem_limit_bytes=VMEM_BYTES, **kw)


def along_plane(value, step):
    count = lax.axis_size("fsdp")
    return lax.ppermute(value, "fsdp", [(i, i ^ step) for i in range(count)])


def to_sibling(value):
    return lax.ppermute(value, "core", [(0, 1), (1, 0)])


def along_line(value, shift):
    count = lax.axis_size("z")
    return lax.ppermute(
        value, "z", [(i, i + shift) for i in range(count) if 0 <= i + shift < count]
    )


def plane_bits():
    count = lax.axis_size("fsdp")
    return [1 << b for b in range(count.bit_length() - 1)]


def plane_gather(block):
    half = block.shape[0] // 2
    parts = []
    for which, bits in ((0, plane_bits()), (1, plane_bits()[::-1])):
        held = {0: block[which * half : (which + 1) * half]}
        for bit in bits:
            order = sorted(held)
            got = along_plane(jnp.stack([held[j] for j in order]), bit)
            for n, j in enumerate(order):
                held[j ^ bit] = got[n]
        parts.append(held)
    return [jnp.concatenate([parts[0][j], parts[1][j]]) for j in range(lax.axis_size("fsdp"))]


def plane_reduce(partial):
    half = partial.shape[1] // 2
    done = []
    for which, bits in ((0, plane_bits()[::-1]), (1, plane_bits())):
        held = {j: partial[j, which * half : (which + 1) * half] for j in range(partial.shape[0])}
        for bit in bits:
            going = [j for j in sorted(held) if j & bit]
            got = along_plane(jnp.stack([held[j].astype(BF) for j in going]), bit)
            for n, j in enumerate(going):
                held[j ^ bit] = held[j ^ bit].astype(F32) + got[n].astype(F32)
                del held[j]
        done.append(held[0])
    return jnp.concatenate(done)


def line_sum(value):
    count = lax.axis_size("z")
    place = lax.axis_index("z")
    half = count // 2
    for i in range(half - 1):
        got = lax.ppermute(value, "z", [(i, i + 1), (count - 1 - i, count - 2 - i)])
        value = value + got
    value = value + lax.ppermute(value, "z", [(half - 1, half), (half, half - 1)])
    for i in range(half - 2, -1, -1):
        got = lax.ppermute(value, "z", [(i + 1, i), (count - 2 - i, count - 1 - i)])
        outer = (place == i) | (place == count - 1 - i)
        value = jnp.where(outer, got, value)
    return value


def move_kernel(idx_ref, x_ref, o_ref):
    o_ref[...] = x_ref[...]


def pick_columns(x, index, count):
    rows, width = x.shape
    size = width // count
    spec = pltpu.PrefetchScalarGridSpec(
        num_scalar_prefetch=1,
        grid=(count,),
        in_specs=[pl.BlockSpec((rows, size), lambda b, idx: (0, idx[b]))],
        out_specs=pl.BlockSpec((rows, size), lambda b, idx: (0, b)),
    )
    return pl.pallas_call(
        move_kernel,
        grid_spec=spec,
        out_shape=jax.ShapeDtypeStruct(x.shape, x.dtype),
        compiler_params=params(),
        name="pick_columns",
    )(index, x)


def put_columns(x, index, count):
    rows, width = x.shape
    size = width // count
    spec = pltpu.PrefetchScalarGridSpec(
        num_scalar_prefetch=1,
        grid=(count,),
        in_specs=[pl.BlockSpec((rows, size), lambda b, idx: (0, b))],
        out_specs=pl.BlockSpec((rows, size), lambda b, idx: (0, idx[b])),
    )
    return pl.pallas_call(
        move_kernel,
        grid_spec=spec,
        out_shape=jax.ShapeDtypeStruct(x.shape, x.dtype),
        compiler_params=params(),
        name="put_columns",
    )(index, x)


def cut_blocks(weight, f, k, count, dtype=BF):
    rows, full = weight.shape
    width, half = full // count, rows // 2
    if width % 128:
        own = lax.dynamic_slice_in_dim(weight, k * half, half, 0).reshape(half, count, width)
        return jnp.stack(
            [lax.dynamic_index_in_dim(own, f ^ j, 1, keepdims=False) for j in range(count)]
        )
    spec = pltpu.PrefetchScalarGridSpec(
        num_scalar_prefetch=1,
        grid=(count,),
        in_specs=[pl.BlockSpec((half, width), lambda j, at: (at[1], at[0] ^ j))],
        out_specs=pl.BlockSpec((None, half, width), lambda j, at: (j, 0, 0)),
    )
    return pl.pallas_call(
        move_kernel,
        grid_spec=spec,
        out_shape=jax.ShapeDtypeStruct((count, half, width), weight.dtype),
        compiler_params=params(),
        name="cut_blocks",
    )(jnp.stack([f, k]), weight)


def join_kernel(at_ref, own_ref, sib_ref, o_ref):
    @pl.when(pl.program_id(0) == 0)
    def _():
        o_ref[...] = own_ref[...].astype(o_ref.dtype)

    @pl.when(pl.program_id(0) == 1)
    def _():
        o_ref[...] = sib_ref[...].astype(o_ref.dtype)


def join_rows(own, sib, f, k):
    count, half, width = own.shape
    if width % 128:
        halves = jnp.stack([own, sib])
        return jnp.concatenate(
            [
                jnp.concatenate(
                    [
                        lax.dynamic_index_in_dim(
                            lax.dynamic_index_in_dim(halves, k ^ h, 0, keepdims=False),
                            f ^ i,
                            0,
                            keepdims=False,
                        )
                        for i in range(count)
                    ],
                    axis=1,
                )
                for h in range(2)
            ],
            axis=0,
        ).astype(F32)
    spec = pltpu.PrefetchScalarGridSpec(
        num_scalar_prefetch=1,
        grid=(2, count),
        in_specs=[
            pl.BlockSpec(
                (None, half, width),
                lambda s, i, at: (at[0] ^ jnp.where(s == 0, i, count - 1), 0, 0),
            ),
            pl.BlockSpec(
                (None, half, width), lambda s, i, at: (at[0] ^ jnp.where(s == 1, i, 0), 0, 0)
            ),
        ],
        out_specs=pl.BlockSpec((half, width), lambda s, i, at: (at[1] ^ s, i)),
    )
    return pl.pallas_call(
        join_kernel,
        grid_spec=spec,
        out_shape=jax.ShapeDtypeStruct((2 * half, count * width), F32),
        compiler_params=params(),
        name="join_rows",
    )(jnp.stack([f, k]), own, sib)


def join_columns(own, sib, k):
    rows, half = own.shape
    count = 4
    size = rows // count
    spec = pltpu.PrefetchScalarGridSpec(
        num_scalar_prefetch=1,
        grid=(2, count),
        in_specs=[
            pl.BlockSpec((size, half), lambda s, i, at: (jnp.where(s == 0, i, count - 1), 0)),
            pl.BlockSpec((size, half), lambda s, i, at: (jnp.where(s == 1, i, 0), 0)),
        ],
        out_specs=pl.BlockSpec((size, half), lambda s, i, at: (i, at[0] ^ s)),
    )
    return pl.pallas_call(
        join_kernel,
        grid_spec=spec,
        out_shape=jax.ShapeDtypeStruct((rows, 2 * half), F32),
        compiler_params=params(),
        name="join_columns",
    )(k.reshape(1), own, sib)


def swap_halves(block):
    lane = lax.broadcasted_iota(jnp.int32, block.shape, 1)
    return jnp.where(lane % 64 < 32, pltpu.roll(block, 96, 1), pltpu.roll(block, 32, 1))


def qkv_kernel(idx_ref, x_ref, gain_ref, w_ref, cos_ref, sin_ref, h_ref, q_ref, kv_ref):
    blocks = idx_ref.shape[0]
    size = x_ref.shape[1] // blocks
    x = x_ref[...].astype(F32)
    inverse = lax.rsqrt(jnp.mean(x * x, axis=1, keepdims=True) + EPSILON)
    for b in range(blocks):
        at = pl.ds(pl.multiple_of(idx_ref[b] * size, 128), size)
        part = x_ref[:, at].astype(F32) * inverse * gain_ref[:, at]
        h_ref[:, b * size : (b + 1) * size] = part.astype(BF)
    out = jnp.dot(h_ref[...], w_ref[...], preferred_element_type=F32)
    cosine, sine = cos_ref[...], sin_ref[...]
    pairs = q_ref.shape[1] // 128
    for c in range(pairs):
        block = out[:, c * 128 : (c + 1) * 128]
        q_ref[:, c * 128 : (c + 1) * 128] = (block * cosine + swap_halves(block) * sine).astype(BF)
    block = out[:, pairs * 128 :]
    lane = lax.broadcasted_iota(jnp.int32, block.shape, 1)
    turned = block * cosine + swap_halves(block) * sine
    kv_ref[...] = jnp.where(lane < 64, turned, block).astype(BF)


def qkv_project(idx, x, gain, weight, cosine, sine, rows):
    total, depth = x.shape
    width = weight.shape[1]
    spec = pltpu.PrefetchScalarGridSpec(
        num_scalar_prefetch=1,
        grid=(total // rows,),
        in_specs=[
            pl.BlockSpec((rows, depth), lambda i, idx: (i, 0)),
            pl.BlockSpec((1, depth), lambda i, idx: (0, 0)),
            pl.BlockSpec((depth, width), lambda i, idx: (0, 0)),
            pl.BlockSpec((rows, 128), lambda i, idx: (0, 0)),
            pl.BlockSpec((rows, 128), lambda i, idx: (0, 0)),
        ],
        out_specs=[
            pl.BlockSpec((rows, depth), lambda i, idx: (i, 0)),
            pl.BlockSpec((rows, width - 128), lambda i, idx: (i, 0)),
            pl.BlockSpec((rows, 128), lambda i, idx: (i, 0)),
        ],
    )
    return pl.pallas_call(
        qkv_kernel,
        grid_spec=spec,
        out_shape=[
            jax.ShapeDtypeStruct((total, depth), BF),
            jax.ShapeDtypeStruct((total, width - 128), BF),
            jax.ShapeDtypeStruct((total, 128), BF),
        ],
        compiler_params=params(),
        cost_estimate=pl.CostEstimate(
            flops=2 * total * depth * width,
            bytes_accessed=4 * total * depth + 2 * depth * width + 2 * total * width,
            transcendentals=0,
        ),
        name="qkv_project",
    )(idx, x, gain, weight, cosine, sine)


def nt(a, b):
    return lax.dot_general(a, b, (((1,), (1,)), ((), ())), preferred_element_type=F32)


def tn(a, b):
    return lax.dot_general(a, b, (((0,), (0,)), ((), ())), preferred_element_type=F32)


def nn(a, b):
    return jnp.dot(a, b, preferred_element_type=F32)


def limits(at_ref, rows):
    j = pl.program_id(0)
    place = at_ref[0] - lax.broadcasted_iota(jnp.int32, (rows, 1), 0)
    return jnp.minimum(place, at_ref[1 + j] - 1)


def attend_kernel(at_ref, q_ref, kv_ref, kp_ref, o_ref, lse_ref, vk_ref):
    rows = q_ref.shape[0]
    keys = vk_ref.shape[0]
    kv = kv_ref[...].reshape(keys, 128)

    @pl.when(pl.program_id(1) == 0)
    def _():
        vk_ref[...] = pltpu.roll(kv.astype(F32), 64, 1).astype(BF)

    vk = vk_ref[...]
    allowed = kp_ref[...] <= limits(at_ref, rows)
    lane = lax.broadcasted_iota(jnp.int32, (rows, 128), 1)
    q = q_ref[...]
    zero = jnp.zeros_like(q)
    outs, logs = [], []
    for first in (True, False):
        mine = lane < 64 if first else lane >= 64
        scores = nt(jnp.where(mine, q, zero), kv if first else vk) * (HEAD_DIM**-0.5)
        scores = jnp.where(allowed, scores, MASKED)
        top = jnp.max(scores, axis=1, keepdims=True)
        weights = jnp.exp(scores - top)
        total = jnp.sum(weights, axis=1, keepdims=True)
        outs.append(nn(weights.astype(BF), vk if first else kv) / total)
        logs.append(jnp.broadcast_to(top + jnp.log(total), (rows, 128)))
    o_ref[...] = jnp.where(lane < 64, outs[0], outs[1]).astype(BF)
    lse_ref[...] = jnp.where(lane < 64, logs[0], logs[1])


def attend(at, q, kv, kp):
    chunks, seqs, rows, _ = kv.shape
    pairs = q.shape[2] // 128
    keys = chunks * rows
    spec = pltpu.PrefetchScalarGridSpec(
        num_scalar_prefetch=1,
        grid=(seqs, pairs),
        in_specs=[
            pl.BlockSpec((None, rows, 128), lambda j, p, at: (j, 0, p)),
            pl.BlockSpec((chunks, None, rows, 128), lambda j, p, at: (0, j, 0, 0)),
            pl.BlockSpec((1, keys), lambda j, p, at: (0, 0)),
        ],
        out_specs=[
            pl.BlockSpec((None, rows, 128), lambda j, p, at: (j, 0, p)),
            pl.BlockSpec((None, rows, 128), lambda j, p, at: (j, 0, p)),
        ],
        scratch_shapes=[pltpu.VMEM((keys, 128), BF)],
    )
    size = seqs * pairs * 2 * rows * keys
    return pl.pallas_call(
        attend_kernel,
        grid_spec=spec,
        out_shape=[
            jax.ShapeDtypeStruct(q.shape, BF),
            jax.ShapeDtypeStruct(q.shape, F32),
        ],
        compiler_params=params(),
        cost_estimate=pl.CostEstimate(
            flops=size * 4 * 128, bytes_accessed=4 << 20, transcendentals=size
        ),
        name="attend",
    )(at, q, kv, kp)


def attend_back_kernel(
    at_ref, q_ref, do_ref, lse_ref, kv_ref, kp_ref, cos_ref, sin_ref, dq_ref, dkv_ref, vk_ref, dk_ref, dv_ref
):
    rows = q_ref.shape[0]
    keys = vk_ref.shape[0]
    pair = pl.program_id(1)
    kv = kv_ref[...].reshape(keys, 128)

    @pl.when(pair == 0)
    def _():
        vk_ref[...] = pltpu.roll(kv.astype(F32), 64, 1).astype(BF)
        dk_ref[...] = jnp.zeros_like(dk_ref)
        dv_ref[...] = jnp.zeros_like(dv_ref)

    vk = vk_ref[...]
    allowed = kp_ref[...] <= limits(at_ref, rows)
    lane = lax.broadcasted_iota(jnp.int32, (rows, 128), 1)
    q, do = q_ref[...], do_ref[...]
    zero = jnp.zeros_like(q)
    parts = []
    for first in (True, False):
        mine = lane < 64 if first else lane >= 64
        keyed, valued = (kv, vk) if first else (vk, kv)
        q_own, do_own = jnp.where(mine, q, zero), jnp.where(mine, do, zero)
        scores = nt(q_own, keyed) * (HEAD_DIM**-0.5)
        log_total = lse_ref[:, 0:1] if first else lse_ref[:, 64:65]
        weights = jnp.where(allowed, jnp.exp(scores - log_total), 0.0)
        joint = weights * nt(do_own, valued)
        back = (joint - weights * jnp.sum(joint, axis=1, keepdims=True)).astype(BF)
        parts.append(nn(back, keyed))
        dk_ref[...] += tn(back, q_own)
        dv_ref[...] += tn(weights.astype(BF), do_own)
    turned = jnp.where(lane < 64, parts[0], parts[1]) * (HEAD_DIM**-0.5)
    dq_ref[...] = (turned * cos_ref[...] - swap_halves(turned) * sin_ref[...]).astype(BF)

    @pl.when(pair == pl.num_programs(1) - 1)
    def _():
        dk = dk_ref[...]
        dv = dv_ref[...]
        dk = (dk + pltpu.roll(dk, 64, 1)) * (HEAD_DIM**-0.5)
        dv = dv + pltpu.roll(dv, 64, 1)
        wide = lax.broadcasted_iota(jnp.int32, dk.shape, 1)
        dkv_ref[...] = jnp.where(wide < 64, dk, dv).astype(BF).reshape(dkv_ref.shape)


def attend_back(at, q, do, lse, kv, kp, cosine, sine):
    chunks, seqs, rows, _ = kv.shape
    pairs = q.shape[2] // 128
    keys = chunks * rows
    tall = pl.BlockSpec((None, rows, 128), lambda j, p, at: (j, 0, p))
    whole = pl.BlockSpec((chunks, None, rows, 128), lambda j, p, at: (0, j, 0, 0))
    flat = pl.BlockSpec((rows, 128), lambda j, p, at: (0, 0))
    spec = pltpu.PrefetchScalarGridSpec(
        num_scalar_prefetch=1,
        grid=(seqs, pairs),
        in_specs=[tall, tall, tall, whole, pl.BlockSpec((1, keys), lambda j, p, at: (0, 0)), flat, flat],
        out_specs=[tall, whole],
        scratch_shapes=[
            pltpu.VMEM((keys, 128), BF),
            pltpu.VMEM((keys, 128), F32),
            pltpu.VMEM((keys, 128), F32),
        ],
    )
    size = seqs * pairs * 2 * rows * keys
    return pl.pallas_call(
        attend_back_kernel,
        grid_spec=spec,
        out_shape=[
            jax.ShapeDtypeStruct(q.shape, BF),
            jax.ShapeDtypeStruct(kv.shape, BF),
        ],
        compiler_params=params(),
        cost_estimate=pl.CostEstimate(
            flops=size * 10 * 128, bytes_accessed=8 << 20, transcendentals=size
        ),
        name="attend_back",
    )(at, q, do, lse, kv, kp, cosine, sine)


def rms_backward(row_block, inverse, gain_vec, gradient):
    normed = row_block * inverse
    gain_grad = jnp.sum(gradient * normed, axis=0)
    scaled = gradient * gain_vec
    back = inverse * (scaled - normed * jnp.mean(scaled * normed, axis=1, keepdims=True))
    return (back, gain_grad)


def body(
    tokens, cotangent, lengths, attn_gain, w_query, w_key, w_value, w_out, mlp_gain, w_gate, w_up, w_down
):
    seqs, rows, depth = tokens.shape
    count, line = lax.axis_size("fsdp"), lax.axis_size("z")
    f, z, k = lax.axis_index("fsdp"), lax.axis_index("z"), lax.axis_index("core")
    slot = rows * line * 2
    total = count * rows
    slab = depth // count
    half = slab // 2
    q_width = HEADS * HEAD_DIM // count
    shared = max(1, count // KV_HEADS)

    x_own = tokens.reshape(rows, depth)
    chunk = 2 * z + k
    first_pos = slot - 1 - chunk * rows

    length = lengths[0]
    words = jnp.zeros((slab,), F32).at[0].set((length // 64).astype(F32)).at[1].set((length % 64).astype(F32))
    note = jnp.stack([attn_gain, mlp_gain, words.astype(BF), jnp.zeros((slab,), BF)])
    notes = [note] + [along_plane(note, j) for j in range(1, count)]
    notes_abs = [lax.dynamic_index_in_dim(jnp.stack(notes), f ^ i, 0, keepdims=False) for i in range(count)]
    gain_one = jnp.concatenate([n[0] for n in notes_abs]).astype(F32).reshape(1, depth)
    gain_two = jnp.concatenate([n[1] for n in notes_abs]).astype(F32).reshape(1, depth)
    all_lengths = jnp.stack(
        [n[2, 0].astype(jnp.int32) * 64 + n[2, 1].astype(jnp.int32) for n in notes]
    )

    x_all = jnp.concatenate(plane_gather(x_own))

    wq = cut_blocks(w_query, f, k, count)
    key_cols = lax.dynamic_slice_in_dim(w_key, k * half, half, 0).reshape(half, KV_HEADS, HEAD_DIM)
    value_cols = lax.dynamic_slice_in_dim(w_value, k * half, half, 0).reshape(half, KV_HEADS, HEAD_DIM)

    def head_of(j):
        return (f ^ j) // shared

    wkv = jnp.stack(
        [
            jnp.concatenate(
                [
                    lax.dynamic_index_in_dim(key_cols, head_of(j), 1, keepdims=False),
                    lax.dynamic_index_in_dim(value_cols, head_of(j), 1, keepdims=False),
                ],
                axis=1,
            )
            for j in range(count)
        ]
    )
    wqkv = jnp.concatenate([wq, wkv], axis=2)
    wqkv_own = jnp.stack([wqkv[0]] + [along_plane(wqkv[j], j) for j in range(1, count)])
    wqkv_sib = to_sibling(wqkv_own)
    wqkv_all = jnp.concatenate([wqkv_own, wqkv_sib]).reshape(depth, q_width + 128)

    def fetch(weight):
        cut = cut_blocks(weight, f, k, count)
        width = cut.shape[2]
        own = jnp.stack([cut[0]] + [along_plane(cut[j], j) for j in range(1, count)])
        sib = to_sibling(own)
        return own.reshape(depth // 2, width), sib.reshape(depth // 2, width)

    gate_own, gate_sib = fetch(w_gate)
    up_own, up_sib = fetch(w_up)

    order = jnp.stack([(f ^ j) * 2 + (k ^ h) for h in range(2) for j in range(count)]).astype(jnp.int32)

    half_dim = HEAD_DIM // 2
    frequency = jnp.power(ROPE_BASE, jnp.arange(half_dim, dtype=F32) * (-2.0 / HEAD_DIM))
    positions = first_pos - jnp.arange(rows, dtype=jnp.int32)
    angles = positions.astype(F32)[:, None] * frequency[None, :]
    cos32, sin32 = jnp.cos(angles), jnp.sin(angles)
    cosine = jnp.concatenate([cos32] * 4, axis=1)
    sine = jnp.concatenate([-sin32, sin32, -sin32, sin32], axis=1)

    normed_one, queries, kv = qkv_project(order, x_all, gain_one, wqkv_all, cosine, sine, rows)
    queries = queries.reshape(count, rows, q_width)
    kv = kv.reshape(count, rows, 128)

    mine = [kv] + [along_line(kv, -s) for s in range(1, line)]
    mine = jnp.stack(mine)
    kv_all = jnp.concatenate([mine, to_sibling(mine)])
    places = []
    for h in range(2):
        for s in range(line):
            start = slot - 1 - (2 * (z + s) + (k ^ h)) * rows
            places.append(start - jnp.arange(rows, dtype=jnp.int32))
    kp = jnp.concatenate(places)
    kp = jnp.where(kp < 0, FAR, kp).reshape(1, -1)
    at = jnp.concatenate([first_pos.reshape(1), all_lengths]).astype(jnp.int32)

    attended, log_total = attend(at, queries, kv_all, kp)
    attended = attended.reshape(total, q_width)

    mixed_part = nn(attended, w_out).astype(BF).reshape(count, rows, depth)
    inputs = x_own.astype(F32)
    mixed = inputs + plane_reduce(mixed_part)
    inv_two = lax.rsqrt(jnp.mean(mixed * mixed, axis=1, keepdims=True) + EPSILON)
    normed_two_own = (mixed * inv_two * gain_two).astype(BF)
    normed_two = jnp.concatenate(plane_gather(normed_two_own))
    normed_two = pick_columns(normed_two, order, 2 * count)
    n2_own, n2_sib = normed_two[:, : depth // 2], normed_two[:, depth // 2 :]

    valid = (positions < length).astype(F32)[:, None]
    out_back = cotangent.reshape(rows, depth).astype(F32) * valid
    branch_own = out_back.astype(BF)
    branch = jnp.concatenate(plane_gather(branch_own))

    gate = nn(n2_own, gate_own) + nn(n2_sib, gate_sib)
    up = nn(n2_own, up_own) + nn(n2_sib, up_sib)
    sigmoid = jax.nn.sigmoid(gate)
    hidden = (gate * sigmoid * up).astype(BF)

    half_depth = depth // 2
    branch_mine = lax.dynamic_slice_in_dim(branch, k * half_depth, half_depth, 1)
    branch_other = lax.dynamic_slice_in_dim(branch, (1 - k) * half_depth, half_depth, 1)

    def pair_sum(own, other):
        return (own + to_sibling(other.astype(BF)).astype(F32)).astype(BF)

    def swap_slabs(own):
        return jnp.stack([own[0]] + [along_plane(own[j], j) for j in range(1, count)])

    down_half = line_sum(pair_sum(tn(hidden, branch_mine), tn(hidden, branch_other)))
    down_grad = join_columns(down_half, to_sibling(down_half), k)

    hidden_grad = nt(branch, w_down)
    gate_back = (hidden_grad * up * sigmoid * (1.0 + gate * (1.0 - sigmoid))).astype(BF)
    up_back = (hidden_grad * gate * sigmoid).astype(BF)

    def slab_grad(left_own, left_other, right):
        width = right.shape[1]
        own = pair_sum(tn(left_own, right), tn(left_other, right)).reshape(count, half, width)
        return line_sum(swap_slabs(own))

    gate_half = slab_grad(n2_own, n2_sib, gate_back)
    gate_grad = join_rows(gate_half, to_sibling(gate_half), f, k)
    up_half = slab_grad(n2_own, n2_sib, up_back)
    up_grad = join_rows(up_half, to_sibling(up_half), f, k)

    back_own = (nt(gate_back, gate_own) + nt(up_back, up_own)).astype(BF)
    back_sib = (nt(gate_back, gate_sib) + nt(up_back, up_sib)).astype(BF)
    normed_back = put_columns(jnp.concatenate([back_own, back_sib], axis=1), order, 2 * count)
    normed_back = plane_reduce(normed_back.reshape(count, rows, depth))

    out_part = nn(hidden, w_down).astype(BF).reshape(count, rows, depth)
    outputs = mixed + plane_reduce(out_part)

    mixed_back, gain_two_grad = rms_backward(mixed, inv_two, gain_two, normed_back)
    mixed_grad = out_back + mixed_back
    attn_back = jnp.concatenate(plane_gather(mixed_grad.astype(BF)))
    attended_grad = nt(attn_back, w_out).astype(BF).reshape(count, rows, q_width)

    back_mine = lax.dynamic_slice_in_dim(attn_back, k * half_depth, half_depth, 1)
    back_other = lax.dynamic_slice_in_dim(attn_back, (1 - k) * half_depth, half_depth, 1)
    out_half = line_sum(pair_sum(tn(attended, back_mine), tn(attended, back_other)))
    out_grad = join_columns(out_half, to_sibling(out_half), k)

    query_back, kv_part = attend_back(at, queries, attended_grad, log_total, kv_all, kp, cosine, sine)
    kv_mine = kv_part[:line].astype(F32) + to_sibling(kv_part[line:]).astype(F32)
    kv_back = kv_mine[0]
    for s in range(1, line):
        kv_back = kv_back + along_line(kv_mine[s].astype(BF), s).astype(F32)
    lead, trail, flat = kv_back[..., :32], kv_back[..., 32:64], kv_back[..., 64:]
    kv_back = jnp.concatenate(
        [lead * cos32 + trail * sin32, trail * cos32 - lead * sin32, flat], axis=-1
    ).astype(BF)
    qkv_back = jnp.concatenate(
        [query_back.reshape(total, q_width), kv_back.reshape(total, 128)], axis=1
    )

    normed_one_back = nt(qkv_back, wqkv_all).astype(BF)
    normed_one_back = put_columns(normed_one_back, order, 2 * count)
    normed_one_back = plane_reduce(normed_one_back.reshape(count, rows, depth))
    inv_one = lax.rsqrt(jnp.mean(inputs * inputs, axis=1, keepdims=True) + EPSILON)
    input_back, gain_one_grad = rms_backward(inputs, inv_one, gain_one, normed_one_back)
    input_grad = mixed_grad + input_back

    n1_own, n1_sib = normed_one[:, :half_depth], normed_one[:, half_depth:]
    qkv_own = pair_sum(tn(n1_own, qkv_back), tn(n1_sib, qkv_back)).reshape(count, half, q_width + 128)
    gains = jnp.stack([gain_one_grad, gain_two_grad]).reshape(2, count, slab)
    gains = jnp.stack(
        [lax.dynamic_index_in_dim(gains, f ^ j, 1, keepdims=False) for j in range(count)]
    ).astype(BF)
    gains = line_sum(swap_slabs(gains))
    qkv_half = line_sum(swap_slabs(qkv_own))
    gains = jnp.sum(gains.astype(F32), axis=0) + jnp.sum(to_sibling(gains).astype(F32), axis=0)
    qkv_other = to_sibling(qkv_half)
    query_grad = join_rows(qkv_half[:, :, :q_width], qkv_other[:, :, :q_width], f, k)
    halves = jnp.stack([qkv_half[:, :, q_width:], qkv_other[:, :, q_width:]])

    def by_head(lo, hi):
        both = [lax.dynamic_index_in_dim(halves, k ^ h, 0, keepdims=False) for h in range(2)]
        both = jnp.concatenate(both, axis=1).astype(F32)[:, :, lo:hi]
        cols = jnp.stack([lax.dynamic_index_in_dim(both, f ^ i, 0, keepdims=False) for i in range(count)])
        cols = cols.reshape(KV_HEADS, shared, slab, HEAD_DIM).sum(1)
        return jnp.transpose(cols, (1, 0, 2)).reshape(slab, KV_HEADS * HEAD_DIM)

    key_grad = by_head(0, 64)
    value_grad = by_head(64, 128)

    return (
        outputs.reshape(seqs, rows, depth),
        input_grad.reshape(seqs, rows, depth),
        gains[0],
        query_grad,
        key_grad,
        value_grad,
        out_grad,
        gains[1],
        gate_grad,
        up_grad,
        down_grad,
    )


def solution(mesh):
    count, ctx = mesh.shape["fsdp"], mesh.shape["ctx"]
    split = Mesh(mesh.devices.reshape(count, ctx // 2, 2), ("fsdp", "z", "core"))
    act = P("fsdp", ("z", "core"), None)
    row, mat = P("fsdp"), P("fsdp", None)
    return jax.shard_map(
        body,
        mesh=split,
        in_specs=(act, act, row, row, mat, mat, mat, mat, row, mat, mat, mat),
        out_specs=(act, act, row, mat, mat, mat, mat, row, mat, mat, mat),
        check_vma=False,
    )
```

```python
import functools

import jax
import jax.numpy as jnp
from jax import lax
from jax.experimental import pallas as pl
from jax.experimental.pallas import tpu as pltpu
from jax.sharding import Mesh
from jax.sharding import PartitionSpec as P

HEADS = 32
KV_HEADS = 4
HEAD_DIM = 64
EPSILON = 1e-05
ROPE_BASE = 10000.0
MASKED = -1e30
FAR = 1 << 30
BF = jnp.bfloat16
F32 = jnp.float32
VMEM_BYTES = 56 * 1024 * 1024


def params(**kw):
    return pltpu.CompilerParams(vmem_limit_bytes=VMEM_BYTES, **kw)


def along_plane(value, step):
    count = lax.axis_size("fsdp")
    return lax.ppermute(value, "fsdp", [(i, i ^ step) for i in range(count)])


def to_sibling(value):
    return lax.ppermute(value, "core", [(0, 1), (1, 0)])


def along_line(value, shift):
    count = lax.axis_size("z")
    return lax.ppermute(
        value, "z", [(i, i + shift) for i in range(count) if 0 <= i + shift < count]
    )


def plane_bits():
    count = lax.axis_size("fsdp")
    return [1 << b for b in range(count.bit_length() - 1)]


def plane_gather(block):
    half = block.shape[0] // 2
    parts = []
    for which, bits in ((0, plane_bits()), (1, plane_bits()[::-1])):
        held = {0: block[which * half : (which + 1) * half]}
        for bit in bits:
            order = sorted(held)
            got = along_plane(jnp.stack([held[j] for j in order]), bit)
            for n, j in enumerate(order):
                held[j ^ bit] = got[n]
        parts.append(held)
    return [jnp.concatenate([parts[0][j], parts[1][j]]) for j in range(lax.axis_size("fsdp"))]


def plane_reduce(partial):
    half = partial.shape[1] // 2
    done = []
    for which, bits in ((0, plane_bits()[::-1]), (1, plane_bits())):
        held = {j: partial[j, which * half : (which + 1) * half] for j in range(partial.shape[0])}
        for bit in bits:
            going = [j for j in sorted(held) if j & bit]
            got = along_plane(jnp.stack([held[j].astype(BF) for j in going]), bit)
            for n, j in enumerate(going):
                held[j ^ bit] = held[j ^ bit].astype(F32) + got[n].astype(F32)
                del held[j]
        done.append(held[0])
    return jnp.concatenate(done)


def line_sum(value):
    count = lax.axis_size("z")
    place = lax.axis_index("z")
    half = count // 2
    for i in range(half - 1):
        got = lax.ppermute(value, "z", [(i, i + 1), (count - 1 - i, count - 2 - i)])
        value = value + got
    value = value + lax.ppermute(value, "z", [(half - 1, half), (half, half - 1)])
    for i in range(half - 2, -1, -1):
        got = lax.ppermute(value, "z", [(i + 1, i), (count - 2 - i, count - 1 - i)])
        outer = (place == i) | (place == count - 1 - i)
        value = jnp.where(outer, got, value)
    return value


def move_kernel(idx_ref, x_ref, o_ref):
    o_ref[...] = x_ref[...]


def pick_columns(x, index, count):
    rows, width = x.shape
    size = width // count
    spec = pltpu.PrefetchScalarGridSpec(
        num_scalar_prefetch=1,
        grid=(count,),
        in_specs=[pl.BlockSpec((rows, size), lambda b, idx: (0, idx[b]))],
        out_specs=pl.BlockSpec((rows, size), lambda b, idx: (0, b)),
    )
    return pl.pallas_call(
        move_kernel,
        grid_spec=spec,
        out_shape=jax.ShapeDtypeStruct(x.shape, x.dtype),
        compiler_params=params(),
        name="pick_columns",
    )(index, x)


def put_columns(x, index, count):
    rows, width = x.shape
    size = width // count
    spec = pltpu.PrefetchScalarGridSpec(
        num_scalar_prefetch=1,
        grid=(count,),
        in_specs=[pl.BlockSpec((rows, size), lambda b, idx: (0, b))],
        out_specs=pl.BlockSpec((rows, size), lambda b, idx: (0, idx[b])),
    )
    return pl.pallas_call(
        move_kernel,
        grid_spec=spec,
        out_shape=jax.ShapeDtypeStruct(x.shape, x.dtype),
        compiler_params=params(),
        name="put_columns",
    )(index, x)


def cut_blocks(weight, f, k, count, dtype=BF):
    rows, full = weight.shape
    width, half = full // count, rows // 2
    if width % 128:
        own = lax.dynamic_slice_in_dim(weight, k * half, half, 0).reshape(half, count, width)
        return jnp.stack(
            [lax.dynamic_index_in_dim(own, f ^ j, 1, keepdims=False) for j in range(count)]
        )
    spec = pltpu.PrefetchScalarGridSpec(
        num_scalar_prefetch=1,
        grid=(count,),
        in_specs=[pl.BlockSpec((half, width), lambda j, at: (at[1], at[0] ^ j))],
        out_specs=pl.BlockSpec((None, half, width), lambda j, at: (j, 0, 0)),
    )
    return pl.pallas_call(
        move_kernel,
        grid_spec=spec,
        out_shape=jax.ShapeDtypeStruct((count, half, width), weight.dtype),
        compiler_params=params(),
        name="cut_blocks",
    )(jnp.stack([f, k]), weight)


def join_kernel(at_ref, own_ref, sib_ref, o_ref):
    @pl.when(pl.program_id(0) == 0)
    def _():
        o_ref[...] = own_ref[...].astype(o_ref.dtype)

    @pl.when(pl.program_id(0) == 1)
    def _():
        o_ref[...] = sib_ref[...].astype(o_ref.dtype)


def join_rows(own, sib, f, k):
    count, half, width = own.shape
    if width % 128:
        halves = jnp.stack([own, sib])
        return jnp.concatenate(
            [
                jnp.concatenate(
                    [
                        lax.dynamic_index_in_dim(
                            lax.dynamic_index_in_dim(halves, k ^ h, 0, keepdims=False),
                            f ^ i,
                            0,
                            keepdims=False,
                        )
                        for i in range(count)
                    ],
                    axis=1,
                )
                for h in range(2)
            ],
            axis=0,
        ).astype(F32)
    spec = pltpu.PrefetchScalarGridSpec(
        num_scalar_prefetch=1,
        grid=(2, count),
        in_specs=[
            pl.BlockSpec(
                (None, half, width),
                lambda s, i, at: (at[0] ^ jnp.where(s == 0, i, count - 1), 0, 0),
            ),
            pl.BlockSpec(
                (None, half, width), lambda s, i, at: (at[0] ^ jnp.where(s == 1, i, 0), 0, 0)
            ),
        ],
        out_specs=pl.BlockSpec((half, width), lambda s, i, at: (at[1] ^ s, i)),
    )
    return pl.pallas_call(
        join_kernel,
        grid_spec=spec,
        out_shape=jax.ShapeDtypeStruct((2 * half, count * width), F32),
        compiler_params=params(),
        name="join_rows",
    )(jnp.stack([f, k]), own, sib)


def join_columns(own, sib, k):
    rows, half = own.shape
    count = 4
    size = rows // count
    spec = pltpu.PrefetchScalarGridSpec(
        num_scalar_prefetch=1,
        grid=(2, count),
        in_specs=[
            pl.BlockSpec((size, half), lambda s, i, at: (jnp.where(s == 0, i, count - 1), 0)),
            pl.BlockSpec((size, half), lambda s, i, at: (jnp.where(s == 1, i, 0), 0)),
        ],
        out_specs=pl.BlockSpec((size, half), lambda s, i, at: (i, at[0] ^ s)),
    )
    return pl.pallas_call(
        join_kernel,
        grid_spec=spec,
        out_shape=jax.ShapeDtypeStruct((rows, 2 * half), F32),
        compiler_params=params(),
        name="join_columns",
    )(k.reshape(1), own, sib)


def swap_halves(block):
    lane = lax.broadcasted_iota(jnp.int32, block.shape, 1)
    return jnp.where(lane % 64 < 32, pltpu.roll(block, 96, 1), pltpu.roll(block, 32, 1))


def qkv_kernel(idx_ref, x_ref, gain_ref, w_ref, cos_ref, sin_ref, h_ref, q_ref, kv_ref):
    blocks = idx_ref.shape[0]
    size = x_ref.shape[1] // blocks
    x = x_ref[...].astype(F32)
    inverse = lax.rsqrt(jnp.mean(x * x, axis=1, keepdims=True) + EPSILON)
    for b in range(blocks):
        at = pl.ds(pl.multiple_of(idx_ref[b] * size, 128), size)
        part = x_ref[:, at].astype(F32) * inverse * gain_ref[:, at]
        h_ref[:, b * size : (b + 1) * size] = part.astype(BF)
    out = jnp.dot(h_ref[...], w_ref[...], preferred_element_type=F32)
    cosine, sine = cos_ref[...], sin_ref[...]
    pairs = q_ref.shape[1] // 128
    for c in range(pairs):
        block = out[:, c * 128 : (c + 1) * 128]
        q_ref[:, c * 128 : (c + 1) * 128] = (block * cosine + swap_halves(block) * sine).astype(BF)
    block = out[:, pairs * 128 :]
    lane = lax.broadcasted_iota(jnp.int32, block.shape, 1)
    turned = block * cosine + swap_halves(block) * sine
    kv_ref[...] = jnp.where(lane < 64, turned, block).astype(BF)


def qkv_project(idx, x, gain, weight, cosine, sine, rows):
    total, depth = x.shape
    width = weight.shape[1]
    spec = pltpu.PrefetchScalarGridSpec(
        num_scalar_prefetch=1,
        grid=(total // rows,),
        in_specs=[
            pl.BlockSpec((rows, depth), lambda i, idx: (i, 0)),
            pl.BlockSpec((1, depth), lambda i, idx: (0, 0)),
            pl.BlockSpec((depth, width), lambda i, idx: (0, 0)),
            pl.BlockSpec((rows, 128), lambda i, idx: (0, 0)),
            pl.BlockSpec((rows, 128), lambda i, idx: (0, 0)),
        ],
        out_specs=[
            pl.BlockSpec((rows, depth), lambda i, idx: (i, 0)),
            pl.BlockSpec((rows, width - 128), lambda i, idx: (i, 0)),
            pl.BlockSpec((rows, 128), lambda i, idx: (i, 0)),
        ],
    )
    return pl.pallas_call(
        qkv_kernel,
        grid_spec=spec,
        out_shape=[
            jax.ShapeDtypeStruct((total, depth), BF),
            jax.ShapeDtypeStruct((total, width - 128), BF),
            jax.ShapeDtypeStruct((total, 128), BF),
        ],
        compiler_params=params(),
        cost_estimate=pl.CostEstimate(
            flops=2 * total * depth * width,
            bytes_accessed=4 * total * depth + 2 * depth * width + 2 * total * width,
            transcendentals=0,
        ),
        name="qkv_project",
    )(idx, x, gain, weight, cosine, sine)


def nt(a, b):
    return lax.dot_general(a, b, (((1,), (1,)), ((), ())), preferred_element_type=F32)


def tn(a, b):
    return lax.dot_general(a, b, (((0,), (0,)), ((), ())), preferred_element_type=F32)


def nn(a, b):
    return jnp.dot(a, b, preferred_element_type=F32)


def limits(at_ref, rows):
    j = pl.program_id(0)
    place = at_ref[0] - lax.broadcasted_iota(jnp.int32, (rows, 1), 0)
    return jnp.minimum(place, at_ref[1 + j] - 1)


def attend_kernel(at_ref, q_ref, kv_ref, kp_ref, o_ref, lse_ref, vk_ref):
    rows = q_ref.shape[0]
    keys = vk_ref.shape[0]
    kv = kv_ref[...].reshape(keys, 128)

    @pl.when(pl.program_id(1) == 0)
    def _():
        vk_ref[...] = pltpu.roll(kv.astype(F32), 64, 1).astype(BF)

    vk = vk_ref[...]
    allowed = kp_ref[...] <= limits(at_ref, rows)
    lane = lax.broadcasted_iota(jnp.int32, (rows, 128), 1)
    q = q_ref[...]
    zero = jnp.zeros_like(q)
    outs, logs = [], []
    for first in (True, False):
        mine = lane < 64 if first else lane >= 64
        scores = nt(jnp.where(mine, q, zero), kv if first else vk) * (HEAD_DIM**-0.5)
        scores = jnp.where(allowed, scores, MASKED)
        top = jnp.max(scores, axis=1, keepdims=True)
        weights = jnp.exp(scores - top)
        total = jnp.sum(weights, axis=1, keepdims=True)
        outs.append(nn(weights.astype(BF), vk if first else kv) / total)
        logs.append(jnp.broadcast_to(top + jnp.log(total), (rows, 128)))
    o_ref[...] = jnp.where(lane < 64, outs[0], outs[1]).astype(BF)
    lse_ref[...] = jnp.where(lane < 64, logs[0], logs[1])


def attend(at, q, kv, kp):
    chunks, seqs, rows, _ = kv.shape
    pairs = q.shape[2] // 128
    keys = chunks * rows
    spec = pltpu.PrefetchScalarGridSpec(
        num_scalar_prefetch=1,
        grid=(seqs, pairs),
        in_specs=[
            pl.BlockSpec((None, rows, 128), lambda j, p, at: (j, 0, p)),
            pl.BlockSpec((chunks, None, rows, 128), lambda j, p, at: (0, j, 0, 0)),
            pl.BlockSpec((1, keys), lambda j, p, at: (0, 0)),
        ],
        out_specs=[
            pl.BlockSpec((None, rows, 128), lambda j, p, at: (j, 0, p)),
            pl.BlockSpec((None, rows, 128), lambda j, p, at: (j, 0, p)),
        ],
        scratch_shapes=[pltpu.VMEM((keys, 128), BF)],
    )
    size = seqs * pairs * 2 * rows * keys
    return pl.pallas_call(
        attend_kernel,
        grid_spec=spec,
        out_shape=[
            jax.ShapeDtypeStruct(q.shape, BF),
            jax.ShapeDtypeStruct(q.shape, F32),
        ],
        compiler_params=params(),
        cost_estimate=pl.CostEstimate(
            flops=size * 4 * 128, bytes_accessed=4 << 20, transcendentals=size
        ),
        name="attend",
    )(at, q, kv, kp)


def attend_back_kernel(
    at_ref, q_ref, do_ref, lse_ref, kv_ref, kp_ref, cos_ref, sin_ref, dq_ref, dkv_ref, vk_ref, dk_ref, dv_ref
):
    rows = q_ref.shape[0]
    keys = vk_ref.shape[0]
    pair = pl.program_id(1)
    kv = kv_ref[...].reshape(keys, 128)

    @pl.when(pair == 0)
    def _():
        vk_ref[...] = pltpu.roll(kv.astype(F32), 64, 1).astype(BF)
        dk_ref[...] = jnp.zeros_like(dk_ref)
        dv_ref[...] = jnp.zeros_like(dv_ref)

    vk = vk_ref[...]
    allowed = kp_ref[...] <= limits(at_ref, rows)
    lane = lax.broadcasted_iota(jnp.int32, (rows, 128), 1)
    q, do = q_ref[...], do_ref[...]
    zero = jnp.zeros_like(q)
    parts = []
    for first in (True, False):
        mine = lane < 64 if first else lane >= 64
        keyed, valued = (kv, vk) if first else (vk, kv)
        q_own, do_own = jnp.where(mine, q, zero), jnp.where(mine, do, zero)
        scores = nt(q_own, keyed) * (HEAD_DIM**-0.5)
        log_total = lse_ref[:, 0:1] if first else lse_ref[:, 64:65]
        weights = jnp.where(allowed, jnp.exp(scores - log_total), 0.0)
        joint = weights * nt(do_own, valued)
        back = (joint - weights * jnp.sum(joint, axis=1, keepdims=True)).astype(BF)
        parts.append(nn(back, keyed))
        dk_ref[...] += tn(back, q_own)
        dv_ref[...] += tn(weights.astype(BF), do_own)
    turned = jnp.where(lane < 64, parts[0], parts[1]) * (HEAD_DIM**-0.5)
    dq_ref[...] = (turned * cos_ref[...] - swap_halves(turned) * sin_ref[...]).astype(BF)

    @pl.when(pair == pl.num_programs(1) - 1)
    def _():
        dk = dk_ref[...]
        dv = dv_ref[...]
        dk = (dk + pltpu.roll(dk, 64, 1)) * (HEAD_DIM**-0.5)
        dv = dv + pltpu.roll(dv, 64, 1)
        wide = lax.broadcasted_iota(jnp.int32, dk.shape, 1)
        dkv_ref[...] = jnp.where(wide < 64, dk, dv).astype(BF).reshape(dkv_ref.shape)


def attend_back(at, q, do, lse, kv, kp, cosine, sine):
    chunks, seqs, rows, _ = kv.shape
    pairs = q.shape[2] // 128
    keys = chunks * rows
    tall = pl.BlockSpec((None, rows, 128), lambda j, p, at: (j, 0, p))
    whole = pl.BlockSpec((chunks, None, rows, 128), lambda j, p, at: (0, j, 0, 0))
    flat = pl.BlockSpec((rows, 128), lambda j, p, at: (0, 0))
    spec = pltpu.PrefetchScalarGridSpec(
        num_scalar_prefetch=1,
        grid=(seqs, pairs),
        in_specs=[tall, tall, tall, whole, pl.BlockSpec((1, keys), lambda j, p, at: (0, 0)), flat, flat],
        out_specs=[tall, whole],
        scratch_shapes=[
            pltpu.VMEM((keys, 128), BF),
            pltpu.VMEM((keys, 128), F32),
            pltpu.VMEM((keys, 128), F32),
        ],
    )
    size = seqs * pairs * 2 * rows * keys
    return pl.pallas_call(
        attend_back_kernel,
        grid_spec=spec,
        out_shape=[
            jax.ShapeDtypeStruct(q.shape, BF),
            jax.ShapeDtypeStruct(kv.shape, BF),
        ],
        compiler_params=params(),
        cost_estimate=pl.CostEstimate(
            flops=size * 10 * 128, bytes_accessed=8 << 20, transcendentals=size
        ),
        name="attend_back",
    )(at, q, do, lse, kv, kp, cosine, sine)


def add_into(target, other):
    @pl.loop(0, target.shape[0] // 16)
    def _(i):
        at = pl.ds(pl.multiple_of(i * 16, 16), 16)
        target[at, :] = (target[at, :].astype(F32) + other[at, :].astype(F32)).astype(BF)


def sums_kernel(plan, *refs):
    kinds = len(plan)
    own, other = refs[:kinds], refs[kinds : 2 * kinds]
    fin_own, fin_sib = refs[2 * kinds : 3 * kinds], refs[3 * kinds : 4 * kinds]
    src, swap, first, second, load = (refs[(4 + g) * kinds : (5 + g) * kinds] for g in range(5))
    (pair_s, pair_r, load_s, swap_s, swap_r, in_s, in_r, mid_s, mid_r, out_s, done_s, back_s, back_r) = refs[
        9 * kinds :
    ]
    f, z, k = lax.axis_index("fsdp"), lax.axis_index("z"), lax.axis_index("core")
    line = lax.axis_size("z")
    outer = (z == 0) | (z == line - 1)
    inner = jnp.logical_not(outer)
    inward = jnp.where(z < line // 2, z + 1, z - 1)
    outward = jnp.where(z < line // 2, z - 1, z + 1)

    chunks = []
    for a, (n, swapped) in enumerate(plan):
        for i in range(n):
            chunks.append((a, i, i if swapped else 0))
    count = len(chunks)

    def remote(source, target, send, recv, where):
        return pltpu.make_async_remote_copy(
            src_ref=source,
            dst_ref=target,
            send_sem=send,
            recv_sem=recv,
            device_id=where,
            device_id_type=pl.DeviceIdType.MESH,
        )

    def pair_copy(c):
        a, i, _ = chunks[c]
        return remote(other[a].at[i], src[a].at[i], pair_s.at[c], pair_r.at[c], {"core": 1 - k})

    def load_copy(c):
        a, i, _ = chunks[c]
        return pltpu.make_async_copy(own[a].at[i], load[a].at[i % 2], load_s.at[c])

    def swap_copy(c):
        a, i, j = chunks[c]
        return remote(src[a].at[i], swap[a].at[i], swap_s.at[c], swap_r.at[c], {"fsdp": f ^ j})

    def base(c):
        a, i, j = chunks[c]
        return swap[a].at[i] if j else src[a].at[i]

    def in_copy(c):
        a, i, _ = chunks[c]
        return remote(base(c), first[a].at[i], in_s.at[c], in_r.at[c], {"z": inward})

    def mid_copy(c):
        a, i, _ = chunks[c]
        return remote(first[a].at[i], second[a].at[i], mid_s.at[c], mid_r.at[c], {"z": inward})

    def out_copy(c):
        a, i, _ = chunks[c]
        return remote(second[a].at[i], second[a].at[i], out_s.at[c], mid_r.at[c], {"z": outward})

    def keep_copy(c):
        a, i, _ = chunks[c]
        return pltpu.make_async_copy(second[a].at[i], fin_own[a].at[i], done_s.at[c])

    def back_copy(c):
        a, i, _ = chunks[c]
        return remote(second[a].at[i], fin_sib[a].at[i], back_s.at[c], back_r.at[c], {"core": 1 - k})

    def stage_pair(c):
        a, i, j = chunks[c]
        pair_copy(c).wait_recv()
        load_copy(c).wait()
        add_into(src[a].at[i], load[a].at[i % 2])
        nxt = c + 2
        if nxt < count:
            load_copy(nxt).start()
        if j:
            swap_copy(c).start()

    def stage_in(c):
        if chunks[c][2]:
            swap_copy(c).wait_recv()

        @pl.when(outer)
        def _():
            in_copy(c).start()

    def stage_mid(c):
        a, i, _ = chunks[c]

        @pl.when(inner)
        def _():
            in_copy(c).wait_recv()
            add_into(first[a].at[i], base(c))
            mid_copy(c).start()

    def stage_out(c):
        a, i, _ = chunks[c]

        @pl.when(inner)
        def _():
            mid_copy(c).wait_recv()
            add_into(second[a].at[i], first[a].at[i])
            out_copy(c).start()

    def stage_keep(c):
        @pl.when(outer)
        def _():
            out_copy(c).wait_recv()

        keep_copy(c).start()
        back_copy(c).start()

    for c in range(count):
        pair_copy(c).start()
    for c in range(min(2, count)):
        load_copy(c).start()
    stages = ((0, stage_pair), (1, stage_in), (2, stage_mid), (4, stage_out), (6, stage_keep))
    for tick in range(count + stages[-1][0]):
        for lag, stage in stages:
            if 0 <= tick - lag < count:
                stage(tick - lag)
    for c in range(count):
        pair_copy(c).wait_send()
        if chunks[c][2]:
            swap_copy(c).wait_send()
        keep_copy(c).wait()
        back_copy(c).wait_send()
        back_copy(c).wait_recv()

        @pl.when(outer)
        def _():
            in_copy(c).wait_send()

        @pl.when(inner)
        def _():
            mid_copy(c).wait_send()
            out_copy(c).wait_send()


def sum_gradients_plain(owns, others, swapped):
    ends = []
    for own, other, slabs in zip(owns, others, swapped):
        value = (own.astype(F32) + to_sibling(other).astype(F32)).astype(BF)
        if slabs:
            value = jnp.stack([value[0]] + [along_plane(value[j], j) for j in range(1, value.shape[0])])
        ends.append(line_sum(value))
    return ends, [to_sibling(e) for e in ends]


def sum_gradients(owns, others, swapped):
    plan = tuple((x.shape[0], s) for x, s in zip(owns, swapped))
    count = sum(n for n, _ in plan)
    shapes = [jax.ShapeDtypeStruct(x.shape, BF) for x in owns]
    anywhere = pl.BlockSpec(memory_space=pl.ANY)
    whole = [pltpu.VMEM(x.shape, BF) for x in owns]
    swaps = [pltpu.VMEM(x.shape if s else (1, 16, 128), BF) for x, s in zip(owns, swapped)]
    loads = [pltpu.VMEM((2,) + x.shape[1:], BF) for x in owns]
    size = sum(x.size for x in owns)
    out = pl.pallas_call(
        functools.partial(sums_kernel, plan),
        out_shape=shapes + shapes,
        in_specs=[anywhere] * (2 * len(owns)),
        out_specs=[anywhere] * (2 * len(owns)),
        scratch_shapes=whole + swaps + whole + whole + loads + [pltpu.SemaphoreType.DMA((count,))] * 13,
        compiler_params=params(has_side_effects=True),
        cost_estimate=pl.CostEstimate(flops=4 * size, bytes_accessed=400 * size, transcendentals=0),
        name="sum_gradients",
    )(*owns, *others)
    return out[: len(owns)], out[len(owns) :]


def rms_backward(row_block, inverse, gain_vec, gradient):
    normed = row_block * inverse
    gain_grad = jnp.sum(gradient * normed, axis=0)
    scaled = gradient * gain_vec
    back = inverse * (scaled - normed * jnp.mean(scaled * normed, axis=1, keepdims=True))
    return (back, gain_grad)


def body(
    tokens, cotangent, lengths, attn_gain, w_query, w_key, w_value, w_out, mlp_gain, w_gate, w_up, w_down
):
    seqs, rows, depth = tokens.shape
    count, line = lax.axis_size("fsdp"), lax.axis_size("z")
    f, z, k = lax.axis_index("fsdp"), lax.axis_index("z"), lax.axis_index("core")
    slot = rows * line * 2
    total = count * rows
    slab = depth // count
    half = slab // 2
    q_width = HEADS * HEAD_DIM // count
    shared = max(1, count // KV_HEADS)

    x_own = tokens.reshape(rows, depth)
    chunk = 2 * z + k
    first_pos = slot - 1 - chunk * rows

    length = lengths[0]
    words = jnp.zeros((slab,), F32).at[0].set((length // 64).astype(F32)).at[1].set((length % 64).astype(F32))
    note = jnp.stack([attn_gain, mlp_gain, words.astype(BF), jnp.zeros((slab,), BF)])
    notes = [note] + [along_plane(note, j) for j in range(1, count)]
    notes_abs = [lax.dynamic_index_in_dim(jnp.stack(notes), f ^ i, 0, keepdims=False) for i in range(count)]
    gain_one = jnp.concatenate([n[0] for n in notes_abs]).astype(F32).reshape(1, depth)
    gain_two = jnp.concatenate([n[1] for n in notes_abs]).astype(F32).reshape(1, depth)
    all_lengths = jnp.stack(
        [n[2, 0].astype(jnp.int32) * 64 + n[2, 1].astype(jnp.int32) for n in notes]
    )

    x_all = jnp.concatenate(plane_gather(x_own))

    wq = cut_blocks(w_query, f, k, count)
    key_cols = lax.dynamic_slice_in_dim(w_key, k * half, half, 0).reshape(half, KV_HEADS, HEAD_DIM)
    value_cols = lax.dynamic_slice_in_dim(w_value, k * half, half, 0).reshape(half, KV_HEADS, HEAD_DIM)

    def head_of(j):
        return (f ^ j) // shared

    wkv = jnp.stack(
        [
            jnp.concatenate(
                [
                    lax.dynamic_index_in_dim(key_cols, head_of(j), 1, keepdims=False),
                    lax.dynamic_index_in_dim(value_cols, head_of(j), 1, keepdims=False),
                ],
                axis=1,
            )
            for j in range(count)
        ]
    )
    wqkv = jnp.concatenate([wq, wkv], axis=2)
    wqkv_own = jnp.stack([wqkv[0]] + [along_plane(wqkv[j], j) for j in range(1, count)])
    wqkv_sib = to_sibling(wqkv_own)
    wqkv_all = jnp.concatenate([wqkv_own, wqkv_sib]).reshape(depth, q_width + 128)

    def fetch(weight):
        cut = cut_blocks(weight, f, k, count)
        width = cut.shape[2]
        own = jnp.stack([cut[0]] + [along_plane(cut[j], j) for j in range(1, count)])
        sib = to_sibling(own)
        return own.reshape(depth // 2, width), sib.reshape(depth // 2, width)

    gate_own, gate_sib = fetch(w_gate)
    up_own, up_sib = fetch(w_up)

    order = jnp.stack([(f ^ j) * 2 + (k ^ h) for h in range(2) for j in range(count)]).astype(jnp.int32)

    half_dim = HEAD_DIM // 2
    frequency = jnp.power(ROPE_BASE, jnp.arange(half_dim, dtype=F32) * (-2.0 / HEAD_DIM))
    positions = first_pos - jnp.arange(rows, dtype=jnp.int32)
    angles = positions.astype(F32)[:, None] * frequency[None, :]
    cos32, sin32 = jnp.cos(angles), jnp.sin(angles)
    cosine = jnp.concatenate([cos32] * 4, axis=1)
    sine = jnp.concatenate([-sin32, sin32, -sin32, sin32], axis=1)

    normed_one, queries, kv = qkv_project(order, x_all, gain_one, wqkv_all, cosine, sine, rows)
    queries = queries.reshape(count, rows, q_width)
    kv = kv.reshape(count, rows, 128)

    mine = [kv] + [along_line(kv, -s) for s in range(1, line)]
    mine = jnp.stack(mine)
    kv_all = jnp.concatenate([mine, to_sibling(mine)])
    places = []
    for h in range(2):
        for s in range(line):
            start = slot - 1 - (2 * (z + s) + (k ^ h)) * rows
            places.append(start - jnp.arange(rows, dtype=jnp.int32))
    kp = jnp.concatenate(places)
    kp = jnp.where(kp < 0, FAR, kp).reshape(1, -1)
    at = jnp.concatenate([first_pos.reshape(1), all_lengths]).astype(jnp.int32)

    attended, log_total = attend(at, queries, kv_all, kp)
    attended = attended.reshape(total, q_width)

    mixed_part = nn(attended, w_out).astype(BF).reshape(count, rows, depth)
    inputs = x_own.astype(F32)
    mixed = inputs + plane_reduce(mixed_part)
    inv_two = lax.rsqrt(jnp.mean(mixed * mixed, axis=1, keepdims=True) + EPSILON)
    normed_two_own = (mixed * inv_two * gain_two).astype(BF)
    normed_two = jnp.concatenate(plane_gather(normed_two_own))
    normed_two = pick_columns(normed_two, order, 2 * count)
    n2_own, n2_sib = normed_two[:, : depth // 2], normed_two[:, depth // 2 :]

    valid = (positions < length).astype(F32)[:, None]
    out_back = cotangent.reshape(rows, depth).astype(F32) * valid
    branch_own = out_back.astype(BF)
    branch = jnp.concatenate(plane_gather(branch_own))

    gate = nn(n2_own, gate_own) + nn(n2_sib, gate_sib)
    up = nn(n2_own, up_own) + nn(n2_sib, up_sib)
    sigmoid = jax.nn.sigmoid(gate)
    hidden = (gate * sigmoid * up).astype(BF)

    half_depth = depth // 2
    branch_mine = lax.dynamic_slice_in_dim(branch, k * half_depth, half_depth, 1)
    branch_other = lax.dynamic_slice_in_dim(branch, (1 - k) * half_depth, half_depth, 1)

    def pair_sum(own, other):
        return (own + to_sibling(other.astype(BF)).astype(F32)).astype(BF)

    def swap_slabs(own):
        return jnp.stack([own[0]] + [along_plane(own[j], j) for j in range(1, count)])

    terms = {"down": (tn(hidden, branch_mine).astype(BF), tn(hidden, branch_other).astype(BF))}

    hidden_grad = nt(branch, w_down)
    gate_back = (hidden_grad * up * sigmoid * (1.0 + gate * (1.0 - sigmoid))).astype(BF)
    up_back = (hidden_grad * gate * sigmoid).astype(BF)

    def slab_terms(left_own, left_other, right):
        return tuple(
            tn(left, right).astype(BF).reshape(count, half, right.shape[1]) for left in (left_own, left_other)
        )

    terms["gate"] = slab_terms(n2_own, n2_sib, gate_back)
    terms["up"] = slab_terms(n2_own, n2_sib, up_back)

    back_own = (nt(gate_back, gate_own) + nt(up_back, up_own)).astype(BF)
    back_sib = (nt(gate_back, gate_sib) + nt(up_back, up_sib)).astype(BF)
    normed_back = put_columns(jnp.concatenate([back_own, back_sib], axis=1), order, 2 * count)
    normed_back = plane_reduce(normed_back.reshape(count, rows, depth))

    out_part = nn(hidden, w_down).astype(BF).reshape(count, rows, depth)
    outputs = mixed + plane_reduce(out_part)

    mixed_back, gain_two_grad = rms_backward(mixed, inv_two, gain_two, normed_back)
    mixed_grad = out_back + mixed_back
    attn_back = jnp.concatenate(plane_gather(mixed_grad.astype(BF)))
    attended_grad = nt(attn_back, w_out).astype(BF).reshape(count, rows, q_width)

    back_mine = lax.dynamic_slice_in_dim(attn_back, k * half_depth, half_depth, 1)
    back_other = lax.dynamic_slice_in_dim(attn_back, (1 - k) * half_depth, half_depth, 1)
    terms["out"] = (tn(attended, back_mine).astype(BF), tn(attended, back_other).astype(BF))

    query_back, kv_part = attend_back(at, queries, attended_grad, log_total, kv_all, kp, cosine, sine)
    kv_mine = kv_part[:line].astype(F32) + to_sibling(kv_part[line:]).astype(F32)
    kv_back = kv_mine[0]
    for s in range(1, line):
        kv_back = kv_back + along_line(kv_mine[s].astype(BF), s).astype(F32)
    lead, trail, flat = kv_back[..., :32], kv_back[..., 32:64], kv_back[..., 64:]
    kv_back = jnp.concatenate(
        [lead * cos32 + trail * sin32, trail * cos32 - lead * sin32, flat], axis=-1
    ).astype(BF)
    qkv_back = jnp.concatenate(
        [query_back.reshape(total, q_width), kv_back.reshape(total, 128)], axis=1
    )

    normed_one_back = nt(qkv_back, wqkv_all).astype(BF)
    normed_one_back = put_columns(normed_one_back, order, 2 * count)
    normed_one_back = plane_reduce(normed_one_back.reshape(count, rows, depth))
    inv_one = lax.rsqrt(jnp.mean(inputs * inputs, axis=1, keepdims=True) + EPSILON)
    input_back, gain_one_grad = rms_backward(inputs, inv_one, gain_one, normed_one_back)
    input_grad = mixed_grad + input_back

    n1_own, n1_sib = normed_one[:, :half_depth], normed_one[:, half_depth:]
    qkv_own, qkv_other = slab_terms(n1_own, n1_sib, qkv_back)
    gains = jnp.stack([gain_one_grad, gain_two_grad]).reshape(2, count, slab)
    gains = jnp.stack(
        [lax.dynamic_index_in_dim(gains, f ^ j, 1, keepdims=False) for j in range(count)]
    ).astype(BF)
    width = q_width + 128
    gains = jnp.pad(gains, ((0, 0), (0, 14), (0, width - slab)))
    qkv_own = jnp.concatenate([qkv_own, gains], axis=1)
    qkv_other = jnp.concatenate([qkv_other, jnp.zeros_like(gains)], axis=1)
    terms["qkv"] = (qkv_own, qkv_other)

    cut = {"down": (4, -1, half_depth), "out": (2, -1, half_depth)}
    names = ("down", "gate", "up", "out", "qkv")
    owns = [terms[n][0].reshape(cut[n]) if n in cut else terms[n][0] for n in names]
    others = [terms[n][1].reshape(cut[n]) if n in cut else terms[n][1] for n in names]
    summed = sum_gradients if line == 4 else sum_gradients_plain
    owns, sibs = summed(owns, others, (False, True, True, False, True))
    ends = dict(zip(names, zip(owns, sibs)))

    def columns(name):
        return join_columns(*(x.reshape(-1, half_depth) for x in ends[name]), k)

    down_grad, out_grad = columns("down"), columns("out")
    gate_grad, up_grad = join_rows(*ends["gate"], f, k), join_rows(*ends["up"], f, k)
    qkv_half, qkv_sib = ends["qkv"]
    gains = jnp.sum(qkv_half[:, half : half + 2, :slab].astype(F32), axis=0)
    gains = gains + jnp.sum(qkv_sib[:, half : half + 2, :slab].astype(F32), axis=0)
    query_grad = join_rows(qkv_half[:, :half, :q_width], qkv_sib[:, :half, :q_width], f, k)
    halves = jnp.stack([qkv_half[:, :half, q_width:], qkv_sib[:, :half, q_width:]])

    def by_head(lo, hi):
        both = [lax.dynamic_index_in_dim(halves, k ^ h, 0, keepdims=False) for h in range(2)]
        both = jnp.concatenate(both, axis=1).astype(F32)[:, :, lo:hi]
        cols = jnp.stack([lax.dynamic_index_in_dim(both, f ^ i, 0, keepdims=False) for i in range(count)])
        cols = cols.reshape(KV_HEADS, shared, slab, HEAD_DIM).sum(1)
        return jnp.transpose(cols, (1, 0, 2)).reshape(slab, KV_HEADS * HEAD_DIM)

    key_grad = by_head(0, 64)
    value_grad = by_head(64, 128)

    return (
        outputs.reshape(seqs, rows, depth),
        input_grad.reshape(seqs, rows, depth),
        gains[0],
        query_grad,
        key_grad,
        value_grad,
        out_grad,
        gains[1],
        gate_grad,
        up_grad,
        down_grad,
    )


def solution(mesh):
    count, ctx = mesh.shape["fsdp"], mesh.shape["ctx"]
    split = Mesh(mesh.devices.reshape(count, ctx // 2, 2), ("fsdp", "z", "core"))
    act = P("fsdp", ("z", "core"), None)
    row, mat = P("fsdp"), P("fsdp", None)
    return jax.shard_map(
        body,
        mesh=split,
        in_specs=(act, act, row, row, mat, mat, mat, mat, row, mat, mat, mat),
        out_specs=(act, act, row, mat, mat, mat, mat, row, mat, mat, mat),
        check_vma=False,
    )
```

```python
import functools

import jax
import jax.numpy as jnp
from jax import lax
from jax.experimental import pallas as pl
from jax.experimental.pallas import tpu as pltpu
from jax.sharding import Mesh
from jax.sharding import PartitionSpec as P

HEADS = 32
KV_HEADS = 4
HEAD_DIM = 64
EPSILON = 1e-05
ROPE_BASE = 10000.0
MASKED = -1e30
FAR = 1 << 30
BF = jnp.bfloat16
F32 = jnp.float32
VMEM_BYTES = 56 * 1024 * 1024


def params(**kw):
    return pltpu.CompilerParams(vmem_limit_bytes=VMEM_BYTES, **kw)


def along_plane(value, step):
    count = lax.axis_size("fsdp")
    return lax.ppermute(value, "fsdp", [(i, i ^ step) for i in range(count)])


def to_sibling(value):
    return lax.ppermute(value, "core", [(0, 1), (1, 0)])


def along_line(value, shift):
    count = lax.axis_size("z")
    return lax.ppermute(
        value, "z", [(i, i + shift) for i in range(count) if 0 <= i + shift < count]
    )


def plane_bits():
    count = lax.axis_size("fsdp")
    return [1 << b for b in range(count.bit_length() - 1)]


def plane_gather(block):
    half = block.shape[0] // 2
    parts = []
    for which, bits in ((0, plane_bits()), (1, plane_bits()[::-1])):
        held = {0: block[which * half : (which + 1) * half]}
        for bit in bits:
            order = sorted(held)
            got = along_plane(jnp.stack([held[j] for j in order]), bit)
            for n, j in enumerate(order):
                held[j ^ bit] = got[n]
        parts.append(held)
    return [jnp.concatenate([parts[0][j], parts[1][j]]) for j in range(lax.axis_size("fsdp"))]


def plane_reduce(partial):
    half = partial.shape[1] // 2
    done = []
    for which, bits in ((0, plane_bits()[::-1]), (1, plane_bits())):
        held = {j: partial[j, which * half : (which + 1) * half] for j in range(partial.shape[0])}
        for bit in bits:
            going = [j for j in sorted(held) if j & bit]
            got = along_plane(jnp.stack([held[j].astype(BF) for j in going]), bit)
            for n, j in enumerate(going):
                held[j ^ bit] = held[j ^ bit].astype(F32) + got[n].astype(F32)
                del held[j]
        done.append(held[0])
    return jnp.concatenate(done)


def line_sum(value):
    count = lax.axis_size("z")
    place = lax.axis_index("z")
    half = count // 2
    for i in range(half - 1):
        got = lax.ppermute(value, "z", [(i, i + 1), (count - 1 - i, count - 2 - i)])
        value = value + got
    value = value + lax.ppermute(value, "z", [(half - 1, half), (half, half - 1)])
    for i in range(half - 2, -1, -1):
        got = lax.ppermute(value, "z", [(i + 1, i), (count - 2 - i, count - 1 - i)])
        outer = (place == i) | (place == count - 1 - i)
        value = jnp.where(outer, got, value)
    return value


def move_kernel(idx_ref, x_ref, o_ref):
    o_ref[...] = x_ref[...]


def pick_columns(x, index, count):
    rows, width = x.shape
    size = width // count
    spec = pltpu.PrefetchScalarGridSpec(
        num_scalar_prefetch=1,
        grid=(count,),
        in_specs=[pl.BlockSpec((rows, size), lambda b, idx: (0, idx[b]))],
        out_specs=pl.BlockSpec((rows, size), lambda b, idx: (0, b)),
    )
    return pl.pallas_call(
        move_kernel,
        grid_spec=spec,
        out_shape=jax.ShapeDtypeStruct(x.shape, x.dtype),
        compiler_params=params(),
        name="pick_columns",
    )(index, x)


def put_columns(x, index, count):
    rows, width = x.shape
    size = width // count
    spec = pltpu.PrefetchScalarGridSpec(
        num_scalar_prefetch=1,
        grid=(count,),
        in_specs=[pl.BlockSpec((rows, size), lambda b, idx: (0, b))],
        out_specs=pl.BlockSpec((rows, size), lambda b, idx: (0, idx[b])),
    )
    return pl.pallas_call(
        move_kernel,
        grid_spec=spec,
        out_shape=jax.ShapeDtypeStruct(x.shape, x.dtype),
        compiler_params=params(),
        name="put_columns",
    )(index, x)


def cut_blocks(weight, f, k, count, dtype=BF):
    rows, full = weight.shape
    width, half = full // count, rows // 2
    if width % 128:
        own = lax.dynamic_slice_in_dim(weight, k * half, half, 0).reshape(half, count, width)
        return jnp.stack(
            [lax.dynamic_index_in_dim(own, f ^ j, 1, keepdims=False) for j in range(count)]
        )
    spec = pltpu.PrefetchScalarGridSpec(
        num_scalar_prefetch=1,
        grid=(count,),
        in_specs=[pl.BlockSpec((half, width), lambda j, at: (at[1], at[0] ^ j))],
        out_specs=pl.BlockSpec((None, half, width), lambda j, at: (j, 0, 0)),
    )
    return pl.pallas_call(
        move_kernel,
        grid_spec=spec,
        out_shape=jax.ShapeDtypeStruct((count, half, width), weight.dtype),
        compiler_params=params(),
        name="cut_blocks",
    )(jnp.stack([f, k]), weight)


def join_kernel(at_ref, own_ref, sib_ref, o_ref):
    @pl.when(pl.program_id(0) == 0)
    def _():
        o_ref[...] = own_ref[...].astype(o_ref.dtype)

    @pl.when(pl.program_id(0) == 1)
    def _():
        o_ref[...] = sib_ref[...].astype(o_ref.dtype)


def join_rows(own, sib, f, k):
    count, half, width = own.shape
    if width % 128:
        halves = jnp.stack([own, sib])
        return jnp.concatenate(
            [
                jnp.concatenate(
                    [
                        lax.dynamic_index_in_dim(
                            lax.dynamic_index_in_dim(halves, k ^ h, 0, keepdims=False),
                            f ^ i,
                            0,
                            keepdims=False,
                        )
                        for i in range(count)
                    ],
                    axis=1,
                )
                for h in range(2)
            ],
            axis=0,
        ).astype(F32)
    spec = pltpu.PrefetchScalarGridSpec(
        num_scalar_prefetch=1,
        grid=(2, count),
        in_specs=[
            pl.BlockSpec(
                (None, half, width),
                lambda s, i, at: (at[0] ^ jnp.where(s == 0, i, count - 1), 0, 0),
            ),
            pl.BlockSpec(
                (None, half, width), lambda s, i, at: (at[0] ^ jnp.where(s == 1, i, 0), 0, 0)
            ),
        ],
        out_specs=pl.BlockSpec((half, width), lambda s, i, at: (at[1] ^ s, i)),
    )
    return pl.pallas_call(
        join_kernel,
        grid_spec=spec,
        out_shape=jax.ShapeDtypeStruct((2 * half, count * width), F32),
        compiler_params=params(),
        name="join_rows",
    )(jnp.stack([f, k]), own, sib)


def join_columns(own, sib, k):
    rows, half = own.shape
    count = 4
    size = rows // count
    spec = pltpu.PrefetchScalarGridSpec(
        num_scalar_prefetch=1,
        grid=(2, count),
        in_specs=[
            pl.BlockSpec((size, half), lambda s, i, at: (jnp.where(s == 0, i, count - 1), 0)),
            pl.BlockSpec((size, half), lambda s, i, at: (jnp.where(s == 1, i, 0), 0)),
        ],
        out_specs=pl.BlockSpec((size, half), lambda s, i, at: (i, at[0] ^ s)),
    )
    return pl.pallas_call(
        join_kernel,
        grid_spec=spec,
        out_shape=jax.ShapeDtypeStruct((rows, 2 * half), F32),
        compiler_params=params(),
        name="join_columns",
    )(k.reshape(1), own, sib)


def swap_halves(block):
    lane = lax.broadcasted_iota(jnp.int32, block.shape, 1)
    return jnp.where(lane % 64 < 32, pltpu.roll(block, 96, 1), pltpu.roll(block, 32, 1))


def qkv_kernel(idx_ref, x_ref, gain_ref, w_ref, cos_ref, sin_ref, h_ref, q_ref, kv_ref):
    blocks = idx_ref.shape[0]
    size = x_ref.shape[1] // blocks
    x = x_ref[...].astype(F32)
    inverse = lax.rsqrt(jnp.mean(x * x, axis=1, keepdims=True) + EPSILON)
    for b in range(blocks):
        at = pl.ds(pl.multiple_of(idx_ref[b] * size, 128), size)
        part = x_ref[:, at].astype(F32) * inverse * gain_ref[:, at]
        h_ref[:, b * size : (b + 1) * size] = part.astype(BF)
    out = jnp.dot(h_ref[...], w_ref[...], preferred_element_type=F32)
    cosine, sine = cos_ref[...], sin_ref[...]
    pairs = q_ref.shape[1] // 128
    for c in range(pairs):
        block = out[:, c * 128 : (c + 1) * 128]
        q_ref[:, c * 128 : (c + 1) * 128] = (block * cosine + swap_halves(block) * sine).astype(BF)
    block = out[:, pairs * 128 :]
    lane = lax.broadcasted_iota(jnp.int32, block.shape, 1)
    turned = block * cosine + swap_halves(block) * sine
    kv_ref[...] = jnp.where(lane < 64, turned, block).astype(BF)


def qkv_project(idx, x, gain, weight, cosine, sine, rows):
    total, depth = x.shape
    width = weight.shape[1]
    spec = pltpu.PrefetchScalarGridSpec(
        num_scalar_prefetch=1,
        grid=(total // rows,),
        in_specs=[
            pl.BlockSpec((rows, depth), lambda i, idx: (i, 0)),
            pl.BlockSpec((1, depth), lambda i, idx: (0, 0)),
            pl.BlockSpec((depth, width), lambda i, idx: (0, 0)),
            pl.BlockSpec((rows, 128), lambda i, idx: (0, 0)),
            pl.BlockSpec((rows, 128), lambda i, idx: (0, 0)),
        ],
        out_specs=[
            pl.BlockSpec((rows, depth), lambda i, idx: (i, 0)),
            pl.BlockSpec((rows, width - 128), lambda i, idx: (i, 0)),
            pl.BlockSpec((rows, 128), lambda i, idx: (i, 0)),
        ],
    )
    return pl.pallas_call(
        qkv_kernel,
        grid_spec=spec,
        out_shape=[
            jax.ShapeDtypeStruct((total, depth), BF),
            jax.ShapeDtypeStruct((total, width - 128), BF),
            jax.ShapeDtypeStruct((total, 128), BF),
        ],
        compiler_params=params(),
        cost_estimate=pl.CostEstimate(
            flops=2 * total * depth * width,
            bytes_accessed=4 * total * depth + 2 * depth * width + 2 * total * width,
            transcendentals=0,
        ),
        name="qkv_project",
    )(idx, x, gain, weight, cosine, sine)


def nt(a, b):
    return lax.dot_general(a, b, (((1,), (1,)), ((), ())), preferred_element_type=F32)


def tn(a, b):
    return lax.dot_general(a, b, (((0,), (0,)), ((), ())), preferred_element_type=F32)


def nn(a, b):
    return jnp.dot(a, b, preferred_element_type=F32)


def limits(at_ref, rows):
    j = pl.program_id(0)
    place = at_ref[0] - lax.broadcasted_iota(jnp.int32, (rows, 1), 0)
    return jnp.minimum(place, at_ref[1 + j] - 1)


def attend_kernel(at_ref, q_ref, kv_ref, kp_ref, o_ref, lse_ref, vk_ref):
    rows = q_ref.shape[0]
    keys = vk_ref.shape[0]
    kv = kv_ref[...].reshape(keys, 128)

    @pl.when(pl.program_id(1) == 0)
    def _():
        vk_ref[...] = pltpu.roll(kv.astype(F32), 64, 1).astype(BF)

    vk = vk_ref[...]
    allowed = kp_ref[...] <= limits(at_ref, rows)
    lane = lax.broadcasted_iota(jnp.int32, (rows, 128), 1)
    q = q_ref[...]
    zero = jnp.zeros_like(q)
    outs, logs = [], []
    for first in (True, False):
        mine = lane < 64 if first else lane >= 64
        scores = nt(jnp.where(mine, q, zero), kv if first else vk) * (HEAD_DIM**-0.5)
        scores = jnp.where(allowed, scores, MASKED)
        top = jnp.max(scores, axis=1, keepdims=True)
        weights = jnp.exp(scores - top)
        total = jnp.sum(weights, axis=1, keepdims=True)
        outs.append(nn(weights.astype(BF), vk if first else kv) / total)
        logs.append(jnp.broadcast_to(top + jnp.log(total), (rows, 128)))
    o_ref[...] = jnp.where(lane < 64, outs[0], outs[1]).astype(BF)
    lse_ref[...] = jnp.where(lane < 64, logs[0], logs[1])


def attend(at, q, kv, kp):
    chunks, seqs, rows, _ = kv.shape
    pairs = q.shape[2] // 128
    keys = chunks * rows
    spec = pltpu.PrefetchScalarGridSpec(
        num_scalar_prefetch=1,
        grid=(seqs, pairs),
        in_specs=[
            pl.BlockSpec((None, rows, 128), lambda j, p, at: (j, 0, p)),
            pl.BlockSpec((chunks, None, rows, 128), lambda j, p, at: (0, j, 0, 0)),
            pl.BlockSpec((1, keys), lambda j, p, at: (0, 0)),
        ],
        out_specs=[
            pl.BlockSpec((None, rows, 128), lambda j, p, at: (j, 0, p)),
            pl.BlockSpec((None, rows, 128), lambda j, p, at: (j, 0, p)),
        ],
        scratch_shapes=[pltpu.VMEM((keys, 128), BF)],
    )
    size = seqs * pairs * 2 * rows * keys
    return pl.pallas_call(
        attend_kernel,
        grid_spec=spec,
        out_shape=[
            jax.ShapeDtypeStruct(q.shape, BF),
            jax.ShapeDtypeStruct(q.shape, F32),
        ],
        compiler_params=params(),
        cost_estimate=pl.CostEstimate(
            flops=size * 4 * 128, bytes_accessed=4 << 20, transcendentals=size
        ),
        name="attend",
    )(at, q, kv, kp)


def attend_back_kernel(
    at_ref, q_ref, do_ref, lse_ref, kv_ref, kp_ref, cos_ref, sin_ref, dq_ref, dkv_ref, vk_ref, dk_ref, dv_ref
):
    rows = q_ref.shape[0]
    keys = vk_ref.shape[0]
    pair = pl.program_id(1)
    kv = kv_ref[...].reshape(keys, 128)

    @pl.when(pair == 0)
    def _():
        vk_ref[...] = pltpu.roll(kv.astype(F32), 64, 1).astype(BF)
        dk_ref[...] = jnp.zeros_like(dk_ref)
        dv_ref[...] = jnp.zeros_like(dv_ref)

    vk = vk_ref[...]
    allowed = kp_ref[...] <= limits(at_ref, rows)
    lane = lax.broadcasted_iota(jnp.int32, (rows, 128), 1)
    q, do = q_ref[...], do_ref[...]
    zero = jnp.zeros_like(q)
    parts = []
    for first in (True, False):
        mine = lane < 64 if first else lane >= 64
        keyed, valued = (kv, vk) if first else (vk, kv)
        q_own, do_own = jnp.where(mine, q, zero), jnp.where(mine, do, zero)
        scores = nt(q_own, keyed) * (HEAD_DIM**-0.5)
        log_total = lse_ref[:, 0:1] if first else lse_ref[:, 64:65]
        weights = jnp.where(allowed, jnp.exp(scores - log_total), 0.0)
        joint = weights * nt(do_own, valued)
        back = (joint - weights * jnp.sum(joint, axis=1, keepdims=True)).astype(BF)
        parts.append(nn(back, keyed))
        dk_ref[...] += tn(back, q_own)
        dv_ref[...] += tn(weights.astype(BF), do_own)
    turned = jnp.where(lane < 64, parts[0], parts[1]) * (HEAD_DIM**-0.5)
    dq_ref[...] = (turned * cos_ref[...] - swap_halves(turned) * sin_ref[...]).astype(BF)

    @pl.when(pair == pl.num_programs(1) - 1)
    def _():
        dk = dk_ref[...]
        dv = dv_ref[...]
        dk = (dk + pltpu.roll(dk, 64, 1)) * (HEAD_DIM**-0.5)
        dv = dv + pltpu.roll(dv, 64, 1)
        wide = lax.broadcasted_iota(jnp.int32, dk.shape, 1)
        dkv_ref[...] = jnp.where(wide < 64, dk, dv).astype(BF).reshape(dkv_ref.shape)


def attend_back(at, q, do, lse, kv, kp, cosine, sine):
    chunks, seqs, rows, _ = kv.shape
    pairs = q.shape[2] // 128
    keys = chunks * rows
    tall = pl.BlockSpec((None, rows, 128), lambda j, p, at: (j, 0, p))
    whole = pl.BlockSpec((chunks, None, rows, 128), lambda j, p, at: (0, j, 0, 0))
    flat = pl.BlockSpec((rows, 128), lambda j, p, at: (0, 0))
    spec = pltpu.PrefetchScalarGridSpec(
        num_scalar_prefetch=1,
        grid=(seqs, pairs),
        in_specs=[tall, tall, tall, whole, pl.BlockSpec((1, keys), lambda j, p, at: (0, 0)), flat, flat],
        out_specs=[tall, whole],
        scratch_shapes=[
            pltpu.VMEM((keys, 128), BF),
            pltpu.VMEM((keys, 128), F32),
            pltpu.VMEM((keys, 128), F32),
        ],
    )
    size = seqs * pairs * 2 * rows * keys
    return pl.pallas_call(
        attend_back_kernel,
        grid_spec=spec,
        out_shape=[
            jax.ShapeDtypeStruct(q.shape, BF),
            jax.ShapeDtypeStruct(kv.shape, BF),
        ],
        compiler_params=params(),
        cost_estimate=pl.CostEstimate(
            flops=size * 10 * 128, bytes_accessed=8 << 20, transcendentals=size
        ),
        name="attend_back",
    )(at, q, do, lse, kv, kp, cosine, sine)


def add_into(target, other):
    @pl.loop(0, target.shape[0] // 16)
    def _(i):
        at = pl.ds(pl.multiple_of(i * 16, 16), 16)
        target[at, :] = (target[at, :].astype(F32) + other[at, :].astype(F32)).astype(BF)


def back_kernel(
    at_ref,
    own_down, own_gate, own_up, other_down, other_gate, other_up,
    back_part, out_part, w_out, wqkv_hbm, h1_hbm,
    mixed, branch_own, x_own, gain_one, gain_two,
    attended, queries, lse, kv_all, kp, cosine, sine,
    fin_down, fin_gate, fin_up, fin_out, fin_qkv, fin_gain,
    sib_down, sib_gate, sib_up, sib_out, sib_qkv, sib_gain,
    outputs, input_grad,
    src_down, src_gate, src_up, src_out, src_qkv, src_gain,
    swap_gate, swap_up, swap_qkv,
    end_down, end_gate, end_up, end_out, end_qkv, end_gain,
    load_down, load_gate, give_out, give_qkv, give_gain,
    landed, landed_out, first_back, first_out, da_all, wide, do_all, dqkv, wqkv, h1,
    vk, dk_sum, dv_sum, kv_part, kv_land, kv_mine, kv_line, gain_acc, gain_all,
    pair_s, pair_r, load_s, swap_s, swap_r, in_s, in_r, mid_s, mid_r, out_s, done_s, back_s, back_r, ready,
    local_s, rs_s, rs_r, ro_s, ro_r, ag_s, ag_r, rq_s, rq_r, kp_s, kp_r, kz_s, kz_r, ga_s, ga_r,
):
    f, z, k = lax.axis_index("fsdp"), lax.axis_index("z"), lax.axis_index("core")
    plane, line = lax.axis_size("fsdp"), lax.axis_size("z")
    outer = (z == 0) | (z == line - 1)
    inner = jnp.logical_not(outer)
    inward = jnp.where(z < line // 2, z + 1, z - 1)
    outward = jnp.where(z < line // 2, z - 1, z + 1)
    rows, depth = mixed.shape
    total = plane * rows
    half_depth = depth // 2
    half = half_depth // plane
    q_width = attended.shape[1]
    pairs = q_width // 128
    peers = range(1, plane)

    kinds = {
        "down": (own_down, other_down, src_down, None, end_down, load_down, fin_down, sib_down),
        "gate": (own_gate, other_gate, src_gate, swap_gate, end_gate, load_gate, fin_gate, sib_gate),
        "up": (own_up, other_up, src_up, swap_up, end_up, load_gate, fin_up, sib_up),
        "out": (None, give_out, src_out, None, end_out, None, fin_out, sib_out),
        "qkv": (None, give_qkv, src_qkv, swap_qkv, end_qkv, None, fin_qkv, sib_qkv),
        "gain": (None, give_gain, src_gain, None, end_gain, None, fin_gain, sib_gain),
    }
    chunks = [(name, i) for name, kind in kinds.items() for i in range(kind[2].shape[0])]
    count = len(chunks)
    loaded = [c for c in range(count) if kinds[chunks[c][0]][0] is not None]

    def remote(source, target, send, recv, where):
        return pltpu.make_async_remote_copy(
            src_ref=source,
            dst_ref=target,
            send_sem=send,
            recv_sem=recv,
            device_id=where,
            device_id_type=pl.DeviceIdType.MESH,
        )

    def part(c, which):
        name, i = chunks[c]
        return kinds[name][which].at[i]

    def swapped(c):
        name, i = chunks[c]
        return i if kinds[name][3] is not None else 0

    def pair_copy(c):
        name, i = chunks[c]
        given = kinds[name][1]
        source = given.at[i] if c in loaded else given.at[i % given.shape[0]]
        return remote(source, part(c, 2), pair_s.at[c], pair_r.at[c], {"core": 1 - k})

    def load_copy(c):
        return pltpu.make_async_copy(part(c, 0), kinds[chunks[c][0]][5].at[c % 2], load_s.at[c])

    def swap_copy(c):
        return remote(part(c, 2), part(c, 3), swap_s.at[c], swap_r.at[c], {"fsdp": f ^ swapped(c)})

    def base(c):
        return part(c, 3) if swapped(c) else part(c, 2)

    def in_copy(c):
        return remote(base(c), part(c, 4), in_s.at[c], in_r.at[c], {"z": inward})

    def mid_copy(c):
        return remote(base(c), part(c, 4), mid_s.at[c], mid_r.at[c], {"z": inward})

    def out_copy(c):
        return remote(part(c, 4), part(c, 4), out_s.at[c], mid_r.at[c], {"z": outward})

    def keep_copy(c):
        return pltpu.make_async_copy(part(c, 4), part(c, 6), done_s.at[c])

    def back_copy(c):
        return remote(part(c, 4), part(c, 7), back_s.at[c], back_r.at[c], {"core": 1 - k})

    own_cols = pl.ds(pl.multiple_of(k * half_depth, 128), half_depth)
    other_cols = pl.ds(pl.multiple_of((1 - k) * half_depth, 128), half_depth)

    def out_term(i, cols):
        size = src_out.shape[1]
        right = da_all[:, :, cols].reshape(total, half_depth)
        return tn(attended[:, i * size : (i + 1) * size], right)

    def qkv_term(i, side):
        start = side * half_depth + i * half
        return tn(h1[:, start : start + half], dqkv[...])

    def term(c, side):
        name, i = chunks[c]
        if name == "out":
            return out_term(i, (own_cols, other_cols)[side])
        if name == "qkv":
            return qkv_term(i, side)
        return gain_all[...].astype(F32).sum(axis=0)

    def stage_give(c):
        name, i = chunks[c]
        if c in loaded:
            return
        given = kinds[name][1]
        slots = given.shape[0]
        if i >= slots:
            pair_copy(c - slots).wait_send()
        given[i % slots] = term(c, 1).astype(BF)
        pair_copy(c).start()

    def stage_pair(c):
        pair_copy(c).wait_recv()
        if c in loaded:
            load_copy(c).wait()
            add_into(part(c, 2), kinds[chunks[c][0]][5].at[c % 2])
            if c + 2 in loaded:
                load_copy(c + 2).start()
        else:
            target = part(c, 2)
            target[...] = (target[...].astype(F32) + term(c, 0)).astype(BF)
        if swapped(c):
            swap_copy(c).start()

    def stage_in(c):
        if swapped(c):
            swap_copy(c).wait_recv()

        @pl.when(outer)
        def _():
            in_copy(c).start()

    def stage_mid(c):
        @pl.when(inner)
        def _():
            in_copy(c).wait_recv()
            add_into(base(c), part(c, 4))
            pl.semaphore_signal(
                ready, inc=1, device_id={"z": inward}, device_id_type=pl.DeviceIdType.MESH
            )
            pl.semaphore_wait(ready, 1)
            mid_copy(c).start()

    def stage_out(c):
        @pl.when(inner)
        def _():
            mid_copy(c).wait_recv()
            add_into(part(c, 4), base(c))
            out_copy(c).start()

    def stage_keep(c):
        @pl.when(outer)
        def _():
            out_copy(c).wait_recv()

        keep_copy(c).start()
        back_copy(c).start()

    def back_send(j):
        return remote(back_part.at[j], landed.at[j - 1], rs_s.at[j - 1], rs_r.at[j - 1], {"fsdp": f ^ j})

    def out_send(j):
        return remote(out_part.at[j], landed_out.at[j - 1], ro_s.at[j - 1], ro_r.at[j - 1], {"fsdp": f ^ j})

    def da_send(j):
        return remote(da_all.at[0], da_all.at[j], ag_s.at[j - 1], ag_r.at[j - 1], {"fsdp": f ^ j})

    def dh_send(j):
        mine = wide.at[pl.ds(j * rows, rows), :]
        return remote(mine, landed.at[j - 1], rq_s.at[j - 1], rq_r.at[j - 1], {"fsdp": f ^ j})

    def gain_send(j):
        return remote(gain_all.at[0], gain_all.at[j], ga_s.at[j - 1], ga_r.at[j - 1], {"fsdp": f ^ j})

    locals_ = [
        pltpu.make_async_copy(back_part.at[0], first_back, local_s.at[0]),
        pltpu.make_async_copy(out_part.at[0], first_out, local_s.at[1]),
        pltpu.make_async_copy(w_out, wide.at[pl.ds(0, w_out.shape[0]), :], local_s.at[2]),
        pltpu.make_async_copy(wqkv_hbm, wqkv, local_s.at[3]),
        pltpu.make_async_copy(h1_hbm, h1, local_s.at[4]),
    ]

    def rms_back(gradient_of, x_ref, gain, acc, write):
        acc[...] = jnp.zeros_like(acc)

        @pl.loop(0, rows // 16)
        def _(i):
            at = pl.ds(pl.multiple_of(i * 16, 16), 16)
            gradient = gradient_of(at)
            x = x_ref[at, :].astype(F32)
            inverse = lax.rsqrt(jnp.mean(x * x, axis=1, keepdims=True) + EPSILON)
            normed = x * inverse
            acc[...] += gradient * normed
            scaled = gradient * gain[...]
            write(at, inverse * (scaled - normed * jnp.mean(scaled * normed, axis=1, keepdims=True)))

    def piece_mixed():
        locals_[0].wait()
        for j in peers:
            back_send(j).wait_recv()

        def gradient_of(at):
            value = first_back[at, :].astype(F32)
            for j in peers:
                value = value + landed[j - 1, at, :].astype(F32)
            return value

        def write(at, value):
            value = value + branch_own[at, :].astype(F32)
            input_grad[at, :] = value
            da_all[0, at, :] = value.astype(BF)

        rms_back(gradient_of, mixed, gain_two, gain_acc.at[1], write)
        for j in peers:
            da_send(j).start()

    def piece_do():
        locals_[2].wait()
        for j in peers:
            da_send(j).wait_recv()
            out_send(j).start()

        @pl.loop(0, plane)
        def _(j):
            do_all[j] = nt(da_all[j], wide[0 : w_out.shape[0], :]).astype(BF)

    def piece_attend(j):
        vk[...] = pltpu.roll(kv_all[:, j].reshape(vk.shape).astype(F32), 64, 1).astype(BF)
        dk_sum[...] = jnp.zeros_like(dk_sum)
        dv_sum[...] = jnp.zeros_like(dv_sum)
        place = at_ref[0] - lax.broadcasted_iota(jnp.int32, (rows, 1), 0)
        limit = jnp.minimum(place, at_ref[1 + j] - 1)
        lane = lax.broadcasted_iota(jnp.int32, (rows, 128), 1)

        @pl.loop(0, pairs)
        def _(p):
            at = pl.ds(pl.multiple_of(p * 128, 128), 128)
            allowed = kp[...] <= limit
            q, do = queries[j, :, at], do_all[j, :, at]
            logs = lse[j, :, at]
            zero = jnp.zeros_like(q)
            parts = []
            for first in (True, False):
                mine = lane < 64 if first else lane >= 64
                kv = kv_all[:, j].reshape(vk.shape)
                keyed, valued = (kv, vk[...]) if first else (vk[...], kv)
                q_own, do_own = jnp.where(mine, q, zero), jnp.where(mine, do, zero)
                scores = nt(q_own, keyed) * (HEAD_DIM**-0.5)
                log_total = logs[:, 0:1] if first else logs[:, 64:65]
                weights = jnp.where(allowed, jnp.exp(scores - log_total), 0.0)
                joint = weights * nt(do_own, valued)
                back = (joint - weights * jnp.sum(joint, axis=1, keepdims=True)).astype(BF)
                parts.append(nn(back, keyed))
                dk_sum[...] += tn(back, q_own)
                dv_sum[...] += tn(weights.astype(BF), do_own)
            turned = jnp.where(lane < 64, parts[0], parts[1]) * (HEAD_DIM**-0.5)
            turned = turned * cosine[...] - swap_halves(turned) * sine[...]
            dqkv[j * rows : (j + 1) * rows, at] = turned.astype(BF)

        dk = dk_sum[...]
        dv = dv_sum[...]
        dk = (dk + pltpu.roll(dk, 64, 1)) * (HEAD_DIM**-0.5)
        dv = dv + pltpu.roll(dv, 64, 1)
        wide_lane = lax.broadcasted_iota(jnp.int32, dk.shape, 1)
        packed = jnp.where(wide_lane < 64, dk, dv).astype(BF)
        kv_part[:, j] = packed.reshape(kv_part.shape[0], rows, 128)

    kv_pair = remote(kv_part.at[pl.ds(line, line)], kv_land, kp_s.at[0], kp_r.at[0], {"core": 1 - k})

    def kv_send(s):
        return remote(kv_mine.at[s], kv_line.at[s - 1], kz_s.at[s - 1], kz_r.at[s - 1], {"z": z + s})

    def piece_kv_line():
        kv_pair.wait_recv()
        for s in range(line):
            kv_mine[s] = (kv_part[s].astype(F32) + kv_land[s].astype(F32)).astype(BF)
        for s in range(1, line):

            @pl.when(z + s < line)
            def _():
                kv_send(s).start()

    def piece_kv_sum():
        for s in range(1, line):

            @pl.when(z >= s)
            def _():
                kv_send(s).wait_recv()
                kv_mine[0] = (kv_mine[0].astype(F32) + kv_line[s - 1].astype(F32)).astype(BF)

        lane = lax.broadcasted_iota(jnp.int32, (rows, 128), 1)
        for j in range(plane):
            value = kv_mine[0, j].astype(F32)
            turned = value * cosine[...] - swap_halves(value) * sine[...]
            value = jnp.where(lane < 64, turned, value).astype(BF)
            dqkv[j * rows : (j + 1) * rows, q_width : q_width + 128] = value

    def piece_dh():
        locals_[3].wait()
        for h in range(2):
            for j in range(plane):
                start = pl.multiple_of(((f ^ j) * 2 + (k ^ h)) * half, 128)
                block = wqkv[(h * plane + j) * half : (h * plane + j + 1) * half, :]
                wide[0:total, pl.ds(start, half)] = nt(dqkv[...], block).astype(BF)
        for j in peers:
            dh_send(j).start()

    def piece_input():
        for j in peers:
            dh_send(j).wait_recv()

        def gradient_of(at):
            value = wide[at, :].astype(F32)
            for j in peers:
                value = value + landed[j - 1, at, :].astype(F32)
            return value

        def write(at, value):
            input_grad[at, :] = input_grad[at, :] + value

        rms_back(gradient_of, x_own, gain_one, gain_acc.at[0], write)
        place = lax.broadcasted_iota(jnp.int32, (16, depth), 0)
        one = jnp.sum(gain_acc[0], axis=0, keepdims=True)
        two = jnp.sum(gain_acc[1], axis=0, keepdims=True)
        gain_all[0] = jnp.where(place == 0, one, jnp.where(place == 1, two, 0.0)).astype(BF)
        for j in peers:
            gain_send(j).start()

    def piece_outputs():
        locals_[1].wait()
        for j in peers:
            out_send(j).wait_recv()

        @pl.loop(0, rows // 16)
        def _(i):
            at = pl.ds(pl.multiple_of(i * 16, 16), 16)
            value = mixed[at, :] + first_out[at, :].astype(F32)
            for j in peers:
                value = value + landed_out[j - 1, at, :].astype(F32)
            outputs[at, :] = value

    def piece_gain():
        for j in peers:
            gain_send(j).wait_recv()
        locals_[4].wait()

    pieces = {2: [piece_mixed], 4: [piece_do]}
    for j in range(plane):
        pieces.setdefault(4 + j, []).append(functools.partial(piece_attend, j))
    pieces[3 + plane].append(lambda: kv_pair.start())
    pieces[4 + plane] = [piece_kv_line, piece_outputs]
    pieces[5 + plane] = [piece_kv_sum, piece_dh]
    pieces[7 + plane] = [piece_input]
    pieces[8 + plane] = [piece_gain]

    for j in peers:
        back_send(j).start()
    for c in loaded:
        pair_copy(c).start()
    for c in loaded[:2]:
        load_copy(c).start()
    for copy in locals_:
        copy.start()
    stages = ((-1, stage_give), (0, stage_pair), (1, stage_in), (2, stage_mid), (4, stage_out), (6, stage_keep))
    for tick in range(count + stages[-1][0]):
        for lag, stage in stages:
            if 0 <= tick - lag < count:
                stage(tick - lag)
        for piece in pieces.get(tick, []):
            piece()

    for c in range(count):
        name, i = chunks[c]
        if c in loaded or i + kinds[name][1].shape[0] >= kinds[name][2].shape[0]:
            pair_copy(c).wait_send()
        if swapped(c):
            swap_copy(c).wait_send()
        keep_copy(c).wait()
        back_copy(c).wait_send()
        back_copy(c).wait_recv()

        @pl.when(outer)
        def _():
            in_copy(c).wait_send()

        @pl.when(inner)
        def _():
            mid_copy(c).wait_send()
            out_copy(c).wait_send()

    for j in peers:
        back_send(j).wait_send()
        out_send(j).wait_send()
        da_send(j).wait_send()
        dh_send(j).wait_send()
        gain_send(j).wait_send()
    kv_pair.wait_send()
    for s in range(1, line):

        @pl.when(z + s < line)
        def _():
            kv_send(s).wait_send()


def back_pass(
    at, own, other, back_part, out_part, w_out, wqkv, h1, mixed, branch_own, x_own, gain_one, gain_two,
    attended, queries, lse, kv_all, kp, cosine, sine,
):
    count, line = lax.axis_size("fsdp"), lax.axis_size("z")
    rows, depth = mixed.shape
    total, half_depth = count * rows, depth // 2
    half = half_depth // count
    q_width = attended.shape[1]
    keys = kv_all.shape[0] * rows
    shapes = [x.shape for x in own] + [
        (2, q_width // 2, half_depth),
        (count, half, q_width + 128),
        (1, 16, depth),
    ]
    anywhere = pl.BlockSpec(memory_space=pl.ANY)
    local = pl.BlockSpec(memory_space=pltpu.VMEM)
    ends = [jax.ShapeDtypeStruct(s, BF) for s in shapes]
    act = jax.ShapeDtypeStruct((rows, depth), F32)
    block = (rows, depth)
    chunk_count = sum(s[0] for s in shapes)
    dma = lambda n: pltpu.SemaphoreType.DMA((n,))
    scratch = (
        [pltpu.VMEM(s, BF) for s in shapes]
        + [pltpu.VMEM(shapes[i], BF) for i in (1, 2, 4)]
        + [pltpu.VMEM(s, BF) for s in shapes]
        + [pltpu.VMEM((2,) + shapes[i][1:], BF) for i in (0, 1, 3, 4)]
        + [pltpu.VMEM(shapes[5], BF)]
        + [
            pltpu.VMEM((count - 1,) + block, BF),
            pltpu.VMEM((count - 1,) + block, BF),
            pltpu.VMEM(block, BF),
            pltpu.VMEM(block, BF),
            pltpu.VMEM((count,) + block, BF),
            pltpu.VMEM((max(total, q_width), depth), BF),
            pltpu.VMEM((count, rows, q_width), BF),
            pltpu.VMEM((total, q_width + 128), BF),
            pltpu.VMEM(wqkv.shape, BF),
            pltpu.VMEM(h1.shape, BF),
            pltpu.VMEM((keys, 128), BF),
            pltpu.VMEM((keys, 128), F32),
            pltpu.VMEM((keys, 128), F32),
            pltpu.VMEM(kv_all.shape, BF),
            pltpu.VMEM((line,) + kv_all.shape[1:], BF),
            pltpu.VMEM((line,) + kv_all.shape[1:], BF),
            pltpu.VMEM((line - 1,) + kv_all.shape[1:], BF),
            pltpu.VMEM((2, 16, depth), F32),
            pltpu.VMEM((count, 16, depth), BF),
        ]
        + [dma(chunk_count)] * 13
        + [pltpu.SemaphoreType.REGULAR, dma(5)]
        + [dma(count - 1)] * 8
        + [dma(1)] * 2
        + [dma(line - 1)] * 2
        + [dma(count - 1)] * 2
    )
    out = pl.pallas_call(
        back_kernel,
        out_shape=ends + ends + [act, act],
        in_specs=[pl.BlockSpec(memory_space=pltpu.SMEM)] + [anywhere] * 11 + [local] * 12,
        out_specs=[anywhere] * 12 + [local] * 2,
        scratch_shapes=scratch,
        compiler_params=pltpu.CompilerParams(
            vmem_limit_bytes=62 * 1024 * 1024, has_side_effects=True
        ),
        cost_estimate=pl.CostEstimate(
            flops=10**11, bytes_accessed=10**9, transcendentals=10**7
        ),
        name="back_pass",
    )(
        at, *own, *other, back_part, out_part, w_out, wqkv, h1, mixed, branch_own, x_own, gain_one, gain_two,
        attended, queries, lse, kv_all, kp, cosine, sine,
    )
    return out[:6], out[6:12], out[12], out[13]

def sum_gradients_plain(owns, others, swapped):
    ends = []
    for own, other, slabs in zip(owns, others, swapped):
        value = (own.astype(F32) + to_sibling(other).astype(F32)).astype(BF)
        if slabs:
            value = jnp.stack([value[0]] + [along_plane(value[j], j) for j in range(1, value.shape[0])])
        ends.append(line_sum(value))
    return ends, [to_sibling(e) for e in ends]


def rms_backward(row_block, inverse, gain_vec, gradient):
    normed = row_block * inverse
    gain_grad = jnp.sum(gradient * normed, axis=0)
    scaled = gradient * gain_vec
    back = inverse * (scaled - normed * jnp.mean(scaled * normed, axis=1, keepdims=True))
    return (back, gain_grad)


def back_plain(
    at, own, other, back_part, out_part, w_out, wqkv, h1, mixed, branch_own, x_own, gain_one, gain_two,
    attended, queries, lse, kv_all, kp, cosine, sine,
):
    count, line = lax.axis_size("fsdp"), lax.axis_size("z")
    k = lax.axis_index("core")
    rows, depth = mixed.shape
    total, half_depth = count * rows, depth // 2
    half = half_depth // count
    q_width = attended.shape[1]
    f = lax.axis_index("fsdp")
    order = jnp.stack([(f ^ j) * 2 + (k ^ h) for h in range(2) for j in range(count)]).astype(jnp.int32)
    outputs = mixed + plane_reduce(out_part)
    inv_two = lax.rsqrt(jnp.mean(mixed * mixed, axis=1, keepdims=True) + EPSILON)
    mixed_back, gain_two_grad = rms_backward(mixed, inv_two, gain_two, plane_reduce(back_part))
    mixed_grad = branch_own.astype(F32) + mixed_back
    attn_back = jnp.concatenate(plane_gather(mixed_grad.astype(BF)))
    attended_grad = nt(attn_back, w_out).astype(BF).reshape(count, rows, q_width)
    own, other = list(own), list(other)
    for place, terms in ((k, own), (1 - k, other)):
        right = lax.dynamic_slice_in_dim(attn_back, place * half_depth, half_depth, 1)
        terms.append(tn(attended, right).astype(BF).reshape(2, -1, half_depth))
    query_back, kv_part = attend_back(at, queries, attended_grad, lse, kv_all, kp, cosine, sine)
    kv_mine = kv_part[:line].astype(F32) + to_sibling(kv_part[line:]).astype(F32)
    kv_back = kv_mine[0]
    for s in range(1, line):
        kv_back = kv_back + along_line(kv_mine[s].astype(BF), s).astype(F32)
    lead, trail, flat = kv_back[..., :32], kv_back[..., 32:64], kv_back[..., 64:]
    cos32, sin32 = cosine[:, :32], sine[:, 32:64]
    kv_back = jnp.concatenate(
        [lead * cos32 + trail * sin32, trail * cos32 - lead * sin32, flat], axis=-1
    ).astype(BF)
    qkv_back = jnp.concatenate(
        [query_back.reshape(total, q_width), kv_back.reshape(total, 128)], axis=1
    )
    normed_back = put_columns(nt(qkv_back, wqkv).astype(BF), order, 2 * count)
    inputs = x_own.astype(F32)
    inv_one = lax.rsqrt(jnp.mean(inputs * inputs, axis=1, keepdims=True) + EPSILON)
    input_back, gain_one_grad = rms_backward(
        inputs, inv_one, gain_one, plane_reduce(normed_back.reshape(count, rows, depth))
    )
    for side, terms in ((0, own), (1, other)):
        left = h1[:, side * half_depth : (side + 1) * half_depth]
        terms.append(tn(left, qkv_back).astype(BF).reshape(count, half, q_width + 128))
    gains = jnp.stack([gain_one_grad, gain_two_grad]).astype(BF)
    for bit in plane_bits():
        gains = (gains.astype(F32) + along_plane(gains, bit).astype(F32)).astype(BF)
    gains = jnp.pad(gains, ((0, 14), (0, 0)))[None]
    ends, sibs = sum_gradients_plain(own + [gains], other + [gains], (False, True, True, False, True, False))
    return ends, sibs, outputs, mixed_grad + input_back


def body(
    tokens, cotangent, lengths, attn_gain, w_query, w_key, w_value, w_out, mlp_gain, w_gate, w_up, w_down
):
    seqs, rows, depth = tokens.shape
    count, line = lax.axis_size("fsdp"), lax.axis_size("z")
    f, z, k = lax.axis_index("fsdp"), lax.axis_index("z"), lax.axis_index("core")
    slot = rows * line * 2
    total = count * rows
    slab = depth // count
    half = slab // 2
    q_width = HEADS * HEAD_DIM // count
    shared = max(1, count // KV_HEADS)

    x_own = tokens.reshape(rows, depth)
    chunk = 2 * z + k
    first_pos = slot - 1 - chunk * rows

    length = lengths[0]
    words = jnp.zeros((slab,), F32).at[0].set((length // 64).astype(F32)).at[1].set((length % 64).astype(F32))
    note = jnp.stack([attn_gain, mlp_gain, words.astype(BF), jnp.zeros((slab,), BF)])
    notes = [note] + [along_plane(note, j) for j in range(1, count)]
    notes_abs = [lax.dynamic_index_in_dim(jnp.stack(notes), f ^ i, 0, keepdims=False) for i in range(count)]
    gain_one = jnp.concatenate([n[0] for n in notes_abs]).astype(F32).reshape(1, depth)
    gain_two = jnp.concatenate([n[1] for n in notes_abs]).astype(F32).reshape(1, depth)
    all_lengths = jnp.stack(
        [n[2, 0].astype(jnp.int32) * 64 + n[2, 1].astype(jnp.int32) for n in notes]
    )

    x_all = jnp.concatenate(plane_gather(x_own))

    wq = cut_blocks(w_query, f, k, count)
    key_cols = lax.dynamic_slice_in_dim(w_key, k * half, half, 0).reshape(half, KV_HEADS, HEAD_DIM)
    value_cols = lax.dynamic_slice_in_dim(w_value, k * half, half, 0).reshape(half, KV_HEADS, HEAD_DIM)

    def head_of(j):
        return (f ^ j) // shared

    wkv = jnp.stack(
        [
            jnp.concatenate(
                [
                    lax.dynamic_index_in_dim(key_cols, head_of(j), 1, keepdims=False),
                    lax.dynamic_index_in_dim(value_cols, head_of(j), 1, keepdims=False),
                ],
                axis=1,
            )
            for j in range(count)
        ]
    )
    wqkv = jnp.concatenate([wq, wkv], axis=2)
    wqkv_own = jnp.stack([wqkv[0]] + [along_plane(wqkv[j], j) for j in range(1, count)])
    wqkv_sib = to_sibling(wqkv_own)
    wqkv_all = jnp.concatenate([wqkv_own, wqkv_sib]).reshape(depth, q_width + 128)

    def fetch(weight):
        cut = cut_blocks(weight, f, k, count)
        width = cut.shape[2]
        own = jnp.stack([cut[0]] + [along_plane(cut[j], j) for j in range(1, count)])
        sib = to_sibling(own)
        return own.reshape(depth // 2, width), sib.reshape(depth // 2, width)

    gate_own, gate_sib = fetch(w_gate)
    up_own, up_sib = fetch(w_up)

    order = jnp.stack([(f ^ j) * 2 + (k ^ h) for h in range(2) for j in range(count)]).astype(jnp.int32)

    half_dim = HEAD_DIM // 2
    frequency = jnp.power(ROPE_BASE, jnp.arange(half_dim, dtype=F32) * (-2.0 / HEAD_DIM))
    positions = first_pos - jnp.arange(rows, dtype=jnp.int32)
    angles = positions.astype(F32)[:, None] * frequency[None, :]
    cos32, sin32 = jnp.cos(angles), jnp.sin(angles)
    cosine = jnp.concatenate([cos32] * 4, axis=1)
    sine = jnp.concatenate([-sin32, sin32, -sin32, sin32], axis=1)

    normed_one, queries, kv = qkv_project(order, x_all, gain_one, wqkv_all, cosine, sine, rows)
    queries = queries.reshape(count, rows, q_width)
    kv = kv.reshape(count, rows, 128)

    mine = [kv] + [along_line(kv, -s) for s in range(1, line)]
    mine = jnp.stack(mine)
    kv_all = jnp.concatenate([mine, to_sibling(mine)])
    places = []
    for h in range(2):
        for s in range(line):
            start = slot - 1 - (2 * (z + s) + (k ^ h)) * rows
            places.append(start - jnp.arange(rows, dtype=jnp.int32))
    kp = jnp.concatenate(places)
    kp = jnp.where(kp < 0, FAR, kp).reshape(1, -1)
    at = jnp.concatenate([first_pos.reshape(1), all_lengths]).astype(jnp.int32)

    attended, log_total = attend(at, queries, kv_all, kp)
    attended = attended.reshape(total, q_width)

    mixed_part = nn(attended, w_out).astype(BF).reshape(count, rows, depth)
    inputs = x_own.astype(F32)
    mixed = inputs + plane_reduce(mixed_part)
    inv_two = lax.rsqrt(jnp.mean(mixed * mixed, axis=1, keepdims=True) + EPSILON)
    normed_two_own = (mixed * inv_two * gain_two).astype(BF)
    normed_two = jnp.concatenate(plane_gather(normed_two_own))
    normed_two = pick_columns(normed_two, order, 2 * count)
    n2_own, n2_sib = normed_two[:, : depth // 2], normed_two[:, depth // 2 :]

    valid = (positions < length).astype(F32)[:, None]
    out_back = cotangent.reshape(rows, depth).astype(F32) * valid
    branch_own = out_back.astype(BF)
    branch = jnp.concatenate(plane_gather(branch_own))

    gate = nn(n2_own, gate_own) + nn(n2_sib, gate_sib)
    up = nn(n2_own, up_own) + nn(n2_sib, up_sib)
    sigmoid = jax.nn.sigmoid(gate)
    hidden = (gate * sigmoid * up).astype(BF)

    half_depth = depth // 2
    branch_mine = lax.dynamic_slice_in_dim(branch, k * half_depth, half_depth, 1)
    branch_other = lax.dynamic_slice_in_dim(branch, (1 - k) * half_depth, half_depth, 1)

    def pair_sum(own, other):
        return (own + to_sibling(other.astype(BF)).astype(F32)).astype(BF)

    def swap_slabs(own):
        return jnp.stack([own[0]] + [along_plane(own[j], j) for j in range(1, count)])

    terms = {"down": (tn(hidden, branch_mine).astype(BF), tn(hidden, branch_other).astype(BF))}

    hidden_grad = nt(branch, w_down)
    gate_back = (hidden_grad * up * sigmoid * (1.0 + gate * (1.0 - sigmoid))).astype(BF)
    up_back = (hidden_grad * gate * sigmoid).astype(BF)

    def slab_terms(left_own, left_other, right):
        return tuple(
            tn(left, right).astype(BF).reshape(count, half, right.shape[1]) for left in (left_own, left_other)
        )

    terms["gate"] = slab_terms(n2_own, n2_sib, gate_back)
    terms["up"] = slab_terms(n2_own, n2_sib, up_back)

    back_own = (nt(gate_back, gate_own) + nt(up_back, up_own)).astype(BF)
    back_sib = (nt(gate_back, gate_sib) + nt(up_back, up_sib)).astype(BF)
    normed_back = put_columns(jnp.concatenate([back_own, back_sib], axis=1), order, 2 * count)
    normed_back = normed_back.reshape(count, rows, depth)
    out_part = nn(hidden, w_down).astype(BF).reshape(count, rows, depth)
    terms["down"] = tuple(t.reshape(4, -1, half_depth) for t in terms["down"])
    names = ("down", "gate", "up")
    own, other = [terms[n][0] for n in names], [terms[n][1] for n in names]
    rest = (mixed, branch_own, x_own, gain_one, gain_two, attended, queries, log_total, kv_all, kp, cosine, sine)
    run = back_pass if line == 4 and q_width % 256 == 0 else back_plain
    owns, sibs, outputs, input_grad = run(
        at, own, other, normed_back, out_part, w_out, wqkv_all, normed_one, *rest
    )

    def columns(i):
        return join_columns(*(x[i].reshape(-1, half_depth) for x in (owns, sibs)), k)

    down_grad, out_grad = columns(0), columns(3)
    gate_grad, up_grad = (join_rows(owns[i], sibs[i], f, k) for i in (1, 2))
    qkv_half, qkv_sib = owns[4], sibs[4]
    query_grad = join_rows(qkv_half[:, :, :q_width], qkv_sib[:, :, :q_width], f, k)
    gains = lax.dynamic_slice_in_dim(owns[5][0, :2], f * slab, slab, 1).astype(F32)
    halves = jnp.stack([qkv_half[:, :, q_width:], qkv_sib[:, :, q_width:]])

    def by_head(lo, hi):
        both = [lax.dynamic_index_in_dim(halves, k ^ h, 0, keepdims=False) for h in range(2)]
        both = jnp.concatenate(both, axis=1).astype(F32)[:, :, lo:hi]
        cols = jnp.stack([lax.dynamic_index_in_dim(both, f ^ i, 0, keepdims=False) for i in range(count)])
        cols = cols.reshape(KV_HEADS, shared, slab, HEAD_DIM).sum(1)
        return jnp.transpose(cols, (1, 0, 2)).reshape(slab, KV_HEADS * HEAD_DIM)

    key_grad = by_head(0, 64)
    value_grad = by_head(64, 128)

    return (
        outputs.reshape(seqs, rows, depth),
        input_grad.reshape(seqs, rows, depth),
        gains[0],
        query_grad,
        key_grad,
        value_grad,
        out_grad,
        gains[1],
        gate_grad,
        up_grad,
        down_grad,
    )


def solution(mesh):
    count, ctx = mesh.shape["fsdp"], mesh.shape["ctx"]
    split = Mesh(mesh.devices.reshape(count, ctx // 2, 2), ("fsdp", "z", "core"))
    act = P("fsdp", ("z", "core"), None)
    row, mat = P("fsdp"), P("fsdp", None)
    return jax.shard_map(
        body,
        mesh=split,
        in_specs=(act, act, row, row, mat, mat, mat, mat, row, mat, mat, mat),
        out_specs=(act, act, row, mat, mat, mat, mat, row, mat, mat, mat),
        check_vma=False,
    )
```

```python
import functools

import jax
import jax.numpy as jnp
import numpy as np
from jax import lax
from jax.experimental import pallas as pl
from jax.experimental.pallas import tpu as pltpu
from jax.sharding import Mesh
from jax.sharding import PartitionSpec as P

HEADS = 32
KV_HEADS = 4
HEAD_DIM = 64
EPSILON = 1e-05
ROPE_BASE = 10000.0
MASKED = -1e30
FAR = 1 << 30
BF = jnp.bfloat16
F32 = jnp.float32
VMEM_BYTES = 56 * 1024 * 1024


def params(**kw):
    return pltpu.CompilerParams(vmem_limit_bytes=VMEM_BYTES, **kw)


def along_plane(value, step):
    count = lax.axis_size("fsdp")
    return lax.ppermute(value, "fsdp", [(i, i ^ step) for i in range(count)])


def to_sibling(value):
    return lax.ppermute(value, "core", [(0, 1), (1, 0)])


def along_line(value, shift):
    count = lax.axis_size("z")
    return lax.ppermute(
        value, "z", [(i, i + shift) for i in range(count) if 0 <= i + shift < count]
    )


def plane_bits():
    count = lax.axis_size("fsdp")
    return [1 << b for b in range(count.bit_length() - 1)]


def plane_gather(block):
    half = block.shape[0] // 2
    parts = []
    for which, bits in ((0, plane_bits()), (1, plane_bits()[::-1])):
        held = {0: block[which * half : (which + 1) * half]}
        for bit in bits:
            order = sorted(held)
            got = along_plane(jnp.stack([held[j] for j in order]), bit)
            for n, j in enumerate(order):
                held[j ^ bit] = got[n]
        parts.append(held)
    return [jnp.concatenate([parts[0][j], parts[1][j]]) for j in range(lax.axis_size("fsdp"))]


def plane_reduce(partial):
    half = partial.shape[1] // 2
    done = []
    for which, bits in ((0, plane_bits()[::-1]), (1, plane_bits())):
        held = {j: partial[j, which * half : (which + 1) * half] for j in range(partial.shape[0])}
        for bit in bits:
            going = [j for j in sorted(held) if j & bit]
            got = along_plane(jnp.stack([held[j].astype(BF) for j in going]), bit)
            for n, j in enumerate(going):
                held[j ^ bit] = held[j ^ bit].astype(F32) + got[n].astype(F32)
                del held[j]
        done.append(held[0])
    return jnp.concatenate(done)


def line_sum(value):
    count = lax.axis_size("z")
    place = lax.axis_index("z")
    half = count // 2
    for i in range(half - 1):
        got = lax.ppermute(value, "z", [(i, i + 1), (count - 1 - i, count - 2 - i)])
        value = value + got
    value = value + lax.ppermute(value, "z", [(half - 1, half), (half, half - 1)])
    for i in range(half - 2, -1, -1):
        got = lax.ppermute(value, "z", [(i + 1, i), (count - 2 - i, count - 1 - i)])
        outer = (place == i) | (place == count - 1 - i)
        value = jnp.where(outer, got, value)
    return value


def move_kernel(idx_ref, x_ref, o_ref):
    o_ref[...] = x_ref[...]


def pick_columns(x, index, count):
    rows, width = x.shape
    size = width // count
    spec = pltpu.PrefetchScalarGridSpec(
        num_scalar_prefetch=1,
        grid=(count,),
        in_specs=[pl.BlockSpec((rows, size), lambda b, idx: (0, idx[b]))],
        out_specs=pl.BlockSpec((rows, size), lambda b, idx: (0, b)),
    )
    return pl.pallas_call(
        move_kernel,
        grid_spec=spec,
        out_shape=jax.ShapeDtypeStruct(x.shape, x.dtype),
        compiler_params=params(),
        name="pick_columns",
    )(index, x)


def put_columns(x, index, count):
    rows, width = x.shape
    size = width // count
    spec = pltpu.PrefetchScalarGridSpec(
        num_scalar_prefetch=1,
        grid=(count,),
        in_specs=[pl.BlockSpec((rows, size), lambda b, idx: (0, b))],
        out_specs=pl.BlockSpec((rows, size), lambda b, idx: (0, idx[b])),
    )
    return pl.pallas_call(
        move_kernel,
        grid_spec=spec,
        out_shape=jax.ShapeDtypeStruct(x.shape, x.dtype),
        compiler_params=params(),
        name="put_columns",
    )(index, x)


def cut_blocks(weight, f, k, count, dtype=BF):
    rows, full = weight.shape
    width, half = full // count, rows // 2
    if width % 128:
        own = lax.dynamic_slice_in_dim(weight, k * half, half, 0).reshape(half, count, width)
        return jnp.stack(
            [lax.dynamic_index_in_dim(own, f ^ j, 1, keepdims=False) for j in range(count)]
        )
    spec = pltpu.PrefetchScalarGridSpec(
        num_scalar_prefetch=1,
        grid=(count,),
        in_specs=[pl.BlockSpec((half, width), lambda j, at: (at[1], at[0] ^ j))],
        out_specs=pl.BlockSpec((None, half, width), lambda j, at: (j, 0, 0)),
    )
    return pl.pallas_call(
        move_kernel,
        grid_spec=spec,
        out_shape=jax.ShapeDtypeStruct((count, half, width), weight.dtype),
        compiler_params=params(),
        name="cut_blocks",
    )(jnp.stack([f, k]), weight)


def join_kernel(at_ref, own_ref, sib_ref, o_ref):
    @pl.when(pl.program_id(0) == 0)
    def _():
        o_ref[...] = own_ref[...].astype(o_ref.dtype)

    @pl.when(pl.program_id(0) == 1)
    def _():
        o_ref[...] = sib_ref[...].astype(o_ref.dtype)


def join_rows(own, sib, f, k):
    count, half, width = own.shape
    if width % 128:
        halves = jnp.stack([own, sib])
        return jnp.concatenate(
            [
                jnp.concatenate(
                    [
                        lax.dynamic_index_in_dim(
                            lax.dynamic_index_in_dim(halves, k ^ h, 0, keepdims=False),
                            f ^ i,
                            0,
                            keepdims=False,
                        )
                        for i in range(count)
                    ],
                    axis=1,
                )
                for h in range(2)
            ],
            axis=0,
        ).astype(F32)
    spec = pltpu.PrefetchScalarGridSpec(
        num_scalar_prefetch=1,
        grid=(2, count),
        in_specs=[
            pl.BlockSpec(
                (None, half, width),
                lambda s, i, at: (at[0] ^ jnp.where(s == 0, i, count - 1), 0, 0),
            ),
            pl.BlockSpec(
                (None, half, width), lambda s, i, at: (at[0] ^ jnp.where(s == 1, i, 0), 0, 0)
            ),
        ],
        out_specs=pl.BlockSpec((half, width), lambda s, i, at: (at[1] ^ s, i)),
    )
    return pl.pallas_call(
        join_kernel,
        grid_spec=spec,
        out_shape=jax.ShapeDtypeStruct((2 * half, count * width), F32),
        compiler_params=params(),
        name="join_rows",
    )(jnp.stack([f, k]), own, sib)


def join_columns(own, sib, k):
    rows, half = own.shape
    count = 4
    size = rows // count
    spec = pltpu.PrefetchScalarGridSpec(
        num_scalar_prefetch=1,
        grid=(2, count),
        in_specs=[
            pl.BlockSpec((size, half), lambda s, i, at: (jnp.where(s == 0, i, count - 1), 0)),
            pl.BlockSpec((size, half), lambda s, i, at: (jnp.where(s == 1, i, 0), 0)),
        ],
        out_specs=pl.BlockSpec((size, half), lambda s, i, at: (i, at[0] ^ s)),
    )
    return pl.pallas_call(
        join_kernel,
        grid_spec=spec,
        out_shape=jax.ShapeDtypeStruct((rows, 2 * half), F32),
        compiler_params=params(),
        name="join_columns",
    )(k.reshape(1), own, sib)


def swap_halves(block):
    lane = lax.broadcasted_iota(jnp.int32, block.shape, 1)
    return jnp.where(lane % 64 < 32, pltpu.roll(block, 96, 1), pltpu.roll(block, 32, 1))


def qkv_kernel(idx_ref, x_ref, gain_ref, w_ref, cos_ref, sin_ref, h_ref, q_ref, kv_ref):
    blocks = idx_ref.shape[0]
    size = x_ref.shape[1] // blocks
    x = x_ref[...].astype(F32)
    inverse = lax.rsqrt(jnp.mean(x * x, axis=1, keepdims=True) + EPSILON)
    for b in range(blocks):
        at = pl.ds(pl.multiple_of(idx_ref[b] * size, 128), size)
        part = x_ref[:, at].astype(F32) * inverse * gain_ref[:, at]
        h_ref[:, b * size : (b + 1) * size] = part.astype(BF)
    out = jnp.dot(h_ref[...], w_ref[...], preferred_element_type=F32)
    cosine, sine = cos_ref[...], sin_ref[...]
    pairs = q_ref.shape[1] // 128
    for c in range(pairs):
        block = out[:, c * 128 : (c + 1) * 128]
        q_ref[:, c * 128 : (c + 1) * 128] = (block * cosine + swap_halves(block) * sine).astype(BF)
    block = out[:, pairs * 128 :]
    lane = lax.broadcasted_iota(jnp.int32, block.shape, 1)
    turned = block * cosine + swap_halves(block) * sine
    kv_ref[...] = jnp.where(lane < 64, turned, block).astype(BF)


def qkv_project(idx, x, gain, weight, cosine, sine, rows):
    total, depth = x.shape
    width = weight.shape[1]
    spec = pltpu.PrefetchScalarGridSpec(
        num_scalar_prefetch=1,
        grid=(total // rows,),
        in_specs=[
            pl.BlockSpec((rows, depth), lambda i, idx: (i, 0)),
            pl.BlockSpec((1, depth), lambda i, idx: (0, 0)),
            pl.BlockSpec((depth, width), lambda i, idx: (0, 0)),
            pl.BlockSpec((rows, 128), lambda i, idx: (0, 0)),
            pl.BlockSpec((rows, 128), lambda i, idx: (0, 0)),
        ],
        out_specs=[
            pl.BlockSpec((rows, depth), lambda i, idx: (i, 0)),
            pl.BlockSpec((rows, width - 128), lambda i, idx: (i, 0)),
            pl.BlockSpec((rows, 128), lambda i, idx: (i, 0)),
        ],
    )
    return pl.pallas_call(
        qkv_kernel,
        grid_spec=spec,
        out_shape=[
            jax.ShapeDtypeStruct((total, depth), BF),
            jax.ShapeDtypeStruct((total, width - 128), BF),
            jax.ShapeDtypeStruct((total, 128), BF),
        ],
        compiler_params=params(),
        cost_estimate=pl.CostEstimate(
            flops=2 * total * depth * width,
            bytes_accessed=4 * total * depth + 2 * depth * width + 2 * total * width,
            transcendentals=0,
        ),
        name="qkv_project",
    )(idx, x, gain, weight, cosine, sine)


def nt(a, b):
    return lax.dot_general(a, b, (((1,), (1,)), ((), ())), preferred_element_type=F32)


def tn(a, b):
    return lax.dot_general(a, b, (((0,), (0,)), ((), ())), preferred_element_type=F32)


def nn(a, b):
    return jnp.dot(a, b, preferred_element_type=F32)


def limits(at_ref, rows):
    j = pl.program_id(0)
    place = at_ref[0] - lax.broadcasted_iota(jnp.int32, (rows, 1), 0)
    return jnp.minimum(place, at_ref[1 + j] - 1)


def attend_kernel(at_ref, q_ref, kv_ref, kp_ref, o_ref, lse_ref, vk_ref):
    rows = q_ref.shape[0]
    keys = vk_ref.shape[0]
    kv = kv_ref[...].reshape(keys, 128)

    @pl.when(pl.program_id(1) == 0)
    def _():
        vk_ref[...] = pltpu.roll(kv.astype(F32), 64, 1).astype(BF)

    vk = vk_ref[...]
    allowed = kp_ref[...] <= limits(at_ref, rows)
    lane = lax.broadcasted_iota(jnp.int32, (rows, 128), 1)
    q = q_ref[...]
    zero = jnp.zeros_like(q)
    outs, logs = [], []
    for first in (True, False):
        mine = lane < 64 if first else lane >= 64
        scores = nt(jnp.where(mine, q, zero), kv if first else vk) * (HEAD_DIM**-0.5)
        scores = jnp.where(allowed, scores, MASKED)
        top = jnp.max(scores, axis=1, keepdims=True)
        weights = jnp.exp(scores - top)
        total = jnp.sum(weights, axis=1, keepdims=True)
        outs.append(nn(weights.astype(BF), vk if first else kv) / total)
        logs.append(jnp.broadcast_to(top + jnp.log(total), (rows, 128)))
    o_ref[...] = jnp.where(lane < 64, outs[0], outs[1]).astype(BF)
    lse_ref[...] = jnp.where(lane < 64, logs[0], logs[1])


def attend(at, q, kv, kp):
    chunks, seqs, rows, _ = kv.shape
    pairs = q.shape[2] // 128
    keys = chunks * rows
    spec = pltpu.PrefetchScalarGridSpec(
        num_scalar_prefetch=1,
        grid=(seqs, pairs),
        in_specs=[
            pl.BlockSpec((None, rows, 128), lambda j, p, at: (j, 0, p)),
            pl.BlockSpec((chunks, None, rows, 128), lambda j, p, at: (0, j, 0, 0)),
            pl.BlockSpec((1, keys), lambda j, p, at: (0, 0)),
        ],
        out_specs=[
            pl.BlockSpec((None, rows, 128), lambda j, p, at: (j, 0, p)),
            pl.BlockSpec((None, rows, 128), lambda j, p, at: (j, 0, p)),
        ],
        scratch_shapes=[pltpu.VMEM((keys, 128), BF)],
    )
    size = seqs * pairs * 2 * rows * keys
    return pl.pallas_call(
        attend_kernel,
        grid_spec=spec,
        out_shape=[
            jax.ShapeDtypeStruct(q.shape, BF),
            jax.ShapeDtypeStruct(q.shape, F32),
        ],
        compiler_params=params(),
        cost_estimate=pl.CostEstimate(
            flops=size * 4 * 128, bytes_accessed=4 << 20, transcendentals=size
        ),
        name="attend",
    )(at, q, kv, kp)


def attend_back_kernel(
    at_ref, q_ref, do_ref, lse_ref, kv_ref, kp_ref, cos_ref, sin_ref, dq_ref, dkv_ref, vk_ref, dk_ref, dv_ref
):
    rows = q_ref.shape[0]
    keys = vk_ref.shape[0]
    pair = pl.program_id(1)
    kv = kv_ref[...].reshape(keys, 128)

    @pl.when(pair == 0)
    def _():
        vk_ref[...] = pltpu.roll(kv.astype(F32), 64, 1).astype(BF)
        dk_ref[...] = jnp.zeros_like(dk_ref)
        dv_ref[...] = jnp.zeros_like(dv_ref)

    vk = vk_ref[...]
    allowed = kp_ref[...] <= limits(at_ref, rows)
    lane = lax.broadcasted_iota(jnp.int32, (rows, 128), 1)
    q, do = q_ref[...], do_ref[...]
    zero = jnp.zeros_like(q)
    parts = []
    for first in (True, False):
        mine = lane < 64 if first else lane >= 64
        keyed, valued = (kv, vk) if first else (vk, kv)
        q_own, do_own = jnp.where(mine, q, zero), jnp.where(mine, do, zero)
        scores = nt(q_own, keyed) * (HEAD_DIM**-0.5)
        log_total = lse_ref[:, 0:1] if first else lse_ref[:, 64:65]
        weights = jnp.where(allowed, jnp.exp(scores - log_total), 0.0)
        joint = weights * nt(do_own, valued)
        back = (joint - weights * jnp.sum(joint, axis=1, keepdims=True)).astype(BF)
        parts.append(nn(back, keyed))
        dk_ref[...] += tn(back, q_own)
        dv_ref[...] += tn(weights.astype(BF), do_own)
    turned = jnp.where(lane < 64, parts[0], parts[1]) * (HEAD_DIM**-0.5)
    dq_ref[...] = (turned * cos_ref[...] - swap_halves(turned) * sin_ref[...]).astype(BF)

    @pl.when(pair == pl.num_programs(1) - 1)
    def _():
        dk = dk_ref[...]
        dv = dv_ref[...]
        dk = (dk + pltpu.roll(dk, 64, 1)) * (HEAD_DIM**-0.5)
        dv = dv + pltpu.roll(dv, 64, 1)
        wide = lax.broadcasted_iota(jnp.int32, dk.shape, 1)
        dkv_ref[...] = jnp.where(wide < 64, dk, dv).astype(BF).reshape(dkv_ref.shape)


def attend_back(at, q, do, lse, kv, kp, cosine, sine):
    chunks, seqs, rows, _ = kv.shape
    pairs = q.shape[2] // 128
    keys = chunks * rows
    tall = pl.BlockSpec((None, rows, 128), lambda j, p, at: (j, 0, p))
    whole = pl.BlockSpec((chunks, None, rows, 128), lambda j, p, at: (0, j, 0, 0))
    flat = pl.BlockSpec((rows, 128), lambda j, p, at: (0, 0))
    spec = pltpu.PrefetchScalarGridSpec(
        num_scalar_prefetch=1,
        grid=(seqs, pairs),
        in_specs=[tall, tall, tall, whole, pl.BlockSpec((1, keys), lambda j, p, at: (0, 0)), flat, flat],
        out_specs=[tall, whole],
        scratch_shapes=[
            pltpu.VMEM((keys, 128), BF),
            pltpu.VMEM((keys, 128), F32),
            pltpu.VMEM((keys, 128), F32),
        ],
    )
    size = seqs * pairs * 2 * rows * keys
    return pl.pallas_call(
        attend_back_kernel,
        grid_spec=spec,
        out_shape=[
            jax.ShapeDtypeStruct(q.shape, BF),
            jax.ShapeDtypeStruct(kv.shape, BF),
        ],
        compiler_params=params(),
        cost_estimate=pl.CostEstimate(
            flops=size * 10 * 128, bytes_accessed=8 << 20, transcendentals=size
        ),
        name="attend_back",
    )(at, q, do, lse, kv, kp, cosine, sine)


def rms_backward(row_block, inverse, gain_vec, gradient):
    normed = row_block * inverse
    gain_grad = jnp.sum(gradient * normed, axis=0)
    scaled = gradient * gain_vec
    back = inverse * (scaled - normed * jnp.mean(scaled * normed, axis=1, keepdims=True))
    return (back, gain_grad)


def body_plain(
    tokens, cotangent, lengths, attn_gain, w_query, w_key, w_value, w_out, mlp_gain, w_gate, w_up, w_down
):
    seqs, rows, depth = tokens.shape
    count, line = lax.axis_size("fsdp"), lax.axis_size("z")
    f, z, k = lax.axis_index("fsdp"), lax.axis_index("z"), lax.axis_index("core")
    slot = rows * line * 2
    total = count * rows
    slab = depth // count
    half = slab // 2
    q_width = HEADS * HEAD_DIM // count
    shared = max(1, count // KV_HEADS)

    x_own = tokens.reshape(rows, depth)
    chunk = 2 * z + k
    first_pos = slot - 1 - chunk * rows

    length = lengths[0]
    words = jnp.zeros((slab,), F32).at[0].set((length // 64).astype(F32)).at[1].set((length % 64).astype(F32))
    note = jnp.stack([attn_gain, mlp_gain, words.astype(BF), jnp.zeros((slab,), BF)])
    notes = [note] + [along_plane(note, j) for j in range(1, count)]
    notes_abs = [lax.dynamic_index_in_dim(jnp.stack(notes), f ^ i, 0, keepdims=False) for i in range(count)]
    gain_one = jnp.concatenate([n[0] for n in notes_abs]).astype(F32).reshape(1, depth)
    gain_two = jnp.concatenate([n[1] for n in notes_abs]).astype(F32).reshape(1, depth)
    all_lengths = jnp.stack(
        [n[2, 0].astype(jnp.int32) * 64 + n[2, 1].astype(jnp.int32) for n in notes]
    )

    x_all = jnp.concatenate(plane_gather(x_own))

    wq = cut_blocks(w_query, f, k, count)
    key_cols = lax.dynamic_slice_in_dim(w_key, k * half, half, 0).reshape(half, KV_HEADS, HEAD_DIM)
    value_cols = lax.dynamic_slice_in_dim(w_value, k * half, half, 0).reshape(half, KV_HEADS, HEAD_DIM)

    def head_of(j):
        return (f ^ j) // shared

    wkv = jnp.stack(
        [
            jnp.concatenate(
                [
                    lax.dynamic_index_in_dim(key_cols, head_of(j), 1, keepdims=False),
                    lax.dynamic_index_in_dim(value_cols, head_of(j), 1, keepdims=False),
                ],
                axis=1,
            )
            for j in range(count)
        ]
    )
    wqkv = jnp.concatenate([wq, wkv], axis=2)
    wqkv_own = jnp.stack([wqkv[0]] + [along_plane(wqkv[j], j) for j in range(1, count)])
    wqkv_sib = to_sibling(wqkv_own)
    wqkv_all = jnp.concatenate([wqkv_own, wqkv_sib]).reshape(depth, q_width + 128)

    def fetch(weight):
        cut = cut_blocks(weight, f, k, count)
        width = cut.shape[2]
        own = jnp.stack([cut[0]] + [along_plane(cut[j], j) for j in range(1, count)])
        sib = to_sibling(own)
        return own.reshape(depth // 2, width), sib.reshape(depth // 2, width)

    gate_own, gate_sib = fetch(w_gate)
    up_own, up_sib = fetch(w_up)

    order = jnp.stack([(f ^ j) * 2 + (k ^ h) for h in range(2) for j in range(count)]).astype(jnp.int32)

    half_dim = HEAD_DIM // 2
    frequency = jnp.power(ROPE_BASE, jnp.arange(half_dim, dtype=F32) * (-2.0 / HEAD_DIM))
    positions = first_pos - jnp.arange(rows, dtype=jnp.int32)
    angles = positions.astype(F32)[:, None] * frequency[None, :]
    cos32, sin32 = jnp.cos(angles), jnp.sin(angles)
    cosine = jnp.concatenate([cos32] * 4, axis=1)
    sine = jnp.concatenate([-sin32, sin32, -sin32, sin32], axis=1)

    normed_one, queries, kv = qkv_project(order, x_all, gain_one, wqkv_all, cosine, sine, rows)
    queries = queries.reshape(count, rows, q_width)
    kv = kv.reshape(count, rows, 128)

    mine = [kv] + [along_line(kv, -s) for s in range(1, line)]
    mine = jnp.stack(mine)
    kv_all = jnp.concatenate([mine, to_sibling(mine)])
    places = []
    for h in range(2):
        for s in range(line):
            start = slot - 1 - (2 * (z + s) + (k ^ h)) * rows
            places.append(start - jnp.arange(rows, dtype=jnp.int32))
    kp = jnp.concatenate(places)
    kp = jnp.where(kp < 0, FAR, kp).reshape(1, -1)
    at = jnp.concatenate([first_pos.reshape(1), all_lengths]).astype(jnp.int32)

    attended, log_total = attend(at, queries, kv_all, kp)
    attended = attended.reshape(total, q_width)

    mixed_part = nn(attended, w_out).astype(BF).reshape(count, rows, depth)
    inputs = x_own.astype(F32)
    mixed = inputs + plane_reduce(mixed_part)
    inv_two = lax.rsqrt(jnp.mean(mixed * mixed, axis=1, keepdims=True) + EPSILON)
    normed_two_own = (mixed * inv_two * gain_two).astype(BF)
    normed_two = jnp.concatenate(plane_gather(normed_two_own))
    normed_two = pick_columns(normed_two, order, 2 * count)
    n2_own, n2_sib = normed_two[:, : depth // 2], normed_two[:, depth // 2 :]

    valid = (positions < length).astype(F32)[:, None]
    out_back = cotangent.reshape(rows, depth).astype(F32) * valid
    branch_own = out_back.astype(BF)
    branch = jnp.concatenate(plane_gather(branch_own))

    gate = nn(n2_own, gate_own) + nn(n2_sib, gate_sib)
    up = nn(n2_own, up_own) + nn(n2_sib, up_sib)
    sigmoid = jax.nn.sigmoid(gate)
    hidden = (gate * sigmoid * up).astype(BF)

    half_depth = depth // 2
    branch_mine = lax.dynamic_slice_in_dim(branch, k * half_depth, half_depth, 1)
    branch_other = lax.dynamic_slice_in_dim(branch, (1 - k) * half_depth, half_depth, 1)

    def pair_sum(own, other):
        return (own + to_sibling(other.astype(BF)).astype(F32)).astype(BF)

    def swap_slabs(own):
        return jnp.stack([own[0]] + [along_plane(own[j], j) for j in range(1, count)])

    down_half = line_sum(pair_sum(tn(hidden, branch_mine), tn(hidden, branch_other)))
    down_grad = join_columns(down_half, to_sibling(down_half), k)

    hidden_grad = nt(branch, w_down)
    gate_back = (hidden_grad * up * sigmoid * (1.0 + gate * (1.0 - sigmoid))).astype(BF)
    up_back = (hidden_grad * gate * sigmoid).astype(BF)

    def slab_grad(left_own, left_other, right):
        width = right.shape[1]
        own = pair_sum(tn(left_own, right), tn(left_other, right)).reshape(count, half, width)
        return line_sum(swap_slabs(own))

    gate_half = slab_grad(n2_own, n2_sib, gate_back)
    gate_grad = join_rows(gate_half, to_sibling(gate_half), f, k)
    up_half = slab_grad(n2_own, n2_sib, up_back)
    up_grad = join_rows(up_half, to_sibling(up_half), f, k)

    back_own = (nt(gate_back, gate_own) + nt(up_back, up_own)).astype(BF)
    back_sib = (nt(gate_back, gate_sib) + nt(up_back, up_sib)).astype(BF)
    normed_back = put_columns(jnp.concatenate([back_own, back_sib], axis=1), order, 2 * count)
    normed_back = plane_reduce(normed_back.reshape(count, rows, depth))

    out_part = nn(hidden, w_down).astype(BF).reshape(count, rows, depth)
    outputs = mixed + plane_reduce(out_part)

    mixed_back, gain_two_grad = rms_backward(mixed, inv_two, gain_two, normed_back)
    mixed_grad = out_back + mixed_back
    attn_back = jnp.concatenate(plane_gather(mixed_grad.astype(BF)))
    attended_grad = nt(attn_back, w_out).astype(BF).reshape(count, rows, q_width)

    back_mine = lax.dynamic_slice_in_dim(attn_back, k * half_depth, half_depth, 1)
    back_other = lax.dynamic_slice_in_dim(attn_back, (1 - k) * half_depth, half_depth, 1)
    out_half = line_sum(pair_sum(tn(attended, back_mine), tn(attended, back_other)))
    out_grad = join_columns(out_half, to_sibling(out_half), k)

    query_back, kv_part = attend_back(at, queries, attended_grad, log_total, kv_all, kp, cosine, sine)
    kv_mine = kv_part[:line].astype(F32) + to_sibling(kv_part[line:]).astype(F32)
    kv_back = kv_mine[0]
    for s in range(1, line):
        kv_back = kv_back + along_line(kv_mine[s].astype(BF), s).astype(F32)
    lead, trail, flat = kv_back[..., :32], kv_back[..., 32:64], kv_back[..., 64:]
    kv_back = jnp.concatenate(
        [lead * cos32 + trail * sin32, trail * cos32 - lead * sin32, flat], axis=-1
    ).astype(BF)
    qkv_back = jnp.concatenate(
        [query_back.reshape(total, q_width), kv_back.reshape(total, 128)], axis=1
    )

    normed_one_back = nt(qkv_back, wqkv_all).astype(BF)
    normed_one_back = put_columns(normed_one_back, order, 2 * count)
    normed_one_back = plane_reduce(normed_one_back.reshape(count, rows, depth))
    inv_one = lax.rsqrt(jnp.mean(inputs * inputs, axis=1, keepdims=True) + EPSILON)
    input_back, gain_one_grad = rms_backward(inputs, inv_one, gain_one, normed_one_back)
    input_grad = mixed_grad + input_back

    n1_own, n1_sib = normed_one[:, :half_depth], normed_one[:, half_depth:]
    qkv_own = pair_sum(tn(n1_own, qkv_back), tn(n1_sib, qkv_back)).reshape(count, half, q_width + 128)
    gains = jnp.stack([gain_one_grad, gain_two_grad]).reshape(2, count, slab)
    gains = jnp.stack(
        [lax.dynamic_index_in_dim(gains, f ^ j, 1, keepdims=False) for j in range(count)]
    ).astype(BF)
    gains = line_sum(swap_slabs(gains))
    qkv_half = line_sum(swap_slabs(qkv_own))
    gains = jnp.sum(gains.astype(F32), axis=0) + jnp.sum(to_sibling(gains).astype(F32), axis=0)
    qkv_other = to_sibling(qkv_half)
    query_grad = join_rows(qkv_half[:, :, :q_width], qkv_other[:, :, :q_width], f, k)
    halves = jnp.stack([qkv_half[:, :, q_width:], qkv_other[:, :, q_width:]])

    def by_head(lo, hi):
        both = [lax.dynamic_index_in_dim(halves, k ^ h, 0, keepdims=False) for h in range(2)]
        both = jnp.concatenate(both, axis=1).astype(F32)[:, :, lo:hi]
        cols = jnp.stack([lax.dynamic_index_in_dim(both, f ^ i, 0, keepdims=False) for i in range(count)])
        cols = cols.reshape(KV_HEADS, shared, slab, HEAD_DIM).sum(1)
        return jnp.transpose(cols, (1, 0, 2)).reshape(slab, KV_HEADS * HEAD_DIM)

    key_grad = by_head(0, 64)
    value_grad = by_head(64, 128)

    return (
        outputs.reshape(seqs, rows, depth),
        input_grad.reshape(seqs, rows, depth),
        gains[0],
        query_grad,
        key_grad,
        value_grad,
        out_grad,
        gains[1],
        gate_grad,
        up_grad,
        down_grad,
    )


def rotary_parts(slot, rows):
    lane = np.arange(128) % (HEAD_DIM // 2)
    frequency = ROPE_BASE ** (lane * (-2.0 / HEAD_DIM))
    starts = (slot - 1 - rows * np.arange(slot // rows))[:, None] * frequency[None, :]
    steps = np.arange(rows)[:, None] * frequency[None, :]
    return [jnp.asarray(t(a), F32) for a in (starts, steps) for t in (np.cos, np.sin)]


def front_kernel(
    length_ref, attn_gain, mlp_gain, start_cos, start_sin, step_cos, step_sin,
    tokens, cotangent, w_query, w_key, w_value, w_out, w_gate, w_up, w_down,
    h1, queries, lse, attended, mixed, n2, hidden, gate_back, up_back, back_part, out_part,
    gain_one, gain_two, limits, cosine, sine, kp,
    kv_out, branch_out, wqkv_out,
    notes, x_all, wqkv, keys_in, values_in, kv_give, gate_own, gate_sib, up_own, up_sib, down,
    kv_all, vk, w_o, part, landed, relay, relayed, n2_all, branch_all, cot_in,
    local_s, note_s, note_r, tok_s, tok_r, tof_s, tof_r, wq_s, wq_r, wk_s, wk_r, wp_s, wp_r, wkp_s, wkp_r,
    kz_s, kz_r, kp_s, kp_r, gt_s, gt_r, up_s, up_r, gz_s, gz_r, gs_s, gs_r, us_s, us_r,
    bt_s, bt_r, btf_s, btf_r, mx_s, mx_r, nt_s, nt_r, ntf_s, ntf_r,
):
    f, z, k = lax.axis_index("fsdp"), lax.axis_index("z"), lax.axis_index("core")
    plane, line = 4, 4
    rows, depth = tokens.shape
    total = plane * rows
    slab = depth // plane
    half = slab // 2
    hr = rows // 2
    q_width = w_out.shape[0]
    pairs = q_width // 128
    ff = w_down.shape[0]
    keys = vk.shape[0]
    slot = rows * line * 2
    even = z % 2 == 0
    across = z + 1 - 2 * (z % 2)
    peers = (1, 2, 3)
    first_pos = slot - 1 - (2 * z + k) * rows

    def remote(source, target, send, recv, where):
        return pltpu.make_async_remote_copy(
            src_ref=source,
            dst_ref=target,
            send_sem=send,
            recv_sem=recv,
            device_id=where,
            device_id_type=pl.DeviceIdType.MESH,
        )

    sib = {"core": 1 - k}

    def chip(j):
        return {"fsdp": f ^ j}

    def cols(weight, j, side, width):
        start = pl.multiple_of((f ^ j) * width, 128)
        return weight.at[pl.ds(pl.multiple_of((k ^ side) * half, 16), half), pl.ds(start, width)]

    class Gather:
        def __init__(self, source, target, send, recv, fsend, frecv):
            self.near = {
                j: remote(source, target.at[j], send.at[j - 1], recv.at[j - 1], chip(j)) for j in (1, 2)
            }
            self.far = {
                j: remote(
                    target.at[j, pl.ds((j - 1) * hr, hr), :],
                    target.at[3, pl.ds((j - 1) * hr, hr), :],
                    fsend.at[j - 1],
                    frecv.at[j - 1],
                    chip(3 - j),
                )
                for j in (1, 2)
            }

        def start(self):
            for j in (1, 2):
                self.near[j].start()

        def forward(self):
            for j in (1, 2):
                self.near[j].wait_recv()
                self.far[j].start()

        def arrive(self):
            for j in (1, 2):
                self.far[j].wait_recv()

        def close(self):
            for j in (1, 2):
                self.near[j].wait_send()
                self.far[j].wait_send()

    def note_send(j):
        return remote(notes.at[0], notes.at[j], note_s.at[j - 1], note_r.at[j - 1], chip(j))

    token_gather = Gather(tokens, x_all, tok_s, tok_r, tof_s, tof_r)
    branch_gather = Gather(branch_all.at[0], branch_all, bt_s, bt_r, btf_s, btf_r)
    n2_gather = Gather(n2_all.at[0], n2_all, nt_s, nt_r, ntf_s, ntf_r)

    def wq_send(j):
        target = wqkv.at[pl.ds(j * half, half), pl.ds(0, q_width)]
        return remote(cols(w_query, j, 0, q_width), target, wq_s.at[j - 1], wq_r.at[j - 1], chip(j))

    def wk_send(j):
        target = wqkv.at[pl.ds(j * half, half), pl.ds(q_width, 128)]
        return remote(kv_give.at[j], target, wk_s.at[j - 1], wk_r.at[j - 1], chip(j))

    def wp_send(j):
        source = wqkv.at[pl.ds(j * half, half), :]
        target = wqkv.at[pl.ds((plane + j) * half, half), :]
        return remote(source, target, wp_s.at[j - 1], wp_r.at[j - 1], sib)

    def kv_send(s):
        return remote(kv_all.at[0], kv_all.at[s], kz_s.at[s - 1], kz_r.at[s - 1], {"z": z - s})

    def kv_pair(s):
        return remote(kv_all.at[s], kv_all.at[line + s], kp_s.at[s], kp_r.at[s], sib)

    def gate_send(j):
        return remote(cols(w_gate, j, 0, ff), gate_own.at[j], gt_s.at[j - 1], gt_r.at[j - 1], chip(j))

    def up_send(j):
        return remote(cols(w_up, j, 0, ff), up_own.at[j], up_s.at[j - 1], up_r.at[j - 1], chip(j))

    gate_across = remote(gate_own.at[3], gate_own.at[3], gz_s.at[0], gz_r.at[0], {"z": across})
    up_across = remote(up_own.at[3], up_own.at[3], gz_s.at[0], gz_r.at[0], {"z": across})

    def gate_pair(j):
        return remote(gate_own.at[j], gate_sib.at[j], gs_s.at[j - 1], gs_r.at[j - 1], sib)

    def up_pair(j):
        return remote(up_own.at[j], up_sib.at[j], us_s.at[j - 1], us_r.at[j - 1], sib)

    def span(which):
        return pl.ds(which * hr, hr)

    mix_first = {
        "one": remote(part.at[1, span(0), :], landed.at[0, span(0), :], mx_s.at[0], mx_r.at[0], chip(1)),
        "two": remote(part.at[2, span(1), :], landed.at[1, span(1), :], mx_s.at[1], mx_r.at[1], chip(2)),
        "far_one": remote(part.at[3, span(0), :], relay.at[0], mx_s.at[2], mx_r.at[2], chip(1)),
        "far_two": remote(part.at[3, span(1), :], relay.at[1], mx_s.at[3], mx_r.at[3], chip(2)),
        "late_two": remote(relayed.at[0], landed.at[1, span(0), :], mx_s.at[4], mx_r.at[4], chip(2)),
        "late_one": remote(relayed.at[1], landed.at[0, span(1), :], mx_s.at[5], mx_r.at[5], chip(1)),
    }

    local = [
        pltpu.make_async_copy(source, target, local_s.at[n])
        for n, (source, target) in enumerate(
            [
                (tokens, x_all.at[0]),
                (w_key, keys_in),
                (w_value, values_in),
                (cols(w_query, 0, 0, q_width), wqkv.at[pl.ds(0, half), pl.ds(0, q_width)]),
                (cols(w_query, 0, 1, q_width), wqkv.at[pl.ds(plane * half, half), pl.ds(0, q_width)]),
                (cotangent, cot_in),
                (w_out, w_o),
                (cols(w_gate, 0, 0, ff), gate_own.at[0]),
                (cols(w_gate, 0, 1, ff), gate_sib.at[0]),
                (cols(w_up, 0, 0, ff), up_own.at[0]),
                (cols(w_up, 0, 1, ff), up_sib.at[0]),
                (w_down, down),
            ]
        )
    ]

    length = length_ref[0]
    place = lax.broadcasted_iota(jnp.int32, (16, slab), 0)
    high, low = (length // 64).astype(F32), (length % 64).astype(F32)
    note = jnp.where(place == 0, attn_gain[...].astype(F32), mlp_gain[...].astype(F32))
    note = jnp.where(place == 2, high, jnp.where(place == 3, low, note))
    notes[0] = note.astype(BF)
    for j in peers:
        note_send(j).start()
    token_gather.start()
    for j in (3, 1, 2):
        wq_send(j).start()
    for copy in local:
        copy.start()

    local[1].wait()
    local[2].wait()

    def head_columns(j, side):
        at = pl.ds(pl.multiple_of((k ^ side) * half, 16), half)
        head = f ^ j
        width = KV_HEADS * HEAD_DIM
        key = pltpu.roll(keys_in[at, :].astype(F32), (width - head * 64) % width, 1)[:, :128]
        value = pltpu.roll(values_in[at, :].astype(F32), (width - head * 64 + 64) % width, 1)[:, :128]
        lane = lax.broadcasted_iota(jnp.int32, key.shape, 1)
        return jnp.where(lane < 64, key, value).astype(BF)

    for j in (3, 1, 2):
        kv_give[j] = head_columns(j, 0)
        wk_send(j).start()
    wqkv[0:half, q_width : q_width + 128] = head_columns(0, 0)
    wqkv[plane * half : (plane + 1) * half, q_width : q_width + 128] = head_columns(0, 1)

    chunk = pl.ds(2 * z + k, 1)
    cos_at, sin_at = start_cos[chunk, :], start_sin[chunk, :]
    lane = lax.broadcasted_iota(jnp.int32, (rows, 128), 1)
    cosine[...] = cos_at * step_cos[...] + sin_at * step_sin[...]
    turn = sin_at * step_cos[...] - cos_at * step_sin[...]
    sine[...] = jnp.where(lane % 64 < 32, -turn, turn)
    for h in range(2):
        for s in range(line):
            start = slot - 1 - (2 * (z + s) + (k ^ h)) * rows
            spot = start - lax.broadcasted_iota(jnp.int32, (8, rows), 1)
            spot = jnp.where(spot < 0, FAR, spot).astype(F32)
            kp[:, (h * line + s) * rows : (h * line + s + 1) * rows] = spot

    for s in range(1, line):

        @pl.when(z + s >= line)
        def _():
            kv_all[s] = jnp.zeros(kv_all.shape[1:], BF)
            kv_all[line + s] = jnp.zeros(kv_all.shape[1:], BF)

    local[5].wait()
    row_pos = (first_pos - lax.broadcasted_iota(jnp.int32, (rows, 1), 0)).astype(F32)
    valid = row_pos < jnp.full((rows, 1), length.astype(F32))
    branch_all[0] = jnp.where(valid, cot_in[...].astype(F32), 0.0).astype(BF)

    token_gather.forward()
    for j in (1, 2, 3):
        wq_send(j).wait_recv()
        wk_send(j).wait_recv()
        wp_send(j).start()

    @pl.when(even)
    def _():
        gate_send(3).start()

    @pl.when(jnp.logical_not(even))
    def _():
        up_send(3).start()

    for j in (1, 2):
        gate_send(j).start()
    for j in (1, 2):
        up_send(j).start()

    for j in peers:
        note_send(j).wait_recv()
    for j in range(plane):
        at = pl.ds(pl.multiple_of((f ^ j) * slab, 128), slab)
        gain_one[:, at] = jnp.broadcast_to(notes[j, 0:1, :].astype(F32), (8, slab))
        gain_two[:, at] = jnp.broadcast_to(notes[j, 1:2, :].astype(F32), (8, slab))
        theirs = notes[j, 2:3, 0:1].astype(F32) * 64.0 + notes[j, 3:4, 0:1].astype(F32)
        limits[j] = jnp.broadcast_to(jnp.minimum(row_pos, theirs - 1.0), (rows, 128))

    def normalize(j, x_ref):
        @pl.loop(0, rows // 16)
        def _(i):
            at = pl.ds(pl.multiple_of(i * 16, 16), 16)
            x = x_ref[at, :].astype(F32)
            inverse = lax.rsqrt(jnp.mean(x * x, axis=1, keepdims=True) + EPSILON)
            to = pl.ds(pl.multiple_of(j * rows + i * 16, 16), 16)
            for h in range(2):
                for b in range(plane):
                    from_ = pl.ds(pl.multiple_of(((f ^ b) * 2 + (k ^ h)) * half, 128), half)
                    value = x_ref[at, from_].astype(F32) * inverse * gain_one[0:1, from_]
                    c = (h * plane + b) * half
                    h1[to, c : c + half] = value.astype(BF)

    local[0].wait()
    normalize(0, x_all.at[0])
    normalize(1, x_all.at[1])
    normalize(2, x_all.at[2])
    token_gather.arrive()
    normalize(3, x_all.at[3])
    local[3].wait()
    local[4].wait()
    for j in (1, 2, 3):
        wp_send(j).wait_recv()

    kv_cols = nn(h1[...], wqkv[:, q_width : q_width + 128])
    for j in range(plane):
        value = kv_cols[j * rows : (j + 1) * rows]
        turned = value * cosine[...] + swap_halves(value) * sine[...]
        kv_all[0, j] = jnp.where(lane < 64, turned, value).astype(BF)
    for s in range(1, line):

        @pl.when(z >= s)
        def _():
            kv_send(s).start()

    kv_pair(0).start()
    branch_gather.start()

    @pl.loop(0, pairs // 2)
    def _(p):
        at = pl.ds(pl.multiple_of(p * 256, 256), 256)
        out = nn(h1[...], wqkv[:, at])
        for j in range(plane):
            for c in range(2):
                value = out[j * rows : (j + 1) * rows, c * 128 : (c + 1) * 128]
                turned = value * cosine[...] + swap_halves(value) * sine[...]
                queries[j, :, pl.ds(pl.multiple_of(p * 256 + c * 128, 128), 128)] = turned.astype(BF)

    for s in range(1, line):

        @pl.when(z + s < line)
        def _():
            kv_send(s).wait_recv()
            kv_pair(s).start()

    @pl.when(even)
    def _():
        gate_send(3).wait_recv()
        gate_across.start()

    @pl.when(jnp.logical_not(even))
    def _():
        up_send(3).wait_recv()
        up_across.start()

    kv_pair(0).wait_recv()
    for s in range(1, line):

        @pl.when(z + s < line)
        def _():
            kv_pair(s).wait_recv()

    local[6].wait()

    def attend_block(j):
        vk[...] = pltpu.roll(kv_all[:, j].reshape(keys, 128).astype(F32), 64, 1).astype(BF)
        limit = limits[j, :, 0:1]

        @pl.loop(0, pairs)
        def _(p):
            at = pl.ds(pl.multiple_of(p * 128, 128), 128)
            allowed = kp[0:1, :] <= limit
            q = queries[j, :, at]
            zero = jnp.zeros_like(q)
            outs, logs = [], []
            for first in (True, False):
                mine = lane < 64 if first else lane >= 64
                kv = kv_all[:, j].reshape(keys, 128)
                keyed, valued = (kv, vk[...]) if first else (vk[...], kv)
                scores = nt(jnp.where(mine, q, zero), keyed) * (HEAD_DIM**-0.5)
                scores = jnp.where(allowed, scores, MASKED)
                top = jnp.max(scores, axis=1, keepdims=True)
                weights = jnp.exp(scores - top)
                sums = jnp.sum(weights, axis=1, keepdims=True)
                outs.append(nn(weights.astype(BF), valued) / sums)
                logs.append(jnp.broadcast_to(top + jnp.log(sums), (rows, 128)))
            attended[j * rows : (j + 1) * rows, at] = jnp.where(lane < 64, outs[0], outs[1]).astype(BF)
            lse[j, :, at] = jnp.where(lane < 64, logs[0], logs[1])

        part[j] = nn(attended[j * rows : (j + 1) * rows, :], w_o[...]).astype(BF)

    attend_block(3)
    mix_first["far_one"].start()
    mix_first["far_two"].start()
    branch_gather.forward()
    attend_block(1)
    mix_first["one"].start()
    attend_block(2)
    mix_first["two"].start()

    def relay_on(far, late, which, j):
        mix_first[far].wait_recv()
        value = relay[which].astype(F32) + part[j, which * hr : (which + 1) * hr, :].astype(F32)
        relayed[which] = value.astype(BF)
        mix_first[late].start()

    relay_on("far_one", "late_two", 0, 2)
    relay_on("far_two", "late_one", 1, 1)
    attend_block(0)
    for name in ("one", "late_one", "two", "late_two"):
        mix_first[name].wait_recv()

    @pl.loop(0, rows // 16)
    def _(i):
        at = pl.ds(pl.multiple_of(i * 16, 16), 16)
        value = x_all[0, at, :].astype(F32) + part[0, at, :].astype(F32)
        value = value + landed[0, at, :].astype(F32) + landed[1, at, :].astype(F32)
        mixed[at, :] = value
        inverse = lax.rsqrt(jnp.mean(value * value, axis=1, keepdims=True) + EPSILON)
        n2_all[0, at, :] = (value * inverse * gain_two[0:1, :]).astype(BF)

    n2_gather.start()

    for j in (1, 2):
        gate_send(j).wait_recv()
        gate_pair(j).start()
    n2_gather.forward()
    for j in (1, 2):
        up_send(j).wait_recv()
        up_pair(j).start()

    @pl.when(even)
    def _():
        up_across.wait_recv()

    @pl.when(jnp.logical_not(even))
    def _():
        gate_across.wait_recv()

    gate_pair(3).start()
    up_pair(3).start()
    branch_gather.arrive()
    n2_gather.arrive()

    @pl.loop(0, total // 16)
    def _(i):
        at = pl.ds(pl.multiple_of(i * 16, 16), 16)
        j = i // (rows // 16)
        from_row = pl.ds(pl.multiple_of((i % (rows // 16)) * 16, 16), 16)
        for h in range(2):
            for b in range(plane):
                from_ = pl.ds(pl.multiple_of(((f ^ b) * 2 + (k ^ h)) * half, 128), half)
                c = (h * plane + b) * half
                n2[at, c : c + half] = n2_all[j, from_row, from_]

    for n in range(7, 12):
        local[n].wait()
    for j in peers:
        gate_pair(j).wait_recv()
        up_pair(j).wait_recv()

    def feed(at):
        width = at.size
        n2_own, n2_sib = n2[:, 0 : depth // 2], n2[:, depth // 2 : depth]

        def through(own, other):
            first = nn(n2_own, own[:, :, at].reshape(depth // 2, width))
            return first + nn(n2_sib, other[:, :, at].reshape(depth // 2, width))

        gate = through(gate_own, gate_sib)
        up = through(up_own, up_sib)
        sigmoid = 1.0 / (1.0 + jnp.exp(-gate))
        hidden[:, at] = (gate * sigmoid * up).astype(BF)
        grad = nt(branch_all[...].reshape(total, depth), down[at, :])
        gate_back[:, at] = (grad * up * sigmoid * (1.0 + gate * (1.0 - sigmoid))).astype(BF)
        up_back[:, at] = (grad * gate * sigmoid).astype(BF)

    @pl.loop(0, ff // 256)
    def _(n):
        feed(pl.ds(pl.multiple_of(n * 256, 256), 256))

    if ff % 256:
        feed(pl.ds(ff // 256 * 256, ff % 256))

    for h, gate_side, up_side in ((0, gate_own, up_own), (1, gate_sib, up_sib)):

        @pl.loop(0, plane)
        def _(b):
            to = pl.ds(pl.multiple_of(((f ^ b) * 2 + (k ^ h)) * half, 128), half)
            value = nt(gate_back[...], gate_side[b]) + nt(up_back[...], up_side[b])
            back_part[:, to] = value.astype(BF)

    @pl.loop(0, depth // 256)
    def _(n):
        at = pl.ds(pl.multiple_of(n * 256, 256), 256)
        out_part[:, at] = nn(hidden[...], down[:, at]).astype(BF)

    stores = [
        pltpu.make_async_copy(kv_all, kv_out, local_s.at[12]),
        pltpu.make_async_copy(branch_all, branch_out, local_s.at[13]),
        pltpu.make_async_copy(wqkv, wqkv_out, local_s.at[14]),
    ]
    for copy in stores:
        copy.start()
    for gather in (token_gather, branch_gather, n2_gather):
        gather.close()
    for copy in mix_first.values():
        copy.wait_send()
    for j in peers:
        note_send(j).wait_send()
        wq_send(j).wait_send()
        wk_send(j).wait_send()
        wp_send(j).wait_send()
        gate_pair(j).wait_send()
        up_pair(j).wait_send()
    for j in (1, 2):
        gate_send(j).wait_send()
        up_send(j).wait_send()

    @pl.when(even)
    def _():
        gate_send(3).wait_send()
        gate_across.wait_send()

    @pl.when(jnp.logical_not(even))
    def _():
        up_send(3).wait_send()
        up_across.wait_send()

    kv_pair(0).wait_send()
    for s in range(1, line):

        @pl.when(z >= s)
        def _():
            kv_send(s).wait_send()

        @pl.when(z + s < line)
        def _():
            kv_pair(s).wait_send()

    for copy in stores:
        copy.wait()


def front_pass(tokens, cotangent, lengths, attn_gain, mlp_gain, w_query, w_key, w_value, w_out, w_gate, w_up, w_down):
    rows, depth = tokens.shape
    plane, line = 4, 4
    total, slab = plane * rows, depth // plane
    half = slab // 2
    q_width = HEADS * HEAD_DIM // plane
    width = q_width + 128
    ff = w_down.shape[0]
    slot = rows * line * 2
    keys = slot
    act = (rows, depth)
    local = pl.BlockSpec(memory_space=pltpu.VMEM)
    anywhere = pl.BlockSpec(memory_space=pl.ANY)
    dma = lambda n: pltpu.SemaphoreType.DMA((n,))
    kv_shape = (2 * line, plane, rows, 128)
    sds = jax.ShapeDtypeStruct
    outs = [
        sds((total, depth), BF),
        sds((plane, rows, q_width), BF),
        sds((plane, rows, q_width), F32),
        sds((total, q_width), BF),
        sds(act, F32),
        sds((total, depth), BF),
        sds((total, ff), BF),
        sds((total, ff), BF),
        sds((total, ff), BF),
        sds((total, depth), BF),
        sds((total, depth), BF),
        sds((8, depth), F32),
        sds((8, depth), F32),
        sds((plane, rows, 128), F32),
        sds((rows, 128), F32),
        sds((rows, 128), F32),
        sds((8, keys), F32),
        sds(kv_shape, BF),
        sds((plane,) + act, BF),
        sds((depth, width), BF),
    ]
    slabs = pltpu.VMEM((plane, half, ff), BF)
    scratch = [
        pltpu.VMEM((plane, 16, slab), BF),
        pltpu.VMEM((plane,) + act, BF),
        pltpu.VMEM((depth, width), BF),
        pltpu.VMEM(w_key.shape, BF),
        pltpu.VMEM(w_value.shape, BF),
        pltpu.VMEM((plane, half, 128), BF),
        slabs,
        slabs,
        slabs,
        slabs,
        pltpu.VMEM(w_down.shape, BF),
        pltpu.VMEM(kv_shape, BF),
        pltpu.VMEM((keys, 128), BF),
        pltpu.VMEM(w_out.shape, BF),
        pltpu.VMEM((plane,) + act, BF),
        pltpu.VMEM((2,) + act, BF),
        pltpu.VMEM((2, rows // 2, depth), BF),
        pltpu.VMEM((2, rows // 2, depth), BF),
        pltpu.VMEM((plane,) + act, BF),
        pltpu.VMEM((plane,) + act, BF),
        pltpu.VMEM(act, BF),
    ]
    sems = [15, 3, 3, 2, 2, 2, 2, 3, 3, 3, 3, 3, 3, 1, 1, 3, 3, 4, 4, 3, 3, 3, 3, 1, 1, 3, 3, 3, 3]
    sems += [2, 2, 2, 2, 6, 6, 2, 2, 2, 2]
    return pl.pallas_call(
        front_kernel,
        out_shape=outs,
        in_specs=[pl.BlockSpec(memory_space=pltpu.SMEM)] + [local] * 6 + [anywhere] * 9,
        out_specs=[local] * 17 + [anywhere] * 3,
        scratch_shapes=scratch + [dma(n) for n in sems],
        compiler_params=pltpu.CompilerParams(
            vmem_limit_bytes=62 * 1024 * 1024, has_side_effects=True
        ),
        name="front_pass",
    )(
        lengths, attn_gain.reshape(1, slab), mlp_gain.reshape(1, slab), *rotary_parts(slot, rows),
        tokens, cotangent, w_query, w_key, w_value, w_out, w_gate, w_up, w_down,
    )


def add_into(target, other):
    @pl.loop(0, target.shape[0] // 16)
    def _(i):
        at = pl.ds(pl.multiple_of(i * 16, 16), 16)
        target[at, :] = (target[at, :].astype(F32) + other[at, :].astype(F32)).astype(BF)


def back_kernel(
    limits,
    own_down, own_gate, own_up, other_down, other_gate, other_up,
    back_part, out_part, w_out, wqkv_hbm, h1_hbm,
    mixed, branch_own, x_own, gain_one, gain_two,
    attended, queries, lse, kv_all, kp, cosine, sine,
    fin_down, fin_gate, fin_up, fin_out, fin_qkv, fin_gain,
    sib_down, sib_gate, sib_up, sib_out, sib_qkv, sib_gain,
    outputs, input_grad,
    src_down, src_gate, src_up, src_out, src_qkv, src_gain,
    swap_gate, swap_up, swap_qkv,
    end_down, end_gate, end_up, end_out, end_qkv, end_gain,
    load_down, load_gate, give_out, give_qkv, give_gain,
    landed, landed_out, first_back, first_out, da_all, wide, do_all, dqkv, wqkv, h1,
    vk, dk_sum, dv_sum, kv_part, kv_land, kv_mine, kv_line, gain_acc, gain_all,
    pair_s, pair_r, load_s, swap_s, swap_r, in_s, in_r, mid_s, mid_r, out_s, done_s, back_s, back_r, ready,
    local_s, rs_s, rs_r, ro_s, ro_r, ag_s, ag_r, rq_s, rq_r, kp_s, kp_r, kz_s, kz_r, ga_s, ga_r,
):
    f, z, k = lax.axis_index("fsdp"), lax.axis_index("z"), lax.axis_index("core")
    plane, line = lax.axis_size("fsdp"), lax.axis_size("z")
    outer = (z == 0) | (z == line - 1)
    inner = jnp.logical_not(outer)
    inward = jnp.where(z < line // 2, z + 1, z - 1)
    outward = jnp.where(z < line // 2, z - 1, z + 1)
    rows, depth = mixed.shape
    total = plane * rows
    half_depth = depth // 2
    half = half_depth // plane
    q_width = attended.shape[1]
    pairs = q_width // 128
    peers = range(1, plane)

    kinds = {
        "down": (own_down, other_down, src_down, None, end_down, load_down, fin_down, sib_down),
        "gate": (own_gate, other_gate, src_gate, swap_gate, end_gate, load_gate, fin_gate, sib_gate),
        "up": (own_up, other_up, src_up, swap_up, end_up, load_gate, fin_up, sib_up),
        "out": (None, give_out, src_out, None, end_out, None, fin_out, sib_out),
        "qkv": (None, give_qkv, src_qkv, swap_qkv, end_qkv, None, fin_qkv, sib_qkv),
        "gain": (None, give_gain, src_gain, None, end_gain, None, fin_gain, sib_gain),
    }
    chunks = [(name, i) for name, kind in kinds.items() for i in range(kind[2].shape[0])]
    count = len(chunks)
    loaded = [c for c in range(count) if kinds[chunks[c][0]][0] is not None]

    def remote(source, target, send, recv, where):
        return pltpu.make_async_remote_copy(
            src_ref=source,
            dst_ref=target,
            send_sem=send,
            recv_sem=recv,
            device_id=where,
            device_id_type=pl.DeviceIdType.MESH,
        )

    def part(c, which):
        name, i = chunks[c]
        return kinds[name][which].at[i]

    def swapped(c):
        name, i = chunks[c]
        return i if kinds[name][3] is not None else 0

    def pair_copy(c):
        name, i = chunks[c]
        given = kinds[name][1]
        source = given.at[i] if c in loaded else given.at[i % given.shape[0]]
        return remote(source, part(c, 2), pair_s.at[c], pair_r.at[c], {"core": 1 - k})

    def load_copy(c):
        return pltpu.make_async_copy(part(c, 0), kinds[chunks[c][0]][5].at[c % 2], load_s.at[c])

    def swap_copy(c):
        return remote(part(c, 2), part(c, 3), swap_s.at[c], swap_r.at[c], {"fsdp": f ^ swapped(c)})

    def base(c):
        return part(c, 3) if swapped(c) else part(c, 2)

    def in_copy(c):
        return remote(base(c), part(c, 4), in_s.at[c], in_r.at[c], {"z": inward})

    def mid_copy(c):
        return remote(base(c), part(c, 4), mid_s.at[c], mid_r.at[c], {"z": inward})

    def out_copy(c):
        return remote(part(c, 4), part(c, 4), out_s.at[c], mid_r.at[c], {"z": outward})

    def keep_copy(c):
        return pltpu.make_async_copy(part(c, 4), part(c, 6), done_s.at[c])

    def back_copy(c):
        return remote(part(c, 4), part(c, 7), back_s.at[c], back_r.at[c], {"core": 1 - k})

    own_cols = pl.ds(pl.multiple_of(k * half_depth, 128), half_depth)
    other_cols = pl.ds(pl.multiple_of((1 - k) * half_depth, 128), half_depth)

    def out_term(i, cols):
        size = src_out.shape[1]
        right = da_all[:, :, cols].reshape(total, half_depth)
        return tn(attended[:, i * size : (i + 1) * size], right)

    def qkv_term(i, side):
        start = side * half_depth + i * half
        return tn(h1[:, start : start + half], dqkv[...])

    def term(c, side):
        name, i = chunks[c]
        if name == "out":
            return out_term(i, (own_cols, other_cols)[side])
        if name == "qkv":
            return qkv_term(i, side)
        return gain_all[...].astype(F32).sum(axis=0)

    def stage_give(c):
        name, i = chunks[c]
        if c in loaded:
            return
        given = kinds[name][1]
        slots = given.shape[0]
        if i >= slots:
            pair_copy(c - slots).wait_send()
        given[i % slots] = term(c, 1).astype(BF)
        pair_copy(c).start()

    def stage_pair(c):
        pair_copy(c).wait_recv()
        if c in loaded:
            load_copy(c).wait()
            add_into(part(c, 2), kinds[chunks[c][0]][5].at[c % 2])
            if c + 2 in loaded:
                load_copy(c + 2).start()
        else:
            target = part(c, 2)
            target[...] = (target[...].astype(F32) + term(c, 0)).astype(BF)
        if swapped(c):
            swap_copy(c).start()

    def stage_in(c):
        if swapped(c):
            swap_copy(c).wait_recv()

        @pl.when(outer)
        def _():
            in_copy(c).start()

    def stage_mid(c):
        @pl.when(inner)
        def _():
            in_copy(c).wait_recv()
            add_into(base(c), part(c, 4))
            pl.semaphore_signal(
                ready, inc=1, device_id={"z": inward}, device_id_type=pl.DeviceIdType.MESH
            )
            pl.semaphore_wait(ready, 1)
            mid_copy(c).start()

    def stage_out(c):
        @pl.when(inner)
        def _():
            mid_copy(c).wait_recv()
            add_into(part(c, 4), base(c))
            out_copy(c).start()

    def stage_keep(c):
        @pl.when(outer)
        def _():
            out_copy(c).wait_recv()

        keep_copy(c).start()
        back_copy(c).start()

    def back_send(j):
        return remote(back_part.at[j], landed.at[j - 1], rs_s.at[j - 1], rs_r.at[j - 1], {"fsdp": f ^ j})

    def out_send(j):
        return remote(out_part.at[j], landed_out.at[j - 1], ro_s.at[j - 1], ro_r.at[j - 1], {"fsdp": f ^ j})

    def da_send(j):
        return remote(da_all.at[0], da_all.at[j], ag_s.at[j - 1], ag_r.at[j - 1], {"fsdp": f ^ j})

    def dh_send(j):
        mine = wide.at[pl.ds(j * rows, rows), :]
        return remote(mine, landed.at[j - 1], rq_s.at[j - 1], rq_r.at[j - 1], {"fsdp": f ^ j})

    def gain_send(j):
        return remote(gain_all.at[0], gain_all.at[j], ga_s.at[j - 1], ga_r.at[j - 1], {"fsdp": f ^ j})

    locals_ = [
        pltpu.make_async_copy(back_part.at[0], first_back, local_s.at[0]),
        pltpu.make_async_copy(out_part.at[0], first_out, local_s.at[1]),
        pltpu.make_async_copy(w_out, wide.at[pl.ds(0, w_out.shape[0]), :], local_s.at[2]),
        pltpu.make_async_copy(wqkv_hbm, wqkv, local_s.at[3]),
        pltpu.make_async_copy(h1_hbm, h1, local_s.at[4]),
    ]

    def rms_back(gradient_of, x_ref, gain, acc, write):
        acc[...] = jnp.zeros_like(acc)

        @pl.loop(0, rows // 16)
        def _(i):
            at = pl.ds(pl.multiple_of(i * 16, 16), 16)
            gradient = gradient_of(at)
            x = x_ref[at, :].astype(F32)
            inverse = lax.rsqrt(jnp.mean(x * x, axis=1, keepdims=True) + EPSILON)
            normed = x * inverse
            acc[...] += gradient * normed
            scaled = gradient * gain[0:1, :]
            write(at, inverse * (scaled - normed * jnp.mean(scaled * normed, axis=1, keepdims=True)))

    def piece_mixed():
        locals_[0].wait()
        for j in peers:
            back_send(j).wait_recv()

        def gradient_of(at):
            value = first_back[at, :].astype(F32)
            for j in peers:
                value = value + landed[j - 1, at, :].astype(F32)
            return value

        def write(at, value):
            value = value + branch_own[at, :].astype(F32)
            input_grad[at, :] = value
            da_all[0, at, :] = value.astype(BF)

        rms_back(gradient_of, mixed, gain_two, gain_acc.at[1], write)
        for j in peers:
            da_send(j).start()

    def piece_do():
        locals_[2].wait()
        for j in peers:
            da_send(j).wait_recv()
            out_send(j).start()

        @pl.loop(0, plane)
        def _(j):
            do_all[j] = nt(da_all[j], wide[0 : w_out.shape[0], :]).astype(BF)

    def piece_attend(j):
        vk[...] = pltpu.roll(kv_all[:, j].reshape(vk.shape).astype(F32), 64, 1).astype(BF)
        dk_sum[...] = jnp.zeros_like(dk_sum)
        dv_sum[...] = jnp.zeros_like(dv_sum)
        limit = limits[j, :, 0:1]
        lane = lax.broadcasted_iota(jnp.int32, (rows, 128), 1)

        @pl.loop(0, pairs)
        def _(p):
            at = pl.ds(pl.multiple_of(p * 128, 128), 128)
            allowed = kp[0:1, :] <= limit
            q, do = queries[j, :, at], do_all[j, :, at]
            logs = lse[j, :, at]
            zero = jnp.zeros_like(q)
            parts = []
            for first in (True, False):
                mine = lane < 64 if first else lane >= 64
                kv = kv_all[:, j].reshape(vk.shape)
                keyed, valued = (kv, vk[...]) if first else (vk[...], kv)
                q_own, do_own = jnp.where(mine, q, zero), jnp.where(mine, do, zero)
                scores = nt(q_own, keyed) * (HEAD_DIM**-0.5)
                log_total = logs[:, 0:1] if first else logs[:, 64:65]
                weights = jnp.where(allowed, jnp.exp(scores - log_total), 0.0)
                joint = weights * nt(do_own, valued)
                back = (joint - weights * jnp.sum(joint, axis=1, keepdims=True)).astype(BF)
                parts.append(nn(back, keyed))
                dk_sum[...] += tn(back, q_own)
                dv_sum[...] += tn(weights.astype(BF), do_own)
            turned = jnp.where(lane < 64, parts[0], parts[1]) * (HEAD_DIM**-0.5)
            turned = turned * cosine[...] - swap_halves(turned) * sine[...]
            dqkv[j * rows : (j + 1) * rows, at] = turned.astype(BF)

        dk = dk_sum[...]
        dv = dv_sum[...]
        dk = (dk + pltpu.roll(dk, 64, 1)) * (HEAD_DIM**-0.5)
        dv = dv + pltpu.roll(dv, 64, 1)
        wide_lane = lax.broadcasted_iota(jnp.int32, dk.shape, 1)
        packed = jnp.where(wide_lane < 64, dk, dv).astype(BF)
        kv_part[:, j] = packed.reshape(kv_part.shape[0], rows, 128)

    kv_pair = remote(kv_part.at[pl.ds(line, line)], kv_land, kp_s.at[0], kp_r.at[0], {"core": 1 - k})

    def kv_send(s):
        return remote(kv_mine.at[s], kv_line.at[s - 1], kz_s.at[s - 1], kz_r.at[s - 1], {"z": z + s})

    def piece_kv_line():
        kv_pair.wait_recv()
        for s in range(line):
            kv_mine[s] = (kv_part[s].astype(F32) + kv_land[s].astype(F32)).astype(BF)
        for s in range(1, line):

            @pl.when(z + s < line)
            def _():
                kv_send(s).start()

    def piece_kv_sum():
        for s in range(1, line):

            @pl.when(z >= s)
            def _():
                kv_send(s).wait_recv()
                kv_mine[0] = (kv_mine[0].astype(F32) + kv_line[s - 1].astype(F32)).astype(BF)

        lane = lax.broadcasted_iota(jnp.int32, (rows, 128), 1)
        for j in range(plane):
            value = kv_mine[0, j].astype(F32)
            turned = value * cosine[...] - swap_halves(value) * sine[...]
            value = jnp.where(lane < 64, turned, value).astype(BF)
            dqkv[j * rows : (j + 1) * rows, q_width : q_width + 128] = value

    def piece_dh():
        locals_[3].wait()
        for h in range(2):
            for j in range(plane):
                start = pl.multiple_of(((f ^ j) * 2 + (k ^ h)) * half, 128)
                block = wqkv[(h * plane + j) * half : (h * plane + j + 1) * half, :]
                wide[0:total, pl.ds(start, half)] = nt(dqkv[...], block).astype(BF)
        for j in peers:
            dh_send(j).start()

    def piece_input():
        for j in peers:
            dh_send(j).wait_recv()

        def gradient_of(at):
            value = wide[at, :].astype(F32)
            for j in peers:
                value = value + landed[j - 1, at, :].astype(F32)
            return value

        def write(at, value):
            input_grad[at, :] = input_grad[at, :] + value

        rms_back(gradient_of, x_own, gain_one, gain_acc.at[0], write)
        place = lax.broadcasted_iota(jnp.int32, (16, depth), 0)
        one = jnp.sum(gain_acc[0], axis=0, keepdims=True)
        two = jnp.sum(gain_acc[1], axis=0, keepdims=True)
        gain_all[0] = jnp.where(place == 0, one, jnp.where(place == 1, two, 0.0)).astype(BF)
        for j in peers:
            gain_send(j).start()

    def piece_outputs():
        locals_[1].wait()
        for j in peers:
            out_send(j).wait_recv()

        @pl.loop(0, rows // 16)
        def _(i):
            at = pl.ds(pl.multiple_of(i * 16, 16), 16)
            value = mixed[at, :] + first_out[at, :].astype(F32)
            for j in peers:
                value = value + landed_out[j - 1, at, :].astype(F32)
            outputs[at, :] = value

    def piece_gain():
        for j in peers:
            gain_send(j).wait_recv()
        locals_[4].wait()

    pieces = {2: [piece_mixed], 4: [piece_do]}
    for j in range(plane):
        pieces.setdefault(4 + j, []).append(functools.partial(piece_attend, j))
    pieces[3 + plane].append(lambda: kv_pair.start())
    pieces[4 + plane] = [piece_kv_line, piece_outputs]
    pieces[5 + plane] = [piece_kv_sum, piece_dh]
    pieces[7 + plane] = [piece_input]
    pieces[8 + plane] = [piece_gain]

    for j in peers:
        back_send(j).start()
    for c in loaded:
        pair_copy(c).start()
    for c in loaded[:2]:
        load_copy(c).start()
    for copy in locals_:
        copy.start()
    stages = ((-1, stage_give), (0, stage_pair), (1, stage_in), (2, stage_mid), (4, stage_out), (6, stage_keep))
    for tick in range(count + stages[-1][0]):
        for lag, stage in stages:
            if 0 <= tick - lag < count:
                stage(tick - lag)
        for piece in pieces.get(tick, []):
            piece()

    for c in range(count):
        name, i = chunks[c]
        if c in loaded or i + kinds[name][1].shape[0] >= kinds[name][2].shape[0]:
            pair_copy(c).wait_send()
        if swapped(c):
            swap_copy(c).wait_send()
        keep_copy(c).wait()
        back_copy(c).wait_send()
        back_copy(c).wait_recv()

        @pl.when(outer)
        def _():
            in_copy(c).wait_send()

        @pl.when(inner)
        def _():
            mid_copy(c).wait_send()
            out_copy(c).wait_send()

    for j in peers:
        back_send(j).wait_send()
        out_send(j).wait_send()
        da_send(j).wait_send()
        dh_send(j).wait_send()
        gain_send(j).wait_send()
    kv_pair.wait_send()
    for s in range(1, line):

        @pl.when(z + s < line)
        def _():
            kv_send(s).wait_send()


def back_pass(
    limits, own, other, back_part, out_part, w_out, wqkv, h1, mixed, branch_own, x_own, gain_one, gain_two,
    attended, queries, lse, kv_all, kp, cosine, sine,
):
    count, line = lax.axis_size("fsdp"), lax.axis_size("z")
    rows, depth = mixed.shape
    total, half_depth = count * rows, depth // 2
    half = half_depth // count
    q_width = attended.shape[1]
    keys = kv_all.shape[0] * rows
    shapes = [x.shape for x in own] + [
        (2, q_width // 2, half_depth),
        (count, half, q_width + 128),
        (1, 16, depth),
    ]
    anywhere = pl.BlockSpec(memory_space=pl.ANY)
    local = pl.BlockSpec(memory_space=pltpu.VMEM)
    ends = [jax.ShapeDtypeStruct(s, BF) for s in shapes]
    act = jax.ShapeDtypeStruct((rows, depth), F32)
    block = (rows, depth)
    chunk_count = sum(s[0] for s in shapes)
    dma = lambda n: pltpu.SemaphoreType.DMA((n,))
    scratch = (
        [pltpu.VMEM(s, BF) for s in shapes]
        + [pltpu.VMEM(shapes[i], BF) for i in (1, 2, 4)]
        + [pltpu.VMEM(s, BF) for s in shapes]
        + [pltpu.VMEM((2,) + shapes[i][1:], BF) for i in (0, 1, 3, 4)]
        + [pltpu.VMEM(shapes[5], BF)]
        + [
            pltpu.VMEM((count - 1,) + block, BF),
            pltpu.VMEM((count - 1,) + block, BF),
            pltpu.VMEM(block, BF),
            pltpu.VMEM(block, BF),
            pltpu.VMEM((count,) + block, BF),
            pltpu.VMEM((max(total, q_width), depth), BF),
            pltpu.VMEM((count, rows, q_width), BF),
            pltpu.VMEM((total, q_width + 128), BF),
            pltpu.VMEM(wqkv.shape, BF),
            pltpu.VMEM(h1.shape, BF),
            pltpu.VMEM((keys, 128), BF),
            pltpu.VMEM((keys, 128), F32),
            pltpu.VMEM((keys, 128), F32),
            pltpu.VMEM(kv_all.shape, BF),
            pltpu.VMEM((line,) + kv_all.shape[1:], BF),
            pltpu.VMEM((line,) + kv_all.shape[1:], BF),
            pltpu.VMEM((line - 1,) + kv_all.shape[1:], BF),
            pltpu.VMEM((2, 16, depth), F32),
            pltpu.VMEM((count, 16, depth), BF),
        ]
        + [dma(chunk_count)] * 13
        + [pltpu.SemaphoreType.REGULAR, dma(5)]
        + [dma(count - 1)] * 8
        + [dma(1)] * 2
        + [dma(line - 1)] * 2
        + [dma(count - 1)] * 2
    )
    out = pl.pallas_call(
        back_kernel,
        out_shape=ends + ends + [act, act],
        in_specs=[local] + [anywhere] * 11 + [local] * 12,
        out_specs=[anywhere] * 12 + [local] * 2,
        scratch_shapes=scratch,
        compiler_params=pltpu.CompilerParams(
            vmem_limit_bytes=62 * 1024 * 1024, has_side_effects=True
        ),
        cost_estimate=pl.CostEstimate(
            flops=10**11, bytes_accessed=10**9, transcendentals=10**7
        ),
        name="back_pass",
    )(
        limits, *own, *other, back_part, out_part, w_out, wqkv, h1, mixed, branch_own, x_own, gain_one, gain_two,
        attended, queries, lse, kv_all, kp, cosine, sine,
    )
    return out[:6], out[6:12], out[12], out[13]


def body(
    tokens, cotangent, lengths, attn_gain, w_query, w_key, w_value, w_out, mlp_gain, w_gate, w_up, w_down
):
    seqs, rows, depth = tokens.shape
    count = lax.axis_size("fsdp")
    f, k = lax.axis_index("fsdp"), lax.axis_index("core")
    slab = depth // count
    half, half_depth = slab // 2, depth // 2
    q_width = HEADS * HEAD_DIM // count
    x_own = tokens.reshape(rows, depth)
    (
        h1, queries, lse, attended, mixed, n2, hidden, gate_back, up_back, back_part, out_part,
        gain_one, gain_two, limits, cosine, sine, kp, kv_all, branch, wqkv,
    ) = front_pass(
        x_own, cotangent.reshape(rows, depth), lengths, attn_gain, mlp_gain,
        w_query, w_key, w_value, w_out, w_gate, w_up, w_down,
    )
    flat = branch.reshape(count * rows, depth)
    own, other = [], []
    for terms, side in ((own, 0), (other, 1)):
        right = lax.dynamic_slice_in_dim(flat, (k ^ side) * half_depth, half_depth, 1)
        left = n2[:, side * half_depth : (side + 1) * half_depth]
        terms.append(tn(hidden, right).astype(BF).reshape(4, -1, half_depth))
        terms.append(tn(left, gate_back).astype(BF).reshape(count, half, -1))
        terms.append(tn(left, up_back).astype(BF).reshape(count, half, -1))
    owns, sibs, outputs, input_grad = back_pass(
        limits, own, other, back_part.reshape(count, rows, depth), out_part.reshape(count, rows, depth), w_out,
        wqkv, h1, mixed, branch[0], x_own, gain_one, gain_two, attended, queries, lse, kv_all, kp, cosine, sine,
    )

    def columns(i):
        return join_columns(*(x[i].reshape(-1, half_depth) for x in (owns, sibs)), k)

    down_grad, out_grad = columns(0), columns(3)
    gate_grad, up_grad = (join_rows(owns[i], sibs[i], f, k) for i in (1, 2))
    qkv_half, qkv_sib = owns[4], sibs[4]
    query_grad = join_rows(qkv_half[:, :, :q_width], qkv_sib[:, :, :q_width], f, k)
    gains = lax.dynamic_slice_in_dim(owns[5][0, :2], f * slab, slab, 1).astype(F32)
    halves = jnp.stack([qkv_half[:, :, q_width:], qkv_sib[:, :, q_width:]])

    def by_head(lo, hi):
        both = [lax.dynamic_index_in_dim(halves, k ^ h, 0, keepdims=False) for h in range(2)]
        both = jnp.concatenate(both, axis=1).astype(F32)[:, :, lo:hi]
        cols = jnp.stack([lax.dynamic_index_in_dim(both, f ^ i, 0, keepdims=False) for i in range(count)])
        return jnp.transpose(cols, (1, 0, 2)).reshape(slab, KV_HEADS * HEAD_DIM)

    return (
        outputs.reshape(seqs, rows, depth),
        input_grad.reshape(seqs, rows, depth),
        gains[0],
        query_grad,
        by_head(0, 64),
        by_head(64, 128),
        out_grad,
        gains[1],
        gate_grad,
        up_grad,
        down_grad,
    )


def solution(mesh):
    count, ctx = mesh.shape["fsdp"], mesh.shape["ctx"]
    split = Mesh(mesh.devices.reshape(count, ctx // 2, 2), ("fsdp", "z", "core"))
    act = P("fsdp", ("z", "core"), None)
    row, mat = P("fsdp"), P("fsdp", None)
    fast = count == 4 and count == KV_HEADS and ctx == 8
    return jax.shard_map(
        body if fast else body_plain,
        mesh=split,
        in_specs=(act, act, row, row, mat, mat, mat, mat, row, mat, mat, mat),
        out_specs=(act, act, row, mat, mat, mat, mat, row, mat, mat, mat),
        check_vma=False,
    )
```

```python
import functools

import jax
import jax.numpy as jnp
import numpy as np
from jax import lax
from jax.experimental import pallas as pl
from jax.experimental.pallas import tpu as pltpu
from jax.sharding import Mesh
from jax.sharding import PartitionSpec as P

HEADS = 32
KV_HEADS = 4
HEAD_DIM = 64
EPSILON = 1e-05
ROPE_BASE = 10000.0
MASKED = -1e30
FAR = 1 << 30
BF = jnp.bfloat16
F32 = jnp.float32
VMEM_BYTES = 56 * 1024 * 1024


def params(**kw):
    return pltpu.CompilerParams(vmem_limit_bytes=VMEM_BYTES, **kw)


def along_plane(value, step):
    count = lax.axis_size("fsdp")
    return lax.ppermute(value, "fsdp", [(i, i ^ step) for i in range(count)])


def to_sibling(value):
    return lax.ppermute(value, "core", [(0, 1), (1, 0)])


def along_line(value, shift):
    count = lax.axis_size("z")
    return lax.ppermute(
        value, "z", [(i, i + shift) for i in range(count) if 0 <= i + shift < count]
    )


def plane_bits():
    count = lax.axis_size("fsdp")
    return [1 << b for b in range(count.bit_length() - 1)]


def plane_gather(block):
    half = block.shape[0] // 2
    parts = []
    for which, bits in ((0, plane_bits()), (1, plane_bits()[::-1])):
        held = {0: block[which * half : (which + 1) * half]}
        for bit in bits:
            order = sorted(held)
            got = along_plane(jnp.stack([held[j] for j in order]), bit)
            for n, j in enumerate(order):
                held[j ^ bit] = got[n]
        parts.append(held)
    return [jnp.concatenate([parts[0][j], parts[1][j]]) for j in range(lax.axis_size("fsdp"))]


def plane_reduce(partial):
    half = partial.shape[1] // 2
    done = []
    for which, bits in ((0, plane_bits()[::-1]), (1, plane_bits())):
        held = {j: partial[j, which * half : (which + 1) * half] for j in range(partial.shape[0])}
        for bit in bits:
            going = [j for j in sorted(held) if j & bit]
            got = along_plane(jnp.stack([held[j].astype(BF) for j in going]), bit)
            for n, j in enumerate(going):
                held[j ^ bit] = held[j ^ bit].astype(F32) + got[n].astype(F32)
                del held[j]
        done.append(held[0])
    return jnp.concatenate(done)


def line_sum(value):
    count = lax.axis_size("z")
    place = lax.axis_index("z")
    half = count // 2
    for i in range(half - 1):
        got = lax.ppermute(value, "z", [(i, i + 1), (count - 1 - i, count - 2 - i)])
        value = value + got
    value = value + lax.ppermute(value, "z", [(half - 1, half), (half, half - 1)])
    for i in range(half - 2, -1, -1):
        got = lax.ppermute(value, "z", [(i + 1, i), (count - 2 - i, count - 1 - i)])
        outer = (place == i) | (place == count - 1 - i)
        value = jnp.where(outer, got, value)
    return value


def move_kernel(idx_ref, x_ref, o_ref):
    o_ref[...] = x_ref[...]


def pick_columns(x, index, count):
    rows, width = x.shape
    size = width // count
    spec = pltpu.PrefetchScalarGridSpec(
        num_scalar_prefetch=1,
        grid=(count,),
        in_specs=[pl.BlockSpec((rows, size), lambda b, idx: (0, idx[b]))],
        out_specs=pl.BlockSpec((rows, size), lambda b, idx: (0, b)),
    )
    return pl.pallas_call(
        move_kernel,
        grid_spec=spec,
        out_shape=jax.ShapeDtypeStruct(x.shape, x.dtype),
        compiler_params=params(),
        name="pick_columns",
    )(index, x)


def put_columns(x, index, count):
    rows, width = x.shape
    size = width // count
    spec = pltpu.PrefetchScalarGridSpec(
        num_scalar_prefetch=1,
        grid=(count,),
        in_specs=[pl.BlockSpec((rows, size), lambda b, idx: (0, b))],
        out_specs=pl.BlockSpec((rows, size), lambda b, idx: (0, idx[b])),
    )
    return pl.pallas_call(
        move_kernel,
        grid_spec=spec,
        out_shape=jax.ShapeDtypeStruct(x.shape, x.dtype),
        compiler_params=params(),
        name="put_columns",
    )(index, x)


def cut_blocks(weight, f, k, count, dtype=BF):
    rows, full = weight.shape
    width, half = full // count, rows // 2
    if width % 128:
        own = lax.dynamic_slice_in_dim(weight, k * half, half, 0).reshape(half, count, width)
        return jnp.stack(
            [lax.dynamic_index_in_dim(own, f ^ j, 1, keepdims=False) for j in range(count)]
        )
    spec = pltpu.PrefetchScalarGridSpec(
        num_scalar_prefetch=1,
        grid=(count,),
        in_specs=[pl.BlockSpec((half, width), lambda j, at: (at[1], at[0] ^ j))],
        out_specs=pl.BlockSpec((None, half, width), lambda j, at: (j, 0, 0)),
    )
    return pl.pallas_call(
        move_kernel,
        grid_spec=spec,
        out_shape=jax.ShapeDtypeStruct((count, half, width), weight.dtype),
        compiler_params=params(),
        name="cut_blocks",
    )(jnp.stack([f, k]), weight)


def join_kernel(at_ref, own_ref, sib_ref, o_ref):
    @pl.when(pl.program_id(0) == 0)
    def _():
        o_ref[...] = own_ref[...].astype(o_ref.dtype)

    @pl.when(pl.program_id(0) == 1)
    def _():
        o_ref[...] = sib_ref[...].astype(o_ref.dtype)


def join_rows(own, sib, f, k):
    count, half, width = own.shape
    if width % 128:
        halves = jnp.stack([own, sib])
        return jnp.concatenate(
            [
                jnp.concatenate(
                    [
                        lax.dynamic_index_in_dim(
                            lax.dynamic_index_in_dim(halves, k ^ h, 0, keepdims=False),
                            f ^ i,
                            0,
                            keepdims=False,
                        )
                        for i in range(count)
                    ],
                    axis=1,
                )
                for h in range(2)
            ],
            axis=0,
        ).astype(F32)
    spec = pltpu.PrefetchScalarGridSpec(
        num_scalar_prefetch=1,
        grid=(2, count),
        in_specs=[
            pl.BlockSpec(
                (None, half, width),
                lambda s, i, at: (at[0] ^ jnp.where(s == 0, i, count - 1), 0, 0),
            ),
            pl.BlockSpec(
                (None, half, width), lambda s, i, at: (at[0] ^ jnp.where(s == 1, i, 0), 0, 0)
            ),
        ],
        out_specs=pl.BlockSpec((half, width), lambda s, i, at: (at[1] ^ s, i)),
    )
    return pl.pallas_call(
        join_kernel,
        grid_spec=spec,
        out_shape=jax.ShapeDtypeStruct((2 * half, count * width), F32),
        compiler_params=params(),
        name="join_rows",
    )(jnp.stack([f, k]), own, sib)


def join_columns(own, sib, k):
    rows, half = own.shape
    count = 4
    size = rows // count
    spec = pltpu.PrefetchScalarGridSpec(
        num_scalar_prefetch=1,
        grid=(2, count),
        in_specs=[
            pl.BlockSpec((size, half), lambda s, i, at: (jnp.where(s == 0, i, count - 1), 0)),
            pl.BlockSpec((size, half), lambda s, i, at: (jnp.where(s == 1, i, 0), 0)),
        ],
        out_specs=pl.BlockSpec((size, half), lambda s, i, at: (i, at[0] ^ s)),
    )
    return pl.pallas_call(
        join_kernel,
        grid_spec=spec,
        out_shape=jax.ShapeDtypeStruct((rows, 2 * half), F32),
        compiler_params=params(),
        name="join_columns",
    )(k.reshape(1), own, sib)


def swap_halves(block):
    lane = lax.broadcasted_iota(jnp.int32, block.shape, 1)
    return jnp.where(lane % 64 < 32, pltpu.roll(block, 96, 1), pltpu.roll(block, 32, 1))


def qkv_kernel(idx_ref, x_ref, gain_ref, w_ref, cos_ref, sin_ref, h_ref, q_ref, kv_ref):
    blocks = idx_ref.shape[0]
    size = x_ref.shape[1] // blocks
    x = x_ref[...].astype(F32)
    inverse = lax.rsqrt(jnp.mean(x * x, axis=1, keepdims=True) + EPSILON)
    for b in range(blocks):
        at = pl.ds(pl.multiple_of(idx_ref[b] * size, 128), size)
        part = x_ref[:, at].astype(F32) * inverse * gain_ref[:, at]
        h_ref[:, b * size : (b + 1) * size] = part.astype(BF)
    out = jnp.dot(h_ref[...], w_ref[...], preferred_element_type=F32)
    cosine, sine = cos_ref[...], sin_ref[...]
    pairs = q_ref.shape[1] // 128
    for c in range(pairs):
        block = out[:, c * 128 : (c + 1) * 128]
        q_ref[:, c * 128 : (c + 1) * 128] = (block * cosine + swap_halves(block) * sine).astype(BF)
    block = out[:, pairs * 128 :]
    lane = lax.broadcasted_iota(jnp.int32, block.shape, 1)
    turned = block * cosine + swap_halves(block) * sine
    kv_ref[...] = jnp.where(lane < 64, turned, block).astype(BF)


def qkv_project(idx, x, gain, weight, cosine, sine, rows):
    total, depth = x.shape
    width = weight.shape[1]
    spec = pltpu.PrefetchScalarGridSpec(
        num_scalar_prefetch=1,
        grid=(total // rows,),
        in_specs=[
            pl.BlockSpec((rows, depth), lambda i, idx: (i, 0)),
            pl.BlockSpec((1, depth), lambda i, idx: (0, 0)),
            pl.BlockSpec((depth, width), lambda i, idx: (0, 0)),
            pl.BlockSpec((rows, 128), lambda i, idx: (0, 0)),
            pl.BlockSpec((rows, 128), lambda i, idx: (0, 0)),
        ],
        out_specs=[
            pl.BlockSpec((rows, depth), lambda i, idx: (i, 0)),
            pl.BlockSpec((rows, width - 128), lambda i, idx: (i, 0)),
            pl.BlockSpec((rows, 128), lambda i, idx: (i, 0)),
        ],
    )
    return pl.pallas_call(
        qkv_kernel,
        grid_spec=spec,
        out_shape=[
            jax.ShapeDtypeStruct((total, depth), BF),
            jax.ShapeDtypeStruct((total, width - 128), BF),
            jax.ShapeDtypeStruct((total, 128), BF),
        ],
        compiler_params=params(),
        cost_estimate=pl.CostEstimate(
            flops=2 * total * depth * width,
            bytes_accessed=4 * total * depth + 2 * depth * width + 2 * total * width,
            transcendentals=0,
        ),
        name="qkv_project",
    )(idx, x, gain, weight, cosine, sine)


def nt(a, b):
    return lax.dot_general(a, b, (((1,), (1,)), ((), ())), preferred_element_type=F32)


def tn(a, b):
    return lax.dot_general(a, b, (((0,), (0,)), ((), ())), preferred_element_type=F32)


def nn(a, b):
    return jnp.dot(a, b, preferred_element_type=F32)


def limits(at_ref, rows):
    j = pl.program_id(0)
    place = at_ref[0] - lax.broadcasted_iota(jnp.int32, (rows, 1), 0)
    return jnp.minimum(place, at_ref[1 + j] - 1)


def attend_kernel(at_ref, q_ref, kv_ref, kp_ref, o_ref, lse_ref, vk_ref):
    rows = q_ref.shape[0]
    keys = vk_ref.shape[0]
    kv = kv_ref[...].reshape(keys, 128)

    @pl.when(pl.program_id(1) == 0)
    def _():
        vk_ref[...] = pltpu.roll(kv.astype(F32), 64, 1).astype(BF)

    vk = vk_ref[...]
    allowed = kp_ref[...] <= limits(at_ref, rows)
    lane = lax.broadcasted_iota(jnp.int32, (rows, 128), 1)
    q = q_ref[...]
    zero = jnp.zeros_like(q)
    outs, logs = [], []
    for first in (True, False):
        mine = lane < 64 if first else lane >= 64
        scores = nt(jnp.where(mine, q, zero), kv if first else vk) * (HEAD_DIM**-0.5)
        scores = jnp.where(allowed, scores, MASKED)
        top = jnp.max(scores, axis=1, keepdims=True)
        weights = jnp.exp(scores - top)
        total = jnp.sum(weights, axis=1, keepdims=True)
        outs.append(nn(weights.astype(BF), vk if first else kv) / total)
        logs.append(jnp.broadcast_to(top + jnp.log(total), (rows, 128)))
    o_ref[...] = jnp.where(lane < 64, outs[0], outs[1]).astype(BF)
    lse_ref[...] = jnp.where(lane < 64, logs[0], logs[1])


def attend(at, q, kv, kp):
    chunks, seqs, rows, _ = kv.shape
    pairs = q.shape[2] // 128
    keys = chunks * rows
    spec = pltpu.PrefetchScalarGridSpec(
        num_scalar_prefetch=1,
        grid=(seqs, pairs),
        in_specs=[
            pl.BlockSpec((None, rows, 128), lambda j, p, at: (j, 0, p)),
            pl.BlockSpec((chunks, None, rows, 128), lambda j, p, at: (0, j, 0, 0)),
            pl.BlockSpec((1, keys), lambda j, p, at: (0, 0)),
        ],
        out_specs=[
            pl.BlockSpec((None, rows, 128), lambda j, p, at: (j, 0, p)),
            pl.BlockSpec((None, rows, 128), lambda j, p, at: (j, 0, p)),
        ],
        scratch_shapes=[pltpu.VMEM((keys, 128), BF)],
    )
    size = seqs * pairs * 2 * rows * keys
    return pl.pallas_call(
        attend_kernel,
        grid_spec=spec,
        out_shape=[
            jax.ShapeDtypeStruct(q.shape, BF),
            jax.ShapeDtypeStruct(q.shape, F32),
        ],
        compiler_params=params(),
        cost_estimate=pl.CostEstimate(
            flops=size * 4 * 128, bytes_accessed=4 << 20, transcendentals=size
        ),
        name="attend",
    )(at, q, kv, kp)


def attend_back_kernel(
    at_ref, q_ref, do_ref, lse_ref, kv_ref, kp_ref, cos_ref, sin_ref, dq_ref, dkv_ref, vk_ref, dk_ref, dv_ref
):
    rows = q_ref.shape[0]
    keys = vk_ref.shape[0]
    pair = pl.program_id(1)
    kv = kv_ref[...].reshape(keys, 128)

    @pl.when(pair == 0)
    def _():
        vk_ref[...] = pltpu.roll(kv.astype(F32), 64, 1).astype(BF)
        dk_ref[...] = jnp.zeros_like(dk_ref)
        dv_ref[...] = jnp.zeros_like(dv_ref)

    vk = vk_ref[...]
    allowed = kp_ref[...] <= limits(at_ref, rows)
    lane = lax.broadcasted_iota(jnp.int32, (rows, 128), 1)
    q, do = q_ref[...], do_ref[...]
    zero = jnp.zeros_like(q)
    parts = []
    for first in (True, False):
        mine = lane < 64 if first else lane >= 64
        keyed, valued = (kv, vk) if first else (vk, kv)
        q_own, do_own = jnp.where(mine, q, zero), jnp.where(mine, do, zero)
        scores = nt(q_own, keyed) * (HEAD_DIM**-0.5)
        log_total = lse_ref[:, 0:1] if first else lse_ref[:, 64:65]
        weights = jnp.where(allowed, jnp.exp(scores - log_total), 0.0)
        joint = weights * nt(do_own, valued)
        back = (joint - weights * jnp.sum(joint, axis=1, keepdims=True)).astype(BF)
        parts.append(nn(back, keyed))
        dk_ref[...] += tn(back, q_own)
        dv_ref[...] += tn(weights.astype(BF), do_own)
    turned = jnp.where(lane < 64, parts[0], parts[1]) * (HEAD_DIM**-0.5)
    dq_ref[...] = (turned * cos_ref[...] - swap_halves(turned) * sin_ref[...]).astype(BF)

    @pl.when(pair == pl.num_programs(1) - 1)
    def _():
        dk = dk_ref[...]
        dv = dv_ref[...]
        dk = (dk + pltpu.roll(dk, 64, 1)) * (HEAD_DIM**-0.5)
        dv = dv + pltpu.roll(dv, 64, 1)
        wide = lax.broadcasted_iota(jnp.int32, dk.shape, 1)
        dkv_ref[...] = jnp.where(wide < 64, dk, dv).astype(BF).reshape(dkv_ref.shape)


def attend_back(at, q, do, lse, kv, kp, cosine, sine):
    chunks, seqs, rows, _ = kv.shape
    pairs = q.shape[2] // 128
    keys = chunks * rows
    tall = pl.BlockSpec((None, rows, 128), lambda j, p, at: (j, 0, p))
    whole = pl.BlockSpec((chunks, None, rows, 128), lambda j, p, at: (0, j, 0, 0))
    flat = pl.BlockSpec((rows, 128), lambda j, p, at: (0, 0))
    spec = pltpu.PrefetchScalarGridSpec(
        num_scalar_prefetch=1,
        grid=(seqs, pairs),
        in_specs=[tall, tall, tall, whole, pl.BlockSpec((1, keys), lambda j, p, at: (0, 0)), flat, flat],
        out_specs=[tall, whole],
        scratch_shapes=[
            pltpu.VMEM((keys, 128), BF),
            pltpu.VMEM((keys, 128), F32),
            pltpu.VMEM((keys, 128), F32),
        ],
    )
    size = seqs * pairs * 2 * rows * keys
    return pl.pallas_call(
        attend_back_kernel,
        grid_spec=spec,
        out_shape=[
            jax.ShapeDtypeStruct(q.shape, BF),
            jax.ShapeDtypeStruct(kv.shape, BF),
        ],
        compiler_params=params(),
        cost_estimate=pl.CostEstimate(
            flops=size * 10 * 128, bytes_accessed=8 << 20, transcendentals=size
        ),
        name="attend_back",
    )(at, q, do, lse, kv, kp, cosine, sine)


def rms_backward(row_block, inverse, gain_vec, gradient):
    normed = row_block * inverse
    gain_grad = jnp.sum(gradient * normed, axis=0)
    scaled = gradient * gain_vec
    back = inverse * (scaled - normed * jnp.mean(scaled * normed, axis=1, keepdims=True))
    return (back, gain_grad)


def body_plain(
    tokens, cotangent, lengths, attn_gain, w_query, w_key, w_value, w_out, mlp_gain, w_gate, w_up, w_down
):
    seqs, rows, depth = tokens.shape
    count, line = lax.axis_size("fsdp"), lax.axis_size("z")
    f, z, k = lax.axis_index("fsdp"), lax.axis_index("z"), lax.axis_index("core")
    slot = rows * line * 2
    total = count * rows
    slab = depth // count
    half = slab // 2
    q_width = HEADS * HEAD_DIM // count
    shared = max(1, count // KV_HEADS)

    x_own = tokens.reshape(rows, depth)
    chunk = 2 * z + k
    first_pos = slot - 1 - chunk * rows

    length = lengths[0]
    words = jnp.zeros((slab,), F32).at[0].set((length // 64).astype(F32)).at[1].set((length % 64).astype(F32))
    note = jnp.stack([attn_gain, mlp_gain, words.astype(BF), jnp.zeros((slab,), BF)])
    notes = [note] + [along_plane(note, j) for j in range(1, count)]
    notes_abs = [lax.dynamic_index_in_dim(jnp.stack(notes), f ^ i, 0, keepdims=False) for i in range(count)]
    gain_one = jnp.concatenate([n[0] for n in notes_abs]).astype(F32).reshape(1, depth)
    gain_two = jnp.concatenate([n[1] for n in notes_abs]).astype(F32).reshape(1, depth)
    all_lengths = jnp.stack(
        [n[2, 0].astype(jnp.int32) * 64 + n[2, 1].astype(jnp.int32) for n in notes]
    )

    x_all = jnp.concatenate(plane_gather(x_own))

    wq = cut_blocks(w_query, f, k, count)
    key_cols = lax.dynamic_slice_in_dim(w_key, k * half, half, 0).reshape(half, KV_HEADS, HEAD_DIM)
    value_cols = lax.dynamic_slice_in_dim(w_value, k * half, half, 0).reshape(half, KV_HEADS, HEAD_DIM)

    def head_of(j):
        return (f ^ j) // shared

    wkv = jnp.stack(
        [
            jnp.concatenate(
                [
                    lax.dynamic_index_in_dim(key_cols, head_of(j), 1, keepdims=False),
                    lax.dynamic_index_in_dim(value_cols, head_of(j), 1, keepdims=False),
                ],
                axis=1,
            )
            for j in range(count)
        ]
    )
    wqkv = jnp.concatenate([wq, wkv], axis=2)
    wqkv_own = jnp.stack([wqkv[0]] + [along_plane(wqkv[j], j) for j in range(1, count)])
    wqkv_sib = to_sibling(wqkv_own)
    wqkv_all = jnp.concatenate([wqkv_own, wqkv_sib]).reshape(depth, q_width + 128)

    def fetch(weight):
        cut = cut_blocks(weight, f, k, count)
        width = cut.shape[2]
        own = jnp.stack([cut[0]] + [along_plane(cut[j], j) for j in range(1, count)])
        sib = to_sibling(own)
        return own.reshape(depth // 2, width), sib.reshape(depth // 2, width)

    gate_own, gate_sib = fetch(w_gate)
    up_own, up_sib = fetch(w_up)

    order = jnp.stack([(f ^ j) * 2 + (k ^ h) for h in range(2) for j in range(count)]).astype(jnp.int32)

    half_dim = HEAD_DIM // 2
    frequency = jnp.power(ROPE_BASE, jnp.arange(half_dim, dtype=F32) * (-2.0 / HEAD_DIM))
    positions = first_pos - jnp.arange(rows, dtype=jnp.int32)
    angles = positions.astype(F32)[:, None] * frequency[None, :]
    cos32, sin32 = jnp.cos(angles), jnp.sin(angles)
    cosine = jnp.concatenate([cos32] * 4, axis=1)
    sine = jnp.concatenate([-sin32, sin32, -sin32, sin32], axis=1)

    normed_one, queries, kv = qkv_project(order, x_all, gain_one, wqkv_all, cosine, sine, rows)
    queries = queries.reshape(count, rows, q_width)
    kv = kv.reshape(count, rows, 128)

    mine = [kv] + [along_line(kv, -s) for s in range(1, line)]
    mine = jnp.stack(mine)
    kv_all = jnp.concatenate([mine, to_sibling(mine)])
    places = []
    for h in range(2):
        for s in range(line):
            start = slot - 1 - (2 * (z + s) + (k ^ h)) * rows
            places.append(start - jnp.arange(rows, dtype=jnp.int32))
    kp = jnp.concatenate(places)
    kp = jnp.where(kp < 0, FAR, kp).reshape(1, -1)
    at = jnp.concatenate([first_pos.reshape(1), all_lengths]).astype(jnp.int32)

    attended, log_total = attend(at, queries, kv_all, kp)
    attended = attended.reshape(total, q_width)

    mixed_part = nn(attended, w_out).astype(BF).reshape(count, rows, depth)
    inputs = x_own.astype(F32)
    mixed = inputs + plane_reduce(mixed_part)
    inv_two = lax.rsqrt(jnp.mean(mixed * mixed, axis=1, keepdims=True) + EPSILON)
    normed_two_own = (mixed * inv_two * gain_two).astype(BF)
    normed_two = jnp.concatenate(plane_gather(normed_two_own))
    normed_two = pick_columns(normed_two, order, 2 * count)
    n2_own, n2_sib = normed_two[:, : depth // 2], normed_two[:, depth // 2 :]

    valid = (positions < length).astype(F32)[:, None]
    out_back = cotangent.reshape(rows, depth).astype(F32) * valid
    branch_own = out_back.astype(BF)
    branch = jnp.concatenate(plane_gather(branch_own))

    gate = nn(n2_own, gate_own) + nn(n2_sib, gate_sib)
    up = nn(n2_own, up_own) + nn(n2_sib, up_sib)
    sigmoid = jax.nn.sigmoid(gate)
    hidden = (gate * sigmoid * up).astype(BF)

    half_depth = depth // 2
    branch_mine = lax.dynamic_slice_in_dim(branch, k * half_depth, half_depth, 1)
    branch_other = lax.dynamic_slice_in_dim(branch, (1 - k) * half_depth, half_depth, 1)

    def pair_sum(own, other):
        return (own + to_sibling(other.astype(BF)).astype(F32)).astype(BF)

    def swap_slabs(own):
        return jnp.stack([own[0]] + [along_plane(own[j], j) for j in range(1, count)])

    down_half = line_sum(pair_sum(tn(hidden, branch_mine), tn(hidden, branch_other)))
    down_grad = join_columns(down_half, to_sibling(down_half), k)

    hidden_grad = nt(branch, w_down)
    gate_back = (hidden_grad * up * sigmoid * (1.0 + gate * (1.0 - sigmoid))).astype(BF)
    up_back = (hidden_grad * gate * sigmoid).astype(BF)

    def slab_grad(left_own, left_other, right):
        width = right.shape[1]
        own = pair_sum(tn(left_own, right), tn(left_other, right)).reshape(count, half, width)
        return line_sum(swap_slabs(own))

    gate_half = slab_grad(n2_own, n2_sib, gate_back)
    gate_grad = join_rows(gate_half, to_sibling(gate_half), f, k)
    up_half = slab_grad(n2_own, n2_sib, up_back)
    up_grad = join_rows(up_half, to_sibling(up_half), f, k)

    back_own = (nt(gate_back, gate_own) + nt(up_back, up_own)).astype(BF)
    back_sib = (nt(gate_back, gate_sib) + nt(up_back, up_sib)).astype(BF)
    normed_back = put_columns(jnp.concatenate([back_own, back_sib], axis=1), order, 2 * count)
    normed_back = plane_reduce(normed_back.reshape(count, rows, depth))

    out_part = nn(hidden, w_down).astype(BF).reshape(count, rows, depth)
    outputs = mixed + plane_reduce(out_part)

    mixed_back, gain_two_grad = rms_backward(mixed, inv_two, gain_two, normed_back)
    mixed_grad = out_back + mixed_back
    attn_back = jnp.concatenate(plane_gather(mixed_grad.astype(BF)))
    attended_grad = nt(attn_back, w_out).astype(BF).reshape(count, rows, q_width)

    back_mine = lax.dynamic_slice_in_dim(attn_back, k * half_depth, half_depth, 1)
    back_other = lax.dynamic_slice_in_dim(attn_back, (1 - k) * half_depth, half_depth, 1)
    out_half = line_sum(pair_sum(tn(attended, back_mine), tn(attended, back_other)))
    out_grad = join_columns(out_half, to_sibling(out_half), k)

    query_back, kv_part = attend_back(at, queries, attended_grad, log_total, kv_all, kp, cosine, sine)
    kv_mine = kv_part[:line].astype(F32) + to_sibling(kv_part[line:]).astype(F32)
    kv_back = kv_mine[0]
    for s in range(1, line):
        kv_back = kv_back + along_line(kv_mine[s].astype(BF), s).astype(F32)
    lead, trail, flat = kv_back[..., :32], kv_back[..., 32:64], kv_back[..., 64:]
    kv_back = jnp.concatenate(
        [lead * cos32 + trail * sin32, trail * cos32 - lead * sin32, flat], axis=-1
    ).astype(BF)
    qkv_back = jnp.concatenate(
        [query_back.reshape(total, q_width), kv_back.reshape(total, 128)], axis=1
    )

    normed_one_back = nt(qkv_back, wqkv_all).astype(BF)
    normed_one_back = put_columns(normed_one_back, order, 2 * count)
    normed_one_back = plane_reduce(normed_one_back.reshape(count, rows, depth))
    inv_one = lax.rsqrt(jnp.mean(inputs * inputs, axis=1, keepdims=True) + EPSILON)
    input_back, gain_one_grad = rms_backward(inputs, inv_one, gain_one, normed_one_back)
    input_grad = mixed_grad + input_back

    n1_own, n1_sib = normed_one[:, :half_depth], normed_one[:, half_depth:]
    qkv_own = pair_sum(tn(n1_own, qkv_back), tn(n1_sib, qkv_back)).reshape(count, half, q_width + 128)
    gains = jnp.stack([gain_one_grad, gain_two_grad]).reshape(2, count, slab)
    gains = jnp.stack(
        [lax.dynamic_index_in_dim(gains, f ^ j, 1, keepdims=False) for j in range(count)]
    ).astype(BF)
    gains = line_sum(swap_slabs(gains))
    qkv_half = line_sum(swap_slabs(qkv_own))
    gains = jnp.sum(gains.astype(F32), axis=0) + jnp.sum(to_sibling(gains).astype(F32), axis=0)
    qkv_other = to_sibling(qkv_half)
    query_grad = join_rows(qkv_half[:, :, :q_width], qkv_other[:, :, :q_width], f, k)
    halves = jnp.stack([qkv_half[:, :, q_width:], qkv_other[:, :, q_width:]])

    def by_head(lo, hi):
        both = [lax.dynamic_index_in_dim(halves, k ^ h, 0, keepdims=False) for h in range(2)]
        both = jnp.concatenate(both, axis=1).astype(F32)[:, :, lo:hi]
        cols = jnp.stack([lax.dynamic_index_in_dim(both, f ^ i, 0, keepdims=False) for i in range(count)])
        cols = cols.reshape(KV_HEADS, shared, slab, HEAD_DIM).sum(1)
        return jnp.transpose(cols, (1, 0, 2)).reshape(slab, KV_HEADS * HEAD_DIM)

    key_grad = by_head(0, 64)
    value_grad = by_head(64, 128)

    return (
        outputs.reshape(seqs, rows, depth),
        input_grad.reshape(seqs, rows, depth),
        gains[0],
        query_grad,
        key_grad,
        value_grad,
        out_grad,
        gains[1],
        gate_grad,
        up_grad,
        down_grad,
    )


def rotary_parts(slot, rows):
    lane = np.arange(128) % (HEAD_DIM // 2)
    frequency = ROPE_BASE ** (lane * (-2.0 / HEAD_DIM))
    starts = (slot - 1 - rows * np.arange(slot // rows))[:, None] * frequency[None, :]
    steps = np.arange(rows)[:, None] * frequency[None, :]
    return [jnp.asarray(t(a), F32) for a in (starts, steps) for t in (np.cos, np.sin)]


def front_kernel(
    length_ref, attn_gain, mlp_gain, start_cos, start_sin, step_cos, step_sin,
    tokens, cotangent, w_query, w_key, w_value, w_out, w_gate, w_up, w_down,
    h1, queries, lse, attended, mixed, n2, hidden, gate_back, up_back, back_part, out_part,
    gain_one, gain_two, limits, cosine, sine, kp,
    kv_out, branch_out, wqkv_out,
    notes, x_all, wqkv, keys_in, values_in, kv_give, gate_own, gate_sib, up_own, up_sib, down,
    kv_all, vk, w_o, part, landed, relay, relayed, n2_all, branch_all, cot_in,
    local_s, note_s, note_r, tok_s, tok_r, tof_s, tof_r, wq_s, wq_r, wk_s, wk_r, wp_s, wp_r, wkp_s, wkp_r,
    kz_s, kz_r, kp_s, kp_r, gt_s, gt_r, up_s, up_r, gz_s, gz_r, gs_s, gs_r, us_s, us_r,
    bt_s, bt_r, btf_s, btf_r, mx_s, mx_r, nt_s, nt_r, ntf_s, ntf_r,
):
    f, z, k = lax.axis_index("fsdp"), lax.axis_index("z"), lax.axis_index("core")
    plane, line = 4, 4
    rows, depth = tokens.shape
    total = plane * rows
    slab = depth // plane
    half = slab // 2
    hr = rows // 2
    q_width = w_out.shape[0]
    pairs = q_width // 128
    ff = w_down.shape[0]
    keys = vk.shape[0]
    slot = rows * line * 2
    even = z % 2 == 0
    across = z + 1 - 2 * (z % 2)
    peers = (1, 2, 3)
    first_pos = slot - 1 - (2 * z + k) * rows

    def remote(source, target, send, recv, where):
        return pltpu.make_async_remote_copy(
            src_ref=source,
            dst_ref=target,
            send_sem=send,
            recv_sem=recv,
            device_id=where,
            device_id_type=pl.DeviceIdType.MESH,
        )

    sib = {"core": 1 - k}

    def chip(j):
        return {"fsdp": f ^ j}

    def cols(weight, j, side, width):
        start = pl.multiple_of((f ^ j) * width, 128)
        return weight.at[pl.ds(pl.multiple_of((k ^ side) * half, 16), half), pl.ds(start, width)]

    class Gather:
        def __init__(self, source, target, send, recv, fsend, frecv):
            self.near = {
                j: remote(source, target.at[j], send.at[j - 1], recv.at[j - 1], chip(j)) for j in (1, 2)
            }
            self.far = {
                j: remote(
                    target.at[j, pl.ds((j - 1) * hr, hr), :],
                    target.at[3, pl.ds((j - 1) * hr, hr), :],
                    fsend.at[j - 1],
                    frecv.at[j - 1],
                    chip(3 - j),
                )
                for j in (1, 2)
            }

        def start(self):
            for j in (1, 2):
                self.near[j].start()

        def forward(self):
            for j in (1, 2):
                self.near[j].wait_recv()
                self.far[j].start()

        def arrive(self):
            for j in (1, 2):
                self.far[j].wait_recv()

        def close(self):
            for j in (1, 2):
                self.near[j].wait_send()
                self.far[j].wait_send()

    def note_send(j):
        return remote(notes.at[0], notes.at[j], note_s.at[j - 1], note_r.at[j - 1], chip(j))

    token_gather = Gather(tokens, x_all, tok_s, tok_r, tof_s, tof_r)
    branch_gather = Gather(branch_all.at[0], branch_all, bt_s, bt_r, btf_s, btf_r)
    n2_gather = Gather(n2_all.at[0], n2_all, nt_s, nt_r, ntf_s, ntf_r)

    def wq_send(j):
        target = wqkv.at[pl.ds(j * half, half), pl.ds(0, q_width)]
        return remote(cols(w_query, j, 0, q_width), target, wq_s.at[j - 1], wq_r.at[j - 1], chip(j))

    def wk_send(j):
        target = wqkv.at[pl.ds(j * half, half), pl.ds(q_width, 128)]
        return remote(kv_give.at[j], target, wk_s.at[j - 1], wk_r.at[j - 1], chip(j))

    def wp_send(j):
        source = wqkv.at[pl.ds(j * half, half), :]
        target = wqkv.at[pl.ds((plane + j) * half, half), :]
        return remote(source, target, wp_s.at[j - 1], wp_r.at[j - 1], sib)

    def kv_send(s):
        return remote(kv_all.at[0], kv_all.at[s], kz_s.at[s - 1], kz_r.at[s - 1], {"z": z - s})

    def kv_pair(s):
        return remote(kv_all.at[s], kv_all.at[line + s], kp_s.at[s], kp_r.at[s], sib)

    def gate_send(j):
        return remote(cols(w_gate, j, 0, ff), gate_own.at[j], gt_s.at[j - 1], gt_r.at[j - 1], chip(j))

    def up_send(j):
        return remote(cols(w_up, j, 0, ff), up_own.at[j], up_s.at[j - 1], up_r.at[j - 1], chip(j))

    gate_across = remote(gate_own.at[3], gate_own.at[3], gz_s.at[0], gz_r.at[0], {"z": across})
    up_across = remote(up_own.at[3], up_own.at[3], gz_s.at[0], gz_r.at[0], {"z": across})

    def gate_pair(j):
        return remote(gate_own.at[j], gate_sib.at[j], gs_s.at[j - 1], gs_r.at[j - 1], sib)

    def up_pair(j):
        return remote(up_own.at[j], up_sib.at[j], us_s.at[j - 1], us_r.at[j - 1], sib)

    def span(which):
        return pl.ds(which * hr, hr)

    mix_first = {
        "one": remote(part.at[1, span(0), :], landed.at[0, span(0), :], mx_s.at[0], mx_r.at[0], chip(1)),
        "two": remote(part.at[2, span(1), :], landed.at[1, span(1), :], mx_s.at[1], mx_r.at[1], chip(2)),
        "far_one": remote(part.at[3, span(0), :], relay.at[0], mx_s.at[2], mx_r.at[2], chip(1)),
        "far_two": remote(part.at[3, span(1), :], relay.at[1], mx_s.at[3], mx_r.at[3], chip(2)),
        "late_two": remote(relayed.at[0], landed.at[1, span(0), :], mx_s.at[4], mx_r.at[4], chip(2)),
        "late_one": remote(relayed.at[1], landed.at[0, span(1), :], mx_s.at[5], mx_r.at[5], chip(1)),
    }

    local = [
        pltpu.make_async_copy(source, target, local_s.at[n])
        for n, (source, target) in enumerate(
            [
                (tokens, x_all.at[0]),
                (w_key, keys_in),
                (w_value, values_in),
                (cols(w_query, 0, 0, q_width), wqkv.at[pl.ds(0, half), pl.ds(0, q_width)]),
                (cols(w_query, 0, 1, q_width), wqkv.at[pl.ds(plane * half, half), pl.ds(0, q_width)]),
                (cotangent, cot_in),
                (w_out, w_o),
                (cols(w_gate, 0, 0, ff), gate_own.at[0]),
                (cols(w_gate, 0, 1, ff), gate_sib.at[0]),
                (cols(w_up, 0, 0, ff), up_own.at[0]),
                (cols(w_up, 0, 1, ff), up_sib.at[0]),
                (w_down, down),
            ]
        )
    ]

    length = length_ref[0]
    place = lax.broadcasted_iota(jnp.int32, (16, slab), 0)
    high, low = (length // 64).astype(F32), (length % 64).astype(F32)
    note = jnp.where(place == 0, attn_gain[...].astype(F32), mlp_gain[...].astype(F32))
    note = jnp.where(place == 2, high, jnp.where(place == 3, low, note))
    notes[0] = note.astype(BF)
    for j in peers:
        note_send(j).start()
    token_gather.start()
    for j in (3, 1, 2):
        wq_send(j).start()
    for copy in local:
        copy.start()

    local[1].wait()
    local[2].wait()

    def head_columns(j, side):
        at = pl.ds(pl.multiple_of((k ^ side) * half, 16), half)
        head = f ^ j
        width = KV_HEADS * HEAD_DIM
        key = pltpu.roll(keys_in[at, :].astype(F32), (width - head * 64) % width, 1)[:, :128]
        value = pltpu.roll(values_in[at, :].astype(F32), (width - head * 64 + 64) % width, 1)[:, :128]
        lane = lax.broadcasted_iota(jnp.int32, key.shape, 1)
        return jnp.where(lane < 64, key, value).astype(BF)

    for j in (3, 1, 2):
        kv_give[j] = head_columns(j, 0)
        wk_send(j).start()
    wqkv[0:half, q_width : q_width + 128] = head_columns(0, 0)
    wqkv[plane * half : (plane + 1) * half, q_width : q_width + 128] = head_columns(0, 1)

    chunk = pl.ds(2 * z + k, 1)
    cos_at, sin_at = start_cos[chunk, :], start_sin[chunk, :]
    lane = lax.broadcasted_iota(jnp.int32, (rows, 128), 1)
    cosine[...] = cos_at * step_cos[...] + sin_at * step_sin[...]
    turn = sin_at * step_cos[...] - cos_at * step_sin[...]
    sine[...] = jnp.where(lane % 64 < 32, -turn, turn)
    for h in range(2):
        for s in range(line):
            start = slot - 1 - (2 * (z + s) + (k ^ h)) * rows
            spot = start - lax.broadcasted_iota(jnp.int32, (8, rows), 1)
            spot = jnp.where(spot < 0, FAR, spot).astype(F32)
            kp[:, (h * line + s) * rows : (h * line + s + 1) * rows] = spot

    for s in range(1, line):

        @pl.when(z + s >= line)
        def _():
            kv_all[s] = jnp.zeros(kv_all.shape[1:], BF)
            kv_all[line + s] = jnp.zeros(kv_all.shape[1:], BF)

    local[5].wait()
    row_pos = (first_pos - lax.broadcasted_iota(jnp.int32, (rows, 1), 0)).astype(F32)
    valid = row_pos < jnp.full((rows, 1), length.astype(F32))
    branch_all[0] = jnp.where(valid, cot_in[...].astype(F32), 0.0).astype(BF)

    token_gather.forward()
    for j in (1, 2, 3):
        wq_send(j).wait_recv()
        wk_send(j).wait_recv()
        wp_send(j).start()

    @pl.when(even)
    def _():
        gate_send(3).start()

    @pl.when(jnp.logical_not(even))
    def _():
        up_send(3).start()

    for j in (1, 2):
        gate_send(j).start()
    for j in (1, 2):
        up_send(j).start()

    for j in peers:
        note_send(j).wait_recv()
    for j in range(plane):
        at = pl.ds(pl.multiple_of((f ^ j) * slab, 128), slab)
        gain_one[:, at] = jnp.broadcast_to(notes[j, 0:1, :].astype(F32), (8, slab))
        gain_two[:, at] = jnp.broadcast_to(notes[j, 1:2, :].astype(F32), (8, slab))
        theirs = notes[j, 2:3, 0:1].astype(F32) * 64.0 + notes[j, 3:4, 0:1].astype(F32)
        limits[j] = jnp.broadcast_to(jnp.minimum(row_pos, theirs - 1.0), (rows, 128))

    def normalize(j, x_ref):
        @pl.loop(0, rows // 16)
        def _(i):
            at = pl.ds(pl.multiple_of(i * 16, 16), 16)
            x = x_ref[at, :].astype(F32)
            inverse = lax.rsqrt(jnp.mean(x * x, axis=1, keepdims=True) + EPSILON)
            to = pl.ds(pl.multiple_of(j * rows + i * 16, 16), 16)
            for h in range(2):
                for b in range(plane):
                    from_ = pl.ds(pl.multiple_of(((f ^ b) * 2 + (k ^ h)) * half, 128), half)
                    value = x_ref[at, from_].astype(F32) * inverse * gain_one[0:1, from_]
                    c = (h * plane + b) * half
                    h1[to, c : c + half] = value.astype(BF)

    local[0].wait()
    normalize(0, x_all.at[0])
    normalize(1, x_all.at[1])
    normalize(2, x_all.at[2])
    token_gather.arrive()
    normalize(3, x_all.at[3])
    local[3].wait()
    local[4].wait()
    for j in (1, 2, 3):
        wp_send(j).wait_recv()

    kv_cols = nn(h1[...], wqkv[:, q_width : q_width + 128])
    for j in range(plane):
        value = kv_cols[j * rows : (j + 1) * rows]
        turned = value * cosine[...] + swap_halves(value) * sine[...]
        kv_all[0, j] = jnp.where(lane < 64, turned, value).astype(BF)
    for s in range(1, line):

        @pl.when(z >= s)
        def _():
            kv_send(s).start()

    kv_pair(0).start()
    branch_gather.start()

    @pl.loop(0, pairs // 2)
    def _(p):
        at = pl.ds(pl.multiple_of(p * 256, 256), 256)
        out = nn(h1[...], wqkv[:, at])
        for j in range(plane):
            for c in range(2):
                value = out[j * rows : (j + 1) * rows, c * 128 : (c + 1) * 128]
                turned = value * cosine[...] + swap_halves(value) * sine[...]
                queries[j, :, pl.ds(pl.multiple_of(p * 256 + c * 128, 128), 128)] = turned.astype(BF)

    for s in range(1, line):

        @pl.when(z + s < line)
        def _():
            kv_send(s).wait_recv()
            kv_pair(s).start()

    @pl.when(even)
    def _():
        gate_send(3).wait_recv()
        gate_across.start()

    @pl.when(jnp.logical_not(even))
    def _():
        up_send(3).wait_recv()
        up_across.start()

    kv_pair(0).wait_recv()
    for s in range(1, line):

        @pl.when(z + s < line)
        def _():
            kv_pair(s).wait_recv()

    local[6].wait()

    def attend_block(j):
        vk[...] = pltpu.roll(kv_all[:, j].reshape(keys, 128).astype(F32), 64, 1).astype(BF)
        limit = limits[j, :, 0:1]

        @pl.loop(0, pairs)
        def _(p):
            at = pl.ds(pl.multiple_of(p * 128, 128), 128)
            allowed = kp[0:1, :] <= limit
            q = queries[j, :, at]
            zero = jnp.zeros_like(q)
            outs, logs = [], []
            for first in (True, False):
                mine = lane < 64 if first else lane >= 64
                kv = kv_all[:, j].reshape(keys, 128)
                keyed, valued = (kv, vk[...]) if first else (vk[...], kv)
                scores = nt(jnp.where(mine, q, zero), keyed) * (HEAD_DIM**-0.5)
                scores = jnp.where(allowed, scores, MASKED)
                top = jnp.max(scores, axis=1, keepdims=True)
                weights = jnp.exp(scores - top)
                sums = jnp.sum(weights, axis=1, keepdims=True)
                outs.append(nn(weights.astype(BF), valued) / sums)
                logs.append(jnp.broadcast_to(top + jnp.log(sums), (rows, 128)))
            attended[j * rows : (j + 1) * rows, at] = jnp.where(lane < 64, outs[0], outs[1]).astype(BF)
            lse[j, :, at] = jnp.where(lane < 64, logs[0], logs[1])

        part[j] = nn(attended[j * rows : (j + 1) * rows, :], w_o[...]).astype(BF)

    attend_block(3)
    mix_first["far_one"].start()
    mix_first["far_two"].start()
    branch_gather.forward()
    attend_block(1)
    mix_first["one"].start()
    attend_block(2)
    mix_first["two"].start()

    def relay_on(far, late, which, j):
        mix_first[far].wait_recv()
        value = relay[which].astype(F32) + part[j, which * hr : (which + 1) * hr, :].astype(F32)
        relayed[which] = value.astype(BF)
        mix_first[late].start()

    relay_on("far_one", "late_two", 0, 2)
    relay_on("far_two", "late_one", 1, 1)
    attend_block(0)
    for name in ("one", "late_one", "two", "late_two"):
        mix_first[name].wait_recv()

    @pl.loop(0, rows // 16)
    def _(i):
        at = pl.ds(pl.multiple_of(i * 16, 16), 16)
        value = x_all[0, at, :].astype(F32) + part[0, at, :].astype(F32)
        value = value + landed[0, at, :].astype(F32) + landed[1, at, :].astype(F32)
        mixed[at, :] = value
        inverse = lax.rsqrt(jnp.mean(value * value, axis=1, keepdims=True) + EPSILON)
        n2_all[0, at, :] = (value * inverse * gain_two[0:1, :]).astype(BF)

    n2_gather.start()

    for j in (1, 2):
        gate_send(j).wait_recv()
        gate_pair(j).start()
    n2_gather.forward()
    for j in (1, 2):
        up_send(j).wait_recv()
        up_pair(j).start()

    @pl.when(even)
    def _():
        up_across.wait_recv()

    @pl.when(jnp.logical_not(even))
    def _():
        gate_across.wait_recv()

    gate_pair(3).start()
    up_pair(3).start()
    branch_gather.arrive()
    n2_gather.arrive()

    @pl.loop(0, total // 16)
    def _(i):
        at = pl.ds(pl.multiple_of(i * 16, 16), 16)
        j = i // (rows // 16)
        from_row = pl.ds(pl.multiple_of((i % (rows // 16)) * 16, 16), 16)
        for h in range(2):
            for b in range(plane):
                from_ = pl.ds(pl.multiple_of(((f ^ b) * 2 + (k ^ h)) * half, 128), half)
                c = (h * plane + b) * half
                n2[at, c : c + half] = n2_all[j, from_row, from_]

    for n in range(7, 12):
        local[n].wait()
    for j in peers:
        gate_pair(j).wait_recv()
        up_pair(j).wait_recv()

    def feed(at):
        width = at.size
        n2_own, n2_sib = n2[:, 0 : depth // 2], n2[:, depth // 2 : depth]

        def through(own, other):
            first = nn(n2_own, own[:, :, at].reshape(depth // 2, width))
            return first + nn(n2_sib, other[:, :, at].reshape(depth // 2, width))

        gate = through(gate_own, gate_sib)
        up = through(up_own, up_sib)
        sigmoid = 1.0 / (1.0 + jnp.exp(-gate))
        hidden[:, at] = (gate * sigmoid * up).astype(BF)
        grad = nt(branch_all[...].reshape(total, depth), down[at, :])
        gate_back[:, at] = (grad * up * sigmoid * (1.0 + gate * (1.0 - sigmoid))).astype(BF)
        up_back[:, at] = (grad * gate * sigmoid).astype(BF)

    @pl.loop(0, ff // 256)
    def _(n):
        feed(pl.ds(pl.multiple_of(n * 256, 256), 256))

    if ff % 256:
        feed(pl.ds(ff // 256 * 256, ff % 256))

    for h, gate_side, up_side in ((0, gate_own, up_own), (1, gate_sib, up_sib)):

        @pl.loop(0, plane)
        def _(b):
            to = pl.ds(pl.multiple_of(((f ^ b) * 2 + (k ^ h)) * half, 128), half)
            value = nt(gate_back[...], gate_side[b]) + nt(up_back[...], up_side[b])
            back_part[:, to] = value.astype(BF)

    @pl.loop(0, depth // 256)
    def _(n):
        at = pl.ds(pl.multiple_of(n * 256, 256), 256)
        out_part[:, at] = nn(hidden[...], down[:, at]).astype(BF)

    stores = [
        pltpu.make_async_copy(kv_all, kv_out, local_s.at[12]),
        pltpu.make_async_copy(branch_all, branch_out, local_s.at[13]),
        pltpu.make_async_copy(wqkv, wqkv_out, local_s.at[14]),
    ]
    for copy in stores:
        copy.start()
    for gather in (token_gather, branch_gather, n2_gather):
        gather.close()
    for copy in mix_first.values():
        copy.wait_send()
    for j in peers:
        note_send(j).wait_send()
        wq_send(j).wait_send()
        wk_send(j).wait_send()
        wp_send(j).wait_send()
        gate_pair(j).wait_send()
        up_pair(j).wait_send()
    for j in (1, 2):
        gate_send(j).wait_send()
        up_send(j).wait_send()

    @pl.when(even)
    def _():
        gate_send(3).wait_send()
        gate_across.wait_send()

    @pl.when(jnp.logical_not(even))
    def _():
        up_send(3).wait_send()
        up_across.wait_send()

    kv_pair(0).wait_send()
    for s in range(1, line):

        @pl.when(z >= s)
        def _():
            kv_send(s).wait_send()

        @pl.when(z + s < line)
        def _():
            kv_pair(s).wait_send()

    for copy in stores:
        copy.wait()


def front_pass(tokens, cotangent, lengths, attn_gain, mlp_gain, w_query, w_key, w_value, w_out, w_gate, w_up, w_down):
    rows, depth = tokens.shape
    plane, line = 4, 4
    total, slab = plane * rows, depth // plane
    half = slab // 2
    q_width = HEADS * HEAD_DIM // plane
    width = q_width + 128
    ff = w_down.shape[0]
    slot = rows * line * 2
    keys = slot
    act = (rows, depth)
    local = pl.BlockSpec(memory_space=pltpu.VMEM)
    anywhere = pl.BlockSpec(memory_space=pl.ANY)
    dma = lambda n: pltpu.SemaphoreType.DMA((n,))
    kv_shape = (2 * line, plane, rows, 128)
    sds = jax.ShapeDtypeStruct
    outs = [
        sds((total, depth), BF),
        sds((plane, rows, q_width), BF),
        sds((plane, rows, q_width), F32),
        sds((total, q_width), BF),
        sds(act, F32),
        sds((total, depth), BF),
        sds((total, ff), BF),
        sds((total, ff), BF),
        sds((total, ff), BF),
        sds((total, depth), BF),
        sds((total, depth), BF),
        sds((8, depth), F32),
        sds((8, depth), F32),
        sds((plane, rows, 128), F32),
        sds((rows, 128), F32),
        sds((rows, 128), F32),
        sds((8, keys), F32),
        sds(kv_shape, BF),
        sds((plane,) + act, BF),
        sds((depth, width), BF),
    ]
    slabs = pltpu.VMEM((plane, half, ff), BF)
    scratch = [
        pltpu.VMEM((plane, 16, slab), BF),
        pltpu.VMEM((plane,) + act, BF),
        pltpu.VMEM((depth, width), BF),
        pltpu.VMEM(w_key.shape, BF),
        pltpu.VMEM(w_value.shape, BF),
        pltpu.VMEM((plane, half, 128), BF),
        slabs,
        slabs,
        slabs,
        slabs,
        pltpu.VMEM(w_down.shape, BF),
        pltpu.VMEM(kv_shape, BF),
        pltpu.VMEM((keys, 128), BF),
        pltpu.VMEM(w_out.shape, BF),
        pltpu.VMEM((plane,) + act, BF),
        pltpu.VMEM((2,) + act, BF),
        pltpu.VMEM((2, rows // 2, depth), BF),
        pltpu.VMEM((2, rows // 2, depth), BF),
        pltpu.VMEM((plane,) + act, BF),
        pltpu.VMEM((plane,) + act, BF),
        pltpu.VMEM(act, BF),
    ]
    sems = [15, 3, 3, 2, 2, 2, 2, 3, 3, 3, 3, 3, 3, 1, 1, 3, 3, 4, 4, 3, 3, 3, 3, 1, 1, 3, 3, 3, 3]
    sems += [2, 2, 2, 2, 6, 6, 2, 2, 2, 2]
    return pl.pallas_call(
        front_kernel,
        out_shape=outs,
        in_specs=[pl.BlockSpec(memory_space=pltpu.SMEM)] + [local] * 6 + [anywhere] * 9,
        out_specs=[local] * 17 + [anywhere] * 3,
        scratch_shapes=scratch + [dma(n) for n in sems],
        compiler_params=pltpu.CompilerParams(
            vmem_limit_bytes=62 * 1024 * 1024, has_side_effects=True
        ),
        name="front_pass",
    )(
        lengths, attn_gain.reshape(1, slab), mlp_gain.reshape(1, slab), *rotary_parts(slot, rows),
        tokens, cotangent, w_query, w_key, w_value, w_out, w_gate, w_up, w_down,
    )


def add_into(target, other):
    @pl.loop(0, target.shape[0] // 16)
    def _(i):
        at = pl.ds(pl.multiple_of(i * 16, 16), 16)
        target[at, :] = (target[at, :].astype(F32) + other[at, :].astype(F32)).astype(BF)


def back_kernel(
    limits,
    own_down, own_gate, own_up, other_down, other_gate, other_up,
    back_part, out_part, w_out, wqkv_hbm, h1_hbm,
    mixed, branch_own, x_own, gain_one, gain_two,
    attended, queries, lse, kv_all, kp, cosine, sine,
    fin_down, fin_gate, fin_up, fin_out, fin_qkv, fin_gain,
    sib_down, sib_gate, sib_up, sib_out, sib_qkv, sib_gain,
    outputs, input_grad,
    src_down, src_gate, src_up, src_out, src_qkv, src_gain,
    swap_gate, swap_up, swap_qkv,
    end_down, end_gate, end_up, end_out, end_qkv, end_gain,
    load_down, load_gate, give_out, give_qkv, give_gain,
    landed, landed_out, first_back, first_out, da_all, wide, do_all, dqkv, wqkv, h1,
    vk, dk_sum, dv_sum, kv_part, kv_land, kv_mine, kv_line, gain_acc, gain_all,
    pair_s, pair_r, load_s, swap_s, swap_r, in_s, in_r, mid_s, mid_r, out_s, done_s, back_s, back_r, ready,
    local_s, rs_s, rs_r, ro_s, ro_r, ag_s, ag_r, rq_s, rq_r, kp_s, kp_r, kz_s, kz_r, ga_s, ga_r,
):
    f, z, k = lax.axis_index("fsdp"), lax.axis_index("z"), lax.axis_index("core")
    plane, line = lax.axis_size("fsdp"), lax.axis_size("z")
    outer = (z == 0) | (z == line - 1)
    inner = jnp.logical_not(outer)
    inward = jnp.where(z < line // 2, z + 1, z - 1)
    outward = jnp.where(z < line // 2, z - 1, z + 1)
    rows, depth = mixed.shape
    total = plane * rows
    half_depth = depth // 2
    half = half_depth // plane
    q_width = attended.shape[1]
    pairs = q_width // 128
    peers = range(1, plane)

    kinds = {
        "down": (own_down, other_down, src_down, None, end_down, load_down, fin_down, sib_down),
        "gate": (own_gate, other_gate, src_gate, swap_gate, end_gate, load_gate, fin_gate, sib_gate),
        "up": (own_up, other_up, src_up, swap_up, end_up, load_gate, fin_up, sib_up),
        "out": (None, give_out, src_out, None, end_out, None, fin_out, sib_out),
        "qkv": (None, give_qkv, src_qkv, swap_qkv, end_qkv, None, fin_qkv, sib_qkv),
        "gain": (None, give_gain, src_gain, None, end_gain, None, fin_gain, sib_gain),
    }
    chunks = [(name, i) for name, kind in kinds.items() for i in range(kind[2].shape[0])]
    count = len(chunks)
    loaded = [c for c in range(count) if kinds[chunks[c][0]][0] is not None]

    def remote(source, target, send, recv, where):
        return pltpu.make_async_remote_copy(
            src_ref=source,
            dst_ref=target,
            send_sem=send,
            recv_sem=recv,
            device_id=where,
            device_id_type=pl.DeviceIdType.MESH,
        )

    def part(c, which):
        name, i = chunks[c]
        return kinds[name][which].at[i]

    def swapped(c):
        name, i = chunks[c]
        return i if kinds[name][3] is not None else 0

    def pair_copy(c):
        name, i = chunks[c]
        given = kinds[name][1]
        source = given.at[i] if c in loaded else given.at[i % given.shape[0]]
        return remote(source, part(c, 2), pair_s.at[c], pair_r.at[c], {"core": 1 - k})

    def load_copy(c):
        return pltpu.make_async_copy(part(c, 0), kinds[chunks[c][0]][5].at[c % 2], load_s.at[c])

    def swap_copy(c):
        return remote(part(c, 2), part(c, 3), swap_s.at[c], swap_r.at[c], {"fsdp": f ^ swapped(c)})

    def base(c):
        return part(c, 3) if swapped(c) else part(c, 2)

    def in_copy(c):
        return remote(base(c), part(c, 4), in_s.at[c], in_r.at[c], {"z": inward})

    def mid_copy(c):
        return remote(base(c), part(c, 4), mid_s.at[c], mid_r.at[c], {"z": inward})

    def out_copy(c):
        return remote(part(c, 4), part(c, 4), out_s.at[c], mid_r.at[c], {"z": outward})

    def keep_copy(c):
        return pltpu.make_async_copy(part(c, 4), part(c, 6), done_s.at[c])

    def back_copy(c):
        return remote(part(c, 4), part(c, 7), back_s.at[c], back_r.at[c], {"core": 1 - k})

    own_cols = pl.ds(pl.multiple_of(k * half_depth, 128), half_depth)
    other_cols = pl.ds(pl.multiple_of((1 - k) * half_depth, 128), half_depth)

    def out_term(i, cols):
        size = src_out.shape[1]
        right = da_all[:, :, cols].reshape(total, half_depth)
        return tn(attended[:, i * size : (i + 1) * size], right)

    def qkv_term(i, side):
        start = side * half_depth + i * half
        return tn(h1[:, start : start + half], dqkv[...])

    def term(c, side):
        name, i = chunks[c]
        if name == "out":
            return out_term(i, (own_cols, other_cols)[side])
        if name == "qkv":
            return qkv_term(i, side)
        return gain_all[...].astype(F32).sum(axis=0)

    def stage_give(c):
        name, i = chunks[c]
        if c in loaded:
            return
        given = kinds[name][1]
        slots = given.shape[0]
        if i >= slots:
            pair_copy(c - slots).wait_send()
        given[i % slots] = term(c, 1).astype(BF)
        pair_copy(c).start()

    def stage_pair(c):
        pair_copy(c).wait_recv()
        if c in loaded:
            load_copy(c).wait()
            add_into(part(c, 2), kinds[chunks[c][0]][5].at[c % 2])
            if c + 2 in loaded:
                load_copy(c + 2).start()
        else:
            target = part(c, 2)
            target[...] = (target[...].astype(F32) + term(c, 0)).astype(BF)
        if swapped(c):
            swap_copy(c).start()

    def stage_in(c):
        if swapped(c):
            swap_copy(c).wait_recv()

        @pl.when(outer)
        def _():
            in_copy(c).start()

    def stage_mid(c):
        @pl.when(inner)
        def _():
            in_copy(c).wait_recv()
            add_into(base(c), part(c, 4))
            pl.semaphore_signal(
                ready, inc=1, device_id={"z": inward}, device_id_type=pl.DeviceIdType.MESH
            )
            pl.semaphore_wait(ready, 1)
            mid_copy(c).start()

    def stage_out(c):
        @pl.when(inner)
        def _():
            mid_copy(c).wait_recv()
            add_into(part(c, 4), base(c))
            out_copy(c).start()

    def stage_keep(c):
        @pl.when(outer)
        def _():
            out_copy(c).wait_recv()

        keep_copy(c).start()
        back_copy(c).start()

    def back_send(j):
        return remote(back_part.at[j], landed.at[j - 1], rs_s.at[j - 1], rs_r.at[j - 1], {"fsdp": f ^ j})

    def out_send(j):
        return remote(out_part.at[j], landed_out.at[j - 1], ro_s.at[j - 1], ro_r.at[j - 1], {"fsdp": f ^ j})

    def da_send(j):
        return remote(da_all.at[0], da_all.at[j], ag_s.at[j - 1], ag_r.at[j - 1], {"fsdp": f ^ j})

    def dh_send(j):
        mine = wide.at[pl.ds(j * rows, rows), :]
        return remote(mine, landed.at[j - 1], rq_s.at[j - 1], rq_r.at[j - 1], {"fsdp": f ^ j})

    def gain_send(j):
        return remote(gain_all.at[0], gain_all.at[j], ga_s.at[j - 1], ga_r.at[j - 1], {"fsdp": f ^ j})

    locals_ = [
        pltpu.make_async_copy(back_part.at[0], first_back, local_s.at[0]),
        pltpu.make_async_copy(out_part.at[0], first_out, local_s.at[1]),
        pltpu.make_async_copy(w_out, wide.at[pl.ds(0, w_out.shape[0]), :], local_s.at[2]),
        pltpu.make_async_copy(wqkv_hbm, wqkv, local_s.at[3]),
        pltpu.make_async_copy(h1_hbm, h1, local_s.at[4]),
    ]

    def rms_back(gradient_of, x_ref, gain, acc, write):
        acc[...] = jnp.zeros_like(acc)

        @pl.loop(0, rows // 16)
        def _(i):
            at = pl.ds(pl.multiple_of(i * 16, 16), 16)
            gradient = gradient_of(at)
            x = x_ref[at, :].astype(F32)
            inverse = lax.rsqrt(jnp.mean(x * x, axis=1, keepdims=True) + EPSILON)
            normed = x * inverse
            acc[...] += gradient * normed
            scaled = gradient * gain[0:1, :]
            write(at, inverse * (scaled - normed * jnp.mean(scaled * normed, axis=1, keepdims=True)))

    def piece_mixed():
        locals_[0].wait()
        for j in peers:
            back_send(j).wait_recv()

        def gradient_of(at):
            value = first_back[at, :].astype(F32)
            for j in peers:
                value = value + landed[j - 1, at, :].astype(F32)
            return value

        def write(at, value):
            value = value + branch_own[at, :].astype(F32)
            input_grad[at, :] = value
            da_all[0, at, :] = value.astype(BF)

        rms_back(gradient_of, mixed, gain_two, gain_acc.at[1], write)
        for j in peers:
            da_send(j).start()

    def piece_do():
        locals_[2].wait()
        for j in peers:
            da_send(j).wait_recv()
            out_send(j).start()

        @pl.loop(0, plane)
        def _(j):
            do_all[j] = nt(da_all[j], wide[0 : w_out.shape[0], :]).astype(BF)

    def piece_attend(j):
        vk[...] = pltpu.roll(kv_all[:, j].reshape(vk.shape).astype(F32), 64, 1).astype(BF)
        dk_sum[...] = jnp.zeros_like(dk_sum)
        dv_sum[...] = jnp.zeros_like(dv_sum)
        limit = limits[j, :, 0:1]
        lane = lax.broadcasted_iota(jnp.int32, (rows, 128), 1)

        @pl.loop(0, pairs)
        def _(p):
            at = pl.ds(pl.multiple_of(p * 128, 128), 128)
            allowed = kp[0:1, :] <= limit
            q, do = queries[j, :, at], do_all[j, :, at]
            logs = lse[j, :, at]
            zero = jnp.zeros_like(q)
            parts = []
            for first in (True, False):
                mine = lane < 64 if first else lane >= 64
                kv = kv_all[:, j].reshape(vk.shape)
                keyed, valued = (kv, vk[...]) if first else (vk[...], kv)
                q_own, do_own = jnp.where(mine, q, zero), jnp.where(mine, do, zero)
                scores = nt(q_own, keyed) * (HEAD_DIM**-0.5)
                log_total = logs[:, 0:1] if first else logs[:, 64:65]
                weights = jnp.where(allowed, jnp.exp(scores - log_total), 0.0)
                joint = weights * nt(do_own, valued)
                back = (joint - weights * jnp.sum(joint, axis=1, keepdims=True)).astype(BF)
                parts.append(nn(back, keyed))
                dk_sum[...] += tn(back, q_own)
                dv_sum[...] += tn(weights.astype(BF), do_own)
            turned = jnp.where(lane < 64, parts[0], parts[1]) * (HEAD_DIM**-0.5)
            turned = turned * cosine[...] - swap_halves(turned) * sine[...]
            dqkv[j * rows : (j + 1) * rows, at] = turned.astype(BF)

        dk = dk_sum[...]
        dv = dv_sum[...]
        dk = (dk + pltpu.roll(dk, 64, 1)) * (HEAD_DIM**-0.5)
        dv = dv + pltpu.roll(dv, 64, 1)
        wide_lane = lax.broadcasted_iota(jnp.int32, dk.shape, 1)
        packed = jnp.where(wide_lane < 64, dk, dv).astype(BF)
        kv_part[:, j] = packed.reshape(kv_part.shape[0], rows, 128)

    kv_pair = remote(kv_part.at[pl.ds(line, line)], kv_land, kp_s.at[0], kp_r.at[0], {"core": 1 - k})

    def kv_send(s):
        return remote(kv_mine.at[s], kv_line.at[s - 1], kz_s.at[s - 1], kz_r.at[s - 1], {"z": z + s})

    def piece_kv_line():
        kv_pair.wait_recv()
        for s in range(line):
            kv_mine[s] = (kv_part[s].astype(F32) + kv_land[s].astype(F32)).astype(BF)
        for s in range(1, line):

            @pl.when(z + s < line)
            def _():
                kv_send(s).start()

    def piece_kv_sum():
        for s in range(1, line):

            @pl.when(z >= s)
            def _():
                kv_send(s).wait_recv()
                kv_mine[0] = (kv_mine[0].astype(F32) + kv_line[s - 1].astype(F32)).astype(BF)

        lane = lax.broadcasted_iota(jnp.int32, (rows, 128), 1)
        for j in range(plane):
            value = kv_mine[0, j].astype(F32)
            turned = value * cosine[...] - swap_halves(value) * sine[...]
            value = jnp.where(lane < 64, turned, value).astype(BF)
            dqkv[j * rows : (j + 1) * rows, q_width : q_width + 128] = value

    def piece_dh():
        locals_[3].wait()
        locals_[4].wait()
        for h in range(2):
            for j in range(plane):
                start = pl.multiple_of(((f ^ j) * 2 + (k ^ h)) * half, 128)
                block = wqkv[(h * plane + j) * half : (h * plane + j + 1) * half, :]
                wide[0:total, pl.ds(start, half)] = nt(dqkv[...], block).astype(BF)
        for j in peers:
            dh_send(j).start()

    def piece_input():
        for j in peers:
            dh_send(j).wait_recv()

        def gradient_of(at):
            value = wide[at, :].astype(F32)
            for j in peers:
                value = value + landed[j - 1, at, :].astype(F32)
            return value

        def write(at, value):
            input_grad[at, :] = input_grad[at, :] + value

        rms_back(gradient_of, x_own, gain_one, gain_acc.at[0], write)
        place = lax.broadcasted_iota(jnp.int32, (16, depth), 0)
        one = jnp.sum(gain_acc[0], axis=0, keepdims=True)
        two = jnp.sum(gain_acc[1], axis=0, keepdims=True)
        gain_all[0] = jnp.where(place == 0, one, jnp.where(place == 1, two, 0.0)).astype(BF)
        for j in peers:
            gain_send(j).start()

    def piece_outputs():
        locals_[1].wait()
        for j in peers:
            out_send(j).wait_recv()

        @pl.loop(0, rows // 16)
        def _(i):
            at = pl.ds(pl.multiple_of(i * 16, 16), 16)
            value = mixed[at, :] + first_out[at, :].astype(F32)
            for j in peers:
                value = value + landed_out[j - 1, at, :].astype(F32)
            outputs[at, :] = value

    def piece_gain():
        for j in peers:
            gain_send(j).wait_recv()

    def when(lags):
        give, pair, ahead, enter, middle, leave, keep = lags
        events = []
        for c in range(count):
            if c not in loaded:
                events.append((c + give, 0, stage_give, c))
            events.append((max(c - ahead, 0) if c in loaded else c + pair, 1, stage_pair, c))
            events.append((c + enter, 2, stage_in, c))
            events.append((c + middle, 3, stage_mid, c))
            events.append((c + leave, 4, stage_out, c))
            events.append((c + keep, 5, stage_keep, c))
        return events

    events = when((-2, -1, 3, 1, 2, 3, 4))
    order = {
        piece_mixed: 2, piece_do: 4, piece_kv_line: 8, piece_outputs: 8, piece_kv_sum: 9, piece_dh: 9,
        piece_input: 11, piece_gain: 12,
    }
    events += [(tick, 6 + n, piece, None) for n, (piece, tick) in enumerate(order.items())]
    attend_at = (4, 5, 6, 7)
    for j in range(plane):
        events.append((attend_at[j], 14 + j, piece_attend, j))
    events.append((attend_at[-1], 18, kv_pair.start, None))
    events.sort(key=lambda e: e[:2])

    for j in peers:
        back_send(j).start()
    for c in loaded:
        pair_copy(c).start()
    for c in loaded[:2]:
        load_copy(c).start()
    for copy in locals_:
        copy.start()
    for _, _, act, which in events:
        act() if which is None else act(which)

    for c in range(count):
        name, i = chunks[c]
        if c in loaded or i + kinds[name][1].shape[0] >= kinds[name][2].shape[0]:
            pair_copy(c).wait_send()
        if swapped(c):
            swap_copy(c).wait_send()
        keep_copy(c).wait()
        back_copy(c).wait_send()
        back_copy(c).wait_recv()

        @pl.when(outer)
        def _():
            in_copy(c).wait_send()

        @pl.when(inner)
        def _():
            mid_copy(c).wait_send()
            out_copy(c).wait_send()

    for j in peers:
        back_send(j).wait_send()
        out_send(j).wait_send()
        da_send(j).wait_send()
        dh_send(j).wait_send()
        gain_send(j).wait_send()
    kv_pair.wait_send()
    for s in range(1, line):

        @pl.when(z + s < line)
        def _():
            kv_send(s).wait_send()


def back_pass(
    limits, own, other, back_part, out_part, w_out, wqkv, h1, mixed, branch_own, x_own, gain_one, gain_two,
    attended, queries, lse, kv_all, kp, cosine, sine,
):
    count, line = lax.axis_size("fsdp"), lax.axis_size("z")
    rows, depth = mixed.shape
    total, half_depth = count * rows, depth // 2
    half = half_depth // count
    q_width = attended.shape[1]
    keys = kv_all.shape[0] * rows
    shapes = [x.shape for x in own] + [
        (2, q_width // 2, half_depth),
        (count, half, q_width + 128),
        (1, 16, depth),
    ]
    anywhere = pl.BlockSpec(memory_space=pl.ANY)
    local = pl.BlockSpec(memory_space=pltpu.VMEM)
    ends = [jax.ShapeDtypeStruct(s, BF) for s in shapes]
    act = jax.ShapeDtypeStruct((rows, depth), F32)
    block = (rows, depth)
    chunk_count = sum(s[0] for s in shapes)
    dma = lambda n: pltpu.SemaphoreType.DMA((n,))
    scratch = (
        [pltpu.VMEM(s, BF) for s in shapes]
        + [pltpu.VMEM(shapes[i], BF) for i in (1, 2, 4)]
        + [pltpu.VMEM(s, BF) for s in shapes]
        + [pltpu.VMEM((2,) + shapes[i][1:], BF) for i in (0, 1, 3, 4)]
        + [pltpu.VMEM(shapes[5], BF)]
        + [
            pltpu.VMEM((count - 1,) + block, BF),
            pltpu.VMEM((count - 1,) + block, BF),
            pltpu.VMEM(block, BF),
            pltpu.VMEM(block, BF),
            pltpu.VMEM((count,) + block, BF),
            pltpu.VMEM((max(total, q_width), depth), BF),
            pltpu.VMEM((count, rows, q_width), BF),
            pltpu.VMEM((total, q_width + 128), BF),
            pltpu.VMEM(wqkv.shape, BF),
            pltpu.VMEM(h1.shape, BF),
            pltpu.VMEM((keys, 128), BF),
            pltpu.VMEM((keys, 128), F32),
            pltpu.VMEM((keys, 128), F32),
            pltpu.VMEM(kv_all.shape, BF),
            pltpu.VMEM((line,) + kv_all.shape[1:], BF),
            pltpu.VMEM((line,) + kv_all.shape[1:], BF),
            pltpu.VMEM((line - 1,) + kv_all.shape[1:], BF),
            pltpu.VMEM((2, 16, depth), F32),
            pltpu.VMEM((count, 16, depth), BF),
        ]
        + [dma(chunk_count)] * 13
        + [pltpu.SemaphoreType.REGULAR, dma(5)]
        + [dma(count - 1)] * 8
        + [dma(1)] * 2
        + [dma(line - 1)] * 2
        + [dma(count - 1)] * 2
    )
    out = pl.pallas_call(
        back_kernel,
        out_shape=ends + ends + [act, act],
        in_specs=[local] + [anywhere] * 11 + [local] * 12,
        out_specs=[anywhere] * 12 + [local] * 2,
        scratch_shapes=scratch,
        compiler_params=pltpu.CompilerParams(
            vmem_limit_bytes=62 * 1024 * 1024, has_side_effects=True
        ),
        cost_estimate=pl.CostEstimate(
            flops=10**11, bytes_accessed=10**9, transcendentals=10**7
        ),
        name="back_pass",
    )(
        limits, *own, *other, back_part, out_part, w_out, wqkv, h1, mixed, branch_own, x_own, gain_one, gain_two,
        attended, queries, lse, kv_all, kp, cosine, sine,
    )
    return out[:6], out[6:12], out[12], out[13]


def finish_kernel(
    own_down, own_gate, own_up, own_out, own_qkv, own_gain, sib_down, sib_gate, sib_up, sib_out, sib_qkv,
    down, gate, up, out, query, key, value, attn_gain, mlp_gain,
    low_rows, low_cols, high_rows, high_cols, kv, kv_high, gain_in, gain_high, load_s, store_s, side_s,
):
    f, k = lax.axis_index("fsdp"), lax.axis_index("core")
    plane = lax.axis_size("fsdp")
    half, ff = own_gate.shape[1], own_gate.shape[2]
    half_depth = own_down.shape[2]
    slab = 2 * half
    q_width = own_qkv.shape[2] - 128
    tasks = []
    for side, (d, o, g, u, q) in enumerate(
        ((own_down, own_out, own_gate, own_up, own_qkv), (sib_down, sib_out, sib_gate, sib_up, sib_qkv))
    ):
        rows_at = pl.ds(pl.multiple_of((k ^ side) * half, 8), half)
        cols_at = pl.ds(pl.multiple_of((k ^ side) * half_depth, 128), half_depth)
        for source, target in ((d, down), (o, out)):
            for i in range(source.shape[0]):
                size = source.shape[1]
                tasks.append((source.at[i], target.at[pl.ds(i * size, size), cols_at], 0))
        for source, target in ((g, gate), (u, up)):
            for j in range(plane):
                to = pl.ds(pl.multiple_of((f ^ j) * ff, 128), ff)
                tasks.append((source.at[j], target.at[rows_at, to], 1))
        for j in range(plane):
            to = pl.ds(pl.multiple_of((f ^ j) * q_width, 128), q_width)
            tasks.append((q.at[j, :, pl.ds(0, q_width)], query.at[rows_at, to], 1))
    slots = low_rows.shape[0]

    def window(buffer, n, shape):
        return buffer.at[n % slots, pl.ds(0, shape[0]), pl.ds(0, shape[1])]

    def load(n):
        source, _, kind = tasks[n]
        low = (low_rows, low_cols)[kind]
        return pltpu.make_async_copy(source, window(low, n, source.shape), load_s.at[n])

    def store(n):
        source, target, kind = tasks[n]
        high = (high_rows, high_cols)[kind]
        return pltpu.make_async_copy(window(high, n, source.shape), target, store_s.at[n])

    sides = [
        pltpu.make_async_copy(own_gain.at[0], gain_in, side_s.at[0]),
        pltpu.make_async_copy(own_qkv.at[:, :, pl.ds(q_width, 128)], kv.at[0], side_s.at[1]),
        pltpu.make_async_copy(sib_qkv.at[:, :, pl.ds(q_width, 128)], kv.at[1], side_s.at[2]),
    ]
    for n in range(slots):
        load(n).start()
    for copy in sides:
        copy.start()
    for n in range(len(tasks)):
        source, _, kind = tasks[n]
        shape = source.shape
        low, high = ((low_rows, high_rows), (low_cols, high_cols))[kind]
        load(n).wait()
        if n >= slots:
            store(n - slots).wait()

        @pl.loop(0, shape[0] // 16)
        def _(i):
            at = pl.ds(pl.multiple_of(i * 16, 16), 16)
            high[n % slots, at, 0 : shape[1]] = low[n % slots, at, 0 : shape[1]].astype(F32)

        store(n).start()
        if n + slots < len(tasks):
            load(n + slots).start()
    for copy in sides:
        copy.wait()
    mine = pl.ds(pl.multiple_of(f * slab, 128), slab)
    gain_high[...] = gain_in[...].astype(F32)
    attn_gain[...] = gain_high[0:1, mine]
    mlp_gain[...] = gain_high[1:2, mine]
    lane = lax.broadcasted_iota(jnp.int32, (half, 128), 1)
    for side in range(2):
        rows_at = pl.ds(pl.multiple_of((k ^ side) * half, 8), half)
        for pair in range(plane // 2):
            first = kv[side, f ^ (2 * pair)].astype(F32)
            second = kv[side, f ^ (2 * pair + 1)].astype(F32)
            at = slice(pair * 128, (pair + 1) * 128)
            key[rows_at, at] = jnp.where(lane < 64, first, pltpu.roll(second, 64, 1))
            value[rows_at, at] = jnp.where(lane < 64, pltpu.roll(first, 64, 1), second)
    for n in range(max(0, len(tasks) - slots), len(tasks)):
        store(n).wait()


def finish(owns, sibs):
    plane = lax.axis_size("fsdp")
    down, gate, _, out, qkv, gain = (x.shape for x in owns)
    depth = 2 * down[2]
    slab = 2 * gate[1]
    q_width = qkv[2] - 128
    sds = jax.ShapeDtypeStruct
    shapes = [
        (down[0] * down[1], depth), (slab, plane * gate[2]), (slab, plane * gate[2]), (out[0] * out[1], depth),
        (slab, plane * q_width), (slab, KV_HEADS * HEAD_DIM), (slab, KV_HEADS * HEAD_DIM), (1, slab), (1, slab),
    ]
    slots = 4
    tall = (slots, max(down[1], out[1]), down[2])
    wide = (slots, gate[1], max(gate[2], q_width))
    count = 2 * (down[0] + out[0] + 3 * plane)
    anywhere, local = pl.BlockSpec(memory_space=pl.ANY), pl.BlockSpec(memory_space=pltpu.VMEM)
    return pl.pallas_call(
        finish_kernel,
        out_shape=[sds(s, F32) for s in shapes],
        in_specs=[anywhere] * 11,
        out_specs=[anywhere] * 5 + [local] * 4,
        scratch_shapes=[
            pltpu.VMEM(tall, BF),
            pltpu.VMEM(wide, BF),
            pltpu.VMEM(tall, F32),
            pltpu.VMEM(wide, F32),
            pltpu.VMEM((2, plane, gate[1], 128), BF),
            pltpu.VMEM((16, 128), F32),
            pltpu.VMEM(gain[1:], BF),
            pltpu.VMEM(gain[1:], F32),
            pltpu.SemaphoreType.DMA((count,)),
            pltpu.SemaphoreType.DMA((count,)),
            pltpu.SemaphoreType.DMA((3,)),
        ],
        compiler_params=params(),
        name="finish",
    )(*owns, *sibs[:5])


def body(
    tokens, cotangent, lengths, attn_gain, w_query, w_key, w_value, w_out, mlp_gain, w_gate, w_up, w_down
):
    seqs, rows, depth = tokens.shape
    count = lax.axis_size("fsdp")
    k = lax.axis_index("core")
    slab = depth // count
    half, half_depth = slab // 2, depth // 2
    x_own = tokens.reshape(rows, depth)
    (
        h1, queries, lse, attended, mixed, n2, hidden, gate_back, up_back, back_part, out_part,
        gain_one, gain_two, limits, cosine, sine, kp, kv_all, branch, wqkv,
    ) = front_pass(
        x_own, cotangent.reshape(rows, depth), lengths, attn_gain, mlp_gain,
        w_query, w_key, w_value, w_out, w_gate, w_up, w_down,
    )
    flat = branch.reshape(count * rows, depth)
    own, other = [], []
    for terms, side in ((own, 0), (other, 1)):
        right = lax.dynamic_slice_in_dim(flat, (k ^ side) * half_depth, half_depth, 1)
        left = n2[:, side * half_depth : (side + 1) * half_depth]
        terms.append(tn(hidden, right).astype(BF).reshape(4, -1, half_depth))
        terms.append(tn(left, gate_back).astype(BF).reshape(count, half, -1))
        terms.append(tn(left, up_back).astype(BF).reshape(count, half, -1))
    owns, sibs, outputs, input_grad = back_pass(
        limits, own, other, back_part.reshape(count, rows, depth), out_part.reshape(count, rows, depth), w_out,
        wqkv, h1, mixed, branch[0], x_own, gain_one, gain_two, attended, queries, lse, kv_all, kp, cosine, sine,
    )

    down_grad, gate_grad, up_grad, out_grad, query_grad, key_grad, value_grad, gain_a, gain_m = finish(owns, sibs)
    return (
        outputs.reshape(seqs, rows, depth),
        input_grad.reshape(seqs, rows, depth),
        gain_a.reshape(slab),
        query_grad,
        key_grad,
        value_grad,
        out_grad,
        gain_m.reshape(slab),
        gate_grad,
        up_grad,
        down_grad,
    )


def solution(mesh):
    count, ctx = mesh.shape["fsdp"], mesh.shape["ctx"]
    split = Mesh(mesh.devices.reshape(count, ctx // 2, 2), ("fsdp", "z", "core"))
    act = P("fsdp", ("z", "core"), None)
    row, mat = P("fsdp"), P("fsdp", None)
    fast = count == 4 and count == KV_HEADS and ctx == 8
    return jax.shard_map(
        body if fast else body_plain,
        mesh=split,
        in_specs=(act, act, row, row, mat, mat, mat, mat, row, mat, mat, mat),
        out_specs=(act, act, row, mat, mat, mat, mat, row, mat, mat, mat),
        check_vma=False,
    )
```

```python
import functools

import jax
import jax.numpy as jnp
import numpy as np
from jax import lax
from jax.experimental import pallas as pl
from jax.experimental.pallas import tpu as pltpu
from jax.sharding import Mesh
from jax.sharding import PartitionSpec as P

HEADS = 32
KV_HEADS = 4
HEAD_DIM = 64
EPSILON = 1e-05
ROPE_BASE = 10000.0
MASKED = -1e30
FAR = 1 << 30
BF = jnp.bfloat16
F32 = jnp.float32
VMEM_BYTES = 56 * 1024 * 1024
LAGS = (-4, -3, -4, 0, 2, 4, 6)
STEPS = (5, 9, 16, 16, 19, 19, 24, 26)
ATTEND = (10, 13)


def params(**kw):
    return pltpu.CompilerParams(vmem_limit_bytes=VMEM_BYTES, **kw)


def along_plane(value, step):
    count = lax.axis_size("fsdp")
    return lax.ppermute(value, "fsdp", [(i, i ^ step) for i in range(count)])


def to_sibling(value):
    return lax.ppermute(value, "core", [(0, 1), (1, 0)])


def along_line(value, shift):
    count = lax.axis_size("z")
    return lax.ppermute(
        value, "z", [(i, i + shift) for i in range(count) if 0 <= i + shift < count]
    )


def plane_bits():
    count = lax.axis_size("fsdp")
    return [1 << b for b in range(count.bit_length() - 1)]


def plane_gather(block):
    half = block.shape[0] // 2
    parts = []
    for which, bits in ((0, plane_bits()), (1, plane_bits()[::-1])):
        held = {0: block[which * half : (which + 1) * half]}
        for bit in bits:
            order = sorted(held)
            got = along_plane(jnp.stack([held[j] for j in order]), bit)
            for n, j in enumerate(order):
                held[j ^ bit] = got[n]
        parts.append(held)
    return [jnp.concatenate([parts[0][j], parts[1][j]]) for j in range(lax.axis_size("fsdp"))]


def plane_reduce(partial):
    half = partial.shape[1] // 2
    done = []
    for which, bits in ((0, plane_bits()[::-1]), (1, plane_bits())):
        held = {j: partial[j, which * half : (which + 1) * half] for j in range(partial.shape[0])}
        for bit in bits:
            going = [j for j in sorted(held) if j & bit]
            got = along_plane(jnp.stack([held[j].astype(BF) for j in going]), bit)
            for n, j in enumerate(going):
                held[j ^ bit] = held[j ^ bit].astype(F32) + got[n].astype(F32)
                del held[j]
        done.append(held[0])
    return jnp.concatenate(done)


def line_sum(value):
    count = lax.axis_size("z")
    place = lax.axis_index("z")
    half = count // 2
    for i in range(half - 1):
        got = lax.ppermute(value, "z", [(i, i + 1), (count - 1 - i, count - 2 - i)])
        value = value + got
    value = value + lax.ppermute(value, "z", [(half - 1, half), (half, half - 1)])
    for i in range(half - 2, -1, -1):
        got = lax.ppermute(value, "z", [(i + 1, i), (count - 2 - i, count - 1 - i)])
        outer = (place == i) | (place == count - 1 - i)
        value = jnp.where(outer, got, value)
    return value


def move_kernel(idx_ref, x_ref, o_ref):
    o_ref[...] = x_ref[...]


def pick_columns(x, index, count):
    rows, width = x.shape
    size = width // count
    spec = pltpu.PrefetchScalarGridSpec(
        num_scalar_prefetch=1,
        grid=(count,),
        in_specs=[pl.BlockSpec((rows, size), lambda b, idx: (0, idx[b]))],
        out_specs=pl.BlockSpec((rows, size), lambda b, idx: (0, b)),
    )
    return pl.pallas_call(
        move_kernel,
        grid_spec=spec,
        out_shape=jax.ShapeDtypeStruct(x.shape, x.dtype),
        compiler_params=params(),
        name="pick_columns",
    )(index, x)


def put_columns(x, index, count):
    rows, width = x.shape
    size = width // count
    spec = pltpu.PrefetchScalarGridSpec(
        num_scalar_prefetch=1,
        grid=(count,),
        in_specs=[pl.BlockSpec((rows, size), lambda b, idx: (0, b))],
        out_specs=pl.BlockSpec((rows, size), lambda b, idx: (0, idx[b])),
    )
    return pl.pallas_call(
        move_kernel,
        grid_spec=spec,
        out_shape=jax.ShapeDtypeStruct(x.shape, x.dtype),
        compiler_params=params(),
        name="put_columns",
    )(index, x)


def cut_blocks(weight, f, k, count, dtype=BF):
    rows, full = weight.shape
    width, half = full // count, rows // 2
    if width % 128:
        own = lax.dynamic_slice_in_dim(weight, k * half, half, 0).reshape(half, count, width)
        return jnp.stack(
            [lax.dynamic_index_in_dim(own, f ^ j, 1, keepdims=False) for j in range(count)]
        )
    spec = pltpu.PrefetchScalarGridSpec(
        num_scalar_prefetch=1,
        grid=(count,),
        in_specs=[pl.BlockSpec((half, width), lambda j, at: (at[1], at[0] ^ j))],
        out_specs=pl.BlockSpec((None, half, width), lambda j, at: (j, 0, 0)),
    )
    return pl.pallas_call(
        move_kernel,
        grid_spec=spec,
        out_shape=jax.ShapeDtypeStruct((count, half, width), weight.dtype),
        compiler_params=params(),
        name="cut_blocks",
    )(jnp.stack([f, k]), weight)


def join_kernel(at_ref, own_ref, sib_ref, o_ref):
    @pl.when(pl.program_id(0) == 0)
    def _():
        o_ref[...] = own_ref[...].astype(o_ref.dtype)

    @pl.when(pl.program_id(0) == 1)
    def _():
        o_ref[...] = sib_ref[...].astype(o_ref.dtype)


def join_rows(own, sib, f, k):
    count, half, width = own.shape
    if width % 128:
        halves = jnp.stack([own, sib])
        return jnp.concatenate(
            [
                jnp.concatenate(
                    [
                        lax.dynamic_index_in_dim(
                            lax.dynamic_index_in_dim(halves, k ^ h, 0, keepdims=False),
                            f ^ i,
                            0,
                            keepdims=False,
                        )
                        for i in range(count)
                    ],
                    axis=1,
                )
                for h in range(2)
            ],
            axis=0,
        ).astype(F32)
    spec = pltpu.PrefetchScalarGridSpec(
        num_scalar_prefetch=1,
        grid=(2, count),
        in_specs=[
            pl.BlockSpec(
                (None, half, width),
                lambda s, i, at: (at[0] ^ jnp.where(s == 0, i, count - 1), 0, 0),
            ),
            pl.BlockSpec(
                (None, half, width), lambda s, i, at: (at[0] ^ jnp.where(s == 1, i, 0), 0, 0)
            ),
        ],
        out_specs=pl.BlockSpec((half, width), lambda s, i, at: (at[1] ^ s, i)),
    )
    return pl.pallas_call(
        join_kernel,
        grid_spec=spec,
        out_shape=jax.ShapeDtypeStruct((2 * half, count * width), F32),
        compiler_params=params(),
        name="join_rows",
    )(jnp.stack([f, k]), own, sib)


def join_columns(own, sib, k):
    rows, half = own.shape
    count = 4
    size = rows // count
    spec = pltpu.PrefetchScalarGridSpec(
        num_scalar_prefetch=1,
        grid=(2, count),
        in_specs=[
            pl.BlockSpec((size, half), lambda s, i, at: (jnp.where(s == 0, i, count - 1), 0)),
            pl.BlockSpec((size, half), lambda s, i, at: (jnp.where(s == 1, i, 0), 0)),
        ],
        out_specs=pl.BlockSpec((size, half), lambda s, i, at: (i, at[0] ^ s)),
    )
    return pl.pallas_call(
        join_kernel,
        grid_spec=spec,
        out_shape=jax.ShapeDtypeStruct((rows, 2 * half), F32),
        compiler_params=params(),
        name="join_columns",
    )(k.reshape(1), own, sib)


def swap_halves(block):
    lane = lax.broadcasted_iota(jnp.int32, block.shape, 1)
    return jnp.where(lane % 64 < 32, pltpu.roll(block, 96, 1), pltpu.roll(block, 32, 1))


def qkv_kernel(idx_ref, x_ref, gain_ref, w_ref, cos_ref, sin_ref, h_ref, q_ref, kv_ref):
    blocks = idx_ref.shape[0]
    size = x_ref.shape[1] // blocks
    x = x_ref[...].astype(F32)
    inverse = lax.rsqrt(jnp.mean(x * x, axis=1, keepdims=True) + EPSILON)
    for b in range(blocks):
        at = pl.ds(pl.multiple_of(idx_ref[b] * size, 128), size)
        part = x_ref[:, at].astype(F32) * inverse * gain_ref[:, at]
        h_ref[:, b * size : (b + 1) * size] = part.astype(BF)
    out = jnp.dot(h_ref[...], w_ref[...], preferred_element_type=F32)
    cosine, sine = cos_ref[...], sin_ref[...]
    pairs = q_ref.shape[1] // 128
    for c in range(pairs):
        block = out[:, c * 128 : (c + 1) * 128]
        q_ref[:, c * 128 : (c + 1) * 128] = (block * cosine + swap_halves(block) * sine).astype(BF)
    block = out[:, pairs * 128 :]
    lane = lax.broadcasted_iota(jnp.int32, block.shape, 1)
    turned = block * cosine + swap_halves(block) * sine
    kv_ref[...] = jnp.where(lane < 64, turned, block).astype(BF)


def qkv_project(idx, x, gain, weight, cosine, sine, rows):
    total, depth = x.shape
    width = weight.shape[1]
    spec = pltpu.PrefetchScalarGridSpec(
        num_scalar_prefetch=1,
        grid=(total // rows,),
        in_specs=[
            pl.BlockSpec((rows, depth), lambda i, idx: (i, 0)),
            pl.BlockSpec((1, depth), lambda i, idx: (0, 0)),
            pl.BlockSpec((depth, width), lambda i, idx: (0, 0)),
            pl.BlockSpec((rows, 128), lambda i, idx: (0, 0)),
            pl.BlockSpec((rows, 128), lambda i, idx: (0, 0)),
        ],
        out_specs=[
            pl.BlockSpec((rows, depth), lambda i, idx: (i, 0)),
            pl.BlockSpec((rows, width - 128), lambda i, idx: (i, 0)),
            pl.BlockSpec((rows, 128), lambda i, idx: (i, 0)),
        ],
    )
    return pl.pallas_call(
        qkv_kernel,
        grid_spec=spec,
        out_shape=[
            jax.ShapeDtypeStruct((total, depth), BF),
            jax.ShapeDtypeStruct((total, width - 128), BF),
            jax.ShapeDtypeStruct((total, 128), BF),
        ],
        compiler_params=params(),
        cost_estimate=pl.CostEstimate(
            flops=2 * total * depth * width,
            bytes_accessed=4 * total * depth + 2 * depth * width + 2 * total * width,
            transcendentals=0,
        ),
        name="qkv_project",
    )(idx, x, gain, weight, cosine, sine)


def nt(a, b):
    return lax.dot_general(a, b, (((1,), (1,)), ((), ())), preferred_element_type=F32)


def tn(a, b):
    return lax.dot_general(a, b, (((0,), (0,)), ((), ())), preferred_element_type=F32)


def nn(a, b):
    return jnp.dot(a, b, preferred_element_type=F32)


def limits(at_ref, rows):
    j = pl.program_id(0)
    place = at_ref[0] - lax.broadcasted_iota(jnp.int32, (rows, 1), 0)
    return jnp.minimum(place, at_ref[1 + j] - 1)


def attend_kernel(at_ref, q_ref, kv_ref, kp_ref, o_ref, lse_ref, vk_ref):
    rows = q_ref.shape[0]
    keys = vk_ref.shape[0]
    kv = kv_ref[...].reshape(keys, 128)

    @pl.when(pl.program_id(1) == 0)
    def _():
        vk_ref[...] = pltpu.roll(kv.astype(F32), 64, 1).astype(BF)

    vk = vk_ref[...]
    allowed = kp_ref[...] <= limits(at_ref, rows)
    lane = lax.broadcasted_iota(jnp.int32, (rows, 128), 1)
    q = q_ref[...]
    zero = jnp.zeros_like(q)
    outs, logs = [], []
    for first in (True, False):
        mine = lane < 64 if first else lane >= 64
        scores = nt(jnp.where(mine, q, zero), kv if first else vk) * (HEAD_DIM**-0.5)
        scores = jnp.where(allowed, scores, MASKED)
        top = jnp.max(scores, axis=1, keepdims=True)
        weights = jnp.exp(scores - top)
        total = jnp.sum(weights, axis=1, keepdims=True)
        outs.append(nn(weights.astype(BF), vk if first else kv) / total)
        logs.append(jnp.broadcast_to(top + jnp.log(total), (rows, 128)))
    o_ref[...] = jnp.where(lane < 64, outs[0], outs[1]).astype(BF)
    lse_ref[...] = jnp.where(lane < 64, logs[0], logs[1])


def attend(at, q, kv, kp):
    chunks, seqs, rows, _ = kv.shape
    pairs = q.shape[2] // 128
    keys = chunks * rows
    spec = pltpu.PrefetchScalarGridSpec(
        num_scalar_prefetch=1,
        grid=(seqs, pairs),
        in_specs=[
            pl.BlockSpec((None, rows, 128), lambda j, p, at: (j, 0, p)),
            pl.BlockSpec((chunks, None, rows, 128), lambda j, p, at: (0, j, 0, 0)),
            pl.BlockSpec((1, keys), lambda j, p, at: (0, 0)),
        ],
        out_specs=[
            pl.BlockSpec((None, rows, 128), lambda j, p, at: (j, 0, p)),
            pl.BlockSpec((None, rows, 128), lambda j, p, at: (j, 0, p)),
        ],
        scratch_shapes=[pltpu.VMEM((keys, 128), BF)],
    )
    size = seqs * pairs * 2 * rows * keys
    return pl.pallas_call(
        attend_kernel,
        grid_spec=spec,
        out_shape=[
            jax.ShapeDtypeStruct(q.shape, BF),
            jax.ShapeDtypeStruct(q.shape, F32),
        ],
        compiler_params=params(),
        cost_estimate=pl.CostEstimate(
            flops=size * 4 * 128, bytes_accessed=4 << 20, transcendentals=size
        ),
        name="attend",
    )(at, q, kv, kp)


def attend_back_kernel(
    at_ref, q_ref, do_ref, lse_ref, kv_ref, kp_ref, cos_ref, sin_ref, dq_ref, dkv_ref, vk_ref, dk_ref, dv_ref
):
    rows = q_ref.shape[0]
    keys = vk_ref.shape[0]
    pair = pl.program_id(1)
    kv = kv_ref[...].reshape(keys, 128)

    @pl.when(pair == 0)
    def _():
        vk_ref[...] = pltpu.roll(kv.astype(F32), 64, 1).astype(BF)
        dk_ref[...] = jnp.zeros_like(dk_ref)
        dv_ref[...] = jnp.zeros_like(dv_ref)

    vk = vk_ref[...]
    allowed = kp_ref[...] <= limits(at_ref, rows)
    lane = lax.broadcasted_iota(jnp.int32, (rows, 128), 1)
    q, do = q_ref[...], do_ref[...]
    zero = jnp.zeros_like(q)
    parts = []
    for first in (True, False):
        mine = lane < 64 if first else lane >= 64
        keyed, valued = (kv, vk) if first else (vk, kv)
        q_own, do_own = jnp.where(mine, q, zero), jnp.where(mine, do, zero)
        scores = nt(q_own, keyed) * (HEAD_DIM**-0.5)
        log_total = lse_ref[:, 0:1] if first else lse_ref[:, 64:65]
        weights = jnp.where(allowed, jnp.exp(scores - log_total), 0.0)
        joint = weights * nt(do_own, valued)
        back = (joint - weights * jnp.sum(joint, axis=1, keepdims=True)).astype(BF)
        parts.append(nn(back, keyed))
        dk_ref[...] += tn(back, q_own)
        dv_ref[...] += tn(weights.astype(BF), do_own)
    turned = jnp.where(lane < 64, parts[0], parts[1]) * (HEAD_DIM**-0.5)
    dq_ref[...] = (turned * cos_ref[...] - swap_halves(turned) * sin_ref[...]).astype(BF)

    @pl.when(pair == pl.num_programs(1) - 1)
    def _():
        dk = dk_ref[...]
        dv = dv_ref[...]
        dk = (dk + pltpu.roll(dk, 64, 1)) * (HEAD_DIM**-0.5)
        dv = dv + pltpu.roll(dv, 64, 1)
        wide = lax.broadcasted_iota(jnp.int32, dk.shape, 1)
        dkv_ref[...] = jnp.where(wide < 64, dk, dv).astype(BF).reshape(dkv_ref.shape)


def attend_back(at, q, do, lse, kv, kp, cosine, sine):
    chunks, seqs, rows, _ = kv.shape
    pairs = q.shape[2] // 128
    keys = chunks * rows
    tall = pl.BlockSpec((None, rows, 128), lambda j, p, at: (j, 0, p))
    whole = pl.BlockSpec((chunks, None, rows, 128), lambda j, p, at: (0, j, 0, 0))
    flat = pl.BlockSpec((rows, 128), lambda j, p, at: (0, 0))
    spec = pltpu.PrefetchScalarGridSpec(
        num_scalar_prefetch=1,
        grid=(seqs, pairs),
        in_specs=[tall, tall, tall, whole, pl.BlockSpec((1, keys), lambda j, p, at: (0, 0)), flat, flat],
        out_specs=[tall, whole],
        scratch_shapes=[
            pltpu.VMEM((keys, 128), BF),
            pltpu.VMEM((keys, 128), F32),
            pltpu.VMEM((keys, 128), F32),
        ],
    )
    size = seqs * pairs * 2 * rows * keys
    return pl.pallas_call(
        attend_back_kernel,
        grid_spec=spec,
        out_shape=[
            jax.ShapeDtypeStruct(q.shape, BF),
            jax.ShapeDtypeStruct(kv.shape, BF),
        ],
        compiler_params=params(),
        cost_estimate=pl.CostEstimate(
            flops=size * 10 * 128, bytes_accessed=8 << 20, transcendentals=size
        ),
        name="attend_back",
    )(at, q, do, lse, kv, kp, cosine, sine)


def rms_backward(row_block, inverse, gain_vec, gradient):
    normed = row_block * inverse
    gain_grad = jnp.sum(gradient * normed, axis=0)
    scaled = gradient * gain_vec
    back = inverse * (scaled - normed * jnp.mean(scaled * normed, axis=1, keepdims=True))
    return (back, gain_grad)


def body_plain(
    tokens, cotangent, lengths, attn_gain, w_query, w_key, w_value, w_out, mlp_gain, w_gate, w_up, w_down
):
    seqs, rows, depth = tokens.shape
    count, line = lax.axis_size("fsdp"), lax.axis_size("z")
    f, z, k = lax.axis_index("fsdp"), lax.axis_index("z"), lax.axis_index("core")
    slot = rows * line * 2
    total = count * rows
    slab = depth // count
    half = slab // 2
    q_width = HEADS * HEAD_DIM // count
    shared = max(1, count // KV_HEADS)

    x_own = tokens.reshape(rows, depth)
    chunk = 2 * z + k
    first_pos = slot - 1 - chunk * rows

    length = lengths[0]
    words = jnp.zeros((slab,), F32).at[0].set((length // 64).astype(F32)).at[1].set((length % 64).astype(F32))
    note = jnp.stack([attn_gain, mlp_gain, words.astype(BF), jnp.zeros((slab,), BF)])
    notes = [note] + [along_plane(note, j) for j in range(1, count)]
    notes_abs = [lax.dynamic_index_in_dim(jnp.stack(notes), f ^ i, 0, keepdims=False) for i in range(count)]
    gain_one = jnp.concatenate([n[0] for n in notes_abs]).astype(F32).reshape(1, depth)
    gain_two = jnp.concatenate([n[1] for n in notes_abs]).astype(F32).reshape(1, depth)
    all_lengths = jnp.stack(
        [n[2, 0].astype(jnp.int32) * 64 + n[2, 1].astype(jnp.int32) for n in notes]
    )

    x_all = jnp.concatenate(plane_gather(x_own))

    wq = cut_blocks(w_query, f, k, count)
    key_cols = lax.dynamic_slice_in_dim(w_key, k * half, half, 0).reshape(half, KV_HEADS, HEAD_DIM)
    value_cols = lax.dynamic_slice_in_dim(w_value, k * half, half, 0).reshape(half, KV_HEADS, HEAD_DIM)

    def head_of(j):
        return (f ^ j) // shared

    wkv = jnp.stack(
        [
            jnp.concatenate(
                [
                    lax.dynamic_index_in_dim(key_cols, head_of(j), 1, keepdims=False),
                    lax.dynamic_index_in_dim(value_cols, head_of(j), 1, keepdims=False),
                ],
                axis=1,
            )
            for j in range(count)
        ]
    )
    wqkv = jnp.concatenate([wq, wkv], axis=2)
    wqkv_own = jnp.stack([wqkv[0]] + [along_plane(wqkv[j], j) for j in range(1, count)])
    wqkv_sib = to_sibling(wqkv_own)
    wqkv_all = jnp.concatenate([wqkv_own, wqkv_sib]).reshape(depth, q_width + 128)

    def fetch(weight):
        cut = cut_blocks(weight, f, k, count)
        width = cut.shape[2]
        own = jnp.stack([cut[0]] + [along_plane(cut[j], j) for j in range(1, count)])
        sib = to_sibling(own)
        return own.reshape(depth // 2, width), sib.reshape(depth // 2, width)

    gate_own, gate_sib = fetch(w_gate)
    up_own, up_sib = fetch(w_up)

    order = jnp.stack([(f ^ j) * 2 + (k ^ h) for h in range(2) for j in range(count)]).astype(jnp.int32)

    half_dim = HEAD_DIM // 2
    frequency = jnp.power(ROPE_BASE, jnp.arange(half_dim, dtype=F32) * (-2.0 / HEAD_DIM))
    positions = first_pos - jnp.arange(rows, dtype=jnp.int32)
    angles = positions.astype(F32)[:, None] * frequency[None, :]
    cos32, sin32 = jnp.cos(angles), jnp.sin(angles)
    cosine = jnp.concatenate([cos32] * 4, axis=1)
    sine = jnp.concatenate([-sin32, sin32, -sin32, sin32], axis=1)

    normed_one, queries, kv = qkv_project(order, x_all, gain_one, wqkv_all, cosine, sine, rows)
    queries = queries.reshape(count, rows, q_width)
    kv = kv.reshape(count, rows, 128)

    mine = [kv] + [along_line(kv, -s) for s in range(1, line)]
    mine = jnp.stack(mine)
    kv_all = jnp.concatenate([mine, to_sibling(mine)])
    places = []
    for h in range(2):
        for s in range(line):
            start = slot - 1 - (2 * (z + s) + (k ^ h)) * rows
            places.append(start - jnp.arange(rows, dtype=jnp.int32))
    kp = jnp.concatenate(places)
    kp = jnp.where(kp < 0, FAR, kp).reshape(1, -1)
    at = jnp.concatenate([first_pos.reshape(1), all_lengths]).astype(jnp.int32)

    attended, log_total = attend(at, queries, kv_all, kp)
    attended = attended.reshape(total, q_width)

    mixed_part = nn(attended, w_out).astype(BF).reshape(count, rows, depth)
    inputs = x_own.astype(F32)
    mixed = inputs + plane_reduce(mixed_part)
    inv_two = lax.rsqrt(jnp.mean(mixed * mixed, axis=1, keepdims=True) + EPSILON)
    normed_two_own = (mixed * inv_two * gain_two).astype(BF)
    normed_two = jnp.concatenate(plane_gather(normed_two_own))
    normed_two = pick_columns(normed_two, order, 2 * count)
    n2_own, n2_sib = normed_two[:, : depth // 2], normed_two[:, depth // 2 :]

    valid = (positions < length).astype(F32)[:, None]
    out_back = cotangent.reshape(rows, depth).astype(F32) * valid
    branch_own = out_back.astype(BF)
    branch = jnp.concatenate(plane_gather(branch_own))

    gate = nn(n2_own, gate_own) + nn(n2_sib, gate_sib)
    up = nn(n2_own, up_own) + nn(n2_sib, up_sib)
    sigmoid = jax.nn.sigmoid(gate)
    hidden = (gate * sigmoid * up).astype(BF)

    half_depth = depth // 2
    branch_mine = lax.dynamic_slice_in_dim(branch, k * half_depth, half_depth, 1)
    branch_other = lax.dynamic_slice_in_dim(branch, (1 - k) * half_depth, half_depth, 1)

    def pair_sum(own, other):
        return (own + to_sibling(other.astype(BF)).astype(F32)).astype(BF)

    def swap_slabs(own):
        return jnp.stack([own[0]] + [along_plane(own[j], j) for j in range(1, count)])

    down_half = line_sum(pair_sum(tn(hidden, branch_mine), tn(hidden, branch_other)))
    down_grad = join_columns(down_half, to_sibling(down_half), k)

    hidden_grad = nt(branch, w_down)
    gate_back = (hidden_grad * up * sigmoid * (1.0 + gate * (1.0 - sigmoid))).astype(BF)
    up_back = (hidden_grad * gate * sigmoid).astype(BF)

    def slab_grad(left_own, left_other, right):
        width = right.shape[1]
        own = pair_sum(tn(left_own, right), tn(left_other, right)).reshape(count, half, width)
        return line_sum(swap_slabs(own))

    gate_half = slab_grad(n2_own, n2_sib, gate_back)
    gate_grad = join_rows(gate_half, to_sibling(gate_half), f, k)
    up_half = slab_grad(n2_own, n2_sib, up_back)
    up_grad = join_rows(up_half, to_sibling(up_half), f, k)

    back_own = (nt(gate_back, gate_own) + nt(up_back, up_own)).astype(BF)
    back_sib = (nt(gate_back, gate_sib) + nt(up_back, up_sib)).astype(BF)
    normed_back = put_columns(jnp.concatenate([back_own, back_sib], axis=1), order, 2 * count)
    normed_back = plane_reduce(normed_back.reshape(count, rows, depth))

    out_part = nn(hidden, w_down).astype(BF).reshape(count, rows, depth)
    outputs = mixed + plane_reduce(out_part)

    mixed_back, gain_two_grad = rms_backward(mixed, inv_two, gain_two, normed_back)
    mixed_grad = out_back + mixed_back
    attn_back = jnp.concatenate(plane_gather(mixed_grad.astype(BF)))
    attended_grad = nt(attn_back, w_out).astype(BF).reshape(count, rows, q_width)

    back_mine = lax.dynamic_slice_in_dim(attn_back, k * half_depth, half_depth, 1)
    back_other = lax.dynamic_slice_in_dim(attn_back, (1 - k) * half_depth, half_depth, 1)
    out_half = line_sum(pair_sum(tn(attended, back_mine), tn(attended, back_other)))
    out_grad = join_columns(out_half, to_sibling(out_half), k)

    query_back, kv_part = attend_back(at, queries, attended_grad, log_total, kv_all, kp, cosine, sine)
    kv_mine = kv_part[:line].astype(F32) + to_sibling(kv_part[line:]).astype(F32)
    kv_back = kv_mine[0]
    for s in range(1, line):
        kv_back = kv_back + along_line(kv_mine[s].astype(BF), s).astype(F32)
    lead, trail, flat = kv_back[..., :32], kv_back[..., 32:64], kv_back[..., 64:]
    kv_back = jnp.concatenate(
        [lead * cos32 + trail * sin32, trail * cos32 - lead * sin32, flat], axis=-1
    ).astype(BF)
    qkv_back = jnp.concatenate(
        [query_back.reshape(total, q_width), kv_back.reshape(total, 128)], axis=1
    )

    normed_one_back = nt(qkv_back, wqkv_all).astype(BF)
    normed_one_back = put_columns(normed_one_back, order, 2 * count)
    normed_one_back = plane_reduce(normed_one_back.reshape(count, rows, depth))
    inv_one = lax.rsqrt(jnp.mean(inputs * inputs, axis=1, keepdims=True) + EPSILON)
    input_back, gain_one_grad = rms_backward(inputs, inv_one, gain_one, normed_one_back)
    input_grad = mixed_grad + input_back

    n1_own, n1_sib = normed_one[:, :half_depth], normed_one[:, half_depth:]
    qkv_own = pair_sum(tn(n1_own, qkv_back), tn(n1_sib, qkv_back)).reshape(count, half, q_width + 128)
    gains = jnp.stack([gain_one_grad, gain_two_grad]).reshape(2, count, slab)
    gains = jnp.stack(
        [lax.dynamic_index_in_dim(gains, f ^ j, 1, keepdims=False) for j in range(count)]
    ).astype(BF)
    gains = line_sum(swap_slabs(gains))
    qkv_half = line_sum(swap_slabs(qkv_own))
    gains = jnp.sum(gains.astype(F32), axis=0) + jnp.sum(to_sibling(gains).astype(F32), axis=0)
    qkv_other = to_sibling(qkv_half)
    query_grad = join_rows(qkv_half[:, :, :q_width], qkv_other[:, :, :q_width], f, k)
    halves = jnp.stack([qkv_half[:, :, q_width:], qkv_other[:, :, q_width:]])

    def by_head(lo, hi):
        both = [lax.dynamic_index_in_dim(halves, k ^ h, 0, keepdims=False) for h in range(2)]
        both = jnp.concatenate(both, axis=1).astype(F32)[:, :, lo:hi]
        cols = jnp.stack([lax.dynamic_index_in_dim(both, f ^ i, 0, keepdims=False) for i in range(count)])
        cols = cols.reshape(KV_HEADS, shared, slab, HEAD_DIM).sum(1)
        return jnp.transpose(cols, (1, 0, 2)).reshape(slab, KV_HEADS * HEAD_DIM)

    key_grad = by_head(0, 64)
    value_grad = by_head(64, 128)

    return (
        outputs.reshape(seqs, rows, depth),
        input_grad.reshape(seqs, rows, depth),
        gains[0],
        query_grad,
        key_grad,
        value_grad,
        out_grad,
        gains[1],
        gate_grad,
        up_grad,
        down_grad,
    )


def rotary_parts(slot, rows):
    lane = np.arange(128) % (HEAD_DIM // 2)
    frequency = ROPE_BASE ** (lane * (-2.0 / HEAD_DIM))
    starts = (slot - 1 - rows * np.arange(slot // rows))[:, None] * frequency[None, :]
    steps = np.arange(rows)[:, None] * frequency[None, :]
    return [jnp.asarray(t(a), F32) for a in (starts, steps) for t in (np.cos, np.sin)]


def front_kernel(
    length_ref, attn_gain, mlp_gain, start_cos, start_sin, step_cos, step_sin,
    tokens, cotangent, w_query, w_key, w_value, w_out, w_gate, w_up, w_down,
    h1_out, queries_out, lse_out, attended_out, mixed_out, n2_out, limits_out, cosine_out, sine_out, kp_out,
    gain_one_out, gain_two_out, kv_out, branch_out, wqkv_out, gate_back_out, up_back_out, back_out, out_out,
    own_down, other_down,
    h1, queries, lse, attended, mixed, n2, limits, cosine, sine, kp, gain_one, gain_two,
    hidden, gate_back, up_back, back_part, out_part, down_own, down_other,
    notes, x_all, wqkv, keys_in, values_in, kv_give, gate_own, gate_sib, up_own, up_sib, down,
    kv_all, vk, w_o, part, landed, relay, relayed, n2_all, branch_all, cot_in,
    local_s, store_s, note_s, note_r, tok_s, tok_r, tof_s, tof_r, wq_s, wq_r, wk_s, wk_r, wp_s, wp_r, wkp_s, wkp_r,
    kz_s, kz_r, kp_s, kp_r, gt_s, gt_r, up_s, up_r, gz_s, gz_r, gs_s, gs_r, us_s, us_r,
    bt_s, bt_r, btf_s, btf_r, mx_s, mx_r, nt_s, nt_r, ntf_s, ntf_r,
):
    f, z, k = lax.axis_index("fsdp"), lax.axis_index("z"), lax.axis_index("core")
    plane, line = 4, 4
    rows, depth = tokens.shape
    total = plane * rows
    slab = depth // plane
    half = slab // 2
    hr = rows // 2
    q_width = w_out.shape[0]
    pairs = q_width // 128
    ff = w_down.shape[0]
    keys = vk.shape[0]
    slot = rows * line * 2
    even = z % 2 == 0
    across = z + 1 - 2 * (z % 2)
    peers = (1, 2, 3)
    first_pos = slot - 1 - (2 * z + k) * rows

    def remote(source, target, send, recv, where):
        return pltpu.make_async_remote_copy(
            src_ref=source,
            dst_ref=target,
            send_sem=send,
            recv_sem=recv,
            device_id=where,
            device_id_type=pl.DeviceIdType.MESH,
        )

    sib = {"core": 1 - k}

    def chip(j):
        return {"fsdp": f ^ j}

    def cols(weight, j, side, width):
        start = pl.multiple_of((f ^ j) * width, 128)
        return weight.at[pl.ds(pl.multiple_of((k ^ side) * half, 16), half), pl.ds(start, width)]

    class Gather:
        def __init__(self, source, target, send, recv, fsend, frecv):
            self.near = {
                j: remote(source, target.at[j], send.at[j - 1], recv.at[j - 1], chip(j)) for j in (1, 2)
            }
            self.far = {
                j: remote(
                    target.at[j, pl.ds((j - 1) * hr, hr), :],
                    target.at[3, pl.ds((j - 1) * hr, hr), :],
                    fsend.at[j - 1],
                    frecv.at[j - 1],
                    chip(3 - j),
                )
                for j in (1, 2)
            }

        def start(self):
            for j in (1, 2):
                self.near[j].start()

        def forward(self):
            for j in (1, 2):
                self.near[j].wait_recv()
                self.far[j].start()

        def arrive(self):
            for j in (1, 2):
                self.far[j].wait_recv()

        def close(self):
            for j in (1, 2):
                self.near[j].wait_send()
                self.far[j].wait_send()

    def note_send(j):
        return remote(notes.at[0], notes.at[j], note_s.at[j - 1], note_r.at[j - 1], chip(j))

    token_gather = Gather(tokens, x_all, tok_s, tok_r, tof_s, tof_r)
    branch_gather = Gather(branch_all.at[0], branch_all, bt_s, bt_r, btf_s, btf_r)
    n2_gather = Gather(n2_all.at[0], n2_all, nt_s, nt_r, ntf_s, ntf_r)

    def wq_send(j):
        target = wqkv.at[pl.ds(j * half, half), pl.ds(0, q_width)]
        return remote(cols(w_query, j, 0, q_width), target, wq_s.at[j - 1], wq_r.at[j - 1], chip(j))

    def wk_send(j):
        target = wqkv.at[pl.ds(j * half, half), pl.ds(q_width, 128)]
        return remote(kv_give.at[j], target, wk_s.at[j - 1], wk_r.at[j - 1], chip(j))

    def wp_send(j):
        source = wqkv.at[pl.ds(j * half, half), :]
        target = wqkv.at[pl.ds((plane + j) * half, half), :]
        return remote(source, target, wp_s.at[j - 1], wp_r.at[j - 1], sib)

    def kv_send(s):
        return remote(kv_all.at[0], kv_all.at[s], kz_s.at[s - 1], kz_r.at[s - 1], {"z": z - s})

    def kv_pair(s):
        return remote(kv_all.at[s], kv_all.at[line + s], kp_s.at[s], kp_r.at[s], sib)

    def gate_send(j):
        return remote(cols(w_gate, j, 0, ff), gate_own.at[j], gt_s.at[j - 1], gt_r.at[j - 1], chip(j))

    def up_send(j):
        return remote(cols(w_up, j, 0, ff), up_own.at[j], up_s.at[j - 1], up_r.at[j - 1], chip(j))

    def gate_across(j):
        return remote(gate_own.at[j], gate_own.at[j], gz_s.at[j - 1], gz_r.at[j - 1], {"z": across})

    def up_across(j):
        return remote(up_own.at[j], up_own.at[j], gz_s.at[j - 1], gz_r.at[j - 1], {"z": across})

    def by_parity(act_even, act_odd):
        @pl.when(even)
        def _():
            act_even()

        @pl.when(jnp.logical_not(even))
        def _():
            act_odd()

    def fetch_start():
        by_parity(
            lambda: [gate_send(j).start() for j in (3, 1, 2)], lambda: [up_send(j).start() for j in (3, 1, 2)]
        )

    def fetch_on(j):
        def gate_on():
            gate_send(j).wait_recv()
            gate_across(j).start()
            gate_pair(j).start()

        def up_on():
            up_send(j).wait_recv()
            up_across(j).start()
            up_pair(j).start()

        by_parity(gate_on, up_on)

    def cross_on(j):
        def up_on():
            up_across(j).wait_recv()
            up_pair(j).start()

        def gate_on():
            gate_across(j).wait_recv()
            gate_pair(j).start()

        by_parity(up_on, gate_on)

    def gate_pair(j):
        return remote(gate_own.at[j], gate_sib.at[j], gs_s.at[j - 1], gs_r.at[j - 1], sib)

    def up_pair(j):
        return remote(up_own.at[j], up_sib.at[j], us_s.at[j - 1], us_r.at[j - 1], sib)

    def span(which):
        return pl.ds(which * hr, hr)

    mix_first = {
        "one": remote(part.at[1, span(0), :], landed.at[0, span(0), :], mx_s.at[0], mx_r.at[0], chip(1)),
        "two": remote(part.at[2, span(1), :], landed.at[1, span(1), :], mx_s.at[1], mx_r.at[1], chip(2)),
        "far_one": remote(part.at[3, span(0), :], relay.at[0], mx_s.at[2], mx_r.at[2], chip(1)),
        "far_two": remote(part.at[3, span(1), :], relay.at[1], mx_s.at[3], mx_r.at[3], chip(2)),
        "late_two": remote(relayed.at[0], landed.at[1, span(0), :], mx_s.at[4], mx_r.at[4], chip(2)),
        "late_one": remote(relayed.at[1], landed.at[0, span(1), :], mx_s.at[5], mx_r.at[5], chip(1)),
    }

    local = [
        pltpu.make_async_copy(source, target, local_s.at[n])
        for n, (source, target) in enumerate(
            [
                (tokens, x_all.at[0]),
                (w_key, keys_in),
                (w_value, values_in),
                (cols(w_query, 0, 0, q_width), wqkv.at[pl.ds(0, half), pl.ds(0, q_width)]),
                (cols(w_query, 0, 1, q_width), wqkv.at[pl.ds(plane * half, half), pl.ds(0, q_width)]),
                (cotangent, cot_in),
                (w_out, w_o),
                (cols(w_gate, 0, 0, ff), gate_own.at[0]),
                (cols(w_gate, 0, 1, ff), gate_sib.at[0]),
                (cols(w_up, 0, 0, ff), up_own.at[0]),
                (cols(w_up, 0, 1, ff), up_sib.at[0]),
                (w_down, down),
            ]
        )
    ]

    stored = [
        (h1, h1_out), (queries, queries_out), (lse, lse_out), (attended, attended_out), (mixed, mixed_out),
        (n2, n2_out), (limits, limits_out), (cosine, cosine_out), (sine, sine_out), (kp, kp_out),
        (gain_one, gain_one_out), (gain_two, gain_two_out), (kv_all, kv_out), (branch_all, branch_out),
        (wqkv, wqkv_out), (gate_back, gate_back_out), (up_back, up_back_out), (back_part, back_out),
        (out_part, out_out), (down_own, own_down), (down_other, other_down),
    ]

    def store(n):
        return pltpu.make_async_copy(*stored[n], store_s.at[n])

    length = length_ref[0]
    place = lax.broadcasted_iota(jnp.int32, (16, slab), 0)
    high, low = (length // 64).astype(F32), (length % 64).astype(F32)
    note = jnp.where(place == 0, attn_gain[...].astype(F32), mlp_gain[...].astype(F32))
    note = jnp.where(place == 2, high, jnp.where(place == 3, low, note))
    notes[0] = note.astype(BF)
    for j in peers:
        note_send(j).start()
    token_gather.start()
    for j in (3, 1, 2):
        wq_send(j).start()
    for copy in local:
        copy.start()

    local[1].wait()
    local[2].wait()

    def head_columns(j, side):
        at = pl.ds(pl.multiple_of((k ^ side) * half, 16), half)
        head = f ^ j
        width = KV_HEADS * HEAD_DIM
        key = pltpu.roll(keys_in[at, :].astype(F32), (width - head * 64) % width, 1)[:, :128]
        value = pltpu.roll(values_in[at, :].astype(F32), (width - head * 64 + 64) % width, 1)[:, :128]
        lane = lax.broadcasted_iota(jnp.int32, key.shape, 1)
        return jnp.where(lane < 64, key, value).astype(BF)

    for j in (3, 1, 2):
        kv_give[j] = head_columns(j, 0)
        wk_send(j).start()
    wqkv[0:half, q_width : q_width + 128] = head_columns(0, 0)
    wqkv[plane * half : (plane + 1) * half, q_width : q_width + 128] = head_columns(0, 1)

    chunk = pl.ds(2 * z + k, 1)
    cos_at, sin_at = start_cos[chunk, :], start_sin[chunk, :]
    lane = lax.broadcasted_iota(jnp.int32, (rows, 128), 1)
    cosine[...] = cos_at * step_cos[...] + sin_at * step_sin[...]
    turn = sin_at * step_cos[...] - cos_at * step_sin[...]
    sine[...] = jnp.where(lane % 64 < 32, -turn, turn)
    for h in range(2):
        for s in range(line):
            start = slot - 1 - (2 * (z + s) + (k ^ h)) * rows
            spot = start - lax.broadcasted_iota(jnp.int32, (8, rows), 1)
            spot = jnp.where(spot < 0, FAR, spot).astype(F32)
            kp[:, (h * line + s) * rows : (h * line + s + 1) * rows] = spot

    for s in range(1, line):

        @pl.when(z + s >= line)
        def _():
            kv_all[s] = jnp.zeros(kv_all.shape[1:], BF)
            kv_all[line + s] = jnp.zeros(kv_all.shape[1:], BF)

    local[5].wait()
    row_pos = (first_pos - lax.broadcasted_iota(jnp.int32, (rows, 1), 0)).astype(F32)
    valid = row_pos < jnp.full((rows, 1), length.astype(F32))
    branch_all[0] = jnp.where(valid, cot_in[...].astype(F32), 0.0).astype(BF)

    token_gather.forward()
    for j in (1, 2, 3):
        wq_send(j).wait_recv()
        wk_send(j).wait_recv()
        wp_send(j).start()

    fetch_start()

    for j in peers:
        note_send(j).wait_recv()
    for j in range(plane):
        at = pl.ds(pl.multiple_of((f ^ j) * slab, 128), slab)
        gain_one[:, at] = jnp.broadcast_to(notes[j, 0:1, :].astype(F32), (8, slab))
        gain_two[:, at] = jnp.broadcast_to(notes[j, 1:2, :].astype(F32), (8, slab))
        theirs = notes[j, 2:3, 0:1].astype(F32) * 64.0 + notes[j, 3:4, 0:1].astype(F32)
        limits[j] = jnp.broadcast_to(jnp.minimum(row_pos, theirs - 1.0), (rows, 128))

    def normalize(j, x_ref):
        @pl.loop(0, rows // 16)
        def _(i):
            at = pl.ds(pl.multiple_of(i * 16, 16), 16)
            x = x_ref[at, :].astype(F32)
            inverse = lax.rsqrt(jnp.mean(x * x, axis=1, keepdims=True) + EPSILON)
            to = pl.ds(pl.multiple_of(j * rows + i * 16, 16), 16)
            for h in range(2):
                for b in range(plane):
                    from_ = pl.ds(pl.multiple_of(((f ^ b) * 2 + (k ^ h)) * half, 128), half)
                    value = x_ref[at, from_].astype(F32) * inverse * gain_one[0:1, from_]
                    c = (h * plane + b) * half
                    h1[to, c : c + half] = value.astype(BF)

    local[0].wait()
    normalize(0, x_all.at[0])
    normalize(1, x_all.at[1])
    normalize(2, x_all.at[2])
    token_gather.arrive()
    normalize(3, x_all.at[3])
    local[3].wait()
    local[4].wait()
    for j in (1, 2, 3):
        wp_send(j).wait_recv()

    kv_cols = nn(h1[...], wqkv[:, q_width : q_width + 128])
    for j in range(plane):
        value = kv_cols[j * rows : (j + 1) * rows]
        turned = value * cosine[...] + swap_halves(value) * sine[...]
        kv_all[0, j] = jnp.where(lane < 64, turned, value).astype(BF)
    for s in range(1, line):

        @pl.when(z >= s)
        def _():
            kv_send(s).start()

    kv_pair(0).start()
    branch_gather.start()

    @pl.loop(0, pairs // 2)
    def _(p):
        at = pl.ds(pl.multiple_of(p * 256, 256), 256)
        out = nn(h1[...], wqkv[:, at])
        for j in range(plane):
            for c in range(2):
                value = out[j * rows : (j + 1) * rows, c * 128 : (c + 1) * 128]
                turned = value * cosine[...] + swap_halves(value) * sine[...]
                queries[j, :, pl.ds(pl.multiple_of(p * 256 + c * 128, 128), 128)] = turned.astype(BF)

    for s in range(1, line):

        @pl.when(z + s < line)
        def _():
            kv_send(s).wait_recv()
            kv_pair(s).start()

    fetch_on(1)
    fetch_on(2)
    kv_pair(0).wait_recv()
    for s in range(1, line):

        @pl.when(z + s < line)
        def _():
            kv_pair(s).wait_recv()

    local[6].wait()

    def relay_on(far, late, which, j):
        mix_first[far].wait_recv()
        value = relay[which].astype(F32) + part[j, which * hr : (which + 1) * hr, :].astype(F32)
        relayed[which] = value.astype(BF)
        mix_first[late].start()

    @pl.loop(0, plane)
    def _(t):
        j = plane - 1 - t
        here = pl.ds(pl.multiple_of(j * rows, 16), rows)
        vk[...] = pltpu.roll(kv_all[:, j].reshape(keys, 128).astype(F32), 64, 1).astype(BF)
        limit = limits[j, :, 0:1]

        @pl.loop(0, pairs)
        def _(p):
            at = pl.ds(pl.multiple_of(p * 128, 128), 128)
            allowed = kp[0:1, :] <= limit
            q = queries[j, :, at]
            zero = jnp.zeros_like(q)
            outs, logs = [], []
            for first in (True, False):
                mine = lane < 64 if first else lane >= 64
                kv = kv_all[:, j].reshape(keys, 128)
                keyed, valued = (kv, vk[...]) if first else (vk[...], kv)
                scores = nt(jnp.where(mine, q, zero), keyed) * (HEAD_DIM**-0.5)
                scores = jnp.where(allowed, scores, MASKED)
                top = jnp.max(scores, axis=1, keepdims=True)
                weights = jnp.exp(scores - top)
                sums = jnp.sum(weights, axis=1, keepdims=True)
                outs.append(nn(weights.astype(BF), valued) / sums)
                logs.append(jnp.broadcast_to(top + jnp.log(sums), (rows, 128)))
            attended[here, at] = jnp.where(lane < 64, outs[0], outs[1]).astype(BF)
            lse[j, :, at] = jnp.where(lane < 64, logs[0], logs[1])

        part[j] = nn(attended[here, :], w_o[...]).astype(BF)

        @pl.when(t == 0)
        def _():
            mix_first["far_one"].start()
            mix_first["far_two"].start()
            branch_gather.forward()

        @pl.when(t == 1)
        def _():
            mix_first["two"].start()
            fetch_on(3)

        @pl.when(t == 2)
        def _():
            mix_first["one"].start()
            relay_on("far_one", "late_two", 0, 2)
            relay_on("far_two", "late_one", 1, 1)

    early_stores = [store(n) for n in range(12)]
    for n in (0, 1, 2, 3, 6, 7, 8, 9, 10, 11):
        early_stores[n].start()
    cross_on(1)
    cross_on(2)
    for name in ("one", "late_one", "two", "late_two"):
        mix_first[name].wait_recv()

    @pl.loop(0, rows // 16)
    def _(i):
        at = pl.ds(pl.multiple_of(i * 16, 16), 16)
        value = x_all[0, at, :].astype(F32) + part[0, at, :].astype(F32)
        value = value + landed[0, at, :].astype(F32) + landed[1, at, :].astype(F32)
        mixed[at, :] = value
        inverse = lax.rsqrt(jnp.mean(value * value, axis=1, keepdims=True) + EPSILON)
        n2_all[0, at, :] = (value * inverse * gain_two[0:1, :]).astype(BF)

    n2_gather.start()
    early_stores[4].start()
    branch_gather.arrive()
    n2_gather.forward()
    cross_on(3)
    n2_gather.arrive()

    @pl.loop(0, total // 16)
    def _(i):
        at = pl.ds(pl.multiple_of(i * 16, 16), 16)
        j = i // (rows // 16)
        from_row = pl.ds(pl.multiple_of((i % (rows // 16)) * 16, 16), 16)
        for h in range(2):
            for b in range(plane):
                from_ = pl.ds(pl.multiple_of(((f ^ b) * 2 + (k ^ h)) * half, 128), half)
                c = (h * plane + b) * half
                n2[at, c : c + half] = n2_all[j, from_row, from_]

    early_stores[5].start()
    later = [store(n) for n in range(12, 19)]
    for n in range(3):
        later[n].start()
    for n in range(7, 12):
        local[n].wait()
    for j in peers:
        gate_pair(j).wait_recv()
        up_pair(j).wait_recv()

    def feed(at):
        width = at.size
        n2_own, n2_sib = n2[:, 0 : depth // 2], n2[:, depth // 2 : depth]

        def through(own, other):
            first = nn(n2_own, own[:, :, at].reshape(depth // 2, width))
            return first + nn(n2_sib, other[:, :, at].reshape(depth // 2, width))

        gate = through(gate_own, gate_sib)
        up = through(up_own, up_sib)
        sigmoid = 1.0 / (1.0 + jnp.exp(-gate))
        hidden[:, at] = (gate * sigmoid * up).astype(BF)
        grad = nt(branch_all[...].reshape(total, depth), down[at, :])
        gate_back[:, at] = (grad * up * sigmoid * (1.0 + gate * (1.0 - sigmoid))).astype(BF)
        up_back[:, at] = (grad * gate * sigmoid).astype(BF)

    @pl.loop(0, ff // 256)
    def _(n):
        feed(pl.ds(pl.multiple_of(n * 256, 256), 256))

    if ff % 256:
        feed(pl.ds(ff // 256 * 256, ff % 256))

    for h, gate_side, up_side in ((0, gate_own, up_own), (1, gate_sib, up_sib)):

        @pl.loop(0, plane)
        def _(b):
            to = pl.ds(pl.multiple_of(((f ^ b) * 2 + (k ^ h)) * half, 128), half)
            value = nt(gate_back[...], gate_side[b]) + nt(up_back[...], up_side[b])
            back_part[:, to] = value.astype(BF)

    later[3].start()
    later[4].start()
    later[5].start()

    def down_term(at, side, target):
        spot = pl.ds(pl.multiple_of((k ^ side) * (depth // 2), 128), depth // 2)
        right = branch_all[:, :, spot].reshape(total, depth // 2)
        target[at, :] = tn(hidden[:, at], right).astype(BF)

    for side, target in ((0, down_own), (1, down_other)):

        @pl.loop(0, ff // 256)
        def _(n):
            down_term(pl.ds(pl.multiple_of(n * 256, 256), 256), side, target)

        if ff % 256:
            down_term(pl.ds(ff // 256 * 256, ff % 256), side, target)

    ends = [store(19), store(20)]
    for copy in ends:
        copy.start()

    @pl.loop(0, depth // 256)
    def _(n):
        at = pl.ds(pl.multiple_of(n * 256, 256), 256)
        out_part[:, at] = nn(hidden[...], down[:, at]).astype(BF)

    later[6].start()
    for gather in (token_gather, branch_gather, n2_gather):
        gather.close()
    for copy in mix_first.values():
        copy.wait_send()
    for j in peers:
        note_send(j).wait_send()
        wq_send(j).wait_send()
        wk_send(j).wait_send()
        wp_send(j).wait_send()
        gate_pair(j).wait_send()
        up_pair(j).wait_send()
    by_parity(
        lambda: [c(j).wait_send() for j in peers for c in (gate_send, gate_across)],
        lambda: [c(j).wait_send() for j in peers for c in (up_send, up_across)],
    )

    kv_pair(0).wait_send()
    for s in range(1, line):

        @pl.when(z >= s)
        def _():
            kv_send(s).wait_send()

        @pl.when(z + s < line)
        def _():
            kv_pair(s).wait_send()

    for copy in early_stores + later + ends:
        copy.wait()


def front_pass(tokens, cotangent, lengths, attn_gain, mlp_gain, w_query, w_key, w_value, w_out, w_gate, w_up, w_down):
    rows, depth = tokens.shape
    plane, line = 4, 4
    total, slab = plane * rows, depth // plane
    half = slab // 2
    q_width = HEADS * HEAD_DIM // plane
    width = q_width + 128
    ff = w_down.shape[0]
    slot = rows * line * 2
    keys = slot
    act = (rows, depth)
    local = pl.BlockSpec(memory_space=pltpu.VMEM)
    anywhere = pl.BlockSpec(memory_space=pl.ANY)
    dma = lambda n: pltpu.SemaphoreType.DMA((n,))
    kv_shape = (2 * line, plane, rows, 128)
    sds = jax.ShapeDtypeStruct
    outs = [
        sds((total, depth), BF),
        sds((plane, rows, q_width), BF),
        sds((plane, rows, q_width), F32),
        sds((total, q_width), BF),
        sds(act, F32),
        sds((total, depth), BF),
        sds((plane, rows, 128), F32),
        sds((rows, 128), F32),
        sds((rows, 128), F32),
        sds((8, keys), F32),
        sds((8, depth), F32),
        sds((8, depth), F32),
        sds(kv_shape, BF),
        sds((plane,) + act, BF),
        sds((depth, width), BF),
        sds((total, ff), BF),
        sds((total, ff), BF),
        sds((total, depth), BF),
        sds((total, depth), BF),
        sds((ff, depth // 2), BF),
        sds((ff, depth // 2), BF),
    ]
    held = [pltpu.VMEM(o.shape, o.dtype) for o in outs]
    held = held[:12] + [pltpu.VMEM((total, ff), BF)] + held[15:]
    slabs = pltpu.VMEM((plane, half, ff), BF)
    scratch = held + [
        pltpu.VMEM((plane, 16, slab), BF),
        pltpu.VMEM((plane,) + act, BF),
        pltpu.VMEM((depth, width), BF),
        pltpu.VMEM(w_key.shape, BF),
        pltpu.VMEM(w_value.shape, BF),
        pltpu.VMEM((plane, half, 128), BF),
        slabs,
        slabs,
        slabs,
        slabs,
        pltpu.VMEM(w_down.shape, BF),
        pltpu.VMEM(kv_shape, BF),
        pltpu.VMEM((keys, 128), BF),
        pltpu.VMEM(w_out.shape, BF),
        pltpu.VMEM((plane,) + act, BF),
        pltpu.VMEM((2,) + act, BF),
        pltpu.VMEM((2, rows // 2, depth), BF),
        pltpu.VMEM((2, rows // 2, depth), BF),
        pltpu.VMEM((plane,) + act, BF),
        pltpu.VMEM((plane,) + act, BF),
        pltpu.VMEM(act, BF),
    ]
    sems = [12, 21, 3, 3, 2, 2, 2, 2, 3, 3, 3, 3, 3, 3, 1, 1, 3, 3, 4, 4, 3, 3, 3, 3, 3, 3, 3, 3, 3, 3]
    sems += [2, 2, 2, 2, 6, 6, 2, 2, 2, 2]
    return pl.pallas_call(
        front_kernel,
        out_shape=outs,
        in_specs=[pl.BlockSpec(memory_space=pltpu.SMEM)] + [local] * 6 + [anywhere] * 9,
        out_specs=[anywhere] * 21,
        scratch_shapes=scratch + [dma(n) for n in sems],
        compiler_params=pltpu.CompilerParams(
            vmem_limit_bytes=62 * 1024 * 1024, has_side_effects=True
        ),
        name="front_pass",
    )(
        lengths, attn_gain.reshape(1, slab), mlp_gain.reshape(1, slab), *rotary_parts(slot, rows),
        tokens, cotangent, w_query, w_key, w_value, w_out, w_gate, w_up, w_down,
    )


def add_into(target, other):
    @pl.loop(0, target.shape[0] // 16)
    def _(i):
        at = pl.ds(pl.multiple_of(i * 16, 16), 16)
        target[at, :] = (target[at, :].astype(F32) + other[at, :].astype(F32)).astype(BF)


def back_kernel(
    limits,
    own_down, other_down, back_part, out_part, w_out, wqkv_hbm, h1_hbm, n2_hbm,
    gate_back, up_back, mixed, branch_own, x_own, gain_one, gain_two,
    attended, queries, lse, kv_all, kp, cosine, sine,
    fin_down, fin_gate, fin_up, fin_out, fin_qkv, fin_gain,
    sib_down, sib_gate, sib_up, sib_out, sib_qkv, sib_gain,
    outputs, input_grad,
    src_down, src_gate, src_up, src_out, src_qkv, src_gain,
    swap_gate, swap_up, swap_qkv,
    end_down, end_gate, end_up, end_out, end_qkv, end_gain,
    load_down, give_gate, give_out, give_qkv, give_gain,
    landed, landed_out, first_back, first_out, da_all, wide, do_all, dqkv, wqkv, left,
    vk, dk_sum, dv_sum, kv_part, kv_land, kv_mine, kv_line, gain_acc, gain_all,
    pair_s, pair_r, load_s, swap_s, swap_r, in_s, in_r, mid_s, mid_r, out_s, done_s, back_s, back_r, ready,
    local_s, rs_s, rs_r, ro_s, ro_r, ag_s, ag_r, rq_s, rq_r, kp_s, kp_r, kz_s, kz_r, ga_s, ga_r,
):
    f, z, k = lax.axis_index("fsdp"), lax.axis_index("z"), lax.axis_index("core")
    plane, line = lax.axis_size("fsdp"), lax.axis_size("z")
    outer = (z == 0) | (z == line - 1)
    inner = jnp.logical_not(outer)
    inward = jnp.where(z < line // 2, z + 1, z - 1)
    outward = jnp.where(z < line // 2, z - 1, z + 1)
    rows, depth = mixed.shape
    total = plane * rows
    half_depth = depth // 2
    half = half_depth // plane
    q_width = attended.shape[1]
    pairs = q_width // 128
    peers = range(1, plane)

    kinds = {
        "down": (own_down, other_down, src_down, None, end_down, load_down, fin_down, sib_down),
        "gate": (None, give_gate, src_gate, swap_gate, end_gate, None, fin_gate, sib_gate),
        "up": (None, give_gate, src_up, swap_up, end_up, None, fin_up, sib_up),
        "out": (None, give_out, src_out, None, end_out, None, fin_out, sib_out),
        "qkv": (None, give_qkv, src_qkv, swap_qkv, end_qkv, None, fin_qkv, sib_qkv),
        "gain": (None, give_gain, src_gain, None, end_gain, None, fin_gain, sib_gain),
    }
    chunks = [(name, i) for name, kind in kinds.items() for i in range(kind[2].shape[0])]
    count = len(chunks)
    loaded = [c for c in range(count) if kinds[chunks[c][0]][0] is not None]

    def group(c):
        return kinds[chunks[c][0]][1].shape[0]

    heads = [c for c in range(count) if c not in loaded and chunks[c][1] % group(c) == 0]

    def remote(source, target, send, recv, where):
        return pltpu.make_async_remote_copy(
            src_ref=source,
            dst_ref=target,
            send_sem=send,
            recv_sem=recv,
            device_id=where,
            device_id_type=pl.DeviceIdType.MESH,
        )

    def part(c, which):
        name, i = chunks[c]
        return kinds[name][which].at[i]

    def swapped(c):
        name, i = chunks[c]
        return i // group(c) if kinds[name][3] is not None else 0

    def pair_copy(c):
        name, i = chunks[c]
        given = kinds[name][1]
        source = given.at[i % given.shape[0]]
        return remote(source, part(c, 2), pair_s.at[c], pair_r.at[c], {"core": 1 - k})

    def load_copy(c):
        return pltpu.make_async_copy(part(c, 0), kinds[chunks[c][0]][5].at[c % 2], load_s.at[c])

    def landing(c):
        name, i = chunks[c]
        return kinds[name][3].at[i - group(c)]

    def swap_copy(c):
        return remote(part(c, 2), landing(c), swap_s.at[c], swap_r.at[c], {"fsdp": f ^ swapped(c)})

    def base(c):
        return landing(c) if swapped(c) else part(c, 2)

    def in_copy(c):
        return remote(base(c), part(c, 4), in_s.at[c], in_r.at[c], {"z": inward})

    def mid_copy(c):
        return remote(base(c), part(c, 4), mid_s.at[c], mid_r.at[c], {"z": inward})

    def out_copy(c):
        return remote(part(c, 4), part(c, 4), out_s.at[c], mid_r.at[c], {"z": outward})

    def keep_copy(c):
        return pltpu.make_async_copy(part(c, 4), part(c, 6), done_s.at[c])

    def back_copy(c):
        return remote(part(c, 4), part(c, 7), back_s.at[c], back_r.at[c], {"core": 1 - k})

    own_cols = pl.ds(pl.multiple_of(k * half_depth, 128), half_depth)
    other_cols = pl.ds(pl.multiple_of((1 - k) * half_depth, 128), half_depth)

    def slab_term(i, side, right):
        start = side * half_depth + i * (half // 2)
        return tn(left[:, start : start + half], right)

    def term(c, side):
        name, i = chunks[c]
        if name == "gate":
            return slab_term(i, side, gate_back[...])
        if name == "up":
            return slab_term(i, side, up_back[...])
        if name == "qkv":
            return slab_term(i, side, dqkv[...])
        if name == "out":
            size = src_out.shape[1]
            right = da_all[:, :, (own_cols, other_cols)[side]].reshape(total, half_depth)
            return tn(attended[:, i * size : (i + 2) * size], right)
        return gain_all[...].astype(F32).sum(axis=0)

    def stage_give(c):
        given = kinds[chunks[c][0]][1]
        if c - 1 not in loaded and kinds[chunks[c - 1][0]][1] is given:
            for n in range(group(c)):
                pair_copy(c - 1 - n).wait_send()
        given[...] = term(c, 1).astype(BF).reshape(given.shape)
        for n in range(group(c)):
            pair_copy(c + n).start()

    def stage_load(c):
        pair_copy(c).wait_recv()
        load_copy(c).wait()
        add_into(part(c, 2), load_down.at[c % 2])
        if c + 2 in loaded:
            load_copy(c + 2).start()

    def stage_pair(c):
        value = term(c, 0)
        size = value.shape[0] // group(c)
        for n in range(group(c)):
            pair_copy(c + n).wait_recv()
            target = part(c + n, 2)
            target[...] = (target[...].astype(F32) + value[n * size : (n + 1) * size]).astype(BF)
            if swapped(c + n):
                swap_copy(c + n).start()

    def stage_in(c):
        if swapped(c):
            swap_copy(c).wait_recv()

        @pl.when(outer)
        def _():
            in_copy(c).start()

    def stage_mid(c):
        @pl.when(inner)
        def _():
            in_copy(c).wait_recv()
            add_into(base(c), part(c, 4))
            pl.semaphore_signal(
                ready, inc=1, device_id={"z": inward}, device_id_type=pl.DeviceIdType.MESH
            )
            pl.semaphore_wait(ready, 1)
            mid_copy(c).start()

    def stage_out(c):
        @pl.when(inner)
        def _():
            mid_copy(c).wait_recv()
            add_into(part(c, 4), base(c))
            out_copy(c).start()

    def stage_keep(c):
        @pl.when(outer)
        def _():
            out_copy(c).wait_recv()

        keep_copy(c).start()
        back_copy(c).start()

    def back_send(j):
        return remote(back_part.at[j], landed.at[j - 1], rs_s.at[j - 1], rs_r.at[j - 1], {"fsdp": f ^ j})

    def out_send(j):
        return remote(out_part.at[j], landed_out.at[j - 1], ro_s.at[j - 1], ro_r.at[j - 1], {"fsdp": f ^ j})

    def da_send(j):
        return remote(da_all.at[0], da_all.at[j], ag_s.at[j - 1], ag_r.at[j - 1], {"fsdp": f ^ j})

    def dh_send(j):
        mine = wide.at[pl.ds(j * rows, rows), :]
        return remote(mine, landed.at[j - 1], rq_s.at[j - 1], rq_r.at[j - 1], {"fsdp": f ^ j})

    def gain_send(j):
        return remote(gain_all.at[0], gain_all.at[j], ga_s.at[j - 1], ga_r.at[j - 1], {"fsdp": f ^ j})

    locals_ = [
        pltpu.make_async_copy(back_part.at[0], first_back, local_s.at[0]),
        pltpu.make_async_copy(out_part.at[0], first_out, local_s.at[1]),
        pltpu.make_async_copy(w_out, wide.at[pl.ds(0, w_out.shape[0]), :], local_s.at[2]),
        pltpu.make_async_copy(wqkv_hbm, wqkv, local_s.at[3]),
        pltpu.make_async_copy(n2_hbm, left, local_s.at[4]),
        pltpu.make_async_copy(h1_hbm, left, local_s.at[5]),
    ]

    def rms_back(gradient_of, x_ref, gain, acc, write):
        acc[...] = jnp.zeros_like(acc)

        @pl.loop(0, rows // 16)
        def _(i):
            at = pl.ds(pl.multiple_of(i * 16, 16), 16)
            gradient = gradient_of(at)
            x = x_ref[at, :].astype(F32)
            inverse = lax.rsqrt(jnp.mean(x * x, axis=1, keepdims=True) + EPSILON)
            normed = x * inverse
            acc[...] += gradient * normed
            scaled = gradient * gain[0:1, :]
            write(at, inverse * (scaled - normed * jnp.mean(scaled * normed, axis=1, keepdims=True)))

    def piece_mixed():
        locals_[0].wait()
        for j in peers:
            back_send(j).wait_recv()

        def gradient_of(at):
            value = first_back[at, :].astype(F32)
            for j in peers:
                value = value + landed[j - 1, at, :].astype(F32)
            return value

        def write(at, value):
            value = value + branch_own[at, :].astype(F32)
            input_grad[at, :] = value
            da_all[0, at, :] = value.astype(BF)

        rms_back(gradient_of, mixed, gain_two, gain_acc.at[1], write)
        for j in peers:
            da_send(j).start()

    def piece_do():
        locals_[2].wait()
        for j in peers:
            da_send(j).wait_recv()
            out_send(j).start()

        @pl.loop(0, plane)
        def _(j):
            do_all[j] = nt(da_all[j], wide[0 : w_out.shape[0], :]).astype(BF)

    def piece_attend(j0):
        @pl.loop(j0, j0 + 2)
        def _(j):
            attend_one(j)

    def attend_one(j):
        here = pl.ds(pl.multiple_of(j * rows, 16), rows)
        vk[...] = pltpu.roll(kv_all[:, j].reshape(vk.shape).astype(F32), 64, 1).astype(BF)
        dk_sum[...] = jnp.zeros_like(dk_sum)
        dv_sum[...] = jnp.zeros_like(dv_sum)
        limit = limits[j, :, 0:1]
        lane = lax.broadcasted_iota(jnp.int32, (rows, 128), 1)

        @pl.loop(0, pairs)
        def _(p):
            at = pl.ds(pl.multiple_of(p * 128, 128), 128)
            allowed = kp[0:1, :] <= limit
            q, do = queries[j, :, at], do_all[j, :, at]
            logs = lse[j, :, at]
            zero = jnp.zeros_like(q)
            parts = []
            for first in (True, False):
                mine = lane < 64 if first else lane >= 64
                kv = kv_all[:, j].reshape(vk.shape)
                keyed, valued = (kv, vk[...]) if first else (vk[...], kv)
                q_own, do_own = jnp.where(mine, q, zero), jnp.where(mine, do, zero)
                scores = nt(q_own, keyed) * (HEAD_DIM**-0.5)
                log_total = logs[:, 0:1] if first else logs[:, 64:65]
                weights = jnp.where(allowed, jnp.exp(scores - log_total), 0.0)
                joint = weights * nt(do_own, valued)
                back = (joint - weights * jnp.sum(joint, axis=1, keepdims=True)).astype(BF)
                parts.append(nn(back, keyed))
                dk_sum[...] += tn(back, q_own)
                dv_sum[...] += tn(weights.astype(BF), do_own)
            turned = jnp.where(lane < 64, parts[0], parts[1]) * (HEAD_DIM**-0.5)
            turned = turned * cosine[...] - swap_halves(turned) * sine[...]
            dqkv[here, at] = turned.astype(BF)

        dk = dk_sum[...]
        dv = dv_sum[...]
        dk = (dk + pltpu.roll(dk, 64, 1)) * (HEAD_DIM**-0.5)
        dv = dv + pltpu.roll(dv, 64, 1)
        wide_lane = lax.broadcasted_iota(jnp.int32, dk.shape, 1)
        packed = jnp.where(wide_lane < 64, dk, dv).astype(BF)
        kv_part[:, j] = packed.reshape(kv_part.shape[0], rows, 128)

    kv_pair = remote(kv_part.at[pl.ds(line, line)], kv_land, kp_s.at[0], kp_r.at[0], {"core": 1 - k})

    def kv_send(s):
        return remote(kv_mine.at[s], kv_line.at[s - 1], kz_s.at[s - 1], kz_r.at[s - 1], {"z": z + s})

    def piece_kv_line():
        kv_pair.wait_recv()
        for s in range(line):
            kv_mine[s] = (kv_part[s].astype(F32) + kv_land[s].astype(F32)).astype(BF)
        for s in range(1, line):

            @pl.when(z + s < line)
            def _():
                kv_send(s).start()

    def piece_kv_sum():
        for s in range(1, line):

            @pl.when(z >= s)
            def _():
                kv_send(s).wait_recv()
                kv_mine[0] = (kv_mine[0].astype(F32) + kv_line[s - 1].astype(F32)).astype(BF)

        lane = lax.broadcasted_iota(jnp.int32, (rows, 128), 1)
        for j in range(plane):
            value = kv_mine[0, j].astype(F32)
            turned = value * cosine[...] - swap_halves(value) * sine[...]
            value = jnp.where(lane < 64, turned, value).astype(BF)
            dqkv[j * rows : (j + 1) * rows, q_width : q_width + 128] = value

    def piece_dh():
        locals_[3].wait()
        for h in range(2):
            for j in range(plane):
                start = pl.multiple_of(((f ^ j) * 2 + (k ^ h)) * half, 128)
                block = wqkv[(h * plane + j) * half : (h * plane + j + 1) * half, :]
                wide[0:total, pl.ds(start, half)] = nt(dqkv[...], block).astype(BF)
        for j in peers:
            dh_send(j).start()

    def piece_input():
        for j in peers:
            dh_send(j).wait_recv()

        def gradient_of(at):
            value = wide[at, :].astype(F32)
            for j in peers:
                value = value + landed[j - 1, at, :].astype(F32)
            return value

        def write(at, value):
            input_grad[at, :] = input_grad[at, :] + value

        rms_back(gradient_of, x_own, gain_one, gain_acc.at[0], write)
        place = lax.broadcasted_iota(jnp.int32, (16, depth), 0)
        one = jnp.sum(gain_acc[0], axis=0, keepdims=True)
        two = jnp.sum(gain_acc[1], axis=0, keepdims=True)
        gain_all[0] = jnp.where(place == 0, one, jnp.where(place == 1, two, 0.0)).astype(BF)
        for j in peers:
            gain_send(j).start()

    def piece_outputs():
        locals_[1].wait()
        for j in peers:
            out_send(j).wait_recv()

        @pl.loop(0, rows // 16)
        def _(i):
            at = pl.ds(pl.multiple_of(i * 16, 16), 16)
            value = mixed[at, :] + first_out[at, :].astype(F32)
            for j in peers:
                value = value + landed_out[j - 1, at, :].astype(F32)
            outputs[at, :] = value

    def piece_gain():
        for j in peers:
            gain_send(j).wait_recv()

    give_lag, pair_lag, load_lag, in_lag, mid_lag, out_lag, keep_lag = LAGS
    events = []
    for c in loaded:
        events.append((max(c + load_lag, 0), 1, stage_load, c))
    for c in heads:
        events.append((c + give_lag, 0, stage_give, c))
        events.append((c + pair_lag, 1, stage_pair, c))
    for c in range(count):
        events.append((c + in_lag, 2, stage_in, c))
        events.append((c + mid_lag, 3, stage_mid, c))
        events.append((c + out_lag, 4, stage_out, c))
        events.append((c + keep_lag, 5, stage_keep, c))
    steps = (piece_mixed, piece_do, piece_kv_line, piece_outputs, piece_kv_sum, piece_dh, piece_input, piece_gain)
    events += [(tick, 6 + n, piece, None) for n, (piece, tick) in enumerate(zip(steps, STEPS))]
    for j in range(0, plane, 2):
        events.append((ATTEND[j // 2], 20 + j, piece_attend, j))
    events.append((ATTEND[-1], 30, kv_pair.start, None))
    first_qkv = [c for c in heads if chunks[c][0] == "qkv"][0]
    last_up = [c for c in heads if chunks[c][0] == "up"][-1]
    events.append((last_up + pair_lag, 31, locals_[5].start, None))
    events.append((first_qkv + give_lag, -1, locals_[5].wait, None))
    events.sort(key=lambda e: e[:2])

    for j in peers:
        back_send(j).start()
    for c in loaded:
        pair_copy(c).start()
    for c in loaded[:2]:
        load_copy(c).start()
    for copy in locals_[:5]:
        copy.start()
    locals_[4].wait()
    for _, _, act, which in events:
        act() if which is None else act(which)

    for c in range(count):
        given = kinds[chunks[c][0]][1]
        later = [n for n in heads if n > c and kinds[chunks[n][0]][1] is given]
        if c in loaded or not later:
            pair_copy(c).wait_send()
        if swapped(c):
            swap_copy(c).wait_send()
        keep_copy(c).wait()
        back_copy(c).wait_send()
        back_copy(c).wait_recv()

        @pl.when(outer)
        def _():
            in_copy(c).wait_send()

        @pl.when(inner)
        def _():
            mid_copy(c).wait_send()
            out_copy(c).wait_send()

    for j in peers:
        back_send(j).wait_send()
        out_send(j).wait_send()
        da_send(j).wait_send()
        dh_send(j).wait_send()
        gain_send(j).wait_send()
    kv_pair.wait_send()
    for s in range(1, line):

        @pl.when(z + s < line)
        def _():
            kv_send(s).wait_send()


def back_pass(
    limits, own_down, other_down, back_part, out_part, w_out, wqkv, h1, n2, gate_back, up_back,
    mixed, branch_own, x_own, gain_one, gain_two, attended, queries, lse, kv_all, kp, cosine, sine,
):
    count, line = lax.axis_size("fsdp"), lax.axis_size("z")
    rows, depth = mixed.shape
    total, half_depth = count * rows, depth // 2
    half = half_depth // count
    q_width = attended.shape[1]
    keys = kv_all.shape[0] * rows
    ff = gate_back.shape[1]
    slabs = (2 * count, half // 2, ff)
    shapes = [
        own_down.shape,
        slabs,
        slabs,
        (4, q_width // 4, half_depth),
        (2 * count, half // 2, q_width + 128),
        (1, 16, depth),
    ]
    anywhere = pl.BlockSpec(memory_space=pl.ANY)
    local = pl.BlockSpec(memory_space=pltpu.VMEM)
    ends = [jax.ShapeDtypeStruct(s, BF) for s in shapes]
    act = jax.ShapeDtypeStruct((rows, depth), F32)
    block = (rows, depth)
    chunk_count = sum(s[0] for s in shapes)
    dma = lambda n: pltpu.SemaphoreType.DMA((n,))
    scratch = (
        [pltpu.VMEM(s, BF) for s in shapes]
        + [pltpu.VMEM((shapes[i][0] - 2,) + shapes[i][1:], BF) for i in (1, 2, 4)]
        + [pltpu.VMEM(s, BF) for s in shapes]
        + [pltpu.VMEM((2,) + shapes[i][1:], BF) for i in (0, 1, 3, 4)]
        + [pltpu.VMEM(shapes[5], BF)]
        + [
            pltpu.VMEM((count - 1,) + block, BF),
            pltpu.VMEM((count - 1,) + block, BF),
            pltpu.VMEM(block, BF),
            pltpu.VMEM(block, BF),
            pltpu.VMEM((count,) + block, BF),
            pltpu.VMEM((max(total, q_width), depth), BF),
            pltpu.VMEM((count, rows, q_width), BF),
            pltpu.VMEM((total, q_width + 128), BF),
            pltpu.VMEM(wqkv.shape, BF),
            pltpu.VMEM(h1.shape, BF),
            pltpu.VMEM((keys, 128), BF),
            pltpu.VMEM((keys, 128), F32),
            pltpu.VMEM((keys, 128), F32),
            pltpu.VMEM(kv_all.shape, BF),
            pltpu.VMEM((line,) + kv_all.shape[1:], BF),
            pltpu.VMEM((line,) + kv_all.shape[1:], BF),
            pltpu.VMEM((line - 1,) + kv_all.shape[1:], BF),
            pltpu.VMEM((2, 16, depth), F32),
            pltpu.VMEM((count, 16, depth), BF),
        ]
        + [dma(chunk_count)] * 13
        + [pltpu.SemaphoreType.REGULAR, dma(6)]
        + [dma(count - 1)] * 8
        + [dma(1)] * 2
        + [dma(line - 1)] * 2
        + [dma(count - 1)] * 2
    )
    out = pl.pallas_call(
        back_kernel,
        out_shape=ends + ends + [act, act],
        in_specs=[local] + [anywhere] * 8 + [local] * 14,
        out_specs=[anywhere] * 12 + [local] * 2,
        scratch_shapes=scratch,
        compiler_params=pltpu.CompilerParams(
            vmem_limit_bytes=62 * 1024 * 1024, has_side_effects=True
        ),
        cost_estimate=pl.CostEstimate(
            flops=10**11, bytes_accessed=10**9, transcendentals=10**7
        ),
        name="back_pass",
    )(
        limits, own_down, other_down, back_part, out_part, w_out, wqkv, h1, n2, gate_back, up_back,
        mixed, branch_own, x_own, gain_one, gain_two, attended, queries, lse, kv_all, kp, cosine, sine,
    )
    return out[:6], out[6:12], out[12], out[13]


def finish_kernel(
    own_down, own_gate, own_up, own_out, own_qkv, own_gain, sib_down, sib_gate, sib_up, sib_out, sib_qkv,
    down, gate, up, out, query, key, value, attn_gain, mlp_gain,
    low_rows, low_cols, high_rows, high_cols, kv, kv_high, gain_in, gain_high, load_s, store_s, side_s,
):
    f, k = lax.axis_index("fsdp"), lax.axis_index("core")
    plane = lax.axis_size("fsdp")
    half, ff = own_gate.shape[1], own_gate.shape[2]
    half_depth = own_down.shape[2]
    slab = 2 * half
    q_width = own_qkv.shape[2] - 128
    tasks = []
    for side, (d, o, g, u, q) in enumerate(
        ((own_down, own_out, own_gate, own_up, own_qkv), (sib_down, sib_out, sib_gate, sib_up, sib_qkv))
    ):
        rows_at = pl.ds(pl.multiple_of((k ^ side) * half, 8), half)
        cols_at = pl.ds(pl.multiple_of((k ^ side) * half_depth, 128), half_depth)
        for source, target in ((d, down), (o, out)):
            for i in range(source.shape[0]):
                size = source.shape[1]
                tasks.append((source.at[i], target.at[pl.ds(i * size, size), cols_at], 0))
        for source, target in ((g, gate), (u, up)):
            for j in range(plane):
                to = pl.ds(pl.multiple_of((f ^ j) * ff, 128), ff)
                tasks.append((source.at[j], target.at[rows_at, to], 1))
        for j in range(plane):
            to = pl.ds(pl.multiple_of((f ^ j) * q_width, 128), q_width)
            tasks.append((q.at[j, :, pl.ds(0, q_width)], query.at[rows_at, to], 1))
    slots = low_rows.shape[0]

    def window(buffer, n, shape):
        return buffer.at[n % slots, pl.ds(0, shape[0]), pl.ds(0, shape[1])]

    def load(n):
        source, _, kind = tasks[n]
        low = (low_rows, low_cols)[kind]
        return pltpu.make_async_copy(source, window(low, n, source.shape), load_s.at[n])

    def store(n):
        source, target, kind = tasks[n]
        high = (high_rows, high_cols)[kind]
        return pltpu.make_async_copy(window(high, n, source.shape), target, store_s.at[n])

    sides = [
        pltpu.make_async_copy(own_gain.at[0], gain_in, side_s.at[0]),
        pltpu.make_async_copy(own_qkv.at[:, :, pl.ds(q_width, 128)], kv.at[0], side_s.at[1]),
        pltpu.make_async_copy(sib_qkv.at[:, :, pl.ds(q_width, 128)], kv.at[1], side_s.at[2]),
    ]
    for n in range(slots):
        load(n).start()
    for copy in sides:
        copy.start()
    for n in range(len(tasks)):
        source, _, kind = tasks[n]
        shape = source.shape
        low, high = ((low_rows, high_rows), (low_cols, high_cols))[kind]
        load(n).wait()
        if n >= slots:
            store(n - slots).wait()

        @pl.loop(0, shape[0] // 16)
        def _(i):
            at = pl.ds(pl.multiple_of(i * 16, 16), 16)
            high[n % slots, at, 0 : shape[1]] = low[n % slots, at, 0 : shape[1]].astype(F32)

        store(n).start()
        if n + slots < len(tasks):
            load(n + slots).start()
    for copy in sides:
        copy.wait()
    mine = pl.ds(pl.multiple_of(f * slab, 128), slab)
    gain_high[...] = gain_in[...].astype(F32)
    attn_gain[...] = gain_high[0:1, mine]
    mlp_gain[...] = gain_high[1:2, mine]
    lane = lax.broadcasted_iota(jnp.int32, (half, 128), 1)
    for side in range(2):
        rows_at = pl.ds(pl.multiple_of((k ^ side) * half, 8), half)
        for pair in range(plane // 2):
            first = kv[side, f ^ (2 * pair)].astype(F32)
            second = kv[side, f ^ (2 * pair + 1)].astype(F32)
            at = slice(pair * 128, (pair + 1) * 128)
            key[rows_at, at] = jnp.where(lane < 64, first, pltpu.roll(second, 64, 1))
            value[rows_at, at] = jnp.where(lane < 64, pltpu.roll(first, 64, 1), second)
    for n in range(max(0, len(tasks) - slots), len(tasks)):
        store(n).wait()


def finish(owns, sibs):
    plane = lax.axis_size("fsdp")
    down, gate, _, out, qkv, gain = (x.shape for x in owns)
    depth = 2 * down[2]
    slab = 2 * gate[1]
    q_width = qkv[2] - 128
    sds = jax.ShapeDtypeStruct
    shapes = [
        (down[0] * down[1], depth), (slab, plane * gate[2]), (slab, plane * gate[2]), (out[0] * out[1], depth),
        (slab, plane * q_width), (slab, KV_HEADS * HEAD_DIM), (slab, KV_HEADS * HEAD_DIM), (1, slab), (1, slab),
    ]
    slots = 4
    tall = (slots, max(down[1], out[1]), down[2])
    wide = (slots, gate[1], max(gate[2], q_width))
    count = 2 * (down[0] + out[0] + 3 * plane)
    anywhere, local = pl.BlockSpec(memory_space=pl.ANY), pl.BlockSpec(memory_space=pltpu.VMEM)
    return pl.pallas_call(
        finish_kernel,
        out_shape=[sds(s, F32) for s in shapes],
        in_specs=[anywhere] * 11,
        out_specs=[anywhere] * 5 + [local] * 4,
        scratch_shapes=[
            pltpu.VMEM(tall, BF),
            pltpu.VMEM(wide, BF),
            pltpu.VMEM(tall, F32),
            pltpu.VMEM(wide, F32),
            pltpu.VMEM((2, plane, gate[1], 128), BF),
            pltpu.VMEM((16, 128), F32),
            pltpu.VMEM(gain[1:], BF),
            pltpu.VMEM(gain[1:], F32),
            pltpu.SemaphoreType.DMA((count,)),
            pltpu.SemaphoreType.DMA((count,)),
            pltpu.SemaphoreType.DMA((3,)),
        ],
        compiler_params=params(),
        name="finish",
    )(*owns, *sibs[:5])


def body(
    tokens, cotangent, lengths, attn_gain, w_query, w_key, w_value, w_out, mlp_gain, w_gate, w_up, w_down
):
    seqs, rows, depth = tokens.shape
    count = lax.axis_size("fsdp")
    slab = depth // count
    x_own = tokens.reshape(rows, depth)
    (
        h1, queries, lse, attended, mixed, n2, limits, cosine, sine, kp, gain_one, gain_two, kv_all, branch, wqkv,
        gate_back, up_back, back_part, out_part, own_down, other_down,
    ) = front_pass(
        x_own, cotangent.reshape(rows, depth), lengths, attn_gain, mlp_gain,
        w_query, w_key, w_value, w_out, w_gate, w_up, w_down,
    )
    own_down, other_down = (x.reshape(8, -1, depth // 2) for x in (own_down, other_down))
    owns, sibs, outputs, input_grad = back_pass(
        limits, own_down, other_down, back_part.reshape(count, rows, depth), out_part.reshape(count, rows, depth),
        w_out, wqkv, h1, n2, gate_back, up_back,
        mixed, branch[0], x_own, gain_one, gain_two, attended, queries, lse, kv_all, kp, cosine, sine,
    )

    def whole(x):
        return x.reshape(4, -1, x.shape[2]) if x.shape[0] > 1 else x

    owns, sibs = [whole(x) for x in owns], [whole(x) for x in sibs]
    down_grad, gate_grad, up_grad, out_grad, query_grad, key_grad, value_grad, gain_a, gain_m = finish(owns, sibs)
    return (
        outputs.reshape(seqs, rows, depth),
        input_grad.reshape(seqs, rows, depth),
        gain_a.reshape(slab),
        query_grad,
        key_grad,
        value_grad,
        out_grad,
        gain_m.reshape(slab),
        gate_grad,
        up_grad,
        down_grad,
    )


def solution(mesh):
    count, ctx = mesh.shape["fsdp"], mesh.shape["ctx"]
    split = Mesh(mesh.devices.reshape(count, ctx // 2, 2), ("fsdp", "z", "core"))
    act = P("fsdp", ("z", "core"), None)
    row, mat = P("fsdp"), P("fsdp", None)
    fast = count == 4 and count == KV_HEADS and ctx == 8
    return jax.shard_map(
        body if fast else body_plain,
        mesh=split,
        in_specs=(act, act, row, row, mat, mat, mat, mat, row, mat, mat, mat),
        out_specs=(act, act, row, mat, mat, mat, mat, row, mat, mat, mat),
        check_vma=False,
    )
```

```python
import functools

import jax
import jax.numpy as jnp
import numpy as np
from jax import lax
from jax.experimental import pallas as pl
from jax.experimental.pallas import tpu as pltpu
from jax.sharding import Mesh
from jax.sharding import PartitionSpec as P

HEADS = 32
KV_HEADS = 4
HEAD_DIM = 64
EPSILON = 1e-05
ROPE_BASE = 10000.0
MASKED = -1e30
FAR = 1 << 30
BF = jnp.bfloat16
F32 = jnp.float32
VMEM_BYTES = 56 * 1024 * 1024
LAGS = (0, 2, 4, 6)
AHEAD = (1, 4)
STEPS = (0, 1, 6, 11, 12, 13, 14, 16, 17, 19, 23, 23, 22, 27, 29)


def params(**kw):
    return pltpu.CompilerParams(vmem_limit_bytes=VMEM_BYTES, **kw)


def along_plane(value, step):
    count = lax.axis_size("fsdp")
    return lax.ppermute(value, "fsdp", [(i, i ^ step) for i in range(count)])


def to_sibling(value):
    return lax.ppermute(value, "core", [(0, 1), (1, 0)])


def along_line(value, shift):
    count = lax.axis_size("z")
    return lax.ppermute(
        value, "z", [(i, i + shift) for i in range(count) if 0 <= i + shift < count]
    )


def plane_bits():
    count = lax.axis_size("fsdp")
    return [1 << b for b in range(count.bit_length() - 1)]


def plane_gather(block):
    half = block.shape[0] // 2
    parts = []
    for which, bits in ((0, plane_bits()), (1, plane_bits()[::-1])):
        held = {0: block[which * half : (which + 1) * half]}
        for bit in bits:
            order = sorted(held)
            got = along_plane(jnp.stack([held[j] for j in order]), bit)
            for n, j in enumerate(order):
                held[j ^ bit] = got[n]
        parts.append(held)
    return [jnp.concatenate([parts[0][j], parts[1][j]]) for j in range(lax.axis_size("fsdp"))]


def plane_reduce(partial):
    half = partial.shape[1] // 2
    done = []
    for which, bits in ((0, plane_bits()[::-1]), (1, plane_bits())):
        held = {j: partial[j, which * half : (which + 1) * half] for j in range(partial.shape[0])}
        for bit in bits:
            going = [j for j in sorted(held) if j & bit]
            got = along_plane(jnp.stack([held[j].astype(BF) for j in going]), bit)
            for n, j in enumerate(going):
                held[j ^ bit] = held[j ^ bit].astype(F32) + got[n].astype(F32)
                del held[j]
        done.append(held[0])
    return jnp.concatenate(done)


def line_sum(value):
    count = lax.axis_size("z")
    place = lax.axis_index("z")
    half = count // 2
    for i in range(half - 1):
        got = lax.ppermute(value, "z", [(i, i + 1), (count - 1 - i, count - 2 - i)])
        value = value + got
    value = value + lax.ppermute(value, "z", [(half - 1, half), (half, half - 1)])
    for i in range(half - 2, -1, -1):
        got = lax.ppermute(value, "z", [(i + 1, i), (count - 2 - i, count - 1 - i)])
        outer = (place == i) | (place == count - 1 - i)
        value = jnp.where(outer, got, value)
    return value


def move_kernel(idx_ref, x_ref, o_ref):
    o_ref[...] = x_ref[...]


def pick_columns(x, index, count):
    rows, width = x.shape
    size = width // count
    spec = pltpu.PrefetchScalarGridSpec(
        num_scalar_prefetch=1,
        grid=(count,),
        in_specs=[pl.BlockSpec((rows, size), lambda b, idx: (0, idx[b]))],
        out_specs=pl.BlockSpec((rows, size), lambda b, idx: (0, b)),
    )
    return pl.pallas_call(
        move_kernel,
        grid_spec=spec,
        out_shape=jax.ShapeDtypeStruct(x.shape, x.dtype),
        compiler_params=params(),
        name="pick_columns",
    )(index, x)


def put_columns(x, index, count):
    rows, width = x.shape
    size = width // count
    spec = pltpu.PrefetchScalarGridSpec(
        num_scalar_prefetch=1,
        grid=(count,),
        in_specs=[pl.BlockSpec((rows, size), lambda b, idx: (0, b))],
        out_specs=pl.BlockSpec((rows, size), lambda b, idx: (0, idx[b])),
    )
    return pl.pallas_call(
        move_kernel,
        grid_spec=spec,
        out_shape=jax.ShapeDtypeStruct(x.shape, x.dtype),
        compiler_params=params(),
        name="put_columns",
    )(index, x)


def cut_blocks(weight, f, k, count, dtype=BF):
    rows, full = weight.shape
    width, half = full // count, rows // 2
    if width % 128:
        own = lax.dynamic_slice_in_dim(weight, k * half, half, 0).reshape(half, count, width)
        return jnp.stack(
            [lax.dynamic_index_in_dim(own, f ^ j, 1, keepdims=False) for j in range(count)]
        )
    spec = pltpu.PrefetchScalarGridSpec(
        num_scalar_prefetch=1,
        grid=(count,),
        in_specs=[pl.BlockSpec((half, width), lambda j, at: (at[1], at[0] ^ j))],
        out_specs=pl.BlockSpec((None, half, width), lambda j, at: (j, 0, 0)),
    )
    return pl.pallas_call(
        move_kernel,
        grid_spec=spec,
        out_shape=jax.ShapeDtypeStruct((count, half, width), weight.dtype),
        compiler_params=params(),
        name="cut_blocks",
    )(jnp.stack([f, k]), weight)


def join_kernel(at_ref, own_ref, sib_ref, o_ref):
    @pl.when(pl.program_id(0) == 0)
    def _():
        o_ref[...] = own_ref[...].astype(o_ref.dtype)

    @pl.when(pl.program_id(0) == 1)
    def _():
        o_ref[...] = sib_ref[...].astype(o_ref.dtype)


def join_rows(own, sib, f, k):
    count, half, width = own.shape
    if width % 128:
        halves = jnp.stack([own, sib])
        return jnp.concatenate(
            [
                jnp.concatenate(
                    [
                        lax.dynamic_index_in_dim(
                            lax.dynamic_index_in_dim(halves, k ^ h, 0, keepdims=False),
                            f ^ i,
                            0,
                            keepdims=False,
                        )
                        for i in range(count)
                    ],
                    axis=1,
                )
                for h in range(2)
            ],
            axis=0,
        ).astype(F32)
    spec = pltpu.PrefetchScalarGridSpec(
        num_scalar_prefetch=1,
        grid=(2, count),
        in_specs=[
            pl.BlockSpec(
                (None, half, width),
                lambda s, i, at: (at[0] ^ jnp.where(s == 0, i, count - 1), 0, 0),
            ),
            pl.BlockSpec(
                (None, half, width), lambda s, i, at: (at[0] ^ jnp.where(s == 1, i, 0), 0, 0)
            ),
        ],
        out_specs=pl.BlockSpec((half, width), lambda s, i, at: (at[1] ^ s, i)),
    )
    return pl.pallas_call(
        join_kernel,
        grid_spec=spec,
        out_shape=jax.ShapeDtypeStruct((2 * half, count * width), F32),
        compiler_params=params(),
        name="join_rows",
    )(jnp.stack([f, k]), own, sib)


def join_columns(own, sib, k):
    rows, half = own.shape
    count = 4
    size = rows // count
    spec = pltpu.PrefetchScalarGridSpec(
        num_scalar_prefetch=1,
        grid=(2, count),
        in_specs=[
            pl.BlockSpec((size, half), lambda s, i, at: (jnp.where(s == 0, i, count - 1), 0)),
            pl.BlockSpec((size, half), lambda s, i, at: (jnp.where(s == 1, i, 0), 0)),
        ],
        out_specs=pl.BlockSpec((size, half), lambda s, i, at: (i, at[0] ^ s)),
    )
    return pl.pallas_call(
        join_kernel,
        grid_spec=spec,
        out_shape=jax.ShapeDtypeStruct((rows, 2 * half), F32),
        compiler_params=params(),
        name="join_columns",
    )(k.reshape(1), own, sib)


def swap_halves(block):
    lane = lax.broadcasted_iota(jnp.int32, block.shape, 1)
    return jnp.where(lane % 64 < 32, pltpu.roll(block, 96, 1), pltpu.roll(block, 32, 1))


def qkv_kernel(idx_ref, x_ref, gain_ref, w_ref, cos_ref, sin_ref, h_ref, q_ref, kv_ref):
    blocks = idx_ref.shape[0]
    size = x_ref.shape[1] // blocks
    x = x_ref[...].astype(F32)
    inverse = lax.rsqrt(jnp.mean(x * x, axis=1, keepdims=True) + EPSILON)
    for b in range(blocks):
        at = pl.ds(pl.multiple_of(idx_ref[b] * size, 128), size)
        part = x_ref[:, at].astype(F32) * inverse * gain_ref[:, at]
        h_ref[:, b * size : (b + 1) * size] = part.astype(BF)
    out = jnp.dot(h_ref[...], w_ref[...], preferred_element_type=F32)
    cosine, sine = cos_ref[...], sin_ref[...]
    pairs = q_ref.shape[1] // 128
    for c in range(pairs):
        block = out[:, c * 128 : (c + 1) * 128]
        q_ref[:, c * 128 : (c + 1) * 128] = (block * cosine + swap_halves(block) * sine).astype(BF)
    block = out[:, pairs * 128 :]
    lane = lax.broadcasted_iota(jnp.int32, block.shape, 1)
    turned = block * cosine + swap_halves(block) * sine
    kv_ref[...] = jnp.where(lane < 64, turned, block).astype(BF)


def qkv_project(idx, x, gain, weight, cosine, sine, rows):
    total, depth = x.shape
    width = weight.shape[1]
    spec = pltpu.PrefetchScalarGridSpec(
        num_scalar_prefetch=1,
        grid=(total // rows,),
        in_specs=[
            pl.BlockSpec((rows, depth), lambda i, idx: (i, 0)),
            pl.BlockSpec((1, depth), lambda i, idx: (0, 0)),
            pl.BlockSpec((depth, width), lambda i, idx: (0, 0)),
            pl.BlockSpec((rows, 128), lambda i, idx: (0, 0)),
            pl.BlockSpec((rows, 128), lambda i, idx: (0, 0)),
        ],
        out_specs=[
            pl.BlockSpec((rows, depth), lambda i, idx: (i, 0)),
            pl.BlockSpec((rows, width - 128), lambda i, idx: (i, 0)),
            pl.BlockSpec((rows, 128), lambda i, idx: (i, 0)),
        ],
    )
    return pl.pallas_call(
        qkv_kernel,
        grid_spec=spec,
        out_shape=[
            jax.ShapeDtypeStruct((total, depth), BF),
            jax.ShapeDtypeStruct((total, width - 128), BF),
            jax.ShapeDtypeStruct((total, 128), BF),
        ],
        compiler_params=params(),
        cost_estimate=pl.CostEstimate(
            flops=2 * total * depth * width,
            bytes_accessed=4 * total * depth + 2 * depth * width + 2 * total * width,
            transcendentals=0,
        ),
        name="qkv_project",
    )(idx, x, gain, weight, cosine, sine)


def nt(a, b):
    return lax.dot_general(a, b, (((1,), (1,)), ((), ())), preferred_element_type=F32)


def tn(a, b):
    return lax.dot_general(a, b, (((0,), (0,)), ((), ())), preferred_element_type=F32)


def nn(a, b):
    return jnp.dot(a, b, preferred_element_type=F32)


def limits(at_ref, rows):
    j = pl.program_id(0)
    place = at_ref[0] - lax.broadcasted_iota(jnp.int32, (rows, 1), 0)
    return jnp.minimum(place, at_ref[1 + j] - 1)


def attend_kernel(at_ref, q_ref, kv_ref, kp_ref, o_ref, lse_ref, vk_ref):
    rows = q_ref.shape[0]
    keys = vk_ref.shape[0]
    kv = kv_ref[...].reshape(keys, 128)

    @pl.when(pl.program_id(1) == 0)
    def _():
        vk_ref[...] = pltpu.roll(kv.astype(F32), 64, 1).astype(BF)

    vk = vk_ref[...]
    allowed = kp_ref[...] <= limits(at_ref, rows)
    lane = lax.broadcasted_iota(jnp.int32, (rows, 128), 1)
    q = q_ref[...]
    zero = jnp.zeros_like(q)
    outs, logs = [], []
    for first in (True, False):
        mine = lane < 64 if first else lane >= 64
        scores = nt(jnp.where(mine, q, zero), kv if first else vk) * (HEAD_DIM**-0.5)
        scores = jnp.where(allowed, scores, MASKED)
        top = jnp.max(scores, axis=1, keepdims=True)
        weights = jnp.exp(scores - top)
        total = jnp.sum(weights, axis=1, keepdims=True)
        outs.append(nn(weights.astype(BF), vk if first else kv) / total)
        logs.append(jnp.broadcast_to(top + jnp.log(total), (rows, 128)))
    o_ref[...] = jnp.where(lane < 64, outs[0], outs[1]).astype(BF)
    lse_ref[...] = jnp.where(lane < 64, logs[0], logs[1])


def attend(at, q, kv, kp):
    chunks, seqs, rows, _ = kv.shape
    pairs = q.shape[2] // 128
    keys = chunks * rows
    spec = pltpu.PrefetchScalarGridSpec(
        num_scalar_prefetch=1,
        grid=(seqs, pairs),
        in_specs=[
            pl.BlockSpec((None, rows, 128), lambda j, p, at: (j, 0, p)),
            pl.BlockSpec((chunks, None, rows, 128), lambda j, p, at: (0, j, 0, 0)),
            pl.BlockSpec((1, keys), lambda j, p, at: (0, 0)),
        ],
        out_specs=[
            pl.BlockSpec((None, rows, 128), lambda j, p, at: (j, 0, p)),
            pl.BlockSpec((None, rows, 128), lambda j, p, at: (j, 0, p)),
        ],
        scratch_shapes=[pltpu.VMEM((keys, 128), BF)],
    )
    size = seqs * pairs * 2 * rows * keys
    return pl.pallas_call(
        attend_kernel,
        grid_spec=spec,
        out_shape=[
            jax.ShapeDtypeStruct(q.shape, BF),
            jax.ShapeDtypeStruct(q.shape, F32),
        ],
        compiler_params=params(),
        cost_estimate=pl.CostEstimate(
            flops=size * 4 * 128, bytes_accessed=4 << 20, transcendentals=size
        ),
        name="attend",
    )(at, q, kv, kp)


def attend_back_kernel(
    at_ref, q_ref, do_ref, lse_ref, kv_ref, kp_ref, cos_ref, sin_ref, dq_ref, dkv_ref, vk_ref, dk_ref, dv_ref
):
    rows = q_ref.shape[0]
    keys = vk_ref.shape[0]
    pair = pl.program_id(1)
    kv = kv_ref[...].reshape(keys, 128)

    @pl.when(pair == 0)
    def _():
        vk_ref[...] = pltpu.roll(kv.astype(F32), 64, 1).astype(BF)
        dk_ref[...] = jnp.zeros_like(dk_ref)
        dv_ref[...] = jnp.zeros_like(dv_ref)

    vk = vk_ref[...]
    allowed = kp_ref[...] <= limits(at_ref, rows)
    lane = lax.broadcasted_iota(jnp.int32, (rows, 128), 1)
    q, do = q_ref[...], do_ref[...]
    zero = jnp.zeros_like(q)
    parts = []
    for first in (True, False):
        mine = lane < 64 if first else lane >= 64
        keyed, valued = (kv, vk) if first else (vk, kv)
        q_own, do_own = jnp.where(mine, q, zero), jnp.where(mine, do, zero)
        scores = nt(q_own, keyed) * (HEAD_DIM**-0.5)
        log_total = lse_ref[:, 0:1] if first else lse_ref[:, 64:65]
        weights = jnp.where(allowed, jnp.exp(scores - log_total), 0.0)
        joint = weights * nt(do_own, valued)
        back = (joint - weights * jnp.sum(joint, axis=1, keepdims=True)).astype(BF)
        parts.append(nn(back, keyed))
        dk_ref[...] += tn(back, q_own)
        dv_ref[...] += tn(weights.astype(BF), do_own)
    turned = jnp.where(lane < 64, parts[0], parts[1]) * (HEAD_DIM**-0.5)
    dq_ref[...] = (turned * cos_ref[...] - swap_halves(turned) * sin_ref[...]).astype(BF)

    @pl.when(pair == pl.num_programs(1) - 1)
    def _():
        dk = dk_ref[...]
        dv = dv_ref[...]
        dk = (dk + pltpu.roll(dk, 64, 1)) * (HEAD_DIM**-0.5)
        dv = dv + pltpu.roll(dv, 64, 1)
        wide = lax.broadcasted_iota(jnp.int32, dk.shape, 1)
        dkv_ref[...] = jnp.where(wide < 64, dk, dv).astype(BF).reshape(dkv_ref.shape)


def attend_back(at, q, do, lse, kv, kp, cosine, sine):
    chunks, seqs, rows, _ = kv.shape
    pairs = q.shape[2] // 128
    keys = chunks * rows
    tall = pl.BlockSpec((None, rows, 128), lambda j, p, at: (j, 0, p))
    whole = pl.BlockSpec((chunks, None, rows, 128), lambda j, p, at: (0, j, 0, 0))
    flat = pl.BlockSpec((rows, 128), lambda j, p, at: (0, 0))
    spec = pltpu.PrefetchScalarGridSpec(
        num_scalar_prefetch=1,
        grid=(seqs, pairs),
        in_specs=[tall, tall, tall, whole, pl.BlockSpec((1, keys), lambda j, p, at: (0, 0)), flat, flat],
        out_specs=[tall, whole],
        scratch_shapes=[
            pltpu.VMEM((keys, 128), BF),
            pltpu.VMEM((keys, 128), F32),
            pltpu.VMEM((keys, 128), F32),
        ],
    )
    size = seqs * pairs * 2 * rows * keys
    return pl.pallas_call(
        attend_back_kernel,
        grid_spec=spec,
        out_shape=[
            jax.ShapeDtypeStruct(q.shape, BF),
            jax.ShapeDtypeStruct(kv.shape, BF),
        ],
        compiler_params=params(),
        cost_estimate=pl.CostEstimate(
            flops=size * 10 * 128, bytes_accessed=8 << 20, transcendentals=size
        ),
        name="attend_back",
    )(at, q, do, lse, kv, kp, cosine, sine)


def rms_backward(row_block, inverse, gain_vec, gradient):
    normed = row_block * inverse
    gain_grad = jnp.sum(gradient * normed, axis=0)
    scaled = gradient * gain_vec
    back = inverse * (scaled - normed * jnp.mean(scaled * normed, axis=1, keepdims=True))
    return (back, gain_grad)


def body_plain(
    tokens, cotangent, lengths, attn_gain, w_query, w_key, w_value, w_out, mlp_gain, w_gate, w_up, w_down
):
    seqs, rows, depth = tokens.shape
    count, line = lax.axis_size("fsdp"), lax.axis_size("z")
    f, z, k = lax.axis_index("fsdp"), lax.axis_index("z"), lax.axis_index("core")
    slot = rows * line * 2
    total = count * rows
    slab = depth // count
    half = slab // 2
    q_width = HEADS * HEAD_DIM // count
    shared = max(1, count // KV_HEADS)

    x_own = tokens.reshape(rows, depth)
    chunk = 2 * z + k
    first_pos = slot - 1 - chunk * rows

    length = lengths[0]
    words = jnp.zeros((slab,), F32).at[0].set((length // 64).astype(F32)).at[1].set((length % 64).astype(F32))
    note = jnp.stack([attn_gain, mlp_gain, words.astype(BF), jnp.zeros((slab,), BF)])
    notes = [note] + [along_plane(note, j) for j in range(1, count)]
    notes_abs = [lax.dynamic_index_in_dim(jnp.stack(notes), f ^ i, 0, keepdims=False) for i in range(count)]
    gain_one = jnp.concatenate([n[0] for n in notes_abs]).astype(F32).reshape(1, depth)
    gain_two = jnp.concatenate([n[1] for n in notes_abs]).astype(F32).reshape(1, depth)
    all_lengths = jnp.stack(
        [n[2, 0].astype(jnp.int32) * 64 + n[2, 1].astype(jnp.int32) for n in notes]
    )

    x_all = jnp.concatenate(plane_gather(x_own))

    wq = cut_blocks(w_query, f, k, count)
    key_cols = lax.dynamic_slice_in_dim(w_key, k * half, half, 0).reshape(half, KV_HEADS, HEAD_DIM)
    value_cols = lax.dynamic_slice_in_dim(w_value, k * half, half, 0).reshape(half, KV_HEADS, HEAD_DIM)

    def head_of(j):
        return (f ^ j) // shared

    wkv = jnp.stack(
        [
            jnp.concatenate(
                [
                    lax.dynamic_index_in_dim(key_cols, head_of(j), 1, keepdims=False),
                    lax.dynamic_index_in_dim(value_cols, head_of(j), 1, keepdims=False),
                ],
                axis=1,
            )
            for j in range(count)
        ]
    )
    wqkv = jnp.concatenate([wq, wkv], axis=2)
    wqkv_own = jnp.stack([wqkv[0]] + [along_plane(wqkv[j], j) for j in range(1, count)])
    wqkv_sib = to_sibling(wqkv_own)
    wqkv_all = jnp.concatenate([wqkv_own, wqkv_sib]).reshape(depth, q_width + 128)

    def fetch(weight):
        cut = cut_blocks(weight, f, k, count)
        width = cut.shape[2]
        own = jnp.stack([cut[0]] + [along_plane(cut[j], j) for j in range(1, count)])
        sib = to_sibling(own)
        return own.reshape(depth // 2, width), sib.reshape(depth // 2, width)

    gate_own, gate_sib = fetch(w_gate)
    up_own, up_sib = fetch(w_up)

    order = jnp.stack([(f ^ j) * 2 + (k ^ h) for h in range(2) for j in range(count)]).astype(jnp.int32)

    half_dim = HEAD_DIM // 2
    frequency = jnp.power(ROPE_BASE, jnp.arange(half_dim, dtype=F32) * (-2.0 / HEAD_DIM))
    positions = first_pos - jnp.arange(rows, dtype=jnp.int32)
    angles = positions.astype(F32)[:, None] * frequency[None, :]
    cos32, sin32 = jnp.cos(angles), jnp.sin(angles)
    cosine = jnp.concatenate([cos32] * 4, axis=1)
    sine = jnp.concatenate([-sin32, sin32, -sin32, sin32], axis=1)

    normed_one, queries, kv = qkv_project(order, x_all, gain_one, wqkv_all, cosine, sine, rows)
    queries = queries.reshape(count, rows, q_width)
    kv = kv.reshape(count, rows, 128)

    mine = [kv] + [along_line(kv, -s) for s in range(1, line)]
    mine = jnp.stack(mine)
    kv_all = jnp.concatenate([mine, to_sibling(mine)])
    places = []
    for h in range(2):
        for s in range(line):
            start = slot - 1 - (2 * (z + s) + (k ^ h)) * rows
            places.append(start - jnp.arange(rows, dtype=jnp.int32))
    kp = jnp.concatenate(places)
    kp = jnp.where(kp < 0, FAR, kp).reshape(1, -1)
    at = jnp.concatenate([first_pos.reshape(1), all_lengths]).astype(jnp.int32)

    attended, log_total = attend(at, queries, kv_all, kp)
    attended = attended.reshape(total, q_width)

    mixed_part = nn(attended, w_out).astype(BF).reshape(count, rows, depth)
    inputs = x_own.astype(F32)
    mixed = inputs + plane_reduce(mixed_part)
    inv_two = lax.rsqrt(jnp.mean(mixed * mixed, axis=1, keepdims=True) + EPSILON)
    normed_two_own = (mixed * inv_two * gain_two).astype(BF)
    normed_two = jnp.concatenate(plane_gather(normed_two_own))
    normed_two = pick_columns(normed_two, order, 2 * count)
    n2_own, n2_sib = normed_two[:, : depth // 2], normed_two[:, depth // 2 :]

    valid = (positions < length).astype(F32)[:, None]
    out_back = cotangent.reshape(rows, depth).astype(F32) * valid
    branch_own = out_back.astype(BF)
    branch = jnp.concatenate(plane_gather(branch_own))

    gate = nn(n2_own, gate_own) + nn(n2_sib, gate_sib)
    up = nn(n2_own, up_own) + nn(n2_sib, up_sib)
    sigmoid = jax.nn.sigmoid(gate)
    hidden = (gate * sigmoid * up).astype(BF)

    half_depth = depth // 2
    branch_mine = lax.dynamic_slice_in_dim(branch, k * half_depth, half_depth, 1)
    branch_other = lax.dynamic_slice_in_dim(branch, (1 - k) * half_depth, half_depth, 1)

    def pair_sum(own, other):
        return (own + to_sibling(other.astype(BF)).astype(F32)).astype(BF)

    def swap_slabs(own):
        return jnp.stack([own[0]] + [along_plane(own[j], j) for j in range(1, count)])

    down_half = line_sum(pair_sum(tn(hidden, branch_mine), tn(hidden, branch_other)))
    down_grad = join_columns(down_half, to_sibling(down_half), k)

    hidden_grad = nt(branch, w_down)
    gate_back = (hidden_grad * up * sigmoid * (1.0 + gate * (1.0 - sigmoid))).astype(BF)
    up_back = (hidden_grad * gate * sigmoid).astype(BF)

    def slab_grad(left_own, left_other, right):
        width = right.shape[1]
        own = pair_sum(tn(left_own, right), tn(left_other, right)).reshape(count, half, width)
        return line_sum(swap_slabs(own))

    gate_half = slab_grad(n2_own, n2_sib, gate_back)
    gate_grad = join_rows(gate_half, to_sibling(gate_half), f, k)
    up_half = slab_grad(n2_own, n2_sib, up_back)
    up_grad = join_rows(up_half, to_sibling(up_half), f, k)

    back_own = (nt(gate_back, gate_own) + nt(up_back, up_own)).astype(BF)
    back_sib = (nt(gate_back, gate_sib) + nt(up_back, up_sib)).astype(BF)
    normed_back = put_columns(jnp.concatenate([back_own, back_sib], axis=1), order, 2 * count)
    normed_back = plane_reduce(normed_back.reshape(count, rows, depth))

    out_part = nn(hidden, w_down).astype(BF).reshape(count, rows, depth)
    outputs = mixed + plane_reduce(out_part)

    mixed_back, gain_two_grad = rms_backward(mixed, inv_two, gain_two, normed_back)
    mixed_grad = out_back + mixed_back
    attn_back = jnp.concatenate(plane_gather(mixed_grad.astype(BF)))
    attended_grad = nt(attn_back, w_out).astype(BF).reshape(count, rows, q_width)

    back_mine = lax.dynamic_slice_in_dim(attn_back, k * half_depth, half_depth, 1)
    back_other = lax.dynamic_slice_in_dim(attn_back, (1 - k) * half_depth, half_depth, 1)
    out_half = line_sum(pair_sum(tn(attended, back_mine), tn(attended, back_other)))
    out_grad = join_columns(out_half, to_sibling(out_half), k)

    query_back, kv_part = attend_back(at, queries, attended_grad, log_total, kv_all, kp, cosine, sine)
    kv_mine = kv_part[:line].astype(F32) + to_sibling(kv_part[line:]).astype(F32)
    kv_back = kv_mine[0]
    for s in range(1, line):
        kv_back = kv_back + along_line(kv_mine[s].astype(BF), s).astype(F32)
    lead, trail, flat = kv_back[..., :32], kv_back[..., 32:64], kv_back[..., 64:]
    kv_back = jnp.concatenate(
        [lead * cos32 + trail * sin32, trail * cos32 - lead * sin32, flat], axis=-1
    ).astype(BF)
    qkv_back = jnp.concatenate(
        [query_back.reshape(total, q_width), kv_back.reshape(total, 128)], axis=1
    )

    normed_one_back = nt(qkv_back, wqkv_all).astype(BF)
    normed_one_back = put_columns(normed_one_back, order, 2 * count)
    normed_one_back = plane_reduce(normed_one_back.reshape(count, rows, depth))
    inv_one = lax.rsqrt(jnp.mean(inputs * inputs, axis=1, keepdims=True) + EPSILON)
    input_back, gain_one_grad = rms_backward(inputs, inv_one, gain_one, normed_one_back)
    input_grad = mixed_grad + input_back

    n1_own, n1_sib = normed_one[:, :half_depth], normed_one[:, half_depth:]
    qkv_own = pair_sum(tn(n1_own, qkv_back), tn(n1_sib, qkv_back)).reshape(count, half, q_width + 128)
    gains = jnp.stack([gain_one_grad, gain_two_grad]).reshape(2, count, slab)
    gains = jnp.stack(
        [lax.dynamic_index_in_dim(gains, f ^ j, 1, keepdims=False) for j in range(count)]
    ).astype(BF)
    gains = line_sum(swap_slabs(gains))
    qkv_half = line_sum(swap_slabs(qkv_own))
    gains = jnp.sum(gains.astype(F32), axis=0) + jnp.sum(to_sibling(gains).astype(F32), axis=0)
    qkv_other = to_sibling(qkv_half)
    query_grad = join_rows(qkv_half[:, :, :q_width], qkv_other[:, :, :q_width], f, k)
    halves = jnp.stack([qkv_half[:, :, q_width:], qkv_other[:, :, q_width:]])

    def by_head(lo, hi):
        both = [lax.dynamic_index_in_dim(halves, k ^ h, 0, keepdims=False) for h in range(2)]
        both = jnp.concatenate(both, axis=1).astype(F32)[:, :, lo:hi]
        cols = jnp.stack([lax.dynamic_index_in_dim(both, f ^ i, 0, keepdims=False) for i in range(count)])
        cols = cols.reshape(KV_HEADS, shared, slab, HEAD_DIM).sum(1)
        return jnp.transpose(cols, (1, 0, 2)).reshape(slab, KV_HEADS * HEAD_DIM)

    key_grad = by_head(0, 64)
    value_grad = by_head(64, 128)

    return (
        outputs.reshape(seqs, rows, depth),
        input_grad.reshape(seqs, rows, depth),
        gains[0],
        query_grad,
        key_grad,
        value_grad,
        out_grad,
        gains[1],
        gate_grad,
        up_grad,
        down_grad,
    )


def rotary_parts(slot, rows):
    lane = np.arange(128) % (HEAD_DIM // 2)
    frequency = ROPE_BASE ** (lane * (-2.0 / HEAD_DIM))
    starts = (slot - 1 - rows * np.arange(slot // rows))[:, None] * frequency[None, :]
    steps = np.arange(rows)[:, None] * frequency[None, :]
    return [jnp.asarray(t(a), F32) for a in (starts, steps) for t in (np.cos, np.sin)]


def front_kernel(
    length_ref, both_gains, start_cos, start_sin, step_cos, step_sin,
    tokens, cotangent, w_query, w_key, w_value, w_out, w_gate, w_up, w_down,
    h1_out, queries_out, lse_out, attended_out, mixed_out, n2_out, limits_out, cosine_out, sine_out, kp_out,
    gain_one_out, gain_two_out, kv_out, branch_out, wqkv_out, gate_back_out, up_back_out, hidden_out,
    gate_own_out, gate_sib_out, up_own_out, up_sib_out,
    h1, queries, lse, attended, mixed, n2, limits, cosine, sine, kp, gain_one, gain_two,
    gate_back, up_back, hidden, grad,
    notes, x_all, wqkv, keys_in, values_in, kv_give, gate_own, gate_sib, up_own, up_sib, down,
    kv_all, vk, w_o, part, landed, relay, relayed, n2_all, branch_all, cot_in,
    local_s, store_s, note_s, note_r, tok_s, tok_r, tof_s, tof_r, wq_s, wq_r, wk_s, wk_r, wp_s, wp_r, wkp_s, wkp_r,
    kz_s, kz_r, kp_s, kp_r, gt_s, gt_r, up_s, up_r, gz_s, gz_r, gs_s, gs_r, us_s, us_r,
    bt_s, bt_r, btf_s, btf_r, mx_s, mx_r, nt_s, nt_r, ntf_s, ntf_r,
):
    f, z, k = lax.axis_index("fsdp"), lax.axis_index("z"), lax.axis_index("core")
    plane, line = 4, 4
    rows, depth = tokens.shape
    total = plane * rows
    slab = depth // plane
    half = slab // 2
    hr = rows // 2
    q_width = w_out.shape[0]
    pairs = q_width // 128
    ff = w_down.shape[0]
    keys = vk.shape[0]
    slot = rows * line * 2
    even = z % 2 == 0
    across = z + 1 - 2 * (z % 2)
    peers = (1, 2, 3)
    first_pos = slot - 1 - (2 * z + k) * rows

    def remote(source, target, send, recv, where):
        return pltpu.make_async_remote_copy(
            src_ref=source,
            dst_ref=target,
            send_sem=send,
            recv_sem=recv,
            device_id=where,
            device_id_type=pl.DeviceIdType.MESH,
        )

    sib = {"core": 1 - k}

    def chip(j):
        return {"fsdp": f ^ j}

    def cols(weight, j, side, width):
        start = pl.multiple_of((f ^ j) * width, 128)
        return weight.at[pl.ds(pl.multiple_of((k ^ side) * half, 16), half), pl.ds(start, width)]

    class Gather:
        def __init__(self, source, target, send, recv, fsend, frecv):
            self.near = {
                j: remote(source, target.at[j], send.at[j - 1], recv.at[j - 1], chip(j)) for j in (1, 2)
            }
            self.far = {
                j: remote(
                    target.at[j, pl.ds((j - 1) * hr, hr), :],
                    target.at[3, pl.ds((j - 1) * hr, hr), :],
                    fsend.at[j - 1],
                    frecv.at[j - 1],
                    chip(3 - j),
                )
                for j in (1, 2)
            }

        def start(self):
            for j in (1, 2):
                self.near[j].start()

        def forward(self):
            for j in (1, 2):
                self.near[j].wait_recv()
                self.far[j].start()

        def arrive(self):
            for j in (1, 2):
                self.far[j].wait_recv()

        def close(self):
            for j in (1, 2):
                self.near[j].wait_send()
                self.far[j].wait_send()

    def note_send(j):
        return remote(notes.at[0], notes.at[j], note_s.at[j - 1], note_r.at[j - 1], chip(j))

    token_gather = Gather(tokens, x_all, tok_s, tok_r, tof_s, tof_r)
    branch_gather = Gather(branch_all.at[0], branch_all, bt_s, bt_r, btf_s, btf_r)
    n2_gather = Gather(n2_all.at[0], n2_all, nt_s, nt_r, ntf_s, ntf_r)

    def wq_send(j):
        target = wqkv.at[pl.ds(j * half, half), pl.ds(0, q_width)]
        return remote(cols(w_query, j, 0, q_width), target, wq_s.at[j - 1], wq_r.at[j - 1], chip(j))

    def wk_send(j):
        target = wqkv.at[pl.ds(j * half, half), pl.ds(q_width, 128)]
        return remote(kv_give.at[j], target, wk_s.at[j - 1], wk_r.at[j - 1], chip(j))

    def wp_send(j):
        source = wqkv.at[pl.ds(j * half, half), :]
        target = wqkv.at[pl.ds((plane + j) * half, half), :]
        return remote(source, target, wp_s.at[j - 1], wp_r.at[j - 1], sib)

    def kv_send(s):
        return remote(kv_all.at[0], kv_all.at[s], kz_s.at[s - 1], kz_r.at[s - 1], {"z": z - s})

    def kv_pair(s):
        return remote(kv_all.at[s], kv_all.at[line + s], kp_s.at[s], kp_r.at[s], sib)

    def gate_send(j):
        return remote(cols(w_gate, j, 0, ff), gate_own.at[j], gt_s.at[j - 1], gt_r.at[j - 1], chip(j))

    def up_send(j):
        return remote(cols(w_up, j, 0, ff), up_own.at[j], up_s.at[j - 1], up_r.at[j - 1], chip(j))

    def gate_across(j):
        return remote(gate_own.at[j], gate_own.at[j], gz_s.at[j - 1], gz_r.at[j - 1], {"z": across})

    def up_across(j):
        return remote(up_own.at[j], up_own.at[j], gz_s.at[j - 1], gz_r.at[j - 1], {"z": across})

    def by_parity(act_even, act_odd):
        @pl.when(even)
        def _():
            act_even()

        @pl.when(jnp.logical_not(even))
        def _():
            act_odd()

    def fetch_start():
        by_parity(
            lambda: [gate_send(j).start() for j in (3, 1, 2)], lambda: [up_send(j).start() for j in (3, 1, 2)]
        )

    def fetch_on(j):
        def gate_on():
            gate_send(j).wait_recv()
            gate_across(j).start()
            gate_pair(j).start()

        def up_on():
            up_send(j).wait_recv()
            up_across(j).start()
            up_pair(j).start()

        by_parity(gate_on, up_on)

    def cross_on(j):
        def up_on():
            up_across(j).wait_recv()
            up_pair(j).start()

        def gate_on():
            gate_across(j).wait_recv()
            gate_pair(j).start()

        by_parity(up_on, gate_on)

    def gate_pair(j):
        return remote(gate_own.at[j], gate_sib.at[j], gs_s.at[j - 1], gs_r.at[j - 1], sib)

    def up_pair(j):
        return remote(up_own.at[j], up_sib.at[j], us_s.at[j - 1], us_r.at[j - 1], sib)

    def span(which):
        return pl.ds(which * hr, hr)

    mix_first = {
        "one": remote(part.at[1, span(0), :], landed.at[0, span(0), :], mx_s.at[0], mx_r.at[0], chip(1)),
        "two": remote(part.at[2, span(1), :], landed.at[1, span(1), :], mx_s.at[1], mx_r.at[1], chip(2)),
        "far_one": remote(part.at[3, span(0), :], relay.at[0], mx_s.at[2], mx_r.at[2], chip(1)),
        "far_two": remote(part.at[3, span(1), :], relay.at[1], mx_s.at[3], mx_r.at[3], chip(2)),
        "late_two": remote(relayed.at[0], landed.at[1, span(0), :], mx_s.at[4], mx_r.at[4], chip(2)),
        "late_one": remote(relayed.at[1], landed.at[0, span(1), :], mx_s.at[5], mx_r.at[5], chip(1)),
    }

    local = [
        pltpu.make_async_copy(source, target, local_s.at[n])
        for n, (source, target) in enumerate(
            [
                (tokens, x_all.at[0]),
                (w_key, keys_in),
                (w_value, values_in),
                (cols(w_query, 0, 0, q_width), wqkv.at[pl.ds(0, half), pl.ds(0, q_width)]),
                (cols(w_query, 0, 1, q_width), wqkv.at[pl.ds(plane * half, half), pl.ds(0, q_width)]),
                (cotangent, cot_in),
                (w_out, w_o),
                (cols(w_gate, 0, 0, ff), gate_own.at[0]),
                (cols(w_gate, 0, 1, ff), gate_sib.at[0]),
                (cols(w_up, 0, 0, ff), up_own.at[0]),
                (cols(w_up, 0, 1, ff), up_sib.at[0]),
                (w_down, down),
            ]
        )
    ]

    stored = [
        (h1, h1_out), (queries, queries_out), (lse, lse_out), (attended, attended_out), (mixed, mixed_out),
        (n2, n2_out), (limits, limits_out), (cosine, cosine_out), (sine, sine_out), (kp, kp_out),
        (gain_one, gain_one_out), (gain_two, gain_two_out), (kv_all, kv_out), (branch_all, branch_out),
        (wqkv, wqkv_out), (gate_back, gate_back_out), (up_back, up_back_out), (hidden, hidden_out),
        (gate_own, gate_own_out), (gate_sib, gate_sib_out), (up_own, up_own_out), (up_sib, up_sib_out),
    ]

    def store(n):
        return pltpu.make_async_copy(*stored[n], store_s.at[n])

    length = length_ref[0]
    place = lax.broadcasted_iota(jnp.int32, (16, slab), 0)
    high, low = (length // 64).astype(F32), (length % 64).astype(F32)
    note = jnp.where(place == 0, both_gains[0:1, :].astype(F32), both_gains[1:2, :].astype(F32))
    note = jnp.where(place == 2, high, jnp.where(place == 3, low, note))
    notes[0] = note.astype(BF)
    for j in peers:
        note_send(j).start()
    token_gather.start()
    for j in (3, 1, 2):
        wq_send(j).start()
    for copy in local:
        copy.start()

    local[1].wait()
    local[2].wait()

    def head_columns(j, side):
        at = pl.ds(pl.multiple_of((k ^ side) * half, 16), half)
        head = f ^ j
        width = KV_HEADS * HEAD_DIM
        key = pltpu.roll(keys_in[at, :].astype(F32), (width - head * 64) % width, 1)[:, :128]
        value = pltpu.roll(values_in[at, :].astype(F32), (width - head * 64 + 64) % width, 1)[:, :128]
        lane = lax.broadcasted_iota(jnp.int32, key.shape, 1)
        return jnp.where(lane < 64, key, value).astype(BF)

    for j in (3, 1, 2):
        kv_give[j] = head_columns(j, 0)
        wk_send(j).start()
    wqkv[0:half, q_width : q_width + 128] = head_columns(0, 0)
    wqkv[plane * half : (plane + 1) * half, q_width : q_width + 128] = head_columns(0, 1)

    chunk = pl.ds(2 * z + k, 1)
    cos_at, sin_at = start_cos[chunk, :], start_sin[chunk, :]
    lane = lax.broadcasted_iota(jnp.int32, (rows, 128), 1)
    cosine[...] = cos_at * step_cos[...] + sin_at * step_sin[...]
    turn = sin_at * step_cos[...] - cos_at * step_sin[...]
    sine[...] = jnp.where(lane % 64 < 32, -turn, turn)
    for h in range(2):
        for s in range(line):
            start = slot - 1 - (2 * (z + s) + (k ^ h)) * rows
            spot = start - lax.broadcasted_iota(jnp.int32, (8, rows), 1)
            spot = jnp.where(spot < 0, FAR, spot).astype(F32)
            kp[:, (h * line + s) * rows : (h * line + s + 1) * rows] = spot

    for s in range(1, line):

        @pl.when(z + s >= line)
        def _():
            kv_all[s] = jnp.zeros(kv_all.shape[1:], BF)
            kv_all[line + s] = jnp.zeros(kv_all.shape[1:], BF)

    local[5].wait()
    row_pos = (first_pos - lax.broadcasted_iota(jnp.int32, (rows, 1), 0)).astype(F32)
    valid = row_pos < jnp.full((rows, 1), length.astype(F32))
    branch_all[0] = jnp.where(valid, cot_in[...].astype(F32), 0.0).astype(BF)

    token_gather.forward()
    for j in (1, 2, 3):
        wq_send(j).wait_recv()
        wk_send(j).wait_recv()
        wp_send(j).start()

    fetch_start()

    for j in peers:
        note_send(j).wait_recv()
    for j in range(plane):
        at = pl.ds(pl.multiple_of((f ^ j) * slab, 128), slab)
        gain_one[:, at] = jnp.broadcast_to(notes[j, 0:1, :].astype(F32), (8, slab))
        gain_two[:, at] = jnp.broadcast_to(notes[j, 1:2, :].astype(F32), (8, slab))
        theirs = notes[j, 2:3, 0:1].astype(F32) * 64.0 + notes[j, 3:4, 0:1].astype(F32)
        limits[j] = jnp.broadcast_to(jnp.minimum(row_pos, theirs - 1.0), (rows, 128))

    def normalize(j, x_ref):
        @pl.loop(0, rows // 16)
        def _(i):
            at = pl.ds(pl.multiple_of(i * 16, 16), 16)
            x = x_ref[at, :].astype(F32)
            inverse = lax.rsqrt(jnp.mean(x * x, axis=1, keepdims=True) + EPSILON)
            to = pl.ds(pl.multiple_of(j * rows + i * 16, 16), 16)
            for h in range(2):
                for b in range(plane):
                    from_ = pl.ds(pl.multiple_of(((f ^ b) * 2 + (k ^ h)) * half, 128), half)
                    value = x_ref[at, from_].astype(F32) * inverse * gain_one[0:1, from_]
                    c = (h * plane + b) * half
                    h1[to, c : c + half] = value.astype(BF)

    local[0].wait()
    normalize(0, x_all.at[0])
    normalize(1, x_all.at[1])
    normalize(2, x_all.at[2])
    token_gather.arrive()
    normalize(3, x_all.at[3])
    local[3].wait()
    local[4].wait()
    for j in (1, 2, 3):
        wp_send(j).wait_recv()

    kv_cols = nn(h1[...], wqkv[:, q_width : q_width + 128])
    for j in range(plane):
        value = kv_cols[j * rows : (j + 1) * rows]
        turned = value * cosine[...] + swap_halves(value) * sine[...]
        kv_all[0, j] = jnp.where(lane < 64, turned, value).astype(BF)
    for s in range(1, line):

        @pl.when(z >= s)
        def _():
            kv_send(s).start()

    kv_pair(0).start()
    branch_gather.start()

    @pl.loop(0, pairs // 2)
    def _(p):
        at = pl.ds(pl.multiple_of(p * 256, 256), 256)
        out = nn(h1[...], wqkv[:, at])
        for j in range(plane):
            for c in range(2):
                value = out[j * rows : (j + 1) * rows, c * 128 : (c + 1) * 128]
                turned = value * cosine[...] + swap_halves(value) * sine[...]
                queries[j, :, pl.ds(pl.multiple_of(p * 256 + c * 128, 128), 128)] = turned.astype(BF)

    for s in range(1, line):

        @pl.when(z + s < line)
        def _():
            kv_send(s).wait_recv()
            kv_pair(s).start()

    fetch_on(1)
    fetch_on(2)
    kv_pair(0).wait_recv()
    for s in range(1, line):

        @pl.when(z + s < line)
        def _():
            kv_pair(s).wait_recv()

    local[6].wait()

    def by_columns(act):
        @pl.loop(0, ff // 256)
        def _(n):
            act(pl.ds(pl.multiple_of(n * 256, 256), 256))

        if ff % 256:
            act(pl.ds(ff // 256 * 256, ff % 256))

    def relay_on(far, late, which, j):
        mix_first[far].wait_recv()
        value = relay[which].astype(F32) + part[j, which * hr : (which + 1) * hr, :].astype(F32)
        relayed[which] = value.astype(BF)
        mix_first[late].start()

    @pl.loop(0, plane)
    def _(t):
        j = plane - 1 - t
        here = pl.ds(pl.multiple_of(j * rows, 16), rows)
        vk[...] = pltpu.roll(kv_all[:, j].reshape(keys, 128).astype(F32), 64, 1).astype(BF)
        limit = limits[j, :, 0:1]

        @pl.loop(0, pairs)
        def _(p):
            at = pl.ds(pl.multiple_of(p * 128, 128), 128)
            allowed = kp[0:1, :] <= limit
            q = queries[j, :, at]
            zero = jnp.zeros_like(q)
            outs, logs = [], []
            for first in (True, False):
                mine = lane < 64 if first else lane >= 64
                kv = kv_all[:, j].reshape(keys, 128)
                keyed, valued = (kv, vk[...]) if first else (vk[...], kv)
                scores = nt(jnp.where(mine, q, zero), keyed) * (HEAD_DIM**-0.5)
                scores = jnp.where(allowed, scores, MASKED)
                top = jnp.max(scores, axis=1, keepdims=True)
                weights = jnp.exp(scores - top)
                sums = jnp.sum(weights, axis=1, keepdims=True)
                outs.append(nn(weights.astype(BF), valued) / sums)
                logs.append(jnp.broadcast_to(top + jnp.log(sums), (rows, 128)))
            attended[here, at] = jnp.where(lane < 64, outs[0], outs[1]).astype(BF)
            lse[j, :, at] = jnp.where(lane < 64, logs[0], logs[1])

        part[j] = nn(attended[here, :], w_o[...]).astype(BF)

        @pl.when(t == 0)
        def _():
            mix_first["far_one"].start()
            mix_first["far_two"].start()
            branch_gather.forward()

        @pl.when(t == 1)
        def _():
            mix_first["two"].start()
            fetch_on(3)

        @pl.when(t == 2)
        def _():
            mix_first["one"].start()
            relay_on("far_one", "late_two", 0, 2)
            relay_on("far_two", "late_one", 1, 1)

    early_stores = [store(n) for n in range(12)]
    for n in (0, 1, 2, 3, 6, 7, 8, 9, 10, 11):
        early_stores[n].start()
    cross_on(1)
    cross_on(2)
    for name in ("one", "late_one", "two", "late_two"):
        mix_first[name].wait_recv()

    @pl.loop(0, rows // 16)
    def _(i):
        at = pl.ds(pl.multiple_of(i * 16, 16), 16)
        value = x_all[0, at, :].astype(F32) + part[0, at, :].astype(F32)
        value = value + landed[0, at, :].astype(F32) + landed[1, at, :].astype(F32)
        mixed[at, :] = value
        inverse = lax.rsqrt(jnp.mean(value * value, axis=1, keepdims=True) + EPSILON)
        n2_all[0, at, :] = (value * inverse * gain_two[0:1, :]).astype(BF)

    n2_gather.start()
    early_stores[4].start()
    branch_gather.arrive()
    local[11].wait()

    def down_grad(at):
        grad[:, at] = nt(branch_all[...].reshape(total, depth), down[at, :])

    by_columns(down_grad)
    n2_gather.forward()
    cross_on(3)
    for n in range(7, 11):
        local[n].wait()
    for j in peers:
        gate_pair(j).wait_recv()
        up_pair(j).wait_recv()
    weight_stores = [store(n) for n in range(18, 22)]
    for copy in weight_stores:
        copy.start()
    n2_gather.arrive()

    @pl.loop(0, total // 16)
    def _(i):
        at = pl.ds(pl.multiple_of(i * 16, 16), 16)
        j = i // (rows // 16)
        from_row = pl.ds(pl.multiple_of((i % (rows // 16)) * 16, 16), 16)
        for h in range(2):
            for b in range(plane):
                from_ = pl.ds(pl.multiple_of(((f ^ b) * 2 + (k ^ h)) * half, 128), half)
                c = (h * plane + b) * half
                n2[at, c : c + half] = n2_all[j, from_row, from_]

    early_stores[5].start()
    later = [store(n) for n in range(12, 18)]
    for n in range(3):
        later[n].start()

    def feed(at):
        width = at.size
        n2_own, n2_sib = n2[:, 0 : depth // 2], n2[:, depth // 2 : depth]

        def through(own, other):
            first = nn(n2_own, own[:, :, at].reshape(depth // 2, width))
            return first + nn(n2_sib, other[:, :, at].reshape(depth // 2, width))

        gate = through(gate_own, gate_sib)
        up = through(up_own, up_sib)
        sigmoid = 1.0 / (1.0 + jnp.exp(-gate))
        hidden[:, at] = (gate * sigmoid * up).astype(BF)
        back = grad[:, at]
        gate_back[:, at] = (back * up * sigmoid * (1.0 + gate * (1.0 - sigmoid))).astype(BF)
        up_back[:, at] = (back * gate * sigmoid).astype(BF)

    by_columns(feed)
    for n in range(3, 6):
        later[n].start()
    for gather in (token_gather, branch_gather, n2_gather):
        gather.close()
    for copy in mix_first.values():
        copy.wait_send()
    for j in peers:
        note_send(j).wait_send()
        wq_send(j).wait_send()
        wk_send(j).wait_send()
        wp_send(j).wait_send()
        gate_pair(j).wait_send()
        up_pair(j).wait_send()
    by_parity(
        lambda: [c(j).wait_send() for j in peers for c in (gate_send, gate_across)],
        lambda: [c(j).wait_send() for j in peers for c in (up_send, up_across)],
    )

    kv_pair(0).wait_send()
    for s in range(1, line):

        @pl.when(z >= s)
        def _():
            kv_send(s).wait_send()

        @pl.when(z + s < line)
        def _():
            kv_pair(s).wait_send()

    for copy in early_stores + later + weight_stores:
        copy.wait()


def front_pass(tokens, cotangent, lengths, attn_gain, mlp_gain, w_query, w_key, w_value, w_out, w_gate, w_up, w_down):
    rows, depth = tokens.shape
    plane, line = 4, 4
    total, slab = plane * rows, depth // plane
    half = slab // 2
    q_width = HEADS * HEAD_DIM // plane
    width = q_width + 128
    ff = w_down.shape[0]
    slot = rows * line * 2
    keys = slot
    act = (rows, depth)
    local = pl.BlockSpec(memory_space=pltpu.VMEM)
    anywhere = pl.BlockSpec(memory_space=pl.ANY)
    dma = lambda n: pltpu.SemaphoreType.DMA((n,))
    kv_shape = (2 * line, plane, rows, 128)
    sds = jax.ShapeDtypeStruct
    outs = [
        sds((total, depth), BF),
        sds((plane, rows, q_width), BF),
        sds((plane, rows, q_width), F32),
        sds((total, q_width), BF),
        sds(act, F32),
        sds((total, depth), BF),
        sds((plane, rows, 128), F32),
        sds((rows, 128), F32),
        sds((rows, 128), F32),
        sds((8, keys), F32),
        sds((8, depth), F32),
        sds((8, depth), F32),
        sds(kv_shape, BF),
        sds((plane,) + act, BF),
        sds((depth, width), BF),
        sds((total, ff), BF),
        sds((total, ff), BF),
        sds((total, ff), BF),
    ] + [sds((plane, half, ff), BF)] * 4
    held = [pltpu.VMEM(o.shape, o.dtype) for o in outs]
    held = held[:12] + held[15:18] + [pltpu.VMEM((total, ff), F32)]
    slabs = pltpu.VMEM((plane, half, ff), BF)
    scratch = held + [
        pltpu.VMEM((plane, 16, slab), BF),
        pltpu.VMEM((plane,) + act, BF),
        pltpu.VMEM((depth, width), BF),
        pltpu.VMEM(w_key.shape, BF),
        pltpu.VMEM(w_value.shape, BF),
        pltpu.VMEM((plane, half, 128), BF),
        slabs,
        slabs,
        slabs,
        slabs,
        pltpu.VMEM(w_down.shape, BF),
        pltpu.VMEM(kv_shape, BF),
        pltpu.VMEM((keys, 128), BF),
        pltpu.VMEM(w_out.shape, BF),
        pltpu.VMEM((plane,) + act, BF),
        pltpu.VMEM((2,) + act, BF),
        pltpu.VMEM((2, rows // 2, depth), BF),
        pltpu.VMEM((2, rows // 2, depth), BF),
        pltpu.VMEM((plane,) + act, BF),
        pltpu.VMEM((plane,) + act, BF),
        pltpu.VMEM(act, BF),
    ]
    sems = [12, 22, 3, 3, 2, 2, 2, 2, 3, 3, 3, 3, 3, 3, 1, 1, 3, 3, 4, 4, 3, 3, 3, 3, 3, 3, 3, 3, 3, 3]
    sems += [2, 2, 2, 2, 6, 6, 2, 2, 2, 2]
    return pl.pallas_call(
        front_kernel,
        out_shape=outs,
        in_specs=[pl.BlockSpec(memory_space=pltpu.SMEM)] + [local] * 5 + [anywhere] * 9,
        out_specs=[anywhere] * 22,
        scratch_shapes=scratch + [dma(n) for n in sems],
        compiler_params=pltpu.CompilerParams(
            vmem_limit_bytes=62 * 1024 * 1024, has_side_effects=True
        ),
        name="front_pass",
    )(
        lengths, jnp.stack([attn_gain, mlp_gain]), *rotary_parts(slot, rows),
        tokens, cotangent, w_query, w_key, w_value, w_out, w_gate, w_up, w_down,
    )


def add_into(target, other):
    @pl.loop(0, target.shape[0] // 16)
    def _(i):
        at = pl.ds(pl.multiple_of(i * 16, 16), 16)
        target[at, :] = (target[at, :].astype(F32) + other[at, :].astype(F32)).astype(BF)


def back_kernel(
    limits_in, gate_back_in, up_back_in, hidden_in, mixed_in, x_own_in, gain_one_in, gain_two_in,
    attended_in, queries_in, lse_in, kv_all_in, kp_in, cosine_in, sine_in,
    branch, w_out, w_down, wqkv, h1_hbm, n2_hbm, gate_own, gate_sib, up_own, up_sib,
    fin_down, fin_gate, fin_up, fin_out, fin_qkv, fin_gain,
    sib_down, sib_gate, sib_up, sib_out, sib_qkv, sib_gain,
    outputs, input_grad_out,
    limits, gate_back, up_back, hidden, mixed, x_own, gain_one, gain_two,
    attended, queries, lse, kv_all, kp, cosine, sine, branch_own, input_grad,
    src_down, src_gate, src_up, src_out, src_qkv, src_gain,
    swap_gate, swap_up, swap_qkv,
    end_down, end_gate, end_up, end_out, end_qkv, end_gain,
    give_down, give_gate, give_out, give_qkv, give_gain,
    landed, landed_out, weights, down_blocks, qkv_blocks, part, da_all, wide, do_all, dqkv, left,
    vk, dk_sum, dv_sum, kv_part, kv_land, kv_mine, kv_line, gain_acc, gain_all,
    pair_s, pair_r, swap_s, swap_r, in_s, in_r, mid_s, mid_r, out_s, done_s, back_s, back_r, ready,
    local_s, weight_s, rs_s, rs_r, ro_s, ro_r, ag_s, ag_r, rq_s, rq_r, kp_s, kp_r, kz_s, kz_r, ga_s, ga_r,
):
    f, z, k = lax.axis_index("fsdp"), lax.axis_index("z"), lax.axis_index("core")
    plane, line = lax.axis_size("fsdp"), lax.axis_size("z")
    branch_flat = branch
    outer = (z == 0) | (z == line - 1)
    inner = jnp.logical_not(outer)
    inward = jnp.where(z < line // 2, z + 1, z - 1)
    outward = jnp.where(z < line // 2, z - 1, z + 1)
    rows, depth = mixed.shape
    total = plane * rows
    half_depth = depth // 2
    half = half_depth // plane
    q_width = attended.shape[1]
    pairs = q_width // 128
    peers = range(1, plane)

    kinds = {
        "down": (src_down, None, end_down, give_down, fin_down, sib_down),
        "gate": (src_gate, swap_gate, end_gate, give_gate, fin_gate, sib_gate),
        "up": (src_up, swap_up, end_up, give_gate, fin_up, sib_up),
        "out": (src_out, None, end_out, give_out, fin_out, sib_out),
        "qkv": (src_qkv, swap_qkv, end_qkv, give_qkv, fin_qkv, sib_qkv),
        "gain": (src_gain, None, end_gain, give_gain, fin_gain, sib_gain),
    }
    chunks = [(name, i) for name, kind in kinds.items() for i in range(kind[0].shape[0])]
    count = len(chunks)

    def group(c):
        return kinds[chunks[c][0]][3].shape[0]

    heads = [c for c in range(count) if chunks[c][1] % group(c) == 0]

    def remote(source, target, send, recv, where):
        return pltpu.make_async_remote_copy(
            src_ref=source,
            dst_ref=target,
            send_sem=send,
            recv_sem=recv,
            device_id=where,
            device_id_type=pl.DeviceIdType.MESH,
        )

    def swapped(c):
        name, i = chunks[c]
        return i // group(c) if kinds[name][1] is not None else 0

    def source(c):
        return part_of(c, 0)

    def part_of(c, which):
        name, i = chunks[c]
        return kinds[name][which].at[i]

    def given(c):
        return kinds[chunks[c][0]][3]

    def end(c):
        return part_of(c, 2)

    def pair_copy(c):
        start = given(c).at[chunks[c][1] % group(c)]
        return remote(start, source(c), pair_s.at[c], pair_r.at[c], {"core": 1 - k})

    def landing(c):
        name, i = chunks[c]
        return kinds[name][1].at[i - group(c)]

    def swap_copy(c):
        return remote(source(c), landing(c), swap_s.at[c], swap_r.at[c], {"fsdp": f ^ swapped(c)})

    def base(c):
        return landing(c) if swapped(c) else source(c)

    def in_copy(c):
        return remote(base(c), end(c), in_s.at[c], in_r.at[c], {"z": inward})

    def mid_copy(c):
        return remote(base(c), end(c), mid_s.at[c], mid_r.at[c], {"z": inward})

    def out_copy(c):
        return remote(end(c), end(c), out_s.at[c], mid_r.at[c], {"z": outward})

    def keep_copy(c):
        return pltpu.make_async_copy(end(c), part_of(c, 4), done_s.at[c])

    def back_copy(c):
        return remote(end(c), part_of(c, 5), back_s.at[c], back_r.at[c], {"core": 1 - k})

    own_cols = pl.ds(pl.multiple_of(k * half_depth, 128), half_depth)
    other_cols = pl.ds(pl.multiple_of((1 - k) * half_depth, 128), half_depth)

    def slab_term(i, side, right):
        start = side * half_depth + i * (half // 2)
        return tn(left[:, start : start + half], right)

    def term(c, side):
        name, i = chunks[c]
        if name == "down":
            right = wide[0:total, (own_cols, other_cols)[side]]
            return tn(hidden[:, i * 128 : (i + 1) * 128], right)
        if name == "gate":
            return slab_term(i, side, gate_back[...])
        if name == "up":
            return slab_term(i, side, up_back[...])
        if name == "qkv":
            return slab_term(i, side, dqkv[...])
        if name == "out":
            size = src_out.shape[1]
            right = da_all[:, :, (own_cols, other_cols)[side]].reshape(total, half_depth)
            return tn(attended[:, i * size : (i + 2) * size], right)
        return gain_all[...].astype(F32).sum(axis=0)

    def stage_give(c):
        slots = given(c)
        if c and given(c - 1) is slots:
            for n in range(group(c)):
                pair_copy(c - 1 - n).wait_send()
        slots[...] = term(c, 1).astype(BF).reshape(slots.shape)
        for n in range(group(c)):
            pair_copy(c + n).start()

    def stage_pair(c):
        value = term(c, 0)
        size = value.shape[0] // group(c)
        for n in range(group(c)):
            pair_copy(c + n).wait_recv()
            target = source(c + n)
            target[...] = (target[...].astype(F32) + value[n * size : (n + 1) * size]).astype(BF)
            if swapped(c + n):
                swap_copy(c + n).start()

    def stage_in(c):
        if swapped(c):
            swap_copy(c).wait_recv()

        @pl.when(outer)
        def _():
            in_copy(c).start()

    def stage_mid(c):
        @pl.when(inner)
        def _():
            in_copy(c).wait_recv()
            add_into(base(c), end(c))
            pl.semaphore_signal(
                ready, inc=1, device_id={"z": inward}, device_id_type=pl.DeviceIdType.MESH
            )
            pl.semaphore_wait(ready, 1)
            mid_copy(c).start()

    def stage_out(c):
        @pl.when(inner)
        def _():
            mid_copy(c).wait_recv()
            add_into(end(c), base(c))
            out_copy(c).start()

    def stage_keep(c):
        @pl.when(outer)
        def _():
            out_copy(c).wait_recv()

        keep_copy(c).start()
        back_copy(c).start()

    def back_send(j):
        mine = part.at[pl.ds(j * rows, rows), :]
        return remote(mine, landed.at[j - 1], rs_s.at[j - 1], rs_r.at[j - 1], {"fsdp": f ^ j})

    def out_send(j):
        mine = part.at[pl.ds(j * rows, rows), :]
        return remote(mine, landed_out.at[j - 1], ro_s.at[j - 1], ro_r.at[j - 1], {"fsdp": f ^ j})

    def da_send(j):
        return remote(da_all.at[0], da_all.at[j], ag_s.at[j - 1], ag_r.at[j - 1], {"fsdp": f ^ j})

    def dh_send(j):
        mine = wide.at[pl.ds(j * rows, rows), :]
        return remote(mine, landed.at[j - 1], rq_s.at[j - 1], rq_r.at[j - 1], {"fsdp": f ^ j})

    def gain_send(j):
        return remote(gain_all.at[0], gain_all.at[j], ga_s.at[j - 1], ga_r.at[j - 1], {"fsdp": f ^ j})

    moves = {
        "branch": (branch_flat, wide.at[pl.ds(0, total), :]), "hidden": (hidden_in, hidden), "n2": (n2_hbm, left),
        "gate_back": (gate_back_in, gate_back), "up_back": (up_back_in, up_back), "mixed": (mixed_in, mixed),
        "branch_own": (branch_flat.at[pl.ds(0, rows), :], branch_own), "gain_two": (gain_two_in, gain_two),
        "queries": (queries_in, queries), "lse": (lse_in, lse), "kv_all": (kv_all_in, kv_all),
        "limits": (limits_in, limits), "kp": (kp_in, kp), "cosine": (cosine_in, cosine), "sine": (sine_in, sine),
        "attended": (attended_in, attended), "x_own": (x_own_in, x_own), "gain_one": (gain_one_in, gain_one),
        "w_out": (w_out, wide.at[pl.ds(0, w_out.shape[0]), :]), "h1": (h1_hbm, left),
        "outputs": (mixed, outputs), "input_grad": (input_grad, input_grad_out),
    }
    moves = {
        name: pltpu.make_async_copy(*ends, local_s.at[n]) for n, (name, ends) in enumerate(moves.items())
    }

    def weight_loads(h, j):
        pairs_of = ((gate_own, up_own), (gate_sib, up_sib))[h]
        return [
            pltpu.make_async_copy(w.at[j], weights.at[j % 2, n], weight_s.at[j % 2, n])
            for n, w in enumerate(pairs_of)
        ]

    def columns_of(h, j):
        return pl.ds(pl.multiple_of(((f ^ j) * 2 + (k ^ h)) * half, 128), half)

    def piece_back(h):
        @pl.loop(0, plane)
        def _(j):
            @pl.when(j + 1 < plane)
            def _():
                for copy in weight_loads(h, j + 1):
                    copy.start()

            for copy in weight_loads(h, j):
                copy.wait()
            value = nt(gate_back[...], weights[j % 2, 0]) + nt(up_back[...], weights[j % 2, 1])
            part[:, columns_of(h, j)] = value.astype(BF)

        if h == 0:
            for copy in weight_loads(1, 0):
                copy.start()
        if h == 1:
            for j in peers:
                back_send(j).start()

    def down_at(b):
        size = depth // 8
        return pl.ds(pl.multiple_of(b * size, size), size)

    def down_load(b):
        return pltpu.make_async_copy(w_down.at[:, down_at(b)], down_blocks.at[b % 2], weight_s.at[b % 2, 0])

    def piece_out(h):
        if h == 0:
            for j in peers:
                back_send(j).wait_send()
            down_load(0).start()

        @pl.loop(4 * h, 4 * h + 4)
        def _(b):
            @pl.when(b + 1 < 8)
            def _():
                down_load(b + 1).start()

            down_load(b).wait()
            part[:, down_at(b)] = nn(hidden[...], down_blocks[b % 2]).astype(BF)

        if h == 1:
            for j in peers:
                out_send(j).start()

    def dh_load(b):
        block = wqkv.at[pl.ds(pl.multiple_of(b * half, half), half), :]
        return pltpu.make_async_copy(block, qkv_blocks.at[b % 2], weight_s.at[b % 2, 0])

    def rms_back(gradient_of, x_ref, gain, acc, write):
        acc[...] = jnp.zeros_like(acc)

        @pl.loop(0, rows // 16)
        def _(i):
            at = pl.ds(pl.multiple_of(i * 16, 16), 16)
            gradient = gradient_of(at)
            x = x_ref[at, :].astype(F32)
            inverse = lax.rsqrt(jnp.mean(x * x, axis=1, keepdims=True) + EPSILON)
            normed = x * inverse
            acc[...] += gradient * normed
            scaled = gradient * gain[0:1, :]
            write(at, inverse * (scaled - normed * jnp.mean(scaled * normed, axis=1, keepdims=True)))

    def piece_mixed():
        for name in ("mixed", "branch_own", "gain_two"):
            moves[name].wait()
        for j in peers:
            back_send(j).wait_recv()

        def gradient_of(at):
            value = part[at, :].astype(F32)
            for j in peers:
                value = value + landed[j - 1, at, :].astype(F32)
            return value

        def write(at, value):
            value = value + branch_own[at, :].astype(F32)
            input_grad[at, :] = value
            da_all[0, at, :] = value.astype(BF)

        rms_back(gradient_of, mixed, gain_two, gain_acc.at[1], write)
        for j in peers:
            da_send(j).start()

    def piece_do():
        moves["w_out"].wait()
        for j in peers:
            da_send(j).wait_recv()

        @pl.loop(0, plane)
        def _(j):
            do_all[j] = nt(da_all[j], wide[0 : w_out.shape[0], :]).astype(BF)

    def piece_attend(j0):
        @pl.loop(j0, j0 + 2)
        def _(j):
            attend_one(j)

    def attend_one(j):
        here = pl.ds(pl.multiple_of(j * rows, 16), rows)
        vk[...] = pltpu.roll(kv_all[:, j].reshape(vk.shape).astype(F32), 64, 1).astype(BF)
        dk_sum[...] = jnp.zeros_like(dk_sum)
        dv_sum[...] = jnp.zeros_like(dv_sum)
        limit = limits[j, :, 0:1]
        lane = lax.broadcasted_iota(jnp.int32, (rows, 128), 1)

        @pl.loop(0, pairs)
        def _(p):
            at = pl.ds(pl.multiple_of(p * 128, 128), 128)
            allowed = kp[0:1, :] <= limit
            q, do = queries[j, :, at], do_all[j, :, at]
            logs = lse[j, :, at]
            zero = jnp.zeros_like(q)
            parts = []
            for first in (True, False):
                mine = lane < 64 if first else lane >= 64
                kv = kv_all[:, j].reshape(vk.shape)
                keyed, valued = (kv, vk[...]) if first else (vk[...], kv)
                q_own, do_own = jnp.where(mine, q, zero), jnp.where(mine, do, zero)
                scores = nt(q_own, keyed) * (HEAD_DIM**-0.5)
                log_total = logs[:, 0:1] if first else logs[:, 64:65]
                weights = jnp.where(allowed, jnp.exp(scores - log_total), 0.0)
                joint = weights * nt(do_own, valued)
                back = (joint - weights * jnp.sum(joint, axis=1, keepdims=True)).astype(BF)
                parts.append(nn(back, keyed))
                dk_sum[...] += tn(back, q_own)
                dv_sum[...] += tn(weights.astype(BF), do_own)
            turned = jnp.where(lane < 64, parts[0], parts[1]) * (HEAD_DIM**-0.5)
            turned = turned * cosine[...] - swap_halves(turned) * sine[...]
            dqkv[here, at] = turned.astype(BF)

        dk = dk_sum[...]
        dv = dv_sum[...]
        dk = (dk + pltpu.roll(dk, 64, 1)) * (HEAD_DIM**-0.5)
        dv = dv + pltpu.roll(dv, 64, 1)
        wide_lane = lax.broadcasted_iota(jnp.int32, dk.shape, 1)
        packed = jnp.where(wide_lane < 64, dk, dv).astype(BF)
        kv_part[:, j] = packed.reshape(kv_part.shape[0], rows, 128)

    kv_pair = remote(kv_part.at[pl.ds(line, line)], kv_land, kp_s.at[0], kp_r.at[0], {"core": 1 - k})

    def kv_send(s):
        return remote(kv_mine.at[s], kv_line.at[s - 1], kz_s.at[s - 1], kz_r.at[s - 1], {"z": z + s})

    def piece_kv_line():
        kv_pair.wait_recv()
        for s in range(line):
            kv_mine[s] = (kv_part[s].astype(F32) + kv_land[s].astype(F32)).astype(BF)
        for s in range(1, line):

            @pl.when(z + s < line)
            def _():
                kv_send(s).start()

    def piece_kv_sum():
        for s in range(1, line):

            @pl.when(z >= s)
            def _():
                kv_send(s).wait_recv()
                kv_mine[0] = (kv_mine[0].astype(F32) + kv_line[s - 1].astype(F32)).astype(BF)

        lane = lax.broadcasted_iota(jnp.int32, (rows, 128), 1)
        for j in range(plane):
            value = kv_mine[0, j].astype(F32)
            turned = value * cosine[...] - swap_halves(value) * sine[...]
            value = jnp.where(lane < 64, turned, value).astype(BF)
            dqkv[j * rows : (j + 1) * rows, q_width : q_width + 128] = value

    def piece_dh():
        dh_load(0).start()

        @pl.loop(0, 2 * plane)
        def _(b):
            @pl.when(b + 1 < 2 * plane)
            def _():
                dh_load(b + 1).start()

            dh_load(b).wait()
            wide[0:total, columns_of(b // plane, b % plane)] = nt(dqkv[...], qkv_blocks[b % 2]).astype(BF)

        for j in peers:
            dh_send(j).start()

    def piece_input():
        for name in ("x_own", "gain_one"):
            moves[name].wait()
        for j in peers:
            dh_send(j).wait_recv()

        def gradient_of(at):
            value = wide[at, :].astype(F32)
            for j in peers:
                value = value + landed[j - 1, at, :].astype(F32)
            return value

        def write(at, value):
            input_grad[at, :] = input_grad[at, :] + value

        rms_back(gradient_of, x_own, gain_one, gain_acc.at[0], write)
        moves["input_grad"].start()
        place = lax.broadcasted_iota(jnp.int32, (16, depth), 0)
        one = jnp.sum(gain_acc[0], axis=0, keepdims=True)
        two = jnp.sum(gain_acc[1], axis=0, keepdims=True)
        gain_all[0] = jnp.where(place == 0, one, jnp.where(place == 1, two, 0.0)).astype(BF)
        for j in peers:
            gain_send(j).start()

    def piece_outputs():
        for j in peers:
            out_send(j).wait_recv()

        @pl.loop(0, rows // 16)
        def _(i):
            at = pl.ds(pl.multiple_of(i * 16, 16), 16)
            value = mixed[at, :] + part[at, :].astype(F32)
            for j in peers:
                value = value + landed_out[j - 1, at, :].astype(F32)
            mixed[at, :] = value

        moves["outputs"].start()

    def piece_gain():
        for j in peers:
            gain_send(j).wait_recv()

    in_lag, mid_lag, out_lag, keep_lag = LAGS
    events = []

    def give_tick(c):
        return c - (AHEAD[1] if kinds[chunks[c][0]][1] is not None else AHEAD[0])

    for c in heads:
        events.append((give_tick(c), 0, stage_give, c))
        events.append((give_tick(c) + 1, 1, stage_pair, c))
    for c in range(count):
        events.append((c + in_lag, 2, stage_in, c))
        events.append((c + mid_lag, 3, stage_mid, c))
        events.append((c + out_lag, 4, stage_out, c))
        events.append((c + keep_lag, 5, stage_keep, c))
    steps = (
        (piece_back, 0), (piece_back, 1), piece_mixed, piece_do, (piece_out, 0), (piece_out, 1), (piece_attend, 0),
        (piece_attend, 2), kv_pair.start, piece_kv_line, piece_kv_sum, piece_dh, piece_outputs, piece_input, piece_gain,
    )
    for n, (step, tick) in enumerate(zip(steps, STEPS)):
        act, which = step if isinstance(step, tuple) else (step, None)
        events.append((tick, 6 + n, act, which))

    def head_of(name, which):
        return [c for c in heads if chunks[c][0] == name][which]

    def wait_for(*names):
        def act():
            for name in names:
                moves[name].wait()

        return act

    events.append((give_tick(head_of("down", 0)), -1, wait_for("branch", "hidden"), None))
    first = min(STEPS[0], give_tick(head_of("gate", 0)))
    events.append((first, 5.2, wait_for("n2", "gate_back", "up_back"), None))
    events.append((give_tick(head_of("down", -1)) + 1, 31, moves["w_out"].start, None))
    events.append((give_tick(head_of("up", -1)) + 1, 31, moves["h1"].start, None))
    events.append((give_tick(head_of("qkv", 0)), -1, moves["h1"].wait, None))
    events.append((give_tick(head_of("out", 0)), -1, moves["attended"].wait, None))
    attending = ("queries", "lse", "kv_all", "limits", "kp", "cosine", "sine")
    events.append((STEPS[6], 5.5, wait_for(*attending), None))
    events.sort(key=lambda e: e[:2])

    for name, move in moves.items():
        if name not in ("w_out", "h1", "outputs", "input_grad"):
            move.start()
    for copy in weight_loads(0, 0):
        copy.start()
    for _, _, act, which in events:
        act() if which is None else act(which)

    for c in range(count):
        if not [n for n in heads if n > c and given(n) is given(c)]:
            pair_copy(c).wait_send()
        if swapped(c):
            swap_copy(c).wait_send()
        keep_copy(c).wait()
        back_copy(c).wait_send()
        back_copy(c).wait_recv()

        @pl.when(outer)
        def _():
            in_copy(c).wait_send()

        @pl.when(inner)
        def _():
            mid_copy(c).wait_send()
            out_copy(c).wait_send()

    moves["outputs"].wait()
    moves["input_grad"].wait()
    for j in peers:
        out_send(j).wait_send()
        da_send(j).wait_send()
        dh_send(j).wait_send()
        gain_send(j).wait_send()
    kv_pair.wait_send()
    for s in range(1, line):

        @pl.when(z + s < line)
        def _():
            kv_send(s).wait_send()


def back_pass(held, far):
    count, line = lax.axis_size("fsdp"), lax.axis_size("z")
    mixed, attended, kv_all, hidden = held[4], held[8], held[11], held[3]
    rows, depth = mixed.shape
    total, half_depth = count * rows, depth // 2
    half = half_depth // count
    q_width = attended.shape[1]
    ff = hidden.shape[1]
    keys = kv_all.shape[0] * rows
    slabs = (2 * count, half // 2, ff)
    shapes = [
        (ff // 128, 128, half_depth),
        slabs,
        slabs,
        (4, q_width // 4, half_depth),
        (2 * count, half // 2, q_width + 128),
        (1, 16, depth),
    ]
    anywhere = pl.BlockSpec(memory_space=pl.ANY)
    ends = [jax.ShapeDtypeStruct(s, BF) for s in shapes]
    act = jax.ShapeDtypeStruct((rows, depth), F32)
    block = (rows, depth)
    chunk_count = sum(s[0] for s in shapes)
    dma = lambda *n: pltpu.SemaphoreType.DMA(n)
    groups = (1, 2, 2, 2, 1)
    scratch = (
        [pltpu.VMEM(x.shape, x.dtype) for x in held]
        + [pltpu.VMEM(block, BF), pltpu.VMEM(block, F32)]
        + [pltpu.VMEM(s, BF) for s in shapes]
        + [pltpu.VMEM((shapes[i][0] - 2,) + shapes[i][1:], BF) for i in (1, 2, 4)]
        + [pltpu.VMEM(s, BF) for s in shapes]
        + [pltpu.VMEM((g,) + shapes[i][1:], BF) for g, i in zip(groups, (0, 1, 3, 4, 5))]
        + [
            pltpu.VMEM((count - 1,) + block, BF),
            pltpu.VMEM((count - 1,) + block, BF),
            pltpu.VMEM((2, 2, half, ff), BF),
            pltpu.VMEM((2, ff, depth // 8), BF),
            pltpu.VMEM((2, half, q_width + 128), BF),
            pltpu.VMEM((total, depth), BF),
            pltpu.VMEM((count,) + block, BF),
            pltpu.VMEM((max(total, q_width), depth), BF),
            pltpu.VMEM((count, rows, q_width), BF),
            pltpu.VMEM((total, q_width + 128), BF),
            pltpu.VMEM((total, depth), BF),
            pltpu.VMEM((keys, 128), BF),
            pltpu.VMEM((keys, 128), F32),
            pltpu.VMEM((keys, 128), F32),
            pltpu.VMEM(kv_all.shape, BF),
            pltpu.VMEM((line,) + kv_all.shape[1:], BF),
            pltpu.VMEM((line,) + kv_all.shape[1:], BF),
            pltpu.VMEM((line - 1,) + kv_all.shape[1:], BF),
            pltpu.VMEM((2, 16, depth), F32),
            pltpu.VMEM((count, 16, depth), BF),
        ]
        + [dma(chunk_count)] * 12
        + [pltpu.SemaphoreType.REGULAR, dma(22), dma(2, 2)]
        + [dma(count - 1)] * 8
        + [dma(1)] * 2
        + [dma(line - 1)] * 2
        + [dma(count - 1)] * 2
    )
    out = pl.pallas_call(
        back_kernel,
        out_shape=ends + ends + [act, act],
        in_specs=[anywhere] * (len(held) + len(far)),
        out_specs=[anywhere] * 14,
        scratch_shapes=scratch,
        compiler_params=pltpu.CompilerParams(
            vmem_limit_bytes=63 * 1024 * 1024, has_side_effects=True
        ),
        name="back_pass",
    )(*held, *far)
    return out[:6], out[6:12], out[12], out[13]


def finish_kernel(
    own_down, own_gate, own_up, own_out, own_qkv, own_gain, sib_down, sib_gate, sib_up, sib_out, sib_qkv,
    outputs_in, input_grad_in, outputs, input_grad, down, gate, up, out, query, key, value, attn_gain, mlp_gain,
    low_rows, low_cols, high_rows, high_cols, kv, acts, gain_in, gain_high, load_s, store_s, side_s,
):
    f, k = lax.axis_index("fsdp"), lax.axis_index("core")
    plane = lax.axis_size("fsdp")
    half, ff = own_gate.shape[1], own_gate.shape[2]
    half_depth = own_down.shape[2]
    slab = 2 * half
    q_width = own_qkv.shape[2] - 128
    tasks = []
    for side, (d, o, g, u, q) in enumerate(
        ((own_down, own_out, own_gate, own_up, own_qkv), (sib_down, sib_out, sib_gate, sib_up, sib_qkv))
    ):
        rows_at = pl.ds(pl.multiple_of((k ^ side) * half, 8), half)
        cols_at = pl.ds(pl.multiple_of((k ^ side) * half_depth, 128), half_depth)
        for source, target in ((d, down), (o, out)):
            for i in range(source.shape[0]):
                size = source.shape[1]
                tasks.append((source.at[i], target.at[pl.ds(i * size, size), cols_at], 0))
        for source, target in ((g, gate), (u, up)):
            for j in range(plane):
                to = pl.ds(pl.multiple_of((f ^ j) * ff, 128), ff)
                tasks.append((source.at[j], target.at[rows_at, to], 1))
        for j in range(plane):
            to = pl.ds(pl.multiple_of((f ^ j) * q_width, 128), q_width)
            tasks.append((q.at[j, :, pl.ds(0, q_width)], query.at[rows_at, to], 1))
    slots = low_rows.shape[0]

    def window(buffer, n, shape):
        return buffer.at[n % slots, pl.ds(0, shape[0]), pl.ds(0, shape[1])]

    def load(n):
        source, _, kind = tasks[n]
        low = (low_rows, low_cols)[kind]
        return pltpu.make_async_copy(source, window(low, n, source.shape), load_s.at[n])

    def store(n):
        source, target, kind = tasks[n]
        high = (high_rows, high_cols)[kind]
        return pltpu.make_async_copy(window(high, n, source.shape), target, store_s.at[n])

    sides = [
        pltpu.make_async_copy(own_gain.at[0], gain_in, side_s.at[0]),
        pltpu.make_async_copy(own_qkv.at[:, :, pl.ds(q_width, 128)], kv.at[0], side_s.at[1]),
        pltpu.make_async_copy(sib_qkv.at[:, :, pl.ds(q_width, 128)], kv.at[1], side_s.at[2]),
        pltpu.make_async_copy(outputs_in, acts.at[0], side_s.at[3]),
        pltpu.make_async_copy(input_grad_in, acts.at[1], side_s.at[4]),
    ]
    for n in range(slots):
        load(n).start()
    for copy in sides:
        copy.start()
    for n in range(len(tasks)):
        source, _, kind = tasks[n]
        shape = source.shape
        low, high = ((low_rows, high_rows), (low_cols, high_cols))[kind]
        load(n).wait()
        if n >= slots:
            store(n - slots).wait()

        @pl.loop(0, shape[0] // 16)
        def _(i):
            at = pl.ds(pl.multiple_of(i * 16, 16), 16)
            high[n % slots, at, 0 : shape[1]] = low[n % slots, at, 0 : shape[1]].astype(F32)

        store(n).start()
        if n + slots < len(tasks):
            load(n + slots).start()
    for copy in sides:
        copy.wait()
    lasts = [
        pltpu.make_async_copy(acts.at[0], outputs, side_s.at[5]),
        pltpu.make_async_copy(acts.at[1], input_grad, side_s.at[6]),
    ]
    for copy in lasts:
        copy.start()
    mine = pl.ds(pl.multiple_of(f * slab, 128), slab)
    gain_high[...] = gain_in[...].astype(F32)
    attn_gain[...] = gain_high[0:1, mine]
    mlp_gain[...] = gain_high[1:2, mine]
    lane = lax.broadcasted_iota(jnp.int32, (half, 128), 1)
    for side in range(2):
        rows_at = pl.ds(pl.multiple_of((k ^ side) * half, 8), half)
        for pair in range(plane // 2):
            first = kv[side, f ^ (2 * pair)].astype(F32)
            second = kv[side, f ^ (2 * pair + 1)].astype(F32)
            at = slice(pair * 128, (pair + 1) * 128)
            key[rows_at, at] = jnp.where(lane < 64, first, pltpu.roll(second, 64, 1))
            value[rows_at, at] = jnp.where(lane < 64, pltpu.roll(first, 64, 1), second)
    for n in range(max(0, len(tasks) - slots), len(tasks)):
        store(n).wait()
    for copy in lasts:
        copy.wait()


def finish(owns, sibs, outputs, input_grad):
    plane = lax.axis_size("fsdp")
    down, gate, _, out, qkv, gain = (x.shape for x in owns)
    depth = 2 * down[2]
    slab = 2 * gate[1]
    q_width = qkv[2] - 128
    sds = jax.ShapeDtypeStruct
    shapes = [
        outputs.shape, input_grad.shape,
        (down[0] * down[1], depth), (slab, plane * gate[2]), (slab, plane * gate[2]), (out[0] * out[1], depth),
        (slab, plane * q_width), (slab, KV_HEADS * HEAD_DIM), (slab, KV_HEADS * HEAD_DIM), (1, slab), (1, slab),
    ]
    slots = 4
    tall = (slots, max(down[1], out[1]), down[2])
    wide = (slots, gate[1], max(gate[2], q_width))
    count = 2 * (down[0] + out[0] + 3 * plane)
    anywhere, local = pl.BlockSpec(memory_space=pl.ANY), pl.BlockSpec(memory_space=pltpu.VMEM)
    return pl.pallas_call(
        finish_kernel,
        out_shape=[sds(s, F32) for s in shapes],
        in_specs=[anywhere] * 13,
        out_specs=[anywhere] * 7 + [local] * 4,
        scratch_shapes=[
            pltpu.VMEM(tall, BF),
            pltpu.VMEM(wide, BF),
            pltpu.VMEM(tall, F32),
            pltpu.VMEM(wide, F32),
            pltpu.VMEM((2, plane, gate[1], 128), BF),
            pltpu.VMEM((2,) + outputs.shape, F32),
            pltpu.VMEM(gain[1:], BF),
            pltpu.VMEM(gain[1:], F32),
            pltpu.SemaphoreType.DMA((count,)),
            pltpu.SemaphoreType.DMA((count,)),
            pltpu.SemaphoreType.DMA((7,)),
        ],
        compiler_params=params(),
        name="finish",
    )(*owns, *sibs[:5], outputs, input_grad)


def body(
    tokens, cotangent, lengths, attn_gain, w_query, w_key, w_value, w_out, mlp_gain, w_gate, w_up, w_down
):
    seqs, rows, depth = tokens.shape
    count = lax.axis_size("fsdp")
    slab = depth // count
    x_own = tokens.reshape(rows, depth)
    (
        h1, queries, lse, attended, mixed, n2, limits, cosine, sine, kp, gain_one, gain_two, kv_all, branch, wqkv,
        gate_back, up_back, hidden, gate_own, gate_sib, up_own, up_sib,
    ) = front_pass(
        x_own, cotangent.reshape(rows, depth), lengths, attn_gain, mlp_gain,
        w_query, w_key, w_value, w_out, w_gate, w_up, w_down,
    )
    held = (
        limits, gate_back, up_back, hidden, mixed, x_own, gain_one, gain_two,
        attended, queries, lse, kv_all, kp, cosine, sine,
    )
    branch = branch.reshape(count * rows, depth)
    far = (branch, w_out, w_down, wqkv, h1, n2, gate_own, gate_sib, up_own, up_sib)
    owns, sibs, outputs, input_grad = back_pass(held, far)

    def whole(x):
        return x.reshape(4, -1, x.shape[2]) if x.shape[0] > 1 else x

    owns, sibs = [whole(x) for x in owns], [whole(x) for x in sibs]
    (
        outputs, input_grad, down_grad, gate_grad, up_grad, out_grad, query_grad, key_grad, value_grad, gain_a, gain_m
    ) = finish(owns, sibs, outputs, input_grad)
    return (
        outputs.reshape(seqs, rows, depth),
        input_grad.reshape(seqs, rows, depth),
        gain_a.reshape(slab),
        query_grad,
        key_grad,
        value_grad,
        out_grad,
        gain_m.reshape(slab),
        gate_grad,
        up_grad,
        down_grad,
    )


def solution(mesh):
    count, ctx = mesh.shape["fsdp"], mesh.shape["ctx"]
    split = Mesh(mesh.devices.reshape(count, ctx // 2, 2), ("fsdp", "z", "core"))
    act = P("fsdp", ("z", "core"), None)
    row, mat = P("fsdp"), P("fsdp", None)
    fast = count == 4 and count == KV_HEADS and ctx == 8
    return jax.shard_map(
        body if fast else body_plain,
        mesh=split,
        in_specs=(act, act, row, row, mat, mat, mat, mat, row, mat, mat, mat),
        out_specs=(act, act, row, mat, mat, mat, mat, row, mat, mat, mat),
        check_vma=False,
    )
```

```python
import functools

import jax
import jax.numpy as jnp
import numpy as np
from jax import lax
from jax.experimental import pallas as pl
from jax.experimental.pallas import tpu as pltpu
from jax.sharding import Mesh
from jax.sharding import PartitionSpec as P

HEADS = 32
KV_HEADS = 4
HEAD_DIM = 64
EPSILON = 1e-05
ROPE_BASE = 10000.0
MASKED = -1e30
FAR = 1 << 30
BF = jnp.bfloat16
F32 = jnp.float32
VMEM_BYTES = 56 * 1024 * 1024
LAGS = (0, 2, 4, 6)
AHEAD = (1, 4)
STEPS = (0, 1, 7, 12, 13, 14, 15, 16, 17, 18, 18, 20, 24, 24, 23, 28, 30)


def params(**kw):
    return pltpu.CompilerParams(vmem_limit_bytes=VMEM_BYTES, **kw)


def along_plane(value, step):
    count = lax.axis_size("fsdp")
    return lax.ppermute(value, "fsdp", [(i, i ^ step) for i in range(count)])


def to_sibling(value):
    return lax.ppermute(value, "core", [(0, 1), (1, 0)])


def along_line(value, shift):
    count = lax.axis_size("z")
    return lax.ppermute(
        value, "z", [(i, i + shift) for i in range(count) if 0 <= i + shift < count]
    )


def plane_bits():
    count = lax.axis_size("fsdp")
    return [1 << b for b in range(count.bit_length() - 1)]


def plane_gather(block):
    half = block.shape[0] // 2
    parts = []
    for which, bits in ((0, plane_bits()), (1, plane_bits()[::-1])):
        held = {0: block[which * half : (which + 1) * half]}
        for bit in bits:
            order = sorted(held)
            got = along_plane(jnp.stack([held[j] for j in order]), bit)
            for n, j in enumerate(order):
                held[j ^ bit] = got[n]
        parts.append(held)
    return [jnp.concatenate([parts[0][j], parts[1][j]]) for j in range(lax.axis_size("fsdp"))]


def plane_reduce(partial):
    half = partial.shape[1] // 2
    done = []
    for which, bits in ((0, plane_bits()[::-1]), (1, plane_bits())):
        held = {j: partial[j, which * half : (which + 1) * half] for j in range(partial.shape[0])}
        for bit in bits:
            going = [j for j in sorted(held) if j & bit]
            got = along_plane(jnp.stack([held[j].astype(BF) for j in going]), bit)
            for n, j in enumerate(going):
                held[j ^ bit] = held[j ^ bit].astype(F32) + got[n].astype(F32)
                del held[j]
        done.append(held[0])
    return jnp.concatenate(done)


def line_sum(value):
    count = lax.axis_size("z")
    place = lax.axis_index("z")
    half = count // 2
    for i in range(half - 1):
        got = lax.ppermute(value, "z", [(i, i + 1), (count - 1 - i, count - 2 - i)])
        value = value + got
    value = value + lax.ppermute(value, "z", [(half - 1, half), (half, half - 1)])
    for i in range(half - 2, -1, -1):
        got = lax.ppermute(value, "z", [(i + 1, i), (count - 2 - i, count - 1 - i)])
        outer = (place == i) | (place == count - 1 - i)
        value = jnp.where(outer, got, value)
    return value


def move_kernel(idx_ref, x_ref, o_ref):
    o_ref[...] = x_ref[...]


def pick_columns(x, index, count):
    rows, width = x.shape
    size = width // count
    spec = pltpu.PrefetchScalarGridSpec(
        num_scalar_prefetch=1,
        grid=(count,),
        in_specs=[pl.BlockSpec((rows, size), lambda b, idx: (0, idx[b]))],
        out_specs=pl.BlockSpec((rows, size), lambda b, idx: (0, b)),
    )
    return pl.pallas_call(
        move_kernel,
        grid_spec=spec,
        out_shape=jax.ShapeDtypeStruct(x.shape, x.dtype),
        compiler_params=params(),
        name="pick_columns",
    )(index, x)


def put_columns(x, index, count):
    rows, width = x.shape
    size = width // count
    spec = pltpu.PrefetchScalarGridSpec(
        num_scalar_prefetch=1,
        grid=(count,),
        in_specs=[pl.BlockSpec((rows, size), lambda b, idx: (0, b))],
        out_specs=pl.BlockSpec((rows, size), lambda b, idx: (0, idx[b])),
    )
    return pl.pallas_call(
        move_kernel,
        grid_spec=spec,
        out_shape=jax.ShapeDtypeStruct(x.shape, x.dtype),
        compiler_params=params(),
        name="put_columns",
    )(index, x)


def cut_blocks(weight, f, k, count, dtype=BF):
    rows, full = weight.shape
    width, half = full // count, rows // 2
    if width % 128:
        own = lax.dynamic_slice_in_dim(weight, k * half, half, 0).reshape(half, count, width)
        return jnp.stack(
            [lax.dynamic_index_in_dim(own, f ^ j, 1, keepdims=False) for j in range(count)]
        )
    spec = pltpu.PrefetchScalarGridSpec(
        num_scalar_prefetch=1,
        grid=(count,),
        in_specs=[pl.BlockSpec((half, width), lambda j, at: (at[1], at[0] ^ j))],
        out_specs=pl.BlockSpec((None, half, width), lambda j, at: (j, 0, 0)),
    )
    return pl.pallas_call(
        move_kernel,
        grid_spec=spec,
        out_shape=jax.ShapeDtypeStruct((count, half, width), weight.dtype),
        compiler_params=params(),
        name="cut_blocks",
    )(jnp.stack([f, k]), weight)


def join_kernel(at_ref, own_ref, sib_ref, o_ref):
    @pl.when(pl.program_id(0) == 0)
    def _():
        o_ref[...] = own_ref[...].astype(o_ref.dtype)

    @pl.when(pl.program_id(0) == 1)
    def _():
        o_ref[...] = sib_ref[...].astype(o_ref.dtype)


def join_rows(own, sib, f, k):
    count, half, width = own.shape
    if width % 128:
        halves = jnp.stack([own, sib])
        return jnp.concatenate(
            [
                jnp.concatenate(
                    [
                        lax.dynamic_index_in_dim(
                            lax.dynamic_index_in_dim(halves, k ^ h, 0, keepdims=False),
                            f ^ i,
                            0,
                            keepdims=False,
                        )
                        for i in range(count)
                    ],
                    axis=1,
                )
                for h in range(2)
            ],
            axis=0,
        ).astype(F32)
    spec = pltpu.PrefetchScalarGridSpec(
        num_scalar_prefetch=1,
        grid=(2, count),
        in_specs=[
            pl.BlockSpec(
                (None, half, width),
                lambda s, i, at: (at[0] ^ jnp.where(s == 0, i, count - 1), 0, 0),
            ),
            pl.BlockSpec(
                (None, half, width), lambda s, i, at: (at[0] ^ jnp.where(s == 1, i, 0), 0, 0)
            ),
        ],
        out_specs=pl.BlockSpec((half, width), lambda s, i, at: (at[1] ^ s, i)),
    )
    return pl.pallas_call(
        join_kernel,
        grid_spec=spec,
        out_shape=jax.ShapeDtypeStruct((2 * half, count * width), F32),
        compiler_params=params(),
        name="join_rows",
    )(jnp.stack([f, k]), own, sib)


def join_columns(own, sib, k):
    rows, half = own.shape
    count = 4
    size = rows // count
    spec = pltpu.PrefetchScalarGridSpec(
        num_scalar_prefetch=1,
        grid=(2, count),
        in_specs=[
            pl.BlockSpec((size, half), lambda s, i, at: (jnp.where(s == 0, i, count - 1), 0)),
            pl.BlockSpec((size, half), lambda s, i, at: (jnp.where(s == 1, i, 0), 0)),
        ],
        out_specs=pl.BlockSpec((size, half), lambda s, i, at: (i, at[0] ^ s)),
    )
    return pl.pallas_call(
        join_kernel,
        grid_spec=spec,
        out_shape=jax.ShapeDtypeStruct((rows, 2 * half), F32),
        compiler_params=params(),
        name="join_columns",
    )(k.reshape(1), own, sib)


def swap_halves(block):
    lane = lax.broadcasted_iota(jnp.int32, block.shape, 1)
    return jnp.where(lane % 64 < 32, pltpu.roll(block, 96, 1), pltpu.roll(block, 32, 1))


def qkv_kernel(idx_ref, x_ref, gain_ref, w_ref, cos_ref, sin_ref, h_ref, q_ref, kv_ref):
    blocks = idx_ref.shape[0]
    size = x_ref.shape[1] // blocks
    x = x_ref[...].astype(F32)
    inverse = lax.rsqrt(jnp.mean(x * x, axis=1, keepdims=True) + EPSILON)
    for b in range(blocks):
        at = pl.ds(pl.multiple_of(idx_ref[b] * size, 128), size)
        part = x_ref[:, at].astype(F32) * inverse * gain_ref[:, at]
        h_ref[:, b * size : (b + 1) * size] = part.astype(BF)
    out = jnp.dot(h_ref[...], w_ref[...], preferred_element_type=F32)
    cosine, sine = cos_ref[...], sin_ref[...]
    pairs = q_ref.shape[1] // 128
    for c in range(pairs):
        block = out[:, c * 128 : (c + 1) * 128]
        q_ref[:, c * 128 : (c + 1) * 128] = (block * cosine + swap_halves(block) * sine).astype(BF)
    block = out[:, pairs * 128 :]
    lane = lax.broadcasted_iota(jnp.int32, block.shape, 1)
    turned = block * cosine + swap_halves(block) * sine
    kv_ref[...] = jnp.where(lane < 64, turned, block).astype(BF)


def qkv_project(idx, x, gain, weight, cosine, sine, rows):
    total, depth = x.shape
    width = weight.shape[1]
    spec = pltpu.PrefetchScalarGridSpec(
        num_scalar_prefetch=1,
        grid=(total // rows,),
        in_specs=[
            pl.BlockSpec((rows, depth), lambda i, idx: (i, 0)),
            pl.BlockSpec((1, depth), lambda i, idx: (0, 0)),
            pl.BlockSpec((depth, width), lambda i, idx: (0, 0)),
            pl.BlockSpec((rows, 128), lambda i, idx: (0, 0)),
            pl.BlockSpec((rows, 128), lambda i, idx: (0, 0)),
        ],
        out_specs=[
            pl.BlockSpec((rows, depth), lambda i, idx: (i, 0)),
            pl.BlockSpec((rows, width - 128), lambda i, idx: (i, 0)),
            pl.BlockSpec((rows, 128), lambda i, idx: (i, 0)),
        ],
    )
    return pl.pallas_call(
        qkv_kernel,
        grid_spec=spec,
        out_shape=[
            jax.ShapeDtypeStruct((total, depth), BF),
            jax.ShapeDtypeStruct((total, width - 128), BF),
            jax.ShapeDtypeStruct((total, 128), BF),
        ],
        compiler_params=params(),
        cost_estimate=pl.CostEstimate(
            flops=2 * total * depth * width,
            bytes_accessed=4 * total * depth + 2 * depth * width + 2 * total * width,
            transcendentals=0,
        ),
        name="qkv_project",
    )(idx, x, gain, weight, cosine, sine)


def nt(a, b):
    return lax.dot_general(a, b, (((1,), (1,)), ((), ())), preferred_element_type=F32)


def tn(a, b):
    return lax.dot_general(a, b, (((0,), (0,)), ((), ())), preferred_element_type=F32)


def nn(a, b):
    return jnp.dot(a, b, preferred_element_type=F32)


def limits(at_ref, rows):
    j = pl.program_id(0)
    place = at_ref[0] - lax.broadcasted_iota(jnp.int32, (rows, 1), 0)
    return jnp.minimum(place, at_ref[1 + j] - 1)


def attend_kernel(at_ref, q_ref, kv_ref, kp_ref, o_ref, lse_ref, vk_ref):
    rows = q_ref.shape[0]
    keys = vk_ref.shape[0]
    kv = kv_ref[...].reshape(keys, 128)

    @pl.when(pl.program_id(1) == 0)
    def _():
        vk_ref[...] = pltpu.roll(kv.astype(F32), 64, 1).astype(BF)

    vk = vk_ref[...]
    allowed = kp_ref[...] <= limits(at_ref, rows)
    lane = lax.broadcasted_iota(jnp.int32, (rows, 128), 1)
    q = q_ref[...]
    zero = jnp.zeros_like(q)
    outs, logs = [], []
    for first in (True, False):
        mine = lane < 64 if first else lane >= 64
        scores = nt(jnp.where(mine, q, zero), kv if first else vk) * (HEAD_DIM**-0.5)
        scores = jnp.where(allowed, scores, MASKED)
        top = jnp.max(scores, axis=1, keepdims=True)
        weights = jnp.exp(scores - top)
        total = jnp.sum(weights, axis=1, keepdims=True)
        outs.append(nn(weights.astype(BF), vk if first else kv) / total)
        logs.append(jnp.broadcast_to(top + jnp.log(total), (rows, 128)))
    o_ref[...] = jnp.where(lane < 64, outs[0], outs[1]).astype(BF)
    lse_ref[...] = jnp.where(lane < 64, logs[0], logs[1])


def attend(at, q, kv, kp):
    chunks, seqs, rows, _ = kv.shape
    pairs = q.shape[2] // 128
    keys = chunks * rows
    spec = pltpu.PrefetchScalarGridSpec(
        num_scalar_prefetch=1,
        grid=(seqs, pairs),
        in_specs=[
            pl.BlockSpec((None, rows, 128), lambda j, p, at: (j, 0, p)),
            pl.BlockSpec((chunks, None, rows, 128), lambda j, p, at: (0, j, 0, 0)),
            pl.BlockSpec((1, keys), lambda j, p, at: (0, 0)),
        ],
        out_specs=[
            pl.BlockSpec((None, rows, 128), lambda j, p, at: (j, 0, p)),
            pl.BlockSpec((None, rows, 128), lambda j, p, at: (j, 0, p)),
        ],
        scratch_shapes=[pltpu.VMEM((keys, 128), BF)],
    )
    size = seqs * pairs * 2 * rows * keys
    return pl.pallas_call(
        attend_kernel,
        grid_spec=spec,
        out_shape=[
            jax.ShapeDtypeStruct(q.shape, BF),
            jax.ShapeDtypeStruct(q.shape, F32),
        ],
        compiler_params=params(),
        cost_estimate=pl.CostEstimate(
            flops=size * 4 * 128, bytes_accessed=4 << 20, transcendentals=size
        ),
        name="attend",
    )(at, q, kv, kp)


def attend_back_kernel(
    at_ref, q_ref, do_ref, lse_ref, kv_ref, kp_ref, cos_ref, sin_ref, dq_ref, dkv_ref, vk_ref, dk_ref, dv_ref
):
    rows = q_ref.shape[0]
    keys = vk_ref.shape[0]
    pair = pl.program_id(1)
    kv = kv_ref[...].reshape(keys, 128)

    @pl.when(pair == 0)
    def _():
        vk_ref[...] = pltpu.roll(kv.astype(F32), 64, 1).astype(BF)
        dk_ref[...] = jnp.zeros_like(dk_ref)
        dv_ref[...] = jnp.zeros_like(dv_ref)

    vk = vk_ref[...]
    allowed = kp_ref[...] <= limits(at_ref, rows)
    lane = lax.broadcasted_iota(jnp.int32, (rows, 128), 1)
    q, do = q_ref[...], do_ref[...]
    zero = jnp.zeros_like(q)
    parts = []
    for first in (True, False):
        mine = lane < 64 if first else lane >= 64
        keyed, valued = (kv, vk) if first else (vk, kv)
        q_own, do_own = jnp.where(mine, q, zero), jnp.where(mine, do, zero)
        scores = nt(q_own, keyed) * (HEAD_DIM**-0.5)
        log_total = lse_ref[:, 0:1] if first else lse_ref[:, 64:65]
        weights = jnp.where(allowed, jnp.exp(scores - log_total), 0.0)
        joint = weights * nt(do_own, valued)
        back = (joint - weights * jnp.sum(joint, axis=1, keepdims=True)).astype(BF)
        parts.append(nn(back, keyed))
        dk_ref[...] += tn(back, q_own)
        dv_ref[...] += tn(weights.astype(BF), do_own)
    turned = jnp.where(lane < 64, parts[0], parts[1]) * (HEAD_DIM**-0.5)
    dq_ref[...] = (turned * cos_ref[...] - swap_halves(turned) * sin_ref[...]).astype(BF)

    @pl.when(pair == pl.num_programs(1) - 1)
    def _():
        dk = dk_ref[...]
        dv = dv_ref[...]
        dk = (dk + pltpu.roll(dk, 64, 1)) * (HEAD_DIM**-0.5)
        dv = dv + pltpu.roll(dv, 64, 1)
        wide = lax.broadcasted_iota(jnp.int32, dk.shape, 1)
        dkv_ref[...] = jnp.where(wide < 64, dk, dv).astype(BF).reshape(dkv_ref.shape)


def attend_back(at, q, do, lse, kv, kp, cosine, sine):
    chunks, seqs, rows, _ = kv.shape
    pairs = q.shape[2] // 128
    keys = chunks * rows
    tall = pl.BlockSpec((None, rows, 128), lambda j, p, at: (j, 0, p))
    whole = pl.BlockSpec((chunks, None, rows, 128), lambda j, p, at: (0, j, 0, 0))
    flat = pl.BlockSpec((rows, 128), lambda j, p, at: (0, 0))
    spec = pltpu.PrefetchScalarGridSpec(
        num_scalar_prefetch=1,
        grid=(seqs, pairs),
        in_specs=[tall, tall, tall, whole, pl.BlockSpec((1, keys), lambda j, p, at: (0, 0)), flat, flat],
        out_specs=[tall, whole],
        scratch_shapes=[
            pltpu.VMEM((keys, 128), BF),
            pltpu.VMEM((keys, 128), F32),
            pltpu.VMEM((keys, 128), F32),
        ],
    )
    size = seqs * pairs * 2 * rows * keys
    return pl.pallas_call(
        attend_back_kernel,
        grid_spec=spec,
        out_shape=[
            jax.ShapeDtypeStruct(q.shape, BF),
            jax.ShapeDtypeStruct(kv.shape, BF),
        ],
        compiler_params=params(),
        cost_estimate=pl.CostEstimate(
            flops=size * 10 * 128, bytes_accessed=8 << 20, transcendentals=size
        ),
        name="attend_back",
    )(at, q, do, lse, kv, kp, cosine, sine)


def rms_backward(row_block, inverse, gain_vec, gradient):
    normed = row_block * inverse
    gain_grad = jnp.sum(gradient * normed, axis=0)
    scaled = gradient * gain_vec
    back = inverse * (scaled - normed * jnp.mean(scaled * normed, axis=1, keepdims=True))
    return (back, gain_grad)


def body_plain(
    tokens, cotangent, lengths, attn_gain, w_query, w_key, w_value, w_out, mlp_gain, w_gate, w_up, w_down
):
    seqs, rows, depth = tokens.shape
    count, line = lax.axis_size("fsdp"), lax.axis_size("z")
    f, z, k = lax.axis_index("fsdp"), lax.axis_index("z"), lax.axis_index("core")
    slot = rows * line * 2
    total = count * rows
    slab = depth // count
    half = slab // 2
    q_width = HEADS * HEAD_DIM // count
    shared = max(1, count // KV_HEADS)

    x_own = tokens.reshape(rows, depth)
    chunk = 2 * z + k
    first_pos = slot - 1 - chunk * rows

    length = lengths[0]
    words = jnp.zeros((slab,), F32).at[0].set((length // 64).astype(F32)).at[1].set((length % 64).astype(F32))
    note = jnp.stack([attn_gain, mlp_gain, words.astype(BF), jnp.zeros((slab,), BF)])
    notes = [note] + [along_plane(note, j) for j in range(1, count)]
    notes_abs = [lax.dynamic_index_in_dim(jnp.stack(notes), f ^ i, 0, keepdims=False) for i in range(count)]
    gain_one = jnp.concatenate([n[0] for n in notes_abs]).astype(F32).reshape(1, depth)
    gain_two = jnp.concatenate([n[1] for n in notes_abs]).astype(F32).reshape(1, depth)
    all_lengths = jnp.stack(
        [n[2, 0].astype(jnp.int32) * 64 + n[2, 1].astype(jnp.int32) for n in notes]
    )

    x_all = jnp.concatenate(plane_gather(x_own))

    wq = cut_blocks(w_query, f, k, count)
    key_cols = lax.dynamic_slice_in_dim(w_key, k * half, half, 0).reshape(half, KV_HEADS, HEAD_DIM)
    value_cols = lax.dynamic_slice_in_dim(w_value, k * half, half, 0).reshape(half, KV_HEADS, HEAD_DIM)

    def head_of(j):
        return (f ^ j) // shared

    wkv = jnp.stack(
        [
            jnp.concatenate(
                [
                    lax.dynamic_index_in_dim(key_cols, head_of(j), 1, keepdims=False),
                    lax.dynamic_index_in_dim(value_cols, head_of(j), 1, keepdims=False),
                ],
                axis=1,
            )
            for j in range(count)
        ]
    )
    wqkv = jnp.concatenate([wq, wkv], axis=2)
    wqkv_own = jnp.stack([wqkv[0]] + [along_plane(wqkv[j], j) for j in range(1, count)])
    wqkv_sib = to_sibling(wqkv_own)
    wqkv_all = jnp.concatenate([wqkv_own, wqkv_sib]).reshape(depth, q_width + 128)

    def fetch(weight):
        cut = cut_blocks(weight, f, k, count)
        width = cut.shape[2]
        own = jnp.stack([cut[0]] + [along_plane(cut[j], j) for j in range(1, count)])
        sib = to_sibling(own)
        return own.reshape(depth // 2, width), sib.reshape(depth // 2, width)

    gate_own, gate_sib = fetch(w_gate)
    up_own, up_sib = fetch(w_up)

    order = jnp.stack([(f ^ j) * 2 + (k ^ h) for h in range(2) for j in range(count)]).astype(jnp.int32)

    half_dim = HEAD_DIM // 2
    frequency = jnp.power(ROPE_BASE, jnp.arange(half_dim, dtype=F32) * (-2.0 / HEAD_DIM))
    positions = first_pos - jnp.arange(rows, dtype=jnp.int32)
    angles = positions.astype(F32)[:, None] * frequency[None, :]
    cos32, sin32 = jnp.cos(angles), jnp.sin(angles)
    cosine = jnp.concatenate([cos32] * 4, axis=1)
    sine = jnp.concatenate([-sin32, sin32, -sin32, sin32], axis=1)

    normed_one, queries, kv = qkv_project(order, x_all, gain_one, wqkv_all, cosine, sine, rows)
    queries = queries.reshape(count, rows, q_width)
    kv = kv.reshape(count, rows, 128)

    mine = [kv] + [along_line(kv, -s) for s in range(1, line)]
    mine = jnp.stack(mine)
    kv_all = jnp.concatenate([mine, to_sibling(mine)])
    places = []
    for h in range(2):
        for s in range(line):
            start = slot - 1 - (2 * (z + s) + (k ^ h)) * rows
            places.append(start - jnp.arange(rows, dtype=jnp.int32))
    kp = jnp.concatenate(places)
    kp = jnp.where(kp < 0, FAR, kp).reshape(1, -1)
    at = jnp.concatenate([first_pos.reshape(1), all_lengths]).astype(jnp.int32)

    attended, log_total = attend(at, queries, kv_all, kp)
    attended = attended.reshape(total, q_width)

    mixed_part = nn(attended, w_out).astype(BF).reshape(count, rows, depth)
    inputs = x_own.astype(F32)
    mixed = inputs + plane_reduce(mixed_part)
    inv_two = lax.rsqrt(jnp.mean(mixed * mixed, axis=1, keepdims=True) + EPSILON)
    normed_two_own = (mixed * inv_two * gain_two).astype(BF)
    normed_two = jnp.concatenate(plane_gather(normed_two_own))
    normed_two = pick_columns(normed_two, order, 2 * count)
    n2_own, n2_sib = normed_two[:, : depth // 2], normed_two[:, depth // 2 :]

    valid = (positions < length).astype(F32)[:, None]
    out_back = cotangent.reshape(rows, depth).astype(F32) * valid
    branch_own = out_back.astype(BF)
    branch = jnp.concatenate(plane_gather(branch_own))

    gate = nn(n2_own, gate_own) + nn(n2_sib, gate_sib)
    up = nn(n2_own, up_own) + nn(n2_sib, up_sib)
    sigmoid = jax.nn.sigmoid(gate)
    hidden = (gate * sigmoid * up).astype(BF)

    half_depth = depth // 2
    branch_mine = lax.dynamic_slice_in_dim(branch, k * half_depth, half_depth, 1)
    branch_other = lax.dynamic_slice_in_dim(branch, (1 - k) * half_depth, half_depth, 1)

    def pair_sum(own, other):
        return (own + to_sibling(other.astype(BF)).astype(F32)).astype(BF)

    def swap_slabs(own):
        return jnp.stack([own[0]] + [along_plane(own[j], j) for j in range(1, count)])

    down_half = line_sum(pair_sum(tn(hidden, branch_mine), tn(hidden, branch_other)))
    down_grad = join_columns(down_half, to_sibling(down_half), k)

    hidden_grad = nt(branch, w_down)
    gate_back = (hidden_grad * up * sigmoid * (1.0 + gate * (1.0 - sigmoid))).astype(BF)
    up_back = (hidden_grad * gate * sigmoid).astype(BF)

    def slab_grad(left_own, left_other, right):
        width = right.shape[1]
        own = pair_sum(tn(left_own, right), tn(left_other, right)).reshape(count, half, width)
        return line_sum(swap_slabs(own))

    gate_half = slab_grad(n2_own, n2_sib, gate_back)
    gate_grad = join_rows(gate_half, to_sibling(gate_half), f, k)
    up_half = slab_grad(n2_own, n2_sib, up_back)
    up_grad = join_rows(up_half, to_sibling(up_half), f, k)

    back_own = (nt(gate_back, gate_own) + nt(up_back, up_own)).astype(BF)
    back_sib = (nt(gate_back, gate_sib) + nt(up_back, up_sib)).astype(BF)
    normed_back = put_columns(jnp.concatenate([back_own, back_sib], axis=1), order, 2 * count)
    normed_back = plane_reduce(normed_back.reshape(count, rows, depth))

    out_part = nn(hidden, w_down).astype(BF).reshape(count, rows, depth)
    outputs = mixed + plane_reduce(out_part)

    mixed_back, gain_two_grad = rms_backward(mixed, inv_two, gain_two, normed_back)
    mixed_grad = out_back + mixed_back
    attn_back = jnp.concatenate(plane_gather(mixed_grad.astype(BF)))
    attended_grad = nt(attn_back, w_out).astype(BF).reshape(count, rows, q_width)

    back_mine = lax.dynamic_slice_in_dim(attn_back, k * half_depth, half_depth, 1)
    back_other = lax.dynamic_slice_in_dim(attn_back, (1 - k) * half_depth, half_depth, 1)
    out_half = line_sum(pair_sum(tn(attended, back_mine), tn(attended, back_other)))
    out_grad = join_columns(out_half, to_sibling(out_half), k)

    query_back, kv_part = attend_back(at, queries, attended_grad, log_total, kv_all, kp, cosine, sine)
    kv_mine = kv_part[:line].astype(F32) + to_sibling(kv_part[line:]).astype(F32)
    kv_back = kv_mine[0]
    for s in range(1, line):
        kv_back = kv_back + along_line(kv_mine[s].astype(BF), s).astype(F32)
    lead, trail, flat = kv_back[..., :32], kv_back[..., 32:64], kv_back[..., 64:]
    kv_back = jnp.concatenate(
        [lead * cos32 + trail * sin32, trail * cos32 - lead * sin32, flat], axis=-1
    ).astype(BF)
    qkv_back = jnp.concatenate(
        [query_back.reshape(total, q_width), kv_back.reshape(total, 128)], axis=1
    )

    normed_one_back = nt(qkv_back, wqkv_all).astype(BF)
    normed_one_back = put_columns(normed_one_back, order, 2 * count)
    normed_one_back = plane_reduce(normed_one_back.reshape(count, rows, depth))
    inv_one = lax.rsqrt(jnp.mean(inputs * inputs, axis=1, keepdims=True) + EPSILON)
    input_back, gain_one_grad = rms_backward(inputs, inv_one, gain_one, normed_one_back)
    input_grad = mixed_grad + input_back

    n1_own, n1_sib = normed_one[:, :half_depth], normed_one[:, half_depth:]
    qkv_own = pair_sum(tn(n1_own, qkv_back), tn(n1_sib, qkv_back)).reshape(count, half, q_width + 128)
    gains = jnp.stack([gain_one_grad, gain_two_grad]).reshape(2, count, slab)
    gains = jnp.stack(
        [lax.dynamic_index_in_dim(gains, f ^ j, 1, keepdims=False) for j in range(count)]
    ).astype(BF)
    gains = line_sum(swap_slabs(gains))
    qkv_half = line_sum(swap_slabs(qkv_own))
    gains = jnp.sum(gains.astype(F32), axis=0) + jnp.sum(to_sibling(gains).astype(F32), axis=0)
    qkv_other = to_sibling(qkv_half)
    query_grad = join_rows(qkv_half[:, :, :q_width], qkv_other[:, :, :q_width], f, k)
    halves = jnp.stack([qkv_half[:, :, q_width:], qkv_other[:, :, q_width:]])

    def by_head(lo, hi):
        both = [lax.dynamic_index_in_dim(halves, k ^ h, 0, keepdims=False) for h in range(2)]
        both = jnp.concatenate(both, axis=1).astype(F32)[:, :, lo:hi]
        cols = jnp.stack([lax.dynamic_index_in_dim(both, f ^ i, 0, keepdims=False) for i in range(count)])
        cols = cols.reshape(KV_HEADS, shared, slab, HEAD_DIM).sum(1)
        return jnp.transpose(cols, (1, 0, 2)).reshape(slab, KV_HEADS * HEAD_DIM)

    key_grad = by_head(0, 64)
    value_grad = by_head(64, 128)

    return (
        outputs.reshape(seqs, rows, depth),
        input_grad.reshape(seqs, rows, depth),
        gains[0],
        query_grad,
        key_grad,
        value_grad,
        out_grad,
        gains[1],
        gate_grad,
        up_grad,
        down_grad,
    )


def rotary_parts(slot, rows):
    lane = np.arange(128) % (HEAD_DIM // 2)
    frequency = ROPE_BASE ** (lane * (-2.0 / HEAD_DIM))
    starts = (slot - 1 - rows * np.arange(slot // rows))[:, None] * frequency[None, :]
    steps = np.arange(rows)[:, None] * frequency[None, :]
    return [jnp.asarray(t(a), F32) for a in (starts, steps) for t in (np.cos, np.sin)]


def front_kernel(
    length_ref, both_gains, start_cos, start_sin, step_cos, step_sin,
    tokens, cotangent, w_query, w_key, w_value, w_out, w_gate, w_up, w_down,
    h1_out, queries_out, lse_out, attended_out, mixed_out, n2_out, limits_out, cosine_out, sine_out, kp_out,
    gain_one_out, gain_two_out, kv_out, branch_out, wqkv_out, gate_back_out, up_back_out, hidden_out,
    gate_own_out, gate_sib_out, up_own_out, up_sib_out,
    h1, queries, lse, attended, mixed, n2, limits, cosine, sine, kp, gain_one, gain_two,
    gate_back, up_back, hidden, grad,
    notes, x_all, wqkv, keys_in, values_in, kv_give, gate_own, gate_sib, up_own, up_sib, down,
    kv_all, vk, w_o, part, landed, relay, relayed, n2_all, branch_all, cot_in,
    local_s, store_s, wx_s, wx_r, note_s, note_r, tok_s, tok_r, tof_s, tof_r, wq_s, wq_r, wk_s, wk_r, wp_s, wp_r, wkp_s, wkp_r,
    kz_s, kz_r, kp_s, kp_r, gt_s, gt_r, up_s, up_r, gz_s, gz_r, gs_s, gs_r, us_s, us_r,
    bt_s, bt_r, btf_s, btf_r, mx_s, mx_r, nt_s, nt_r, ntf_s, ntf_r,
):
    f, z, k = lax.axis_index("fsdp"), lax.axis_index("z"), lax.axis_index("core")
    plane, line = 4, 4
    rows, depth = tokens.shape
    total = plane * rows
    slab = depth // plane
    half = slab // 2
    hr = rows // 2
    q_width = w_out.shape[0]
    pairs = q_width // 128
    ff = w_down.shape[0]
    keys = vk.shape[0]
    slot = rows * line * 2
    even = z % 2 == 0
    across = z + 1 - 2 * (z % 2)
    peers = (1, 2, 3)
    first_pos = slot - 1 - (2 * z + k) * rows

    def remote(source, target, send, recv, where):
        return pltpu.make_async_remote_copy(
            src_ref=source,
            dst_ref=target,
            send_sem=send,
            recv_sem=recv,
            device_id=where,
            device_id_type=pl.DeviceIdType.MESH,
        )

    sib = {"core": 1 - k}

    def chip(j):
        return {"fsdp": f ^ j}

    def cols(weight, j, side, width):
        start = pl.multiple_of((f ^ j) * width, 128)
        return weight.at[pl.ds(pl.multiple_of((k ^ side) * half, 16), half), pl.ds(start, width)]

    class Gather:
        def __init__(self, source, target, send, recv, fsend, frecv):
            self.near = {
                j: remote(source, target.at[j], send.at[j - 1], recv.at[j - 1], chip(j)) for j in (1, 2)
            }
            self.far = {
                j: remote(
                    target.at[j, pl.ds((j - 1) * hr, hr), :],
                    target.at[3, pl.ds((j - 1) * hr, hr), :],
                    fsend.at[j - 1],
                    frecv.at[j - 1],
                    chip(3 - j),
                )
                for j in (1, 2)
            }

        def start(self):
            for j in (1, 2):
                self.near[j].start()

        def forward(self):
            for j in (1, 2):
                self.near[j].wait_recv()
                self.far[j].start()

        def arrive(self):
            for j in (1, 2):
                self.far[j].wait_recv()

        def close(self):
            for j in (1, 2):
                self.near[j].wait_send()
                self.far[j].wait_send()

    def note_send(j):
        return remote(notes.at[0], notes.at[j], note_s.at[j - 1], note_r.at[j - 1], chip(j))

    token_gather = Gather(tokens, x_all, tok_s, tok_r, tof_s, tof_r)
    branch_gather = Gather(branch_all.at[0], branch_all, bt_s, bt_r, btf_s, btf_r)
    n2_gather = Gather(n2_all.at[0], n2_all, nt_s, nt_r, ntf_s, ntf_r)

    def wq_send(j):
        target = wqkv.at[pl.ds(j * half, half), pl.ds(0, q_width)]
        return remote(cols(w_query, j, 0, q_width), target, wq_s.at[j - 1], wq_r.at[j - 1], chip(j))

    def wk_send(j):
        target = wqkv.at[pl.ds(j * half, half), pl.ds(q_width, 128)]
        return remote(kv_give.at[j], target, wk_s.at[j - 1], wk_r.at[j - 1], chip(j))

    def wp_send(j):
        source = wqkv.at[pl.ds(j * half, half), :]
        target = wqkv.at[pl.ds((plane + j) * half, half), :]
        return remote(source, target, wp_s.at[j - 1], wp_r.at[j - 1], sib)

    def w_across(j):
        block = wqkv.at[pl.ds(j * half, half), :]
        return remote(block, block, wx_s.at[j - 1], wx_r.at[j - 1], {"z": across})

    def kv_send(s):
        return remote(kv_all.at[0], kv_all.at[s], kz_s.at[s - 1], kz_r.at[s - 1], {"z": z - s})

    def kv_pair(s):
        return remote(kv_all.at[s], kv_all.at[line + s], kp_s.at[s], kp_r.at[s], sib)

    def gate_send(j):
        return remote(cols(w_gate, j, 0, ff), gate_own.at[j], gt_s.at[j - 1], gt_r.at[j - 1], chip(j))

    def up_send(j):
        return remote(cols(w_up, j, 0, ff), up_own.at[j], up_s.at[j - 1], up_r.at[j - 1], chip(j))

    def gate_across(j):
        return remote(gate_own.at[j], gate_own.at[j], gz_s.at[j - 1], gz_r.at[j - 1], {"z": across})

    def up_across(j):
        return remote(up_own.at[j], up_own.at[j], gz_s.at[j - 1], gz_r.at[j - 1], {"z": across})

    def by_parity(act_even, act_odd):
        @pl.when(even)
        def _():
            act_even()

        @pl.when(jnp.logical_not(even))
        def _():
            act_odd()

    def fetch_start():
        by_parity(
            lambda: [gate_send(j).start() for j in (3, 1, 2)], lambda: [up_send(j).start() for j in (3, 1, 2)]
        )

    def fetch_on(j):
        def gate_on():
            gate_send(j).wait_recv()
            gate_across(j).start()
            gate_pair(j).start()

        def up_on():
            up_send(j).wait_recv()
            up_across(j).start()
            up_pair(j).start()

        by_parity(gate_on, up_on)

    def cross_on(j):
        def up_on():
            up_across(j).wait_recv()
            up_pair(j).start()

        def gate_on():
            gate_across(j).wait_recv()
            gate_pair(j).start()

        by_parity(up_on, gate_on)

    def gate_pair(j):
        return remote(gate_own.at[j], gate_sib.at[j], gs_s.at[j - 1], gs_r.at[j - 1], sib)

    def up_pair(j):
        return remote(up_own.at[j], up_sib.at[j], us_s.at[j - 1], us_r.at[j - 1], sib)

    def span(which):
        return pl.ds(which * hr, hr)

    mix_first = {
        "one": remote(part.at[1, span(0), :], landed.at[0, span(0), :], mx_s.at[0], mx_r.at[0], chip(1)),
        "two": remote(part.at[2, span(1), :], landed.at[1, span(1), :], mx_s.at[1], mx_r.at[1], chip(2)),
        "far_one": remote(part.at[3, span(0), :], relay.at[0], mx_s.at[2], mx_r.at[2], chip(1)),
        "far_two": remote(part.at[3, span(1), :], relay.at[1], mx_s.at[3], mx_r.at[3], chip(2)),
        "late_two": remote(relayed.at[0], landed.at[1, span(0), :], mx_s.at[4], mx_r.at[4], chip(2)),
        "late_one": remote(relayed.at[1], landed.at[0, span(1), :], mx_s.at[5], mx_r.at[5], chip(1)),
    }

    local = [
        pltpu.make_async_copy(source, target, local_s.at[n])
        for n, (source, target) in enumerate(
            [
                (tokens, x_all.at[0]),
                (w_key, keys_in),
                (w_value, values_in),
                (cols(w_query, 0, 0, q_width), wqkv.at[pl.ds(0, half), pl.ds(0, q_width)]),
                (cols(w_query, 0, 1, q_width), wqkv.at[pl.ds(plane * half, half), pl.ds(0, q_width)]),
                (cotangent, cot_in),
                (w_out, w_o),
                (cols(w_gate, 0, 0, ff), gate_own.at[0]),
                (cols(w_gate, 0, 1, ff), gate_sib.at[0]),
                (cols(w_up, 0, 0, ff), up_own.at[0]),
                (cols(w_up, 0, 1, ff), up_sib.at[0]),
                (w_down, down),
            ]
        )
    ]

    stored = [
        (h1, h1_out), (queries, queries_out), (lse, lse_out), (attended, attended_out), (mixed, mixed_out),
        (n2, n2_out), (limits, limits_out), (cosine, cosine_out), (sine, sine_out), (kp, kp_out),
        (gain_one, gain_one_out), (gain_two, gain_two_out), (kv_all, kv_out), (branch_all, branch_out),
        (wqkv, wqkv_out), (gate_back, gate_back_out), (up_back, up_back_out), (hidden, hidden_out),
        (gate_own, gate_own_out), (gate_sib, gate_sib_out), (up_own, up_own_out), (up_sib, up_sib_out),
    ]

    def store(n):
        return pltpu.make_async_copy(*stored[n], store_s.at[n])

    length = length_ref[0]
    place = lax.broadcasted_iota(jnp.int32, (16, slab), 0)
    high, low = (length // 64).astype(F32), (length % 64).astype(F32)
    note = jnp.where(place == 0, both_gains[0:1, :].astype(F32), both_gains[1:2, :].astype(F32))
    note = jnp.where(place == 2, high, jnp.where(place == 3, low, note))
    notes[0] = note.astype(BF)
    for j in peers:
        note_send(j).start()
    by_parity(lambda: wq_send(3).start(), lambda: [wq_send(j).start() for j in (1, 2)])
    token_gather.start()
    for copy in local:
        copy.start()

    local[1].wait()
    local[2].wait()

    def head_columns(j, side):
        at = pl.ds(pl.multiple_of((k ^ side) * half, 16), half)
        head = f ^ j
        width = KV_HEADS * HEAD_DIM
        key = pltpu.roll(keys_in[at, :].astype(F32), (width - head * 64) % width, 1)[:, :128]
        value = pltpu.roll(values_in[at, :].astype(F32), (width - head * 64 + 64) % width, 1)[:, :128]
        lane = lax.broadcasted_iota(jnp.int32, key.shape, 1)
        return jnp.where(lane < 64, key, value).astype(BF)

    for j in (3, 1, 2):
        kv_give[j] = head_columns(j, 0)
    by_parity(lambda: wk_send(3).start(), lambda: [wk_send(j).start() for j in (1, 2)])
    wqkv[0:half, q_width : q_width + 128] = head_columns(0, 0)
    wqkv[plane * half : (plane + 1) * half, q_width : q_width + 128] = head_columns(0, 1)

    chunk = pl.ds(2 * z + k, 1)
    cos_at, sin_at = start_cos[chunk, :], start_sin[chunk, :]
    lane = lax.broadcasted_iota(jnp.int32, (rows, 128), 1)
    cosine[...] = cos_at * step_cos[...] + sin_at * step_sin[...]
    turn = sin_at * step_cos[...] - cos_at * step_sin[...]
    sine[...] = jnp.where(lane % 64 < 32, -turn, turn)
    for h in range(2):
        for s in range(line):
            start = slot - 1 - (2 * (z + s) + (k ^ h)) * rows
            spot = start - lax.broadcasted_iota(jnp.int32, (8, rows), 1)
            spot = jnp.where(spot < 0, FAR, spot).astype(F32)
            kp[:, (h * line + s) * rows : (h * line + s + 1) * rows] = spot

    for s in range(1, line):

        @pl.when(z + s >= line)
        def _():
            kv_all[s] = jnp.zeros(kv_all.shape[1:], BF)
            kv_all[line + s] = jnp.zeros(kv_all.shape[1:], BF)

    local[5].wait()
    row_pos = (first_pos - lax.broadcasted_iota(jnp.int32, (rows, 1), 0)).astype(F32)
    valid = row_pos < jnp.full((rows, 1), length.astype(F32))
    branch_all[0] = jnp.where(valid, cot_in[...].astype(F32), 0.0).astype(BF)

    def projections_on(j):
        wq_send(j).wait_recv()
        wk_send(j).wait_recv()
        w_across(j).start()
        wp_send(j).start()

    by_parity(lambda: projections_on(3), lambda: [projections_on(j) for j in (1, 2)])
    token_gather.forward()
    fetch_start()

    for j in peers:
        note_send(j).wait_recv()
    for j in range(plane):
        at = pl.ds(pl.multiple_of((f ^ j) * slab, 128), slab)
        gain_one[:, at] = jnp.broadcast_to(notes[j, 0:1, :].astype(F32), (8, slab))
        gain_two[:, at] = jnp.broadcast_to(notes[j, 1:2, :].astype(F32), (8, slab))
        theirs = notes[j, 2:3, 0:1].astype(F32) * 64.0 + notes[j, 3:4, 0:1].astype(F32)
        limits[j] = jnp.broadcast_to(jnp.minimum(row_pos, theirs - 1.0), (rows, 128))

    def normalize(j, x_ref):
        @pl.loop(0, rows // 16)
        def _(i):
            at = pl.ds(pl.multiple_of(i * 16, 16), 16)
            x = x_ref[at, :].astype(F32)
            inverse = lax.rsqrt(jnp.mean(x * x, axis=1, keepdims=True) + EPSILON)
            to = pl.ds(pl.multiple_of(j * rows + i * 16, 16), 16)
            for h in range(2):
                for b in range(plane):
                    from_ = pl.ds(pl.multiple_of(((f ^ b) * 2 + (k ^ h)) * half, 128), half)
                    value = x_ref[at, from_].astype(F32) * inverse * gain_one[0:1, from_]
                    c = (h * plane + b) * half
                    h1[to, c : c + half] = value.astype(BF)

    local[0].wait()
    normalize(0, x_all.at[0])

    def projections_in(js):
        for j in js:
            w_across(j).wait_recv()
            wp_send(j).start()

    by_parity(lambda: projections_in((1, 2)), lambda: projections_in((3,)))

    @pl.loop(1, 3)
    def _(j):
        normalize(j, x_all.at[j])

    token_gather.arrive()
    normalize(3, x_all.at[3])
    local[3].wait()
    local[4].wait()
    for j in (1, 2, 3):
        wp_send(j).wait_recv()

    kv_cols = nn(h1[...], wqkv[:, q_width : q_width + 128])
    for j in range(plane):
        value = kv_cols[j * rows : (j + 1) * rows]
        turned = value * cosine[...] + swap_halves(value) * sine[...]
        kv_all[0, j] = jnp.where(lane < 64, turned, value).astype(BF)
    for s in range(1, line):

        @pl.when(z >= s)
        def _():
            kv_send(s).start()

    kv_pair(0).start()
    branch_gather.start()

    @pl.loop(0, pairs // 2)
    def _(p):
        at = pl.ds(pl.multiple_of(p * 256, 256), 256)
        out = nn(h1[...], wqkv[:, at])
        for j in range(plane):
            for c in range(2):
                value = out[j * rows : (j + 1) * rows, c * 128 : (c + 1) * 128]
                turned = value * cosine[...] + swap_halves(value) * sine[...]
                queries[j, :, pl.ds(pl.multiple_of(p * 256 + c * 128, 128), 128)] = turned.astype(BF)

    for s in range(1, line):

        @pl.when(z + s < line)
        def _():
            kv_send(s).wait_recv()
            kv_pair(s).start()

    fetch_on(1)
    fetch_on(2)
    kv_pair(0).wait_recv()
    for s in range(1, line):

        @pl.when(z + s < line)
        def _():
            kv_pair(s).wait_recv()

    local[6].wait()

    def by_columns(act):
        @pl.loop(0, ff // 256)
        def _(n):
            act(pl.ds(pl.multiple_of(n * 256, 256), 256))

        if ff % 256:
            act(pl.ds(ff // 256 * 256, ff % 256))

    def relay_on(far, late, which, j):
        mix_first[far].wait_recv()
        value = relay[which].astype(F32) + part[j, which * hr : (which + 1) * hr, :].astype(F32)
        relayed[which] = value.astype(BF)
        mix_first[late].start()

    @pl.loop(0, plane)
    def _(t):
        j = plane - 1 - t
        here = pl.ds(pl.multiple_of(j * rows, 16), rows)
        vk[...] = pltpu.roll(kv_all[:, j].reshape(keys, 128).astype(F32), 64, 1).astype(BF)
        limit = limits[j, :, 0:1]

        @pl.loop(0, pairs)
        def _(p):
            at = pl.ds(pl.multiple_of(p * 128, 128), 128)
            allowed = kp[0:1, :] <= limit
            q = queries[j, :, at]
            zero = jnp.zeros_like(q)
            outs, logs = [], []
            for first in (True, False):
                mine = lane < 64 if first else lane >= 64
                kv = kv_all[:, j].reshape(keys, 128)
                keyed, valued = (kv, vk[...]) if first else (vk[...], kv)
                scores = nt(jnp.where(mine, q, zero), keyed) * (HEAD_DIM**-0.5)
                scores = jnp.where(allowed, scores, MASKED)
                top = jnp.max(scores, axis=1, keepdims=True)
                weights = jnp.exp(scores - top)
                sums = jnp.sum(weights, axis=1, keepdims=True)
                outs.append(nn(weights.astype(BF), valued) / sums)
                logs.append(jnp.broadcast_to(top + jnp.log(sums), (rows, 128)))
            attended[here, at] = jnp.where(lane < 64, outs[0], outs[1]).astype(BF)
            lse[j, :, at] = jnp.where(lane < 64, logs[0], logs[1])

        part[j] = nn(attended[here, :], w_o[...]).astype(BF)

        @pl.when(t == 0)
        def _():
            mix_first["far_one"].start()
            mix_first["far_two"].start()
            branch_gather.forward()

        @pl.when(t == 1)
        def _():
            mix_first["two"].start()
            fetch_on(3)

        @pl.when(t == 2)
        def _():
            mix_first["one"].start()
            relay_on("far_one", "late_two", 0, 2)
            relay_on("far_two", "late_one", 1, 1)

    early_stores = [store(n) for n in range(12)]
    for n in (0, 1, 2, 3, 6, 7, 8, 9, 10, 11):
        early_stores[n].start()
    cross_on(1)
    cross_on(2)
    for name in ("one", "late_one", "two", "late_two"):
        mix_first[name].wait_recv()

    @pl.loop(0, rows // 16)
    def _(i):
        at = pl.ds(pl.multiple_of(i * 16, 16), 16)
        value = x_all[0, at, :].astype(F32) + part[0, at, :].astype(F32)
        value = value + landed[0, at, :].astype(F32) + landed[1, at, :].astype(F32)
        mixed[at, :] = value
        inverse = lax.rsqrt(jnp.mean(value * value, axis=1, keepdims=True) + EPSILON)
        n2_all[0, at, :] = (value * inverse * gain_two[0:1, :]).astype(BF)

    n2_gather.start()
    early_stores[4].start()

    def pack(j):
        @pl.loop(0, rows // 16)
        def _(i):
            at = pl.ds(pl.multiple_of(i * 16, 16), 16)
            to = pl.ds(pl.multiple_of(j * rows + i * 16, 16), 16)
            for h in range(2):
                for b in range(plane):
                    from_ = pl.ds(pl.multiple_of(((f ^ b) * 2 + (k ^ h)) * half, 128), half)
                    c = (h * plane + b) * half
                    n2[to, c : c + half] = n2_all[j, at, from_]

    pack(0)
    branch_gather.arrive()
    local[11].wait()

    def down_grad(at):
        grad[:, at] = nt(branch_all[...].reshape(total, depth), down[at, :])

    by_columns(down_grad)
    n2_gather.forward()

    @pl.loop(1, 3)
    def _(j):
        pack(j)

    cross_on(3)
    for n in range(7, 11):
        local[n].wait()
    for j in peers:
        gate_pair(j).wait_recv()
        up_pair(j).wait_recv()
    weight_stores = [store(n) for n in range(18, 22)]
    for copy in weight_stores:
        copy.start()
    n2_gather.arrive()

    pack(3)
    early_stores[5].start()
    later = [store(n) for n in range(12, 18)]
    for n in range(3):
        later[n].start()

    def feed(at):
        width = at.size
        n2_own, n2_sib = n2[:, 0 : depth // 2], n2[:, depth // 2 : depth]

        def through(own, other):
            first = nn(n2_own, own[:, :, at].reshape(depth // 2, width))
            return first + nn(n2_sib, other[:, :, at].reshape(depth // 2, width))

        gate = through(gate_own, gate_sib)
        up = through(up_own, up_sib)
        sigmoid = 1.0 / (1.0 + jnp.exp(-gate))
        hidden[:, at] = (gate * sigmoid * up).astype(BF)
        back = grad[:, at]
        gate_back[:, at] = (back * up * sigmoid * (1.0 + gate * (1.0 - sigmoid))).astype(BF)
        up_back[:, at] = (back * gate * sigmoid).astype(BF)

    by_columns(feed)
    for n in range(3, 6):
        later[n].start()
    for gather in (token_gather, branch_gather, n2_gather):
        gather.close()
    for copy in mix_first.values():
        copy.wait_send()
    for j in peers:
        note_send(j).wait_send()
        wp_send(j).wait_send()
        gate_pair(j).wait_send()
        up_pair(j).wait_send()
    projections = (wq_send, wk_send, w_across)
    by_parity(
        lambda: [c(3).wait_send() for c in projections],
        lambda: [c(j).wait_send() for j in (1, 2) for c in projections],
    )
    by_parity(
        lambda: [c(j).wait_send() for j in peers for c in (gate_send, gate_across)],
        lambda: [c(j).wait_send() for j in peers for c in (up_send, up_across)],
    )

    kv_pair(0).wait_send()
    for s in range(1, line):

        @pl.when(z >= s)
        def _():
            kv_send(s).wait_send()

        @pl.when(z + s < line)
        def _():
            kv_pair(s).wait_send()

    for copy in early_stores + later + weight_stores:
        copy.wait()


def front_pass(tokens, cotangent, lengths, attn_gain, mlp_gain, w_query, w_key, w_value, w_out, w_gate, w_up, w_down):
    rows, depth = tokens.shape
    plane, line = 4, 4
    total, slab = plane * rows, depth // plane
    half = slab // 2
    q_width = HEADS * HEAD_DIM // plane
    width = q_width + 128
    ff = w_down.shape[0]
    slot = rows * line * 2
    keys = slot
    act = (rows, depth)
    local = pl.BlockSpec(memory_space=pltpu.VMEM)
    anywhere = pl.BlockSpec(memory_space=pl.ANY)
    dma = lambda n: pltpu.SemaphoreType.DMA((n,))
    kv_shape = (2 * line, plane, rows, 128)
    sds = jax.ShapeDtypeStruct
    outs = [
        sds((total, depth), BF),
        sds((plane, rows, q_width), BF),
        sds((plane, rows, q_width), F32),
        sds((total, q_width), BF),
        sds(act, F32),
        sds((total, depth), BF),
        sds((plane, rows, 128), F32),
        sds((rows, 128), F32),
        sds((rows, 128), F32),
        sds((8, keys), F32),
        sds((8, depth), F32),
        sds((8, depth), F32),
        sds(kv_shape, BF),
        sds((plane,) + act, BF),
        sds((depth, width), BF),
        sds((total, ff), BF),
        sds((total, ff), BF),
        sds((total, ff), BF),
    ] + [sds((plane, half, ff), BF)] * 4
    held = [pltpu.VMEM(o.shape, o.dtype) for o in outs]
    held = held[:12] + held[15:18] + [pltpu.VMEM((total, ff), F32)]
    slabs = pltpu.VMEM((plane, half, ff), BF)
    scratch = held + [
        pltpu.VMEM((plane, 16, slab), BF),
        pltpu.VMEM((plane,) + act, BF),
        pltpu.VMEM((depth, width), BF),
        pltpu.VMEM(w_key.shape, BF),
        pltpu.VMEM(w_value.shape, BF),
        pltpu.VMEM((plane, half, 128), BF),
        slabs,
        slabs,
        slabs,
        slabs,
        pltpu.VMEM(w_down.shape, BF),
        pltpu.VMEM(kv_shape, BF),
        pltpu.VMEM((keys, 128), BF),
        pltpu.VMEM(w_out.shape, BF),
        pltpu.VMEM((plane,) + act, BF),
        pltpu.VMEM((2,) + act, BF),
        pltpu.VMEM((2, rows // 2, depth), BF),
        pltpu.VMEM((2, rows // 2, depth), BF),
        pltpu.VMEM((plane,) + act, BF),
        pltpu.VMEM((plane,) + act, BF),
        pltpu.VMEM(act, BF),
    ]
    sems = [12, 22, 3, 3, 3, 3, 2, 2, 2, 2, 3, 3, 3, 3, 3, 3, 1, 1, 3, 3, 4, 4, 3, 3, 3, 3, 3, 3, 3, 3, 3, 3]
    sems += [2, 2, 2, 2, 6, 6, 2, 2, 2, 2]
    return pl.pallas_call(
        front_kernel,
        out_shape=outs,
        in_specs=[pl.BlockSpec(memory_space=pltpu.SMEM)] + [local] * 5 + [anywhere] * 9,
        out_specs=[anywhere] * 22,
        scratch_shapes=scratch + [dma(n) for n in sems],
        compiler_params=pltpu.CompilerParams(
            vmem_limit_bytes=62 * 1024 * 1024, has_side_effects=True
        ),
        name="front_pass",
    )(
        lengths, jnp.stack([attn_gain, mlp_gain]), *rotary_parts(slot, rows),
        tokens, cotangent, w_query, w_key, w_value, w_out, w_gate, w_up, w_down,
    )


def add_into(target, other):
    @pl.loop(0, target.shape[0] // 16)
    def _(i):
        at = pl.ds(pl.multiple_of(i * 16, 16), 16)
        target[at, :] = (target[at, :].astype(F32) + other[at, :].astype(F32)).astype(BF)


def back_kernel(
    limits_in, gate_back_in, up_back_in, hidden_in, mixed_in, x_own_in, gain_one_in, gain_two_in,
    attended_in, queries_in, lse_in, kv_all_in, kp_in, cosine_in, sine_in,
    branch, w_out, w_down, wqkv, h1_hbm, n2_hbm, gate_own, gate_sib, up_own, up_sib,
    fin_down, fin_gate, fin_up, fin_out, fin_qkv, fin_gain,
    sib_down, sib_gate, sib_up, sib_out, sib_qkv, sib_gain,
    outputs, input_grad_out,
    limits, gate_back, up_back, hidden, mixed, x_own, gain_one, gain_two,
    attended, queries, lse, kv_all, kp, cosine, sine, branch_own, input_grad,
    src_down, src_gate, src_up, src_out, src_qkv, src_gain,
    swap_gate, swap_up, swap_qkv,
    end_down, end_gate, end_up, end_out, end_qkv, end_gain,
    give_down, give_gate, give_out, give_qkv, give_gain,
    turned, landed, landed_out, weights, down_blocks, qkv_blocks, part, da_all, wide, do_all, dqkv, left,
    vk, dk_sum, dv_sum, kv_part, kv_land, kv_mine, kv_line, gain_acc, gain_all,
    pair_s, pair_r, swap_s, swap_r, in_s, in_r, mid_s, mid_r, out_s, done_s, back_s, back_r, ready,
    local_s, weight_s, rs_s, rs_r, ro_s, ro_r, ag_s, ag_r, rq_s, rq_r, kp_s, kp_r, kz_s, kz_r, ga_s, ga_r,
):
    f, z, k = lax.axis_index("fsdp"), lax.axis_index("z"), lax.axis_index("core")
    plane, line = lax.axis_size("fsdp"), lax.axis_size("z")
    branch_flat = branch
    outer = (z == 0) | (z == line - 1)
    inner = jnp.logical_not(outer)
    inward = jnp.where(z < line // 2, z + 1, z - 1)
    outward = jnp.where(z < line // 2, z - 1, z + 1)
    rows, depth = mixed.shape
    total = plane * rows
    half_depth = depth // 2
    half = half_depth // plane
    q_width = attended.shape[1]
    pairs = q_width // 128
    peers = range(1, plane)

    kinds = {
        "down": (src_down, None, end_down, give_down, fin_down, sib_down),
        "gate": (src_gate, swap_gate, end_gate, give_gate, fin_gate, sib_gate),
        "up": (src_up, swap_up, end_up, give_gate, fin_up, sib_up),
        "out": (src_out, None, end_out, give_out, fin_out, sib_out),
        "qkv": (src_qkv, swap_qkv, end_qkv, give_qkv, fin_qkv, sib_qkv),
        "gain": (src_gain, None, end_gain, give_gain, fin_gain, sib_gain),
    }
    chunks = [(name, i) for name, kind in kinds.items() for i in range(kind[0].shape[0])]
    count = len(chunks)

    def group(c):
        return kinds[chunks[c][0]][3].shape[0]

    heads = [c for c in range(count) if chunks[c][1] % group(c) == 0]

    def remote(source, target, send, recv, where):
        return pltpu.make_async_remote_copy(
            src_ref=source,
            dst_ref=target,
            send_sem=send,
            recv_sem=recv,
            device_id=where,
            device_id_type=pl.DeviceIdType.MESH,
        )

    def swapped(c):
        name, i = chunks[c]
        return i // group(c) if kinds[name][1] is not None else 0

    def source(c):
        return part_of(c, 0)

    def part_of(c, which):
        name, i = chunks[c]
        return kinds[name][which].at[i]

    def given(c):
        return kinds[chunks[c][0]][3]

    def end(c):
        return part_of(c, 2)

    def pair_copy(c):
        start = given(c).at[chunks[c][1] % group(c)]
        return remote(start, source(c), pair_s.at[c], pair_r.at[c], {"core": 1 - k})

    def landing(c):
        name, i = chunks[c]
        return kinds[name][1].at[i - group(c)]

    def swap_copy(c):
        return remote(source(c), landing(c), swap_s.at[c], swap_r.at[c], {"fsdp": f ^ swapped(c)})

    def base(c):
        return landing(c) if swapped(c) else source(c)

    def in_copy(c):
        return remote(base(c), end(c), in_s.at[c], in_r.at[c], {"z": inward})

    def mid_copy(c):
        return remote(base(c), end(c), mid_s.at[c], mid_r.at[c], {"z": inward})

    def out_copy(c):
        return remote(end(c), end(c), out_s.at[c], mid_r.at[c], {"z": outward})

    def keep_copy(c):
        return pltpu.make_async_copy(end(c), part_of(c, 4), done_s.at[c])

    def back_copy(c):
        return remote(end(c), part_of(c, 5), back_s.at[c], back_r.at[c], {"core": 1 - k})

    def term(c, side, act):
        name, i = chunks[c]
        if name == "gain":
            act(slice(None), gain_all[...].astype(F32).sum(axis=0))
            return
        start = pl.multiple_of((k ^ side) * half_depth, 128)
        if name == "down":
            size, width = 128, half_depth
            turned[0:size, :] = hidden[:, i * size : (i + 1) * size].T
        elif name == "out":
            size, width = 2 * src_out.shape[1], half_depth
            turned[0:size, :] = attended[:, i * size // 2 : i * size // 2 + size].T
        else:
            size, width = half, source(c).shape[1]
            at = side * half_depth + i * (half // 2)
            turned[0:size, :] = left[:, at : at + half].T

        def block(first, span):
            if name == "down":
                right = wide[0:total, pl.ds(start + first, span)]
            elif name == "out":
                right = da_all[:, :, pl.ds(start + first, span)].reshape(total, span)
            else:
                right = {"gate": gate_back, "up": up_back, "qkv": dqkv}[name][:, pl.ds(first, span)]
            act(pl.ds(first, span), nn(turned[0:size, :], right))

        @pl.loop(0, width // 256)
        def _(n):
            block(pl.multiple_of(n * 256, 256), 256)

        if width % 256:
            block(width // 256 * 256, width % 256)

    def stage_give(c):
        slots = given(c)
        if c and given(c - 1) is slots:
            for n in range(group(c)):
                pair_copy(c - 1 - n).wait_send()
        size = slots.shape[1]

        def act(lanes, value):
            for n in range(group(c)):
                slots[n, :, lanes] = value[n * size : (n + 1) * size].astype(BF)

        term(c, 1, act)
        for n in range(group(c)):
            pair_copy(c + n).start()

    def stage_pair(c):
        for n in range(group(c)):
            pair_copy(c + n).wait_recv()
        size = source(c).shape[0]

        def act(lanes, value):
            for n in range(group(c)):
                target = source(c + n)
                added = target[:, lanes].astype(F32) + value[n * size : (n + 1) * size]
                target[:, lanes] = added.astype(BF)

        term(c, 0, act)
        for n in range(group(c)):
            if swapped(c + n):
                swap_copy(c + n).start()

    def stage_in(c):
        if swapped(c):
            swap_copy(c).wait_recv()

        @pl.when(outer)
        def _():
            in_copy(c).start()

    def stage_mid(c):
        @pl.when(inner)
        def _():
            in_copy(c).wait_recv()
            add_into(base(c), end(c))
            pl.semaphore_signal(
                ready, inc=1, device_id={"z": inward}, device_id_type=pl.DeviceIdType.MESH
            )
            pl.semaphore_wait(ready, 1)
            mid_copy(c).start()

    def stage_out(c):
        @pl.when(inner)
        def _():
            mid_copy(c).wait_recv()
            add_into(end(c), base(c))
            out_copy(c).start()

    def stage_keep(c):
        @pl.when(outer)
        def _():
            out_copy(c).wait_recv()

        keep_copy(c).start()
        back_copy(c).start()

    def back_send(j):
        mine = part.at[pl.ds(j * rows, rows), :]
        return remote(mine, landed.at[j - 1], rs_s.at[j - 1], rs_r.at[j - 1], {"fsdp": f ^ j})

    def out_send(j):
        mine = part.at[pl.ds(j * rows, rows), :]
        return remote(mine, landed_out.at[j - 1], ro_s.at[j - 1], ro_r.at[j - 1], {"fsdp": f ^ j})

    def da_send(j):
        return remote(da_all.at[0], da_all.at[j], ag_s.at[j - 1], ag_r.at[j - 1], {"fsdp": f ^ j})

    def dh_send(j):
        mine = wide.at[pl.ds(j * rows, rows), :]
        return remote(mine, landed.at[j - 1], rq_s.at[j - 1], rq_r.at[j - 1], {"fsdp": f ^ j})

    def gain_send(j):
        return remote(gain_all.at[0], gain_all.at[j], ga_s.at[j - 1], ga_r.at[j - 1], {"fsdp": f ^ j})

    moves = {
        "branch": (branch_flat, wide.at[pl.ds(0, total), :]), "hidden": (hidden_in, hidden), "n2": (n2_hbm, left),
        "gate_back": (gate_back_in, gate_back), "up_back": (up_back_in, up_back), "mixed": (mixed_in, mixed),
        "branch_own": (branch_flat.at[pl.ds(0, rows), :], branch_own), "gain_two": (gain_two_in, gain_two),
        "queries": (queries_in, queries), "lse": (lse_in, lse), "kv_all": (kv_all_in, kv_all),
        "limits": (limits_in, limits), "kp": (kp_in, kp), "cosine": (cosine_in, cosine), "sine": (sine_in, sine),
        "attended": (attended_in, attended), "x_own": (x_own_in, x_own), "gain_one": (gain_one_in, gain_one),
        "w_out": (w_out, wide.at[pl.ds(0, w_out.shape[0]), :]), "h1": (h1_hbm, left),
        "outputs": (mixed, outputs), "input_grad": (input_grad, input_grad_out),
    }
    moves = {
        name: pltpu.make_async_copy(*ends, local_s.at[n]) for n, (name, ends) in enumerate(moves.items())
    }

    def weight_loads(h, j):
        pairs_of = ((gate_own, up_own), (gate_sib, up_sib))[h]
        return [
            pltpu.make_async_copy(w.at[j], weights.at[j % 2, n], weight_s.at[j % 2, n])
            for n, w in enumerate(pairs_of)
        ]

    def columns_of(h, j):
        return pl.ds(pl.multiple_of(((f ^ j) * 2 + (k ^ h)) * half, 128), half)

    def piece_back(h):
        @pl.loop(0, plane)
        def _(j):
            @pl.when(j + 1 < plane)
            def _():
                for copy in weight_loads(h, j + 1):
                    copy.start()

            for copy in weight_loads(h, j):
                copy.wait()
            value = nt(gate_back[...], weights[j % 2, 0]) + nt(up_back[...], weights[j % 2, 1])
            part[:, columns_of(h, j)] = value.astype(BF)

        if h == 0:
            for copy in weight_loads(1, 0):
                copy.start()
        if h == 1:
            for j in peers:
                back_send(j).start()

    def down_at(b):
        size = depth // 8
        return pl.ds(pl.multiple_of(b * size, size), size)

    def down_load(b):
        return pltpu.make_async_copy(w_down.at[:, down_at(b)], down_blocks.at[b % 2], weight_s.at[b % 2, 0])

    def piece_out(h):
        if h == 0:
            for j in peers:
                back_send(j).wait_send()
            down_load(0).start()

        @pl.loop(4 * h, 4 * h + 4)
        def _(b):
            @pl.when(b + 1 < 8)
            def _():
                down_load(b + 1).start()

            down_load(b).wait()
            part[:, down_at(b)] = nn(hidden[...], down_blocks[b % 2]).astype(BF)

        if h == 1:
            for j in peers:
                out_send(j).start()

    def dh_load(b):
        block = wqkv.at[pl.ds(pl.multiple_of(b * half, half), half), :]
        return pltpu.make_async_copy(block, qkv_blocks.at[b % 2], weight_s.at[b % 2, 0])

    def rms_back(gradient_of, x_ref, gain, acc, write):
        acc[...] = jnp.zeros_like(acc)

        @pl.loop(0, rows // 16)
        def _(i):
            at = pl.ds(pl.multiple_of(i * 16, 16), 16)
            gradient = gradient_of(at)
            x = x_ref[at, :].astype(F32)
            inverse = lax.rsqrt(jnp.mean(x * x, axis=1, keepdims=True) + EPSILON)
            normed = x * inverse
            acc[...] += gradient * normed
            scaled = gradient * gain[0:1, :]
            write(at, inverse * (scaled - normed * jnp.mean(scaled * normed, axis=1, keepdims=True)))

    def piece_mixed():
        for name in ("mixed", "branch_own", "gain_two"):
            moves[name].wait()
        for j in peers:
            back_send(j).wait_recv()

        def gradient_of(at):
            value = part[at, :].astype(F32)
            for j in peers:
                value = value + landed[j - 1, at, :].astype(F32)
            return value

        def write(at, value):
            value = value + branch_own[at, :].astype(F32)
            input_grad[at, :] = value
            da_all[0, at, :] = value.astype(BF)

        rms_back(gradient_of, mixed, gain_two, gain_acc.at[1], write)
        for j in peers:
            da_send(j).start()

    def piece_do():
        moves["w_out"].wait()
        for j in peers:
            da_send(j).wait_recv()

        @pl.loop(0, plane)
        def _(j):
            do_all[j] = nt(da_all[j], wide[0 : w_out.shape[0], :]).astype(BF)

    def piece_attend(j):
        here = pl.ds(pl.multiple_of(j * rows, 16), rows)
        vk[...] = pltpu.roll(kv_all[:, j].reshape(vk.shape).astype(F32), 64, 1).astype(BF)
        dk_sum[...] = jnp.zeros_like(dk_sum)
        dv_sum[...] = jnp.zeros_like(dv_sum)
        limit = limits[j, :, 0:1]
        lane = lax.broadcasted_iota(jnp.int32, (rows, 128), 1)

        @pl.loop(0, pairs)
        def _(p):
            at = pl.ds(pl.multiple_of(p * 128, 128), 128)
            allowed = kp[0:1, :] <= limit
            q, do = queries[j, :, at], do_all[j, :, at]
            logs = lse[j, :, at]
            zero = jnp.zeros_like(q)
            parts = []
            for first in (True, False):
                mine = lane < 64 if first else lane >= 64
                kv = kv_all[:, j].reshape(vk.shape)
                keyed, valued = (kv, vk[...]) if first else (vk[...], kv)
                q_own, do_own = jnp.where(mine, q, zero), jnp.where(mine, do, zero)
                scores = nt(q_own, keyed) * (HEAD_DIM**-0.5)
                log_total = logs[:, 0:1] if first else logs[:, 64:65]
                weights = jnp.where(allowed, jnp.exp(scores - log_total), 0.0)
                joint = weights * nt(do_own, valued)
                back = (joint - weights * jnp.sum(joint, axis=1, keepdims=True)).astype(BF)
                parts.append(nn(back, keyed))
                dk_sum[...] += tn(back, q_own)
                dv_sum[...] += tn(weights.astype(BF), do_own)
            rotated = jnp.where(lane < 64, parts[0], parts[1]) * (HEAD_DIM**-0.5)
            rotated = rotated * cosine[...] - swap_halves(rotated) * sine[...]
            dqkv[here, at] = rotated.astype(BF)

        dk = dk_sum[...]
        dv = dv_sum[...]
        dk = (dk + pltpu.roll(dk, 64, 1)) * (HEAD_DIM**-0.5)
        dv = dv + pltpu.roll(dv, 64, 1)
        wide_lane = lax.broadcasted_iota(jnp.int32, dk.shape, 1)
        packed = jnp.where(wide_lane < 64, dk, dv).astype(BF)
        kv_part[:, j] = packed.reshape(kv_part.shape[0], rows, 128)

    kv_pair = remote(kv_part.at[pl.ds(line, line)], kv_land, kp_s.at[0], kp_r.at[0], {"core": 1 - k})

    def kv_send(s):
        return remote(kv_mine.at[s], kv_line.at[s - 1], kz_s.at[s - 1], kz_r.at[s - 1], {"z": z + s})

    def piece_kv_line():
        kv_pair.wait_recv()
        for s in range(line):
            kv_mine[s] = (kv_part[s].astype(F32) + kv_land[s].astype(F32)).astype(BF)
        for s in range(1, line):

            @pl.when(z + s < line)
            def _():
                kv_send(s).start()

    def piece_kv_sum():
        for s in range(1, line):

            @pl.when(z >= s)
            def _():
                kv_send(s).wait_recv()
                kv_mine[0] = (kv_mine[0].astype(F32) + kv_line[s - 1].astype(F32)).astype(BF)

        lane = lax.broadcasted_iota(jnp.int32, (rows, 128), 1)
        for j in range(plane):
            value = kv_mine[0, j].astype(F32)
            rotated = value * cosine[...] - swap_halves(value) * sine[...]
            value = jnp.where(lane < 64, rotated, value).astype(BF)
            dqkv[j * rows : (j + 1) * rows, q_width : q_width + 128] = value

    def piece_dh():
        dh_load(0).start()

        @pl.loop(0, 2 * plane)
        def _(b):
            @pl.when(b + 1 < 2 * plane)
            def _():
                dh_load(b + 1).start()

            dh_load(b).wait()
            wide[0:total, columns_of(b // plane, b % plane)] = nt(dqkv[...], qkv_blocks[b % 2]).astype(BF)

        for j in peers:
            dh_send(j).start()

    def piece_input():
        for name in ("x_own", "gain_one"):
            moves[name].wait()
        for j in peers:
            dh_send(j).wait_recv()

        def gradient_of(at):
            value = wide[at, :].astype(F32)
            for j in peers:
                value = value + landed[j - 1, at, :].astype(F32)
            return value

        def write(at, value):
            input_grad[at, :] = input_grad[at, :] + value

        rms_back(gradient_of, x_own, gain_one, gain_acc.at[0], write)
        moves["input_grad"].start()
        place = lax.broadcasted_iota(jnp.int32, (16, depth), 0)
        one = jnp.sum(gain_acc[0], axis=0, keepdims=True)
        two = jnp.sum(gain_acc[1], axis=0, keepdims=True)
        gain_all[0] = jnp.where(place == 0, one, jnp.where(place == 1, two, 0.0)).astype(BF)
        for j in peers:
            gain_send(j).start()

    def piece_outputs():
        for j in peers:
            out_send(j).wait_recv()

        @pl.loop(0, rows // 16)
        def _(i):
            at = pl.ds(pl.multiple_of(i * 16, 16), 16)
            value = mixed[at, :] + part[at, :].astype(F32)
            for j in peers:
                value = value + landed_out[j - 1, at, :].astype(F32)
            mixed[at, :] = value

        moves["outputs"].start()

    def piece_gain():
        for j in peers:
            gain_send(j).wait_recv()

    in_lag, mid_lag, out_lag, keep_lag = LAGS
    events = []

    def give_tick(c):
        return c - (AHEAD[1] if kinds[chunks[c][0]][1] is not None else AHEAD[0])

    for c in heads:
        events.append((give_tick(c), 0, stage_give, c))
        events.append((give_tick(c) + 1, 1, stage_pair, c))
    for c in range(count):
        events.append((c + in_lag, 2, stage_in, c))
        events.append((c + mid_lag, 3, stage_mid, c))
        events.append((c + out_lag, 4, stage_out, c))
        events.append((c + keep_lag, 5, stage_keep, c))
    steps = (
        (piece_back, 0), (piece_back, 1), piece_mixed, piece_do, (piece_out, 0), (piece_out, 1), (piece_attend, 0),
        (piece_attend, 1), (piece_attend, 2), (piece_attend, 3), kv_pair.start, piece_kv_line, piece_kv_sum, piece_dh, piece_outputs, piece_input, piece_gain,
    )
    for n, (step, tick) in enumerate(zip(steps, STEPS)):
        act, which = step if isinstance(step, tuple) else (step, None)
        events.append((tick, 6 + n, act, which))

    def head_of(name, which):
        return [c for c in heads if chunks[c][0] == name][which]

    def wait_for(*names):
        def act():
            for name in names:
                moves[name].wait()

        return act

    events.append((give_tick(head_of("down", 0)), -1, wait_for("branch", "hidden"), None))
    first = min(STEPS[0], give_tick(head_of("gate", 0)))
    events.append((first, 5.2, wait_for("n2", "gate_back", "up_back"), None))
    events.append((give_tick(head_of("down", -1)) + 1, 31, moves["w_out"].start, None))
    events.append((give_tick(head_of("up", -1)) + 1, 31, moves["h1"].start, None))
    events.append((give_tick(head_of("qkv", 0)), -1, moves["h1"].wait, None))
    events.append((give_tick(head_of("out", 0)), -1, moves["attended"].wait, None))
    attending = ("queries", "lse", "kv_all", "limits", "kp", "cosine", "sine")
    events.append((STEPS[6], 5.5, wait_for(*attending), None))
    events.sort(key=lambda e: e[:2])

    for name, move in moves.items():
        if name not in ("w_out", "h1", "outputs", "input_grad"):
            move.start()
    for copy in weight_loads(0, 0):
        copy.start()
    for _, _, act, which in events:
        act() if which is None else act(which)

    for c in range(count):
        if not [n for n in heads if n > c and given(n) is given(c)]:
            pair_copy(c).wait_send()
        if swapped(c):
            swap_copy(c).wait_send()
        keep_copy(c).wait()
        back_copy(c).wait_send()
        back_copy(c).wait_recv()

        @pl.when(outer)
        def _():
            in_copy(c).wait_send()

        @pl.when(inner)
        def _():
            mid_copy(c).wait_send()
            out_copy(c).wait_send()

    moves["outputs"].wait()
    moves["input_grad"].wait()
    for j in peers:
        out_send(j).wait_send()
        da_send(j).wait_send()
        dh_send(j).wait_send()
        gain_send(j).wait_send()
    kv_pair.wait_send()
    for s in range(1, line):

        @pl.when(z + s < line)
        def _():
            kv_send(s).wait_send()


def back_pass(held, far):
    count, line = lax.axis_size("fsdp"), lax.axis_size("z")
    mixed, attended, kv_all, hidden = held[4], held[8], held[11], held[3]
    rows, depth = mixed.shape
    total, half_depth = count * rows, depth // 2
    half = half_depth // count
    q_width = attended.shape[1]
    ff = hidden.shape[1]
    keys = kv_all.shape[0] * rows
    slabs = (2 * count, half // 2, ff)
    shapes = [
        (ff // 128, 128, half_depth),
        slabs,
        slabs,
        (4, q_width // 4, half_depth),
        (2 * count, half // 2, q_width + 128),
        (1, 16, depth),
    ]
    anywhere = pl.BlockSpec(memory_space=pl.ANY)
    ends = [jax.ShapeDtypeStruct(s, BF) for s in shapes]
    act = jax.ShapeDtypeStruct((rows, depth), F32)
    block = (rows, depth)
    chunk_count = sum(s[0] for s in shapes)
    dma = lambda *n: pltpu.SemaphoreType.DMA(n)
    groups = (1, 2, 2, 2, 1)
    scratch = (
        [pltpu.VMEM(x.shape, x.dtype) for x in held]
        + [pltpu.VMEM(block, BF), pltpu.VMEM(block, F32)]
        + [pltpu.VMEM(s, BF) for s in shapes]
        + [pltpu.VMEM((shapes[i][0] - 2,) + shapes[i][1:], BF) for i in (1, 2, 4)]
        + [pltpu.VMEM(s, BF) for s in shapes]
        + [pltpu.VMEM((g,) + shapes[i][1:], BF) for g, i in zip(groups, (0, 1, 3, 4, 5))]
        + [
            pltpu.VMEM((max(half, q_width // 2, 128), total), BF),
            pltpu.VMEM((count - 1,) + block, BF),
            pltpu.VMEM((count - 1,) + block, BF),
            pltpu.VMEM((2, 2, half, ff), BF),
            pltpu.VMEM((2, ff, depth // 8), BF),
            pltpu.VMEM((2, half, q_width + 128), BF),
            pltpu.VMEM((total, depth), BF),
            pltpu.VMEM((count,) + block, BF),
            pltpu.VMEM((max(total, q_width), depth), BF),
            pltpu.VMEM((count, rows, q_width), BF),
            pltpu.VMEM((total, q_width + 128), BF),
            pltpu.VMEM((total, depth), BF),
            pltpu.VMEM((keys, 128), BF),
            pltpu.VMEM((keys, 128), F32),
            pltpu.VMEM((keys, 128), F32),
            pltpu.VMEM(kv_all.shape, BF),
            pltpu.VMEM((line,) + kv_all.shape[1:], BF),
            pltpu.VMEM((line,) + kv_all.shape[1:], BF),
            pltpu.VMEM((line - 1,) + kv_all.shape[1:], BF),
            pltpu.VMEM((2, 16, depth), F32),
            pltpu.VMEM((count, 16, depth), BF),
        ]
        + [dma(chunk_count)] * 12
        + [pltpu.SemaphoreType.REGULAR, dma(22), dma(2, 2)]
        + [dma(count - 1)] * 8
        + [dma(1)] * 2
        + [dma(line - 1)] * 2
        + [dma(count - 1)] * 2
    )
    out = pl.pallas_call(
        back_kernel,
        out_shape=ends + ends + [act, act],
        in_specs=[anywhere] * (len(held) + len(far)),
        out_specs=[anywhere] * 14,
        scratch_shapes=scratch,
        compiler_params=pltpu.CompilerParams(
            vmem_limit_bytes=63 * 1024 * 1024, has_side_effects=True
        ),
        name="back_pass",
    )(*held, *far)
    return out[:6], out[6:12], out[12], out[13]


def finish_kernel(
    own_down, own_gate, own_up, own_out, own_qkv, own_gain, sib_down, sib_gate, sib_up, sib_out, sib_qkv,
    outputs_in, input_grad_in, outputs, input_grad, down, gate, up, out, query, key, value, attn_gain, mlp_gain,
    low_rows, low_cols, high_rows, high_cols, kv, acts, gain_in, gain_high, load_s, store_s, side_s,
):
    f, k = lax.axis_index("fsdp"), lax.axis_index("core")
    plane = lax.axis_size("fsdp")
    half, ff = own_gate.shape[1], own_gate.shape[2]
    half_depth = own_down.shape[2]
    slab = 2 * half
    q_width = own_qkv.shape[2] - 128
    tasks = []
    for side, (d, o, g, u, q) in enumerate(
        ((own_down, own_out, own_gate, own_up, own_qkv), (sib_down, sib_out, sib_gate, sib_up, sib_qkv))
    ):
        rows_at = pl.ds(pl.multiple_of((k ^ side) * half, 8), half)
        cols_at = pl.ds(pl.multiple_of((k ^ side) * half_depth, 128), half_depth)
        for source, target in ((d, down), (o, out)):
            for i in range(source.shape[0]):
                size = source.shape[1]
                tasks.append((source.at[i], target.at[pl.ds(i * size, size), cols_at], 0))
        for source, target in ((g, gate), (u, up)):
            for j in range(plane):
                to = pl.ds(pl.multiple_of((f ^ j) * ff, 128), ff)
                tasks.append((source.at[j], target.at[rows_at, to], 1))
        for j in range(plane):
            to = pl.ds(pl.multiple_of((f ^ j) * q_width, 128), q_width)
            tasks.append((q.at[j, :, pl.ds(0, q_width)], query.at[rows_at, to], 1))
    slots = low_rows.shape[0]

    def window(buffer, n, shape):
        return buffer.at[n % slots, pl.ds(0, shape[0]), pl.ds(0, shape[1])]

    def load(n):
        source, _, kind = tasks[n]
        low = (low_rows, low_cols)[kind]
        return pltpu.make_async_copy(source, window(low, n, source.shape), load_s.at[n])

    def store(n):
        source, target, kind = tasks[n]
        high = (high_rows, high_cols)[kind]
        return pltpu.make_async_copy(window(high, n, source.shape), target, store_s.at[n])

    sides = [
        pltpu.make_async_copy(own_gain.at[0], gain_in, side_s.at[0]),
        pltpu.make_async_copy(own_qkv.at[:, :, pl.ds(q_width, 128)], kv.at[0], side_s.at[1]),
        pltpu.make_async_copy(sib_qkv.at[:, :, pl.ds(q_width, 128)], kv.at[1], side_s.at[2]),
        pltpu.make_async_copy(outputs_in, acts.at[0], side_s.at[3]),
        pltpu.make_async_copy(input_grad_in, acts.at[1], side_s.at[4]),
    ]
    for n in range(slots):
        load(n).start()
    for copy in sides:
        copy.start()
    for n in range(len(tasks)):
        source, _, kind = tasks[n]
        shape = source.shape
        low, high = ((low_rows, high_rows), (low_cols, high_cols))[kind]
        load(n).wait()
        if n >= slots:
            store(n - slots).wait()

        @pl.loop(0, shape[0] // 16)
        def _(i):
            at = pl.ds(pl.multiple_of(i * 16, 16), 16)
            high[n % slots, at, 0 : shape[1]] = low[n % slots, at, 0 : shape[1]].astype(F32)

        store(n).start()
        if n + slots < len(tasks):
            load(n + slots).start()
    for copy in sides:
        copy.wait()
    lasts = [
        pltpu.make_async_copy(acts.at[0], outputs, side_s.at[5]),
        pltpu.make_async_copy(acts.at[1], input_grad, side_s.at[6]),
    ]
    for copy in lasts:
        copy.start()
    mine = pl.ds(pl.multiple_of(f * slab, 128), slab)
    gain_high[...] = gain_in[...].astype(F32)
    attn_gain[...] = gain_high[0:1, mine]
    mlp_gain[...] = gain_high[1:2, mine]
    lane = lax.broadcasted_iota(jnp.int32, (half, 128), 1)
    for side in range(2):
        rows_at = pl.ds(pl.multiple_of((k ^ side) * half, 8), half)
        for pair in range(plane // 2):
            first = kv[side, f ^ (2 * pair)].astype(F32)
            second = kv[side, f ^ (2 * pair + 1)].astype(F32)
            at = slice(pair * 128, (pair + 1) * 128)
            key[rows_at, at] = jnp.where(lane < 64, first, pltpu.roll(second, 64, 1))
            value[rows_at, at] = jnp.where(lane < 64, pltpu.roll(first, 64, 1), second)
    for n in range(max(0, len(tasks) - slots), len(tasks)):
        store(n).wait()
    for copy in lasts:
        copy.wait()


def finish(owns, sibs, outputs, input_grad):
    plane = lax.axis_size("fsdp")
    down, gate, _, out, qkv, gain = (x.shape for x in owns)
    depth = 2 * down[2]
    slab = 2 * gate[1]
    q_width = qkv[2] - 128
    sds = jax.ShapeDtypeStruct
    shapes = [
        outputs.shape, input_grad.shape,
        (down[0] * down[1], depth), (slab, plane * gate[2]), (slab, plane * gate[2]), (out[0] * out[1], depth),
        (slab, plane * q_width), (slab, KV_HEADS * HEAD_DIM), (slab, KV_HEADS * HEAD_DIM), (1, slab), (1, slab),
    ]
    slots = 6
    tall = (slots, max(down[1], out[1]), down[2])
    wide = (slots, gate[1], max(gate[2], q_width))
    count = 2 * (down[0] + out[0] + 3 * plane)
    anywhere, local = pl.BlockSpec(memory_space=pl.ANY), pl.BlockSpec(memory_space=pltpu.VMEM)
    return pl.pallas_call(
        finish_kernel,
        out_shape=[sds(s, F32) for s in shapes],
        in_specs=[anywhere] * 13,
        out_specs=[anywhere] * 7 + [local] * 4,
        scratch_shapes=[
            pltpu.VMEM(tall, BF),
            pltpu.VMEM(wide, BF),
            pltpu.VMEM(tall, F32),
            pltpu.VMEM(wide, F32),
            pltpu.VMEM((2, plane, gate[1], 128), BF),
            pltpu.VMEM((2,) + outputs.shape, F32),
            pltpu.VMEM(gain[1:], BF),
            pltpu.VMEM(gain[1:], F32),
            pltpu.SemaphoreType.DMA((count,)),
            pltpu.SemaphoreType.DMA((count,)),
            pltpu.SemaphoreType.DMA((7,)),
        ],
        compiler_params=params(),
        name="finish",
    )(*owns, *sibs[:5], outputs, input_grad)


def body(
    tokens, cotangent, lengths, attn_gain, w_query, w_key, w_value, w_out, mlp_gain, w_gate, w_up, w_down
):
    seqs, rows, depth = tokens.shape
    count = lax.axis_size("fsdp")
    slab = depth // count
    x_own = tokens.reshape(rows, depth)
    (
        h1, queries, lse, attended, mixed, n2, limits, cosine, sine, kp, gain_one, gain_two, kv_all, branch, wqkv,
        gate_back, up_back, hidden, gate_own, gate_sib, up_own, up_sib,
    ) = front_pass(
        x_own, cotangent.reshape(rows, depth), lengths, attn_gain, mlp_gain,
        w_query, w_key, w_value, w_out, w_gate, w_up, w_down,
    )
    held = (
        limits, gate_back, up_back, hidden, mixed, x_own, gain_one, gain_two,
        attended, queries, lse, kv_all, kp, cosine, sine,
    )
    branch = branch.reshape(count * rows, depth)
    far = (branch, w_out, w_down, wqkv, h1, n2, gate_own, gate_sib, up_own, up_sib)
    owns, sibs, outputs, input_grad = back_pass(held, far)

    def whole(x):
        return x.reshape(4, -1, x.shape[2]) if x.shape[0] > 1 else x

    owns, sibs = [whole(x) for x in owns], [whole(x) for x in sibs]
    (
        outputs, input_grad, down_grad, gate_grad, up_grad, out_grad, query_grad, key_grad, value_grad, gain_a, gain_m
    ) = finish(owns, sibs, outputs, input_grad)
    return (
        outputs.reshape(seqs, rows, depth),
        input_grad.reshape(seqs, rows, depth),
        gain_a.reshape(slab),
        query_grad,
        key_grad,
        value_grad,
        out_grad,
        gain_m.reshape(slab),
        gate_grad,
        up_grad,
        down_grad,
    )


def solution(mesh):
    count, ctx = mesh.shape["fsdp"], mesh.shape["ctx"]
    split = Mesh(mesh.devices.reshape(count, ctx // 2, 2), ("fsdp", "z", "core"))
    act = P("fsdp", ("z", "core"), None)
    row, mat = P("fsdp"), P("fsdp", None)
    fast = count == 4 and count == KV_HEADS and ctx == 8
    return jax.shard_map(
        body if fast else body_plain,
        mesh=split,
        in_specs=(act, act, row, row, mat, mat, mat, mat, row, mat, mat, mat),
        out_specs=(act, act, row, mat, mat, mat, mat, row, mat, mat, mat),
        check_vma=False,
    )
```

```python
import functools

import jax
import jax.numpy as jnp
import numpy as np
from jax import lax
from jax.experimental import pallas as pl
from jax.experimental.pallas import tpu as pltpu
from jax.sharding import Mesh
from jax.sharding import PartitionSpec as P

HEADS = 32
KV_HEADS = 4
HEAD_DIM = 64
EPSILON = 1e-05
ROPE_BASE = 10000.0
MASKED = -1e30
FAR = 1 << 30
BF = jnp.bfloat16
F32 = jnp.float32
VMEM_BYTES = 56 * 1024 * 1024
LAGS = (0, 2, 4, 6)
AHEAD = (1, 4)
STEPS = (0, 1, 7, 12, 13, 14, 15, 16, 17, 18, 18, 20, 24, 24, 23, 28, 30)


def params(**kw):
    return pltpu.CompilerParams(vmem_limit_bytes=VMEM_BYTES, **kw)


def along_plane(value, step):
    count = lax.axis_size("fsdp")
    return lax.ppermute(value, "fsdp", [(i, i ^ step) for i in range(count)])


def to_sibling(value):
    return lax.ppermute(value, "core", [(0, 1), (1, 0)])


def along_line(value, shift):
    count = lax.axis_size("z")
    return lax.ppermute(
        value, "z", [(i, i + shift) for i in range(count) if 0 <= i + shift < count]
    )


def plane_bits():
    count = lax.axis_size("fsdp")
    return [1 << b for b in range(count.bit_length() - 1)]


def plane_gather(block):
    half = block.shape[0] // 2
    parts = []
    for which, bits in ((0, plane_bits()), (1, plane_bits()[::-1])):
        held = {0: block[which * half : (which + 1) * half]}
        for bit in bits:
            order = sorted(held)
            got = along_plane(jnp.stack([held[j] for j in order]), bit)
            for n, j in enumerate(order):
                held[j ^ bit] = got[n]
        parts.append(held)
    return [jnp.concatenate([parts[0][j], parts[1][j]]) for j in range(lax.axis_size("fsdp"))]


def plane_reduce(partial):
    half = partial.shape[1] // 2
    done = []
    for which, bits in ((0, plane_bits()[::-1]), (1, plane_bits())):
        held = {j: partial[j, which * half : (which + 1) * half] for j in range(partial.shape[0])}
        for bit in bits:
            going = [j for j in sorted(held) if j & bit]
            got = along_plane(jnp.stack([held[j].astype(BF) for j in going]), bit)
            for n, j in enumerate(going):
                held[j ^ bit] = held[j ^ bit].astype(F32) + got[n].astype(F32)
                del held[j]
        done.append(held[0])
    return jnp.concatenate(done)


def line_sum(value):
    count = lax.axis_size("z")
    place = lax.axis_index("z")
    half = count // 2
    for i in range(half - 1):
        got = lax.ppermute(value, "z", [(i, i + 1), (count - 1 - i, count - 2 - i)])
        value = value + got
    value = value + lax.ppermute(value, "z", [(half - 1, half), (half, half - 1)])
    for i in range(half - 2, -1, -1):
        got = lax.ppermute(value, "z", [(i + 1, i), (count - 2 - i, count - 1 - i)])
        outer = (place == i) | (place == count - 1 - i)
        value = jnp.where(outer, got, value)
    return value


def move_kernel(idx_ref, x_ref, o_ref):
    o_ref[...] = x_ref[...]


def pick_columns(x, index, count):
    rows, width = x.shape
    size = width // count
    spec = pltpu.PrefetchScalarGridSpec(
        num_scalar_prefetch=1,
        grid=(count,),
        in_specs=[pl.BlockSpec((rows, size), lambda b, idx: (0, idx[b]))],
        out_specs=pl.BlockSpec((rows, size), lambda b, idx: (0, b)),
    )
    return pl.pallas_call(
        move_kernel,
        grid_spec=spec,
        out_shape=jax.ShapeDtypeStruct(x.shape, x.dtype),
        compiler_params=params(),
        name="pick_columns",
    )(index, x)


def put_columns(x, index, count):
    rows, width = x.shape
    size = width // count
    spec = pltpu.PrefetchScalarGridSpec(
        num_scalar_prefetch=1,
        grid=(count,),
        in_specs=[pl.BlockSpec((rows, size), lambda b, idx: (0, b))],
        out_specs=pl.BlockSpec((rows, size), lambda b, idx: (0, idx[b])),
    )
    return pl.pallas_call(
        move_kernel,
        grid_spec=spec,
        out_shape=jax.ShapeDtypeStruct(x.shape, x.dtype),
        compiler_params=params(),
        name="put_columns",
    )(index, x)


def cut_blocks(weight, f, k, count, dtype=BF):
    rows, full = weight.shape
    width, half = full // count, rows // 2
    if width % 128:
        own = lax.dynamic_slice_in_dim(weight, k * half, half, 0).reshape(half, count, width)
        return jnp.stack(
            [lax.dynamic_index_in_dim(own, f ^ j, 1, keepdims=False) for j in range(count)]
        )
    spec = pltpu.PrefetchScalarGridSpec(
        num_scalar_prefetch=1,
        grid=(count,),
        in_specs=[pl.BlockSpec((half, width), lambda j, at: (at[1], at[0] ^ j))],
        out_specs=pl.BlockSpec((None, half, width), lambda j, at: (j, 0, 0)),
    )
    return pl.pallas_call(
        move_kernel,
        grid_spec=spec,
        out_shape=jax.ShapeDtypeStruct((count, half, width), weight.dtype),
        compiler_params=params(),
        name="cut_blocks",
    )(jnp.stack([f, k]), weight)


def join_kernel(at_ref, own_ref, sib_ref, o_ref):
    @pl.when(pl.program_id(0) == 0)
    def _():
        o_ref[...] = own_ref[...].astype(o_ref.dtype)

    @pl.when(pl.program_id(0) == 1)
    def _():
        o_ref[...] = sib_ref[...].astype(o_ref.dtype)


def join_rows(own, sib, f, k):
    count, half, width = own.shape
    if width % 128:
        halves = jnp.stack([own, sib])
        return jnp.concatenate(
            [
                jnp.concatenate(
                    [
                        lax.dynamic_index_in_dim(
                            lax.dynamic_index_in_dim(halves, k ^ h, 0, keepdims=False),
                            f ^ i,
                            0,
                            keepdims=False,
                        )
                        for i in range(count)
                    ],
                    axis=1,
                )
                for h in range(2)
            ],
            axis=0,
        ).astype(F32)
    spec = pltpu.PrefetchScalarGridSpec(
        num_scalar_prefetch=1,
        grid=(2, count),
        in_specs=[
            pl.BlockSpec(
                (None, half, width),
                lambda s, i, at: (at[0] ^ jnp.where(s == 0, i, count - 1), 0, 0),
            ),
            pl.BlockSpec(
                (None, half, width), lambda s, i, at: (at[0] ^ jnp.where(s == 1, i, 0), 0, 0)
            ),
        ],
        out_specs=pl.BlockSpec((half, width), lambda s, i, at: (at[1] ^ s, i)),
    )
    return pl.pallas_call(
        join_kernel,
        grid_spec=spec,
        out_shape=jax.ShapeDtypeStruct((2 * half, count * width), F32),
        compiler_params=params(),
        name="join_rows",
    )(jnp.stack([f, k]), own, sib)


def join_columns(own, sib, k):
    rows, half = own.shape
    count = 4
    size = rows // count
    spec = pltpu.PrefetchScalarGridSpec(
        num_scalar_prefetch=1,
        grid=(2, count),
        in_specs=[
            pl.BlockSpec((size, half), lambda s, i, at: (jnp.where(s == 0, i, count - 1), 0)),
            pl.BlockSpec((size, half), lambda s, i, at: (jnp.where(s == 1, i, 0), 0)),
        ],
        out_specs=pl.BlockSpec((size, half), lambda s, i, at: (i, at[0] ^ s)),
    )
    return pl.pallas_call(
        join_kernel,
        grid_spec=spec,
        out_shape=jax.ShapeDtypeStruct((rows, 2 * half), F32),
        compiler_params=params(),
        name="join_columns",
    )(k.reshape(1), own, sib)


def swap_halves(block):
    lane = lax.broadcasted_iota(jnp.int32, block.shape, 1)
    return jnp.where(lane % 64 < 32, pltpu.roll(block, 96, 1), pltpu.roll(block, 32, 1))


def qkv_kernel(idx_ref, x_ref, gain_ref, w_ref, cos_ref, sin_ref, h_ref, q_ref, kv_ref):
    blocks = idx_ref.shape[0]
    size = x_ref.shape[1] // blocks
    x = x_ref[...].astype(F32)
    inverse = lax.rsqrt(jnp.mean(x * x, axis=1, keepdims=True) + EPSILON)
    for b in range(blocks):
        at = pl.ds(pl.multiple_of(idx_ref[b] * size, 128), size)
        part = x_ref[:, at].astype(F32) * inverse * gain_ref[:, at]
        h_ref[:, b * size : (b + 1) * size] = part.astype(BF)
    out = jnp.dot(h_ref[...], w_ref[...], preferred_element_type=F32)
    cosine, sine = cos_ref[...], sin_ref[...]
    pairs = q_ref.shape[1] // 128
    for c in range(pairs):
        block = out[:, c * 128 : (c + 1) * 128]
        q_ref[:, c * 128 : (c + 1) * 128] = (block * cosine + swap_halves(block) * sine).astype(BF)
    block = out[:, pairs * 128 :]
    lane = lax.broadcasted_iota(jnp.int32, block.shape, 1)
    turned = block * cosine + swap_halves(block) * sine
    kv_ref[...] = jnp.where(lane < 64, turned, block).astype(BF)


def qkv_project(idx, x, gain, weight, cosine, sine, rows):
    total, depth = x.shape
    width = weight.shape[1]
    spec = pltpu.PrefetchScalarGridSpec(
        num_scalar_prefetch=1,
        grid=(total // rows,),
        in_specs=[
            pl.BlockSpec((rows, depth), lambda i, idx: (i, 0)),
            pl.BlockSpec((1, depth), lambda i, idx: (0, 0)),
            pl.BlockSpec((depth, width), lambda i, idx: (0, 0)),
            pl.BlockSpec((rows, 128), lambda i, idx: (0, 0)),
            pl.BlockSpec((rows, 128), lambda i, idx: (0, 0)),
        ],
        out_specs=[
            pl.BlockSpec((rows, depth), lambda i, idx: (i, 0)),
            pl.BlockSpec((rows, width - 128), lambda i, idx: (i, 0)),
            pl.BlockSpec((rows, 128), lambda i, idx: (i, 0)),
        ],
    )
    return pl.pallas_call(
        qkv_kernel,
        grid_spec=spec,
        out_shape=[
            jax.ShapeDtypeStruct((total, depth), BF),
            jax.ShapeDtypeStruct((total, width - 128), BF),
            jax.ShapeDtypeStruct((total, 128), BF),
        ],
        compiler_params=params(),
        cost_estimate=pl.CostEstimate(
            flops=2 * total * depth * width,
            bytes_accessed=4 * total * depth + 2 * depth * width + 2 * total * width,
            transcendentals=0,
        ),
        name="qkv_project",
    )(idx, x, gain, weight, cosine, sine)


def nt(a, b):
    return lax.dot_general(a, b, (((1,), (1,)), ((), ())), preferred_element_type=F32)


def tn(a, b):
    return lax.dot_general(a, b, (((0,), (0,)), ((), ())), preferred_element_type=F32)


def nn(a, b):
    return jnp.dot(a, b, preferred_element_type=F32)


def limits(at_ref, rows):
    j = pl.program_id(0)
    place = at_ref[0] - lax.broadcasted_iota(jnp.int32, (rows, 1), 0)
    return jnp.minimum(place, at_ref[1 + j] - 1)


def attend_kernel(at_ref, q_ref, kv_ref, kp_ref, o_ref, lse_ref, vk_ref):
    rows = q_ref.shape[0]
    keys = vk_ref.shape[0]
    kv = kv_ref[...].reshape(keys, 128)

    @pl.when(pl.program_id(1) == 0)
    def _():
        vk_ref[...] = pltpu.roll(kv.astype(F32), 64, 1).astype(BF)

    vk = vk_ref[...]
    allowed = kp_ref[...] <= limits(at_ref, rows)
    lane = lax.broadcasted_iota(jnp.int32, (rows, 128), 1)
    q = q_ref[...]
    zero = jnp.zeros_like(q)
    outs, logs = [], []
    for first in (True, False):
        mine = lane < 64 if first else lane >= 64
        scores = nt(jnp.where(mine, q, zero), kv if first else vk) * (HEAD_DIM**-0.5)
        scores = jnp.where(allowed, scores, MASKED)
        top = jnp.max(scores, axis=1, keepdims=True)
        weights = jnp.exp(scores - top)
        total = jnp.sum(weights, axis=1, keepdims=True)
        outs.append(nn(weights.astype(BF), vk if first else kv) / total)
        logs.append(jnp.broadcast_to(top + jnp.log(total), (rows, 128)))
    o_ref[...] = jnp.where(lane < 64, outs[0], outs[1]).astype(BF)
    lse_ref[...] = jnp.where(lane < 64, logs[0], logs[1])


def attend(at, q, kv, kp):
    chunks, seqs, rows, _ = kv.shape
    pairs = q.shape[2] // 128
    keys = chunks * rows
    spec = pltpu.PrefetchScalarGridSpec(
        num_scalar_prefetch=1,
        grid=(seqs, pairs),
        in_specs=[
            pl.BlockSpec((None, rows, 128), lambda j, p, at: (j, 0, p)),
            pl.BlockSpec((chunks, None, rows, 128), lambda j, p, at: (0, j, 0, 0)),
            pl.BlockSpec((1, keys), lambda j, p, at: (0, 0)),
        ],
        out_specs=[
            pl.BlockSpec((None, rows, 128), lambda j, p, at: (j, 0, p)),
            pl.BlockSpec((None, rows, 128), lambda j, p, at: (j, 0, p)),
        ],
        scratch_shapes=[pltpu.VMEM((keys, 128), BF)],
    )
    size = seqs * pairs * 2 * rows * keys
    return pl.pallas_call(
        attend_kernel,
        grid_spec=spec,
        out_shape=[
            jax.ShapeDtypeStruct(q.shape, BF),
            jax.ShapeDtypeStruct(q.shape, F32),
        ],
        compiler_params=params(),
        cost_estimate=pl.CostEstimate(
            flops=size * 4 * 128, bytes_accessed=4 << 20, transcendentals=size
        ),
        name="attend",
    )(at, q, kv, kp)


def attend_back_kernel(
    at_ref, q_ref, do_ref, lse_ref, kv_ref, kp_ref, cos_ref, sin_ref, dq_ref, dkv_ref, vk_ref, dk_ref, dv_ref
):
    rows = q_ref.shape[0]
    keys = vk_ref.shape[0]
    pair = pl.program_id(1)
    kv = kv_ref[...].reshape(keys, 128)

    @pl.when(pair == 0)
    def _():
        vk_ref[...] = pltpu.roll(kv.astype(F32), 64, 1).astype(BF)
        dk_ref[...] = jnp.zeros_like(dk_ref)
        dv_ref[...] = jnp.zeros_like(dv_ref)

    vk = vk_ref[...]
    allowed = kp_ref[...] <= limits(at_ref, rows)
    lane = lax.broadcasted_iota(jnp.int32, (rows, 128), 1)
    q, do = q_ref[...], do_ref[...]
    zero = jnp.zeros_like(q)
    parts = []
    for first in (True, False):
        mine = lane < 64 if first else lane >= 64
        keyed, valued = (kv, vk) if first else (vk, kv)
        q_own, do_own = jnp.where(mine, q, zero), jnp.where(mine, do, zero)
        scores = nt(q_own, keyed) * (HEAD_DIM**-0.5)
        log_total = lse_ref[:, 0:1] if first else lse_ref[:, 64:65]
        weights = jnp.where(allowed, jnp.exp(scores - log_total), 0.0)
        joint = weights * nt(do_own, valued)
        back = (joint - weights * jnp.sum(joint, axis=1, keepdims=True)).astype(BF)
        parts.append(nn(back, keyed))
        dk_ref[...] += tn(back, q_own)
        dv_ref[...] += tn(weights.astype(BF), do_own)
    turned = jnp.where(lane < 64, parts[0], parts[1]) * (HEAD_DIM**-0.5)
    dq_ref[...] = (turned * cos_ref[...] - swap_halves(turned) * sin_ref[...]).astype(BF)

    @pl.when(pair == pl.num_programs(1) - 1)
    def _():
        dk = dk_ref[...]
        dv = dv_ref[...]
        dk = (dk + pltpu.roll(dk, 64, 1)) * (HEAD_DIM**-0.5)
        dv = dv + pltpu.roll(dv, 64, 1)
        wide = lax.broadcasted_iota(jnp.int32, dk.shape, 1)
        dkv_ref[...] = jnp.where(wide < 64, dk, dv).astype(BF).reshape(dkv_ref.shape)


def attend_back(at, q, do, lse, kv, kp, cosine, sine):
    chunks, seqs, rows, _ = kv.shape
    pairs = q.shape[2] // 128
    keys = chunks * rows
    tall = pl.BlockSpec((None, rows, 128), lambda j, p, at: (j, 0, p))
    whole = pl.BlockSpec((chunks, None, rows, 128), lambda j, p, at: (0, j, 0, 0))
    flat = pl.BlockSpec((rows, 128), lambda j, p, at: (0, 0))
    spec = pltpu.PrefetchScalarGridSpec(
        num_scalar_prefetch=1,
        grid=(seqs, pairs),
        in_specs=[tall, tall, tall, whole, pl.BlockSpec((1, keys), lambda j, p, at: (0, 0)), flat, flat],
        out_specs=[tall, whole],
        scratch_shapes=[
            pltpu.VMEM((keys, 128), BF),
            pltpu.VMEM((keys, 128), F32),
            pltpu.VMEM((keys, 128), F32),
        ],
    )
    size = seqs * pairs * 2 * rows * keys
    return pl.pallas_call(
        attend_back_kernel,
        grid_spec=spec,
        out_shape=[
            jax.ShapeDtypeStruct(q.shape, BF),
            jax.ShapeDtypeStruct(kv.shape, BF),
        ],
        compiler_params=params(),
        cost_estimate=pl.CostEstimate(
            flops=size * 10 * 128, bytes_accessed=8 << 20, transcendentals=size
        ),
        name="attend_back",
    )(at, q, do, lse, kv, kp, cosine, sine)


def rms_backward(row_block, inverse, gain_vec, gradient):
    normed = row_block * inverse
    gain_grad = jnp.sum(gradient * normed, axis=0)
    scaled = gradient * gain_vec
    back = inverse * (scaled - normed * jnp.mean(scaled * normed, axis=1, keepdims=True))
    return (back, gain_grad)


def body_plain(
    tokens, cotangent, lengths, attn_gain, w_query, w_key, w_value, w_out, mlp_gain, w_gate, w_up, w_down
):
    seqs, rows, depth = tokens.shape
    count, line = lax.axis_size("fsdp"), lax.axis_size("z")
    f, z, k = lax.axis_index("fsdp"), lax.axis_index("z"), lax.axis_index("core")
    slot = rows * line * 2
    total = count * rows
    slab = depth // count
    half = slab // 2
    q_width = HEADS * HEAD_DIM // count
    shared = max(1, count // KV_HEADS)

    x_own = tokens.reshape(rows, depth)
    chunk = 2 * z + k
    first_pos = slot - 1 - chunk * rows

    length = lengths[0]
    words = jnp.zeros((slab,), F32).at[0].set((length // 64).astype(F32)).at[1].set((length % 64).astype(F32))
    note = jnp.stack([attn_gain, mlp_gain, words.astype(BF), jnp.zeros((slab,), BF)])
    notes = [note] + [along_plane(note, j) for j in range(1, count)]
    notes_abs = [lax.dynamic_index_in_dim(jnp.stack(notes), f ^ i, 0, keepdims=False) for i in range(count)]
    gain_one = jnp.concatenate([n[0] for n in notes_abs]).astype(F32).reshape(1, depth)
    gain_two = jnp.concatenate([n[1] for n in notes_abs]).astype(F32).reshape(1, depth)
    all_lengths = jnp.stack(
        [n[2, 0].astype(jnp.int32) * 64 + n[2, 1].astype(jnp.int32) for n in notes]
    )

    x_all = jnp.concatenate(plane_gather(x_own))

    wq = cut_blocks(w_query, f, k, count)
    key_cols = lax.dynamic_slice_in_dim(w_key, k * half, half, 0).reshape(half, KV_HEADS, HEAD_DIM)
    value_cols = lax.dynamic_slice_in_dim(w_value, k * half, half, 0).reshape(half, KV_HEADS, HEAD_DIM)

    def head_of(j):
        return (f ^ j) // shared

    wkv = jnp.stack(
        [
            jnp.concatenate(
                [
                    lax.dynamic_index_in_dim(key_cols, head_of(j), 1, keepdims=False),
                    lax.dynamic_index_in_dim(value_cols, head_of(j), 1, keepdims=False),
                ],
                axis=1,
            )
            for j in range(count)
        ]
    )
    wqkv = jnp.concatenate([wq, wkv], axis=2)
    wqkv_own = jnp.stack([wqkv[0]] + [along_plane(wqkv[j], j) for j in range(1, count)])
    wqkv_sib = to_sibling(wqkv_own)
    wqkv_all = jnp.concatenate([wqkv_own, wqkv_sib]).reshape(depth, q_width + 128)

    def fetch(weight):
        cut = cut_blocks(weight, f, k, count)
        width = cut.shape[2]
        own = jnp.stack([cut[0]] + [along_plane(cut[j], j) for j in range(1, count)])
        sib = to_sibling(own)
        return own.reshape(depth // 2, width), sib.reshape(depth // 2, width)

    gate_own, gate_sib = fetch(w_gate)
    up_own, up_sib = fetch(w_up)

    order = jnp.stack([(f ^ j) * 2 + (k ^ h) for h in range(2) for j in range(count)]).astype(jnp.int32)

    half_dim = HEAD_DIM // 2
    frequency = jnp.power(ROPE_BASE, jnp.arange(half_dim, dtype=F32) * (-2.0 / HEAD_DIM))
    positions = first_pos - jnp.arange(rows, dtype=jnp.int32)
    angles = positions.astype(F32)[:, None] * frequency[None, :]
    cos32, sin32 = jnp.cos(angles), jnp.sin(angles)
    cosine = jnp.concatenate([cos32] * 4, axis=1)
    sine = jnp.concatenate([-sin32, sin32, -sin32, sin32], axis=1)

    normed_one, queries, kv = qkv_project(order, x_all, gain_one, wqkv_all, cosine, sine, rows)
    queries = queries.reshape(count, rows, q_width)
    kv = kv.reshape(count, rows, 128)

    mine = [kv] + [along_line(kv, -s) for s in range(1, line)]
    mine = jnp.stack(mine)
    kv_all = jnp.concatenate([mine, to_sibling(mine)])
    places = []
    for h in range(2):
        for s in range(line):
            start = slot - 1 - (2 * (z + s) + (k ^ h)) * rows
            places.append(start - jnp.arange(rows, dtype=jnp.int32))
    kp = jnp.concatenate(places)
    kp = jnp.where(kp < 0, FAR, kp).reshape(1, -1)
    at = jnp.concatenate([first_pos.reshape(1), all_lengths]).astype(jnp.int32)

    attended, log_total = attend(at, queries, kv_all, kp)
    attended = attended.reshape(total, q_width)

    mixed_part = nn(attended, w_out).astype(BF).reshape(count, rows, depth)
    inputs = x_own.astype(F32)
    mixed = inputs + plane_reduce(mixed_part)
    inv_two = lax.rsqrt(jnp.mean(mixed * mixed, axis=1, keepdims=True) + EPSILON)
    normed_two_own = (mixed * inv_two * gain_two).astype(BF)
    normed_two = jnp.concatenate(plane_gather(normed_two_own))
    normed_two = pick_columns(normed_two, order, 2 * count)
    n2_own, n2_sib = normed_two[:, : depth // 2], normed_two[:, depth // 2 :]

    valid = (positions < length).astype(F32)[:, None]
    out_back = cotangent.reshape(rows, depth).astype(F32) * valid
    branch_own = out_back.astype(BF)
    branch = jnp.concatenate(plane_gather(branch_own))

    gate = nn(n2_own, gate_own) + nn(n2_sib, gate_sib)
    up = nn(n2_own, up_own) + nn(n2_sib, up_sib)
    sigmoid = jax.nn.sigmoid(gate)
    hidden = (gate * sigmoid * up).astype(BF)

    half_depth = depth // 2
    branch_mine = lax.dynamic_slice_in_dim(branch, k * half_depth, half_depth, 1)
    branch_other = lax.dynamic_slice_in_dim(branch, (1 - k) * half_depth, half_depth, 1)

    def pair_sum(own, other):
        return (own + to_sibling(other.astype(BF)).astype(F32)).astype(BF)

    def swap_slabs(own):
        return jnp.stack([own[0]] + [along_plane(own[j], j) for j in range(1, count)])

    down_half = line_sum(pair_sum(tn(hidden, branch_mine), tn(hidden, branch_other)))
    down_grad = join_columns(down_half, to_sibling(down_half), k)

    hidden_grad = nt(branch, w_down)
    gate_back = (hidden_grad * up * sigmoid * (1.0 + gate * (1.0 - sigmoid))).astype(BF)
    up_back = (hidden_grad * gate * sigmoid).astype(BF)

    def slab_grad(left_own, left_other, right):
        width = right.shape[1]
        own = pair_sum(tn(left_own, right), tn(left_other, right)).reshape(count, half, width)
        return line_sum(swap_slabs(own))

    gate_half = slab_grad(n2_own, n2_sib, gate_back)
    gate_grad = join_rows(gate_half, to_sibling(gate_half), f, k)
    up_half = slab_grad(n2_own, n2_sib, up_back)
    up_grad = join_rows(up_half, to_sibling(up_half), f, k)

    back_own = (nt(gate_back, gate_own) + nt(up_back, up_own)).astype(BF)
    back_sib = (nt(gate_back, gate_sib) + nt(up_back, up_sib)).astype(BF)
    normed_back = put_columns(jnp.concatenate([back_own, back_sib], axis=1), order, 2 * count)
    normed_back = plane_reduce(normed_back.reshape(count, rows, depth))

    out_part = nn(hidden, w_down).astype(BF).reshape(count, rows, depth)
    outputs = mixed + plane_reduce(out_part)

    mixed_back, gain_two_grad = rms_backward(mixed, inv_two, gain_two, normed_back)
    mixed_grad = out_back + mixed_back
    attn_back = jnp.concatenate(plane_gather(mixed_grad.astype(BF)))
    attended_grad = nt(attn_back, w_out).astype(BF).reshape(count, rows, q_width)

    back_mine = lax.dynamic_slice_in_dim(attn_back, k * half_depth, half_depth, 1)
    back_other = lax.dynamic_slice_in_dim(attn_back, (1 - k) * half_depth, half_depth, 1)
    out_half = line_sum(pair_sum(tn(attended, back_mine), tn(attended, back_other)))
    out_grad = join_columns(out_half, to_sibling(out_half), k)

    query_back, kv_part = attend_back(at, queries, attended_grad, log_total, kv_all, kp, cosine, sine)
    kv_mine = kv_part[:line].astype(F32) + to_sibling(kv_part[line:]).astype(F32)
    kv_back = kv_mine[0]
    for s in range(1, line):
        kv_back = kv_back + along_line(kv_mine[s].astype(BF), s).astype(F32)
    lead, trail, flat = kv_back[..., :32], kv_back[..., 32:64], kv_back[..., 64:]
    kv_back = jnp.concatenate(
        [lead * cos32 + trail * sin32, trail * cos32 - lead * sin32, flat], axis=-1
    ).astype(BF)
    qkv_back = jnp.concatenate(
        [query_back.reshape(total, q_width), kv_back.reshape(total, 128)], axis=1
    )

    normed_one_back = nt(qkv_back, wqkv_all).astype(BF)
    normed_one_back = put_columns(normed_one_back, order, 2 * count)
    normed_one_back = plane_reduce(normed_one_back.reshape(count, rows, depth))
    inv_one = lax.rsqrt(jnp.mean(inputs * inputs, axis=1, keepdims=True) + EPSILON)
    input_back, gain_one_grad = rms_backward(inputs, inv_one, gain_one, normed_one_back)
    input_grad = mixed_grad + input_back

    n1_own, n1_sib = normed_one[:, :half_depth], normed_one[:, half_depth:]
    qkv_own = pair_sum(tn(n1_own, qkv_back), tn(n1_sib, qkv_back)).reshape(count, half, q_width + 128)
    gains = jnp.stack([gain_one_grad, gain_two_grad]).reshape(2, count, slab)
    gains = jnp.stack(
        [lax.dynamic_index_in_dim(gains, f ^ j, 1, keepdims=False) for j in range(count)]
    ).astype(BF)
    gains = line_sum(swap_slabs(gains))
    qkv_half = line_sum(swap_slabs(qkv_own))
    gains = jnp.sum(gains.astype(F32), axis=0) + jnp.sum(to_sibling(gains).astype(F32), axis=0)
    qkv_other = to_sibling(qkv_half)
    query_grad = join_rows(qkv_half[:, :, :q_width], qkv_other[:, :, :q_width], f, k)
    halves = jnp.stack([qkv_half[:, :, q_width:], qkv_other[:, :, q_width:]])

    def by_head(lo, hi):
        both = [lax.dynamic_index_in_dim(halves, k ^ h, 0, keepdims=False) for h in range(2)]
        both = jnp.concatenate(both, axis=1).astype(F32)[:, :, lo:hi]
        cols = jnp.stack([lax.dynamic_index_in_dim(both, f ^ i, 0, keepdims=False) for i in range(count)])
        cols = cols.reshape(KV_HEADS, shared, slab, HEAD_DIM).sum(1)
        return jnp.transpose(cols, (1, 0, 2)).reshape(slab, KV_HEADS * HEAD_DIM)

    key_grad = by_head(0, 64)
    value_grad = by_head(64, 128)

    return (
        outputs.reshape(seqs, rows, depth),
        input_grad.reshape(seqs, rows, depth),
        gains[0],
        query_grad,
        key_grad,
        value_grad,
        out_grad,
        gains[1],
        gate_grad,
        up_grad,
        down_grad,
    )


def rotary_parts(slot, rows):
    lane = np.arange(128) % (HEAD_DIM // 2)
    frequency = ROPE_BASE ** (lane * (-2.0 / HEAD_DIM))
    starts = (slot - 1 - rows * np.arange(slot // rows))[:, None] * frequency[None, :]
    steps = np.arange(rows)[:, None] * frequency[None, :]
    return [jnp.asarray(t(a), F32) for a in (starts, steps) for t in (np.cos, np.sin)]


def front_kernel(
    length_ref, attn_gain, mlp_gain, start_cos, start_sin, step_cos, step_sin,
    tokens, cotangent, w_query, w_key, w_value, w_out, w_gate, w_up, w_down,
    h1_out, queries_out, lse_out, attended_out, mixed_out, n2_out, limits_out, cosine_out, sine_out, kp_out,
    gain_one_out, gain_two_out, kv_out, branch_out, wqkv_out, gate_back_out, up_back_out, hidden_out,
    gate_own_out, gate_sib_out, up_own_out, up_sib_out,
    h1, queries, lse, attended, mixed, n2, limits, cosine, sine, kp, gain_one, gain_two,
    gate_back, up_back, hidden, grad,
    notes, x_all, wqkv, keys_in, values_in, kv_give, gate_own, gate_sib, up_own, up_sib, down,
    kv_all, vk, w_o, part, landed, relay, relayed, n2_all, branch_all, cot_in,
    local_s, store_s, wx_s, wx_r, note_s, note_r, tok_s, tok_r, tof_s, tof_r, wq_s, wq_r, wk_s, wk_r, wp_s, wp_r, wkp_s, wkp_r,
    kz_s, kz_r, kp_s, kp_r, gt_s, gt_r, up_s, up_r, gz_s, gz_r, gs_s, gs_r, us_s, us_r,
    bt_s, bt_r, btf_s, btf_r, mx_s, mx_r, nt_s, nt_r, ntf_s, ntf_r,
):
    f, z, k = lax.axis_index("fsdp"), lax.axis_index("z"), lax.axis_index("core")
    plane, line = 4, 4
    rows, depth = tokens.shape
    total = plane * rows
    slab = depth // plane
    half = slab // 2
    hr = rows // 2
    q_width = w_out.shape[0]
    pairs = q_width // 128
    ff = w_down.shape[0]
    keys = vk.shape[0]
    slot = rows * line * 2
    even = z % 2 == 0
    across = z + 1 - 2 * (z % 2)
    peers = (1, 2, 3)
    first_pos = slot - 1 - (2 * z + k) * rows

    def remote(source, target, send, recv, where):
        return pltpu.make_async_remote_copy(
            src_ref=source,
            dst_ref=target,
            send_sem=send,
            recv_sem=recv,
            device_id=where,
            device_id_type=pl.DeviceIdType.MESH,
        )

    sib = {"core": 1 - k}

    def chip(j):
        return {"fsdp": f ^ j}

    def cols(weight, j, side, width):
        start = pl.multiple_of((f ^ j) * width, 128)
        return weight.at[pl.ds(pl.multiple_of((k ^ side) * half, 16), half), pl.ds(start, width)]

    class Gather:
        def __init__(self, source, target, send, recv, fsend, frecv):
            self.near = {
                j: remote(source, target.at[j], send.at[j - 1], recv.at[j - 1], chip(j)) for j in (1, 2)
            }
            self.far = {
                j: remote(
                    target.at[j, pl.ds((j - 1) * hr, hr), :],
                    target.at[3, pl.ds((j - 1) * hr, hr), :],
                    fsend.at[j - 1],
                    frecv.at[j - 1],
                    chip(3 - j),
                )
                for j in (1, 2)
            }

        def start(self):
            for j in (1, 2):
                self.near[j].start()

        def forward(self):
            for j in (1, 2):
                self.near[j].wait_recv()
                self.far[j].start()

        def arrive(self):
            for j in (1, 2):
                self.far[j].wait_recv()

        def close(self):
            for j in (1, 2):
                self.near[j].wait_send()
                self.far[j].wait_send()

    def note_send(j):
        return remote(notes.at[0], notes.at[j], note_s.at[j - 1], note_r.at[j - 1], chip(j))

    token_gather = Gather(tokens, x_all, tok_s, tok_r, tof_s, tof_r)
    branch_gather = Gather(branch_all.at[0], branch_all, bt_s, bt_r, btf_s, btf_r)
    n2_gather = Gather(n2_all.at[0], n2_all, nt_s, nt_r, ntf_s, ntf_r)

    def wq_send(j):
        target = wqkv.at[pl.ds(j * half, half), pl.ds(0, q_width)]
        return remote(cols(w_query, j, 0, q_width), target, wq_s.at[j - 1], wq_r.at[j - 1], chip(j))

    def wk_send(j):
        target = wqkv.at[pl.ds(j * half, half), pl.ds(q_width, 128)]
        return remote(kv_give.at[j], target, wk_s.at[j - 1], wk_r.at[j - 1], chip(j))

    def wp_send(j):
        source = wqkv.at[pl.ds(j * half, half), :]
        target = wqkv.at[pl.ds((plane + j) * half, half), :]
        return remote(source, target, wp_s.at[j - 1], wp_r.at[j - 1], sib)

    def w_across(j):
        block = wqkv.at[pl.ds(j * half, half), :]
        return remote(block, block, wx_s.at[j - 1], wx_r.at[j - 1], {"z": across})

    def kv_send(s):
        return remote(kv_all.at[0], kv_all.at[s], kz_s.at[s - 1], kz_r.at[s - 1], {"z": z - s})

    def kv_pair(s):
        return remote(kv_all.at[s], kv_all.at[line + s], kp_s.at[s], kp_r.at[s], sib)

    def gate_send(j):
        return remote(cols(w_gate, j, 0, ff), gate_own.at[j], gt_s.at[j - 1], gt_r.at[j - 1], chip(j))

    def up_send(j):
        return remote(cols(w_up, j, 0, ff), up_own.at[j], up_s.at[j - 1], up_r.at[j - 1], chip(j))

    def gate_across(j):
        return remote(gate_own.at[j], gate_own.at[j], gz_s.at[j - 1], gz_r.at[j - 1], {"z": across})

    def up_across(j):
        return remote(up_own.at[j], up_own.at[j], gz_s.at[j - 1], gz_r.at[j - 1], {"z": across})

    def by_parity(act_even, act_odd):
        @pl.when(even)
        def _():
            act_even()

        @pl.when(jnp.logical_not(even))
        def _():
            act_odd()

    def fetch_start():
        by_parity(
            lambda: [gate_send(j).start() for j in (3, 1, 2)], lambda: [up_send(j).start() for j in (3, 1, 2)]
        )

    def fetch_on(j):
        def gate_on():
            gate_send(j).wait_recv()
            gate_across(j).start()
            gate_pair(j).start()

        def up_on():
            up_send(j).wait_recv()
            up_across(j).start()
            up_pair(j).start()

        by_parity(gate_on, up_on)

    def cross_on(j):
        def up_on():
            up_across(j).wait_recv()
            up_pair(j).start()

        def gate_on():
            gate_across(j).wait_recv()
            gate_pair(j).start()

        by_parity(up_on, gate_on)

    def gate_pair(j):
        return remote(gate_own.at[j], gate_sib.at[j], gs_s.at[j - 1], gs_r.at[j - 1], sib)

    def up_pair(j):
        return remote(up_own.at[j], up_sib.at[j], us_s.at[j - 1], us_r.at[j - 1], sib)

    def span(which):
        return pl.ds(which * hr, hr)

    mix_first = {
        "one": remote(part.at[1, span(0), :], landed.at[0, span(0), :], mx_s.at[0], mx_r.at[0], chip(1)),
        "two": remote(part.at[2, span(1), :], landed.at[1, span(1), :], mx_s.at[1], mx_r.at[1], chip(2)),
        "far_one": remote(part.at[3, span(0), :], relay.at[0], mx_s.at[2], mx_r.at[2], chip(1)),
        "far_two": remote(part.at[3, span(1), :], relay.at[1], mx_s.at[3], mx_r.at[3], chip(2)),
        "late_two": remote(relayed.at[0], landed.at[1, span(0), :], mx_s.at[4], mx_r.at[4], chip(2)),
        "late_one": remote(relayed.at[1], landed.at[0, span(1), :], mx_s.at[5], mx_r.at[5], chip(1)),
    }

    local = [
        pltpu.make_async_copy(source, target, local_s.at[n])
        for n, (source, target) in enumerate(
            [
                (tokens, x_all.at[0]),
                (w_key, keys_in),
                (w_value, values_in),
                (cols(w_query, 0, 0, q_width), wqkv.at[pl.ds(0, half), pl.ds(0, q_width)]),
                (cols(w_query, 0, 1, q_width), wqkv.at[pl.ds(plane * half, half), pl.ds(0, q_width)]),
                (cotangent, cot_in),
                (w_out, w_o),
                (cols(w_gate, 0, 0, ff), gate_own.at[0]),
                (cols(w_gate, 0, 1, ff), gate_sib.at[0]),
                (cols(w_up, 0, 0, ff), up_own.at[0]),
                (cols(w_up, 0, 1, ff), up_sib.at[0]),
                (w_down, down),
            ]
        )
    ]

    stored = [
        (h1, h1_out), (queries, queries_out), (lse, lse_out), (attended, attended_out), (mixed, mixed_out),
        (n2, n2_out), (limits, limits_out), (cosine, cosine_out), (sine, sine_out), (kp, kp_out),
        (gain_one, gain_one_out), (gain_two, gain_two_out), (kv_all, kv_out), (branch_all, branch_out),
        (wqkv, wqkv_out), (gate_back, gate_back_out), (up_back, up_back_out), (hidden, hidden_out),
        (gate_own, gate_own_out), (gate_sib, gate_sib_out), (up_own, up_own_out), (up_sib, up_sib_out),
    ]

    def store(n):
        return pltpu.make_async_copy(*stored[n], store_s.at[n])

    length = length_ref[0]
    place = lax.broadcasted_iota(jnp.int32, (16, slab), 0)
    high, low = (length // 64).astype(F32), (length % 64).astype(F32)
    note = jnp.where(place == 0, attn_gain[...].astype(F32)[None, :], mlp_gain[...].astype(F32)[None, :])
    note = jnp.where(place == 2, high, jnp.where(place == 3, low, note))
    notes[0] = note.astype(BF)
    for j in peers:
        note_send(j).start()
    by_parity(lambda: wq_send(3).start(), lambda: [wq_send(j).start() for j in (1, 2)])
    token_gather.start()
    for copy in local:
        copy.start()

    local[1].wait()
    local[2].wait()

    def head_columns(j, side):
        at = pl.ds(pl.multiple_of((k ^ side) * half, 16), half)
        head = f ^ j
        width = KV_HEADS * HEAD_DIM
        key = pltpu.roll(keys_in[at, :].astype(F32), (width - head * 64) % width, 1)[:, :128]
        value = pltpu.roll(values_in[at, :].astype(F32), (width - head * 64 + 64) % width, 1)[:, :128]
        lane = lax.broadcasted_iota(jnp.int32, key.shape, 1)
        return jnp.where(lane < 64, key, value).astype(BF)

    for j in (3, 1, 2):
        kv_give[j] = head_columns(j, 0)
    by_parity(lambda: wk_send(3).start(), lambda: [wk_send(j).start() for j in (1, 2)])
    wqkv[0:half, q_width : q_width + 128] = head_columns(0, 0)
    wqkv[plane * half : (plane + 1) * half, q_width : q_width + 128] = head_columns(0, 1)

    chunk = pl.ds(2 * z + k, 1)
    cos_at, sin_at = start_cos[chunk, :], start_sin[chunk, :]
    lane = lax.broadcasted_iota(jnp.int32, (rows, 128), 1)
    cosine[...] = cos_at * step_cos[...] + sin_at * step_sin[...]
    turn = sin_at * step_cos[...] - cos_at * step_sin[...]
    sine[...] = jnp.where(lane % 64 < 32, -turn, turn)
    for h in range(2):
        for s in range(line):
            start = slot - 1 - (2 * (z + s) + (k ^ h)) * rows
            spot = start - lax.broadcasted_iota(jnp.int32, (8, rows), 1)
            spot = jnp.where(spot < 0, FAR, spot).astype(F32)
            kp[:, (h * line + s) * rows : (h * line + s + 1) * rows] = spot

    for s in range(1, line):

        @pl.when(z + s >= line)
        def _():
            kv_all[s] = jnp.zeros(kv_all.shape[1:], BF)
            kv_all[line + s] = jnp.zeros(kv_all.shape[1:], BF)

    local[5].wait()
    row_pos = (first_pos - lax.broadcasted_iota(jnp.int32, (rows, 1), 0)).astype(F32)
    valid = row_pos < jnp.full((rows, 1), length.astype(F32))
    branch_all[0] = jnp.where(valid, cot_in[...].astype(F32), 0.0).astype(BF)

    def projections_on(j):
        wq_send(j).wait_recv()
        wk_send(j).wait_recv()
        w_across(j).start()
        wp_send(j).start()

    by_parity(lambda: projections_on(3), lambda: [projections_on(j) for j in (1, 2)])
    token_gather.forward()
    fetch_start()

    for j in peers:
        note_send(j).wait_recv()
    for j in range(plane):
        at = pl.ds(pl.multiple_of((f ^ j) * slab, 128), slab)
        gain_one[:, at] = jnp.broadcast_to(notes[j, 0:1, :].astype(F32), (8, slab))
        gain_two[:, at] = jnp.broadcast_to(notes[j, 1:2, :].astype(F32), (8, slab))
        theirs = notes[j, 2:3, 0:1].astype(F32) * 64.0 + notes[j, 3:4, 0:1].astype(F32)
        limits[j] = jnp.broadcast_to(jnp.minimum(row_pos, theirs - 1.0), (rows, 128))

    def normalize(j, x_ref):
        @pl.loop(0, rows // 16)
        def _(i):
            at = pl.ds(pl.multiple_of(i * 16, 16), 16)
            x = x_ref[at, :].astype(F32)
            inverse = lax.rsqrt(jnp.mean(x * x, axis=1, keepdims=True) + EPSILON)
            to = pl.ds(pl.multiple_of(j * rows + i * 16, 16), 16)
            for h in range(2):
                for b in range(plane):
                    from_ = pl.ds(pl.multiple_of(((f ^ b) * 2 + (k ^ h)) * half, 128), half)
                    value = x_ref[at, from_].astype(F32) * inverse * gain_one[0:1, from_]
                    c = (h * plane + b) * half
                    h1[to, c : c + half] = value.astype(BF)

    local[0].wait()
    normalize(0, x_all.at[0])

    def projections_in(js):
        for j in js:
            w_across(j).wait_recv()
            wp_send(j).start()

    by_parity(lambda: projections_in((1, 2)), lambda: projections_in((3,)))

    @pl.loop(1, 3)
    def _(j):
        normalize(j, x_all.at[j])

    token_gather.arrive()
    normalize(3, x_all.at[3])
    local[3].wait()
    local[4].wait()
    for j in (1, 2, 3):
        wp_send(j).wait_recv()

    kv_cols = nn(h1[...], wqkv[:, q_width : q_width + 128])
    for j in range(plane):
        value = kv_cols[j * rows : (j + 1) * rows]
        turned = value * cosine[...] + swap_halves(value) * sine[...]
        kv_all[0, j] = jnp.where(lane < 64, turned, value).astype(BF)
    for s in range(1, line):

        @pl.when(z >= s)
        def _():
            kv_send(s).start()

    kv_pair(0).start()
    branch_gather.start()

    @pl.loop(0, pairs // 2)
    def _(p):
        at = pl.ds(pl.multiple_of(p * 256, 256), 256)
        out = nn(h1[...], wqkv[:, at])
        for j in range(plane):
            for c in range(2):
                value = out[j * rows : (j + 1) * rows, c * 128 : (c + 1) * 128]
                turned = value * cosine[...] + swap_halves(value) * sine[...]
                queries[j, :, pl.ds(pl.multiple_of(p * 256 + c * 128, 128), 128)] = turned.astype(BF)

    for s in range(1, line):

        @pl.when(z + s < line)
        def _():
            kv_send(s).wait_recv()
            kv_pair(s).start()

    fetch_on(1)
    fetch_on(2)
    kv_pair(0).wait_recv()
    for s in range(1, line):

        @pl.when(z + s < line)
        def _():
            kv_pair(s).wait_recv()

    local[6].wait()

    def by_columns(act):
        @pl.loop(0, ff // 256)
        def _(n):
            act(pl.ds(pl.multiple_of(n * 256, 256), 256))

        if ff % 256:
            act(pl.ds(ff // 256 * 256, ff % 256))

    def relay_on(far, late, which, j):
        mix_first[far].wait_recv()
        value = relay[which].astype(F32) + part[j, which * hr : (which + 1) * hr, :].astype(F32)
        relayed[which] = value.astype(BF)
        mix_first[late].start()

    @pl.loop(0, plane)
    def _(t):
        j = plane - 1 - t
        here = pl.ds(pl.multiple_of(j * rows, 16), rows)
        vk[...] = pltpu.roll(kv_all[:, j].reshape(keys, 128).astype(F32), 64, 1).astype(BF)
        limit = limits[j, :, 0:1]

        @pl.loop(0, pairs)
        def _(p):
            at = pl.ds(pl.multiple_of(p * 128, 128), 128)
            allowed = kp[0:1, :] <= limit
            q = queries[j, :, at]
            zero = jnp.zeros_like(q)
            outs, logs = [], []
            for first in (True, False):
                mine = lane < 64 if first else lane >= 64
                kv = kv_all[:, j].reshape(keys, 128)
                keyed, valued = (kv, vk[...]) if first else (vk[...], kv)
                scores = nt(jnp.where(mine, q, zero), keyed) * (HEAD_DIM**-0.5)
                scores = jnp.where(allowed, scores, MASKED)
                top = jnp.max(scores, axis=1, keepdims=True)
                weights = jnp.exp(scores - top)
                sums = jnp.sum(weights, axis=1, keepdims=True)
                outs.append(nn(weights.astype(BF), valued) / sums)
                logs.append(jnp.broadcast_to(top + jnp.log(sums), (rows, 128)))
            attended[here, at] = jnp.where(lane < 64, outs[0], outs[1]).astype(BF)
            lse[j, :, at] = jnp.where(lane < 64, logs[0], logs[1])

        part[j] = nn(attended[here, :], w_o[...]).astype(BF)

        @pl.when(t == 0)
        def _():
            mix_first["far_one"].start()
            mix_first["far_two"].start()
            branch_gather.forward()

        @pl.when(t == 1)
        def _():
            mix_first["two"].start()
            fetch_on(3)

        @pl.when(t == 2)
        def _():
            mix_first["one"].start()
            relay_on("far_one", "late_two", 0, 2)
            relay_on("far_two", "late_one", 1, 1)

    early_stores = [store(n) for n in range(12)]
    for n in (0, 1, 2, 3, 6, 7, 8, 9, 10, 11):
        early_stores[n].start()
    cross_on(1)
    cross_on(2)
    for name in ("one", "late_one", "two", "late_two"):
        mix_first[name].wait_recv()

    @pl.loop(0, rows // 16)
    def _(i):
        at = pl.ds(pl.multiple_of(i * 16, 16), 16)
        value = x_all[0, at, :].astype(F32) + part[0, at, :].astype(F32)
        value = value + landed[0, at, :].astype(F32) + landed[1, at, :].astype(F32)
        mixed[at, :] = value
        inverse = lax.rsqrt(jnp.mean(value * value, axis=1, keepdims=True) + EPSILON)
        n2_all[0, at, :] = (value * inverse * gain_two[0:1, :]).astype(BF)

    n2_gather.start()
    early_stores[4].start()

    def pack(j):
        @pl.loop(0, rows // 16)
        def _(i):
            at = pl.ds(pl.multiple_of(i * 16, 16), 16)
            to = pl.ds(pl.multiple_of(j * rows + i * 16, 16), 16)
            for h in range(2):
                for b in range(plane):
                    from_ = pl.ds(pl.multiple_of(((f ^ b) * 2 + (k ^ h)) * half, 128), half)
                    c = (h * plane + b) * half
                    n2[to, c : c + half] = n2_all[j, at, from_]

    pack(0)
    branch_gather.arrive()
    local[11].wait()

    def down_grad(at):
        grad[:, at] = nt(branch_all[...].reshape(total, depth), down[at, :])

    by_columns(down_grad)
    n2_gather.forward()

    @pl.loop(1, 3)
    def _(j):
        pack(j)

    cross_on(3)
    for n in range(7, 11):
        local[n].wait()
    for j in peers:
        gate_pair(j).wait_recv()
        up_pair(j).wait_recv()
    weight_stores = [store(n) for n in range(18, 22)]
    for copy in weight_stores:
        copy.start()
    n2_gather.arrive()

    pack(3)
    early_stores[5].start()
    later = [store(n) for n in range(12, 18)]
    for n in range(3):
        later[n].start()

    def feed(at):
        width = at.size
        n2_own, n2_sib = n2[:, 0 : depth // 2], n2[:, depth // 2 : depth]

        def through(own, other):
            first = nn(n2_own, own[:, :, at].reshape(depth // 2, width))
            return first + nn(n2_sib, other[:, :, at].reshape(depth // 2, width))

        gate = through(gate_own, gate_sib)
        up = through(up_own, up_sib)
        sigmoid = 1.0 / (1.0 + jnp.exp(-gate))
        hidden[:, at] = (gate * sigmoid * up).astype(BF)
        back = grad[:, at]
        gate_back[:, at] = (back * up * sigmoid * (1.0 + gate * (1.0 - sigmoid))).astype(BF)
        up_back[:, at] = (back * gate * sigmoid).astype(BF)

    by_columns(feed)
    for n in range(3, 6):
        later[n].start()
    for gather in (token_gather, branch_gather, n2_gather):
        gather.close()
    for copy in mix_first.values():
        copy.wait_send()
    for j in peers:
        note_send(j).wait_send()
        wp_send(j).wait_send()
        gate_pair(j).wait_send()
        up_pair(j).wait_send()
    projections = (wq_send, wk_send, w_across)
    by_parity(
        lambda: [c(3).wait_send() for c in projections],
        lambda: [c(j).wait_send() for j in (1, 2) for c in projections],
    )
    by_parity(
        lambda: [c(j).wait_send() for j in peers for c in (gate_send, gate_across)],
        lambda: [c(j).wait_send() for j in peers for c in (up_send, up_across)],
    )

    kv_pair(0).wait_send()
    for s in range(1, line):

        @pl.when(z >= s)
        def _():
            kv_send(s).wait_send()

        @pl.when(z + s < line)
        def _():
            kv_pair(s).wait_send()

    for copy in early_stores + later + weight_stores:
        copy.wait()


def front_pass(tokens, cotangent, lengths, attn_gain, mlp_gain, w_query, w_key, w_value, w_out, w_gate, w_up, w_down):
    rows, depth = tokens.shape
    plane, line = 4, 4
    total, slab = plane * rows, depth // plane
    half = slab // 2
    q_width = HEADS * HEAD_DIM // plane
    width = q_width + 128
    ff = w_down.shape[0]
    slot = rows * line * 2
    keys = slot
    act = (rows, depth)
    local = pl.BlockSpec(memory_space=pltpu.VMEM)
    anywhere = pl.BlockSpec(memory_space=pl.ANY)
    dma = lambda n: pltpu.SemaphoreType.DMA((n,))
    kv_shape = (2 * line, plane, rows, 128)
    sds = jax.ShapeDtypeStruct
    outs = [
        sds((total, depth), BF),
        sds((plane, rows, q_width), BF),
        sds((plane, rows, q_width), F32),
        sds((total, q_width), BF),
        sds(act, F32),
        sds((total, depth), BF),
        sds((plane, rows, 128), F32),
        sds((rows, 128), F32),
        sds((rows, 128), F32),
        sds((8, keys), F32),
        sds((8, depth), F32),
        sds((8, depth), F32),
        sds(kv_shape, BF),
        sds((plane,) + act, BF),
        sds((depth, width), BF),
        sds((total, ff), BF),
        sds((total, ff), BF),
        sds((total, ff), BF),
    ] + [sds((plane, half, ff), BF)] * 4
    held = [pltpu.VMEM(o.shape, o.dtype) for o in outs]
    held = held[:12] + held[15:18] + [pltpu.VMEM((total, ff), F32)]
    slabs = pltpu.VMEM((plane, half, ff), BF)
    scratch = held + [
        pltpu.VMEM((plane, 16, slab), BF),
        pltpu.VMEM((plane,) + act, BF),
        pltpu.VMEM((depth, width), BF),
        pltpu.VMEM(w_key.shape, BF),
        pltpu.VMEM(w_value.shape, BF),
        pltpu.VMEM((plane, half, 128), BF),
        slabs,
        slabs,
        slabs,
        slabs,
        pltpu.VMEM(w_down.shape, BF),
        pltpu.VMEM(kv_shape, BF),
        pltpu.VMEM((keys, 128), BF),
        pltpu.VMEM(w_out.shape, BF),
        pltpu.VMEM((plane,) + act, BF),
        pltpu.VMEM((2,) + act, BF),
        pltpu.VMEM((2, rows // 2, depth), BF),
        pltpu.VMEM((2, rows // 2, depth), BF),
        pltpu.VMEM((plane,) + act, BF),
        pltpu.VMEM((plane,) + act, BF),
        pltpu.VMEM(act, BF),
    ]
    sems = [12, 22, 3, 3, 3, 3, 2, 2, 2, 2, 3, 3, 3, 3, 3, 3, 1, 1, 3, 3, 4, 4, 3, 3, 3, 3, 3, 3, 3, 3, 3, 3]
    sems += [2, 2, 2, 2, 6, 6, 2, 2, 2, 2]
    return pl.pallas_call(
        front_kernel,
        out_shape=outs,
        in_specs=[pl.BlockSpec(memory_space=pltpu.SMEM)] + [local] * 6 + [anywhere] * 9,
        out_specs=[anywhere] * 22,
        scratch_shapes=scratch + [dma(n) for n in sems],
        compiler_params=pltpu.CompilerParams(
            vmem_limit_bytes=62 * 1024 * 1024, has_side_effects=True
        ),
        name="front_pass",
    )(
        lengths, attn_gain, mlp_gain, *rotary_parts(slot, rows),
        tokens, cotangent, w_query, w_key, w_value, w_out, w_gate, w_up, w_down,
    )


def add_into(target, other):
    @pl.loop(0, target.shape[0] // 16)
    def _(i):
        at = pl.ds(pl.multiple_of(i * 16, 16), 16)
        target[at, :] = (target[at, :].astype(F32) + other[at, :].astype(F32)).astype(BF)


def back_kernel(
    limits_in, gate_back_in, up_back_in, hidden_in, mixed_in, x_own_in, gain_one_in, gain_two_in,
    attended_in, queries_in, lse_in, kv_all_in, kp_in, cosine_in, sine_in,
    branch, w_out, w_down, wqkv, h1_hbm, n2_hbm, gate_own, gate_sib, up_own, up_sib,
    fin_down, fin_gate, fin_up, fin_out, fin_qkv, fin_gain,
    sib_down, sib_gate, sib_up, sib_out, sib_qkv, sib_gain,
    outputs, input_grad_out,
    limits, gate_back, up_back, hidden, mixed, x_own, gain_one, gain_two,
    attended, queries, lse, kv_all, kp, cosine, sine, branch_own, input_grad,
    src_down, src_gate, src_up, src_out, src_qkv, src_gain,
    swap_gate, swap_up, swap_qkv,
    end_down, end_gate, end_up, end_out, end_qkv, end_gain,
    give_down, give_gate, give_out, give_qkv, give_gain,
    turned, landed, landed_out, weights, down_blocks, qkv_blocks, part, da_all, wide, do_all, dqkv, left,
    vk, dk_sum, dv_sum, kv_part, kv_land, kv_mine, kv_line, gain_acc, gain_all,
    pair_s, pair_r, swap_s, swap_r, in_s, in_r, mid_s, mid_r, out_s, done_s, back_s, back_r, ready,
    local_s, weight_s, rs_s, rs_r, ro_s, ro_r, ag_s, ag_r, rq_s, rq_r, kp_s, kp_r, kz_s, kz_r, ga_s, ga_r,
):
    f, z, k = lax.axis_index("fsdp"), lax.axis_index("z"), lax.axis_index("core")
    plane, line = lax.axis_size("fsdp"), lax.axis_size("z")
    branch_flat = branch
    outer = (z == 0) | (z == line - 1)
    inner = jnp.logical_not(outer)
    inward = jnp.where(z < line // 2, z + 1, z - 1)
    outward = jnp.where(z < line // 2, z - 1, z + 1)
    rows, depth = mixed.shape
    total = plane * rows
    half_depth = depth // 2
    half = half_depth // plane
    q_width = attended.shape[1]
    pairs = q_width // 128
    peers = range(1, plane)

    kinds = {
        "down": (src_down, None, end_down, give_down, fin_down, sib_down),
        "gate": (src_gate, swap_gate, end_gate, give_gate, fin_gate, sib_gate),
        "up": (src_up, swap_up, end_up, give_gate, fin_up, sib_up),
        "out": (src_out, None, end_out, give_out, fin_out, sib_out),
        "qkv": (src_qkv, swap_qkv, end_qkv, give_qkv, fin_qkv, sib_qkv),
        "gain": (src_gain, None, end_gain, give_gain, fin_gain, sib_gain),
    }
    chunks = [(name, i) for name, kind in kinds.items() for i in range(kind[0].shape[0])]
    chunks.insert(len(chunks) - 5, chunks.pop())
    count = len(chunks)

    def group(c):
        return kinds[chunks[c][0]][3].shape[0]

    heads = [c for c in range(count) if chunks[c][1] % group(c) == 0]

    def remote(source, target, send, recv, where):
        return pltpu.make_async_remote_copy(
            src_ref=source,
            dst_ref=target,
            send_sem=send,
            recv_sem=recv,
            device_id=where,
            device_id_type=pl.DeviceIdType.MESH,
        )

    def swapped(c):
        name, i = chunks[c]
        return i // group(c) if kinds[name][1] is not None else 0

    def source(c):
        return part_of(c, 0)

    def part_of(c, which):
        name, i = chunks[c]
        return kinds[name][which].at[i]

    def given(c):
        return kinds[chunks[c][0]][3]

    def end(c):
        return part_of(c, 2)

    def pair_copy(c):
        start = given(c).at[chunks[c][1] % group(c)]
        return remote(start, source(c), pair_s.at[c], pair_r.at[c], {"core": 1 - k})

    def landing(c):
        name, i = chunks[c]
        return kinds[name][1].at[i - group(c)]

    def swap_copy(c):
        return remote(source(c), landing(c), swap_s.at[c], swap_r.at[c], {"fsdp": f ^ swapped(c)})

    def base(c):
        return landing(c) if swapped(c) else source(c)

    def in_copy(c):
        return remote(base(c), end(c), in_s.at[c], in_r.at[c], {"z": inward})

    def mid_copy(c):
        return remote(base(c), end(c), mid_s.at[c], mid_r.at[c], {"z": inward})

    def out_copy(c):
        return remote(end(c), end(c), out_s.at[c], mid_r.at[c], {"z": outward})

    def keep_copy(c):
        return pltpu.make_async_copy(end(c), part_of(c, 4), done_s.at[c])

    def back_copy(c):
        return remote(end(c), part_of(c, 5), back_s.at[c], back_r.at[c], {"core": 1 - k})

    def term(c, side, act):
        name, i = chunks[c]
        if name == "gain":
            act(slice(None), gain_all[...].astype(F32).sum(axis=0))
            return
        start = pl.multiple_of((k ^ side) * half_depth, 128)
        if name == "down":
            size, width = 128, half_depth
            turned[0:size, :] = hidden[:, i * size : (i + 1) * size].T
        elif name == "out":
            size, width = 2 * src_out.shape[1], half_depth
            turned[0:size, :] = attended[:, i * size // 2 : i * size // 2 + size].T
        else:
            size, width = half, source(c).shape[1]
            at = side * half_depth + i * (half // 2)
            turned[0:size, :] = left[:, at : at + half].T

        def block(first, span):
            if name == "down":
                right = wide[0:total, pl.ds(start + first, span)]
            elif name == "out":
                right = da_all[:, :, pl.ds(start + first, span)].reshape(total, span)
            else:
                right = {"gate": gate_back, "up": up_back, "qkv": dqkv}[name][:, pl.ds(first, span)]
            act(pl.ds(first, span), nn(turned[0:size, :], right))

        @pl.loop(0, width // 256)
        def _(n):
            block(pl.multiple_of(n * 256, 256), 256)

        if width % 256:
            block(width // 256 * 256, width % 256)

    def stage_give(c):
        slots = given(c)
        for n in [n for n in range(c) if given(n) is slots][-group(c) :]:
            pair_copy(n).wait_send()
        size = slots.shape[1]

        def act(lanes, value):
            for n in range(group(c)):
                slots[n, :, lanes] = value[n * size : (n + 1) * size].astype(BF)

        term(c, 1, act)
        for n in range(group(c)):
            pair_copy(c + n).start()

    def stage_pair(c):
        for n in range(group(c)):
            pair_copy(c + n).wait_recv()
        size = source(c).shape[0]

        def act(lanes, value):
            for n in range(group(c)):
                target = source(c + n)
                added = target[:, lanes].astype(F32) + value[n * size : (n + 1) * size]
                target[:, lanes] = added.astype(BF)

        term(c, 0, act)
        for n in range(group(c)):
            if swapped(c + n):
                swap_copy(c + n).start()

    def stage_in(c):
        if swapped(c):
            swap_copy(c).wait_recv()

        @pl.when(outer)
        def _():
            in_copy(c).start()

    def stage_mid(c):
        @pl.when(inner)
        def _():
            in_copy(c).wait_recv()
            add_into(base(c), end(c))
            pl.semaphore_signal(
                ready, inc=1, device_id={"z": inward}, device_id_type=pl.DeviceIdType.MESH
            )
            pl.semaphore_wait(ready, 1)
            mid_copy(c).start()

    def stage_out(c):
        @pl.when(inner)
        def _():
            mid_copy(c).wait_recv()
            add_into(end(c), base(c))
            out_copy(c).start()

    def stage_keep(c):
        @pl.when(outer)
        def _():
            out_copy(c).wait_recv()

        keep_copy(c).start()
        back_copy(c).start()

    def back_send(j):
        mine = part.at[pl.ds(j * rows, rows), :]
        return remote(mine, landed.at[j - 1], rs_s.at[j - 1], rs_r.at[j - 1], {"fsdp": f ^ j})

    def out_send(j):
        mine = part.at[pl.ds(j * rows, rows), :]
        return remote(mine, landed_out.at[j - 1], ro_s.at[j - 1], ro_r.at[j - 1], {"fsdp": f ^ j})

    def da_send(j):
        return remote(da_all.at[0], da_all.at[j], ag_s.at[j - 1], ag_r.at[j - 1], {"fsdp": f ^ j})

    def dh_send(j):
        mine = wide.at[pl.ds(j * rows, rows), :]
        return remote(mine, landed.at[j - 1], rq_s.at[j - 1], rq_r.at[j - 1], {"fsdp": f ^ j})

    def gain_send(j):
        return remote(gain_all.at[0], gain_all.at[j], ga_s.at[j - 1], ga_r.at[j - 1], {"fsdp": f ^ j})

    moves = {
        "branch": (branch_flat, wide.at[pl.ds(0, total), :]), "hidden": (hidden_in, hidden), "n2": (n2_hbm, left),
        "gate_back": (gate_back_in, gate_back), "up_back": (up_back_in, up_back), "mixed": (mixed_in, mixed),
        "branch_own": (branch_flat.at[pl.ds(0, rows), :], branch_own), "gain_two": (gain_two_in, gain_two),
        "queries": (queries_in, queries), "lse": (lse_in, lse), "kv_all": (kv_all_in, kv_all),
        "limits": (limits_in, limits), "kp": (kp_in, kp), "cosine": (cosine_in, cosine), "sine": (sine_in, sine),
        "attended": (attended_in, attended), "x_own": (x_own_in, x_own), "gain_one": (gain_one_in, gain_one),
        "w_out": (w_out, wide.at[pl.ds(0, w_out.shape[0]), :]), "h1": (h1_hbm, left),
        "outputs": (mixed, outputs), "input_grad": (input_grad, input_grad_out),
    }
    moves = {
        name: pltpu.make_async_copy(*ends, local_s.at[n]) for n, (name, ends) in enumerate(moves.items())
    }

    def weight_loads(h, j):
        pairs_of = ((gate_own, up_own), (gate_sib, up_sib))[h]
        return [
            pltpu.make_async_copy(w.at[j], weights.at[j % 2, n], weight_s.at[j % 2, n])
            for n, w in enumerate(pairs_of)
        ]

    def columns_of(h, j):
        return pl.ds(pl.multiple_of(((f ^ j) * 2 + (k ^ h)) * half, 128), half)

    def piece_back(h):
        @pl.loop(0, plane)
        def _(j):
            @pl.when(j + 1 < plane)
            def _():
                for copy in weight_loads(h, j + 1):
                    copy.start()

            for copy in weight_loads(h, j):
                copy.wait()
            value = nt(gate_back[...], weights[j % 2, 0]) + nt(up_back[...], weights[j % 2, 1])
            part[:, columns_of(h, j)] = value.astype(BF)

        if h == 0:
            for copy in weight_loads(1, 0):
                copy.start()
        if h == 1:
            for j in peers:
                back_send(j).start()

    def down_at(b):
        size = depth // 8
        return pl.ds(pl.multiple_of(b * size, size), size)

    def down_load(b):
        return pltpu.make_async_copy(w_down.at[:, down_at(b)], down_blocks.at[b % 2], weight_s.at[b % 2, 0])

    def piece_out(h):
        if h == 0:
            for j in peers:
                back_send(j).wait_send()
            down_load(0).start()

        @pl.loop(4 * h, 4 * h + 4)
        def _(b):
            @pl.when(b + 1 < 8)
            def _():
                down_load(b + 1).start()

            down_load(b).wait()
            part[:, down_at(b)] = nn(hidden[...], down_blocks[b % 2]).astype(BF)

        if h == 1:
            for j in peers:
                out_send(j).start()

    def dh_load(b):
        block = wqkv.at[pl.ds(pl.multiple_of(b * half, half), half), :]
        return pltpu.make_async_copy(block, qkv_blocks.at[b % 2], weight_s.at[b % 2, 0])

    def rms_back(gradient_of, x_ref, gain, acc, write):
        acc[...] = jnp.zeros_like(acc)

        @pl.loop(0, rows // 16)
        def _(i):
            at = pl.ds(pl.multiple_of(i * 16, 16), 16)
            gradient = gradient_of(at)
            x = x_ref[at, :].astype(F32)
            inverse = lax.rsqrt(jnp.mean(x * x, axis=1, keepdims=True) + EPSILON)
            normed = x * inverse
            acc[...] += gradient * normed
            scaled = gradient * gain[0:1, :]
            write(at, inverse * (scaled - normed * jnp.mean(scaled * normed, axis=1, keepdims=True)))

    def piece_mixed():
        for name in ("mixed", "branch_own", "gain_two"):
            moves[name].wait()
        for j in peers:
            back_send(j).wait_recv()

        def gradient_of(at):
            value = part[at, :].astype(F32)
            for j in peers:
                value = value + landed[j - 1, at, :].astype(F32)
            return value

        def write(at, value):
            value = value + branch_own[at, :].astype(F32)
            input_grad[at, :] = value
            da_all[0, at, :] = value.astype(BF)

        rms_back(gradient_of, mixed, gain_two, gain_acc.at[1], write)
        for j in peers:
            da_send(j).start()

    def piece_do():
        moves["w_out"].wait()
        for j in peers:
            da_send(j).wait_recv()

        @pl.loop(0, plane)
        def _(j):
            do_all[j] = nt(da_all[j], wide[0 : w_out.shape[0], :]).astype(BF)

    def piece_attend(j):
        here = pl.ds(pl.multiple_of(j * rows, 16), rows)
        vk[...] = pltpu.roll(kv_all[:, j].reshape(vk.shape).astype(F32), 64, 1).astype(BF)
        dk_sum[...] = jnp.zeros_like(dk_sum)
        dv_sum[...] = jnp.zeros_like(dv_sum)
        limit = limits[j, :, 0:1]
        lane = lax.broadcasted_iota(jnp.int32, (rows, 128), 1)

        @pl.loop(0, pairs)
        def _(p):
            at = pl.ds(pl.multiple_of(p * 128, 128), 128)
            allowed = kp[0:1, :] <= limit
            q, do = queries[j, :, at], do_all[j, :, at]
            logs = lse[j, :, at]
            zero = jnp.zeros_like(q)
            parts = []
            for first in (True, False):
                mine = lane < 64 if first else lane >= 64
                kv = kv_all[:, j].reshape(vk.shape)
                keyed, valued = (kv, vk[...]) if first else (vk[...], kv)
                q_own, do_own = jnp.where(mine, q, zero), jnp.where(mine, do, zero)
                scores = nt(q_own, keyed) * (HEAD_DIM**-0.5)
                log_total = logs[:, 0:1] if first else logs[:, 64:65]
                weights = jnp.where(allowed, jnp.exp(scores - log_total), 0.0)
                joint = weights * nt(do_own, valued)
                back = (joint - weights * jnp.sum(joint, axis=1, keepdims=True)).astype(BF)
                parts.append(nn(back, keyed))
                dk_sum[...] += tn(back, q_own)
                dv_sum[...] += tn(weights.astype(BF), do_own)
            rotated = jnp.where(lane < 64, parts[0], parts[1]) * (HEAD_DIM**-0.5)
            rotated = rotated * cosine[...] - swap_halves(rotated) * sine[...]
            dqkv[here, at] = rotated.astype(BF)

        dk = dk_sum[...]
        dv = dv_sum[...]
        dk = (dk + pltpu.roll(dk, 64, 1)) * (HEAD_DIM**-0.5)
        dv = dv + pltpu.roll(dv, 64, 1)
        wide_lane = lax.broadcasted_iota(jnp.int32, dk.shape, 1)
        packed = jnp.where(wide_lane < 64, dk, dv).astype(BF)
        kv_part[:, j] = packed.reshape(kv_part.shape[0], rows, 128)

    kv_pair = remote(kv_part.at[pl.ds(line, line)], kv_land, kp_s.at[0], kp_r.at[0], {"core": 1 - k})

    def kv_send(s):
        return remote(kv_mine.at[s], kv_line.at[s - 1], kz_s.at[s - 1], kz_r.at[s - 1], {"z": z + s})

    def piece_kv_line():
        kv_pair.wait_recv()
        for s in range(line):
            kv_mine[s] = (kv_part[s].astype(F32) + kv_land[s].astype(F32)).astype(BF)
        for s in range(1, line):

            @pl.when(z + s < line)
            def _():
                kv_send(s).start()

    def piece_kv_sum():
        for s in range(1, line):

            @pl.when(z >= s)
            def _():
                kv_send(s).wait_recv()
                kv_mine[0] = (kv_mine[0].astype(F32) + kv_line[s - 1].astype(F32)).astype(BF)

        lane = lax.broadcasted_iota(jnp.int32, (rows, 128), 1)
        for j in range(plane):
            value = kv_mine[0, j].astype(F32)
            rotated = value * cosine[...] - swap_halves(value) * sine[...]
            value = jnp.where(lane < 64, rotated, value).astype(BF)
            dqkv[j * rows : (j + 1) * rows, q_width : q_width + 128] = value

    def piece_dh():
        dh_load(0).start()

        @pl.loop(0, 2 * plane)
        def _(b):
            @pl.when(b + 1 < 2 * plane)
            def _():
                dh_load(b + 1).start()

            dh_load(b).wait()
            wide[0:total, columns_of(b // plane, b % plane)] = nt(dqkv[...], qkv_blocks[b % 2]).astype(BF)

        for j in peers:
            dh_send(j).start()

    def piece_input():
        for name in ("x_own", "gain_one"):
            moves[name].wait()
        for j in peers:
            dh_send(j).wait_recv()

        def gradient_of(at):
            value = wide[at, :].astype(F32)
            for j in peers:
                value = value + landed[j - 1, at, :].astype(F32)
            return value

        def write(at, value):
            input_grad[at, :] = input_grad[at, :] + value

        rms_back(gradient_of, x_own, gain_one, gain_acc.at[0], write)
        moves["input_grad"].start()
        place = lax.broadcasted_iota(jnp.int32, (16, depth), 0)
        one = jnp.sum(gain_acc[0], axis=0, keepdims=True)
        two = jnp.sum(gain_acc[1], axis=0, keepdims=True)
        gain_all[0] = jnp.where(place == 0, one, jnp.where(place == 1, two, 0.0)).astype(BF)
        for j in peers:
            gain_send(j).start()

    def piece_outputs():
        for j in peers:
            out_send(j).wait_recv()

        @pl.loop(0, rows // 16)
        def _(i):
            at = pl.ds(pl.multiple_of(i * 16, 16), 16)
            value = mixed[at, :] + part[at, :].astype(F32)
            for j in peers:
                value = value + landed_out[j - 1, at, :].astype(F32)
            mixed[at, :] = value

        moves["outputs"].start()

    def piece_gain():
        for j in peers:
            gain_send(j).wait_recv()

    in_lag, mid_lag, out_lag, keep_lag = LAGS
    events = []

    def give_tick(c):
        return c - (AHEAD[1] if kinds[chunks[c][0]][1] is not None else AHEAD[0])

    for c in heads:
        events.append((give_tick(c), 0, stage_give, c))
        events.append((give_tick(c) + 1, 1, stage_pair, c))
    for c in range(count):
        events.append((c + in_lag, 2, stage_in, c))
        events.append((c + mid_lag, 3, stage_mid, c))
        events.append((c + out_lag, 4, stage_out, c))
        events.append((c + keep_lag, 5, stage_keep, c))
    steps = (
        (piece_back, 0), (piece_back, 1), piece_mixed, piece_do, (piece_out, 0), (piece_out, 1), (piece_attend, 0),
        (piece_attend, 1), (piece_attend, 2), (piece_attend, 3), kv_pair.start, piece_kv_line, piece_kv_sum, piece_dh, piece_outputs, piece_input, piece_gain,
    )
    for n, (step, tick) in enumerate(zip(steps, STEPS)):
        act, which = step if isinstance(step, tuple) else (step, None)
        events.append((tick, 6 + n, act, which))

    def head_of(name, which):
        return [c for c in heads if chunks[c][0] == name][which]

    def wait_for(*names):
        def act():
            for name in names:
                moves[name].wait()

        return act

    events.append((give_tick(head_of("down", 0)), -1, wait_for("branch", "hidden"), None))
    first = min(STEPS[0], give_tick(head_of("gate", 0)))
    events.append((first, 5.2, wait_for("n2", "gate_back", "up_back"), None))
    events.append((give_tick(head_of("down", -1)) + 1, 31, moves["w_out"].start, None))
    events.append((give_tick(head_of("up", -1)) + 1, 31, moves["h1"].start, None))
    events.append((give_tick(head_of("qkv", 0)), -1, moves["h1"].wait, None))
    events.append((give_tick(head_of("out", 0)), -1, moves["attended"].wait, None))
    attending = ("queries", "lse", "kv_all", "limits", "kp", "cosine", "sine")
    events.append((STEPS[6], 5.5, wait_for(*attending), None))
    events.sort(key=lambda e: e[:2])

    for name, move in moves.items():
        if name not in ("w_out", "h1", "outputs", "input_grad"):
            move.start()
    for copy in weight_loads(0, 0):
        copy.start()
    for _, _, act, which in events:
        act() if which is None else act(which)

    for c in range(count):
        if not [n for n in heads if n > c and given(n) is given(c)]:
            pair_copy(c).wait_send()
        if swapped(c):
            swap_copy(c).wait_send()
        keep_copy(c).wait()
        back_copy(c).wait_send()
        back_copy(c).wait_recv()

        @pl.when(outer)
        def _():
            in_copy(c).wait_send()

        @pl.when(inner)
        def _():
            mid_copy(c).wait_send()
            out_copy(c).wait_send()

    moves["outputs"].wait()
    moves["input_grad"].wait()
    for j in peers:
        out_send(j).wait_send()
        da_send(j).wait_send()
        dh_send(j).wait_send()
        gain_send(j).wait_send()
    kv_pair.wait_send()
    for s in range(1, line):

        @pl.when(z + s < line)
        def _():
            kv_send(s).wait_send()


def back_pass(held, far):
    count, line = lax.axis_size("fsdp"), lax.axis_size("z")
    mixed, attended, kv_all, hidden = held[4], held[8], held[11], held[3]
    rows, depth = mixed.shape
    total, half_depth = count * rows, depth // 2
    half = half_depth // count
    q_width = attended.shape[1]
    ff = hidden.shape[1]
    keys = kv_all.shape[0] * rows
    slabs = (2 * count, half // 2, ff)
    shapes = [
        (ff // 128, 128, half_depth),
        slabs,
        slabs,
        (4, q_width // 4, half_depth),
        (2 * count, half // 2, q_width + 128),
        (1, 16, depth),
    ]
    anywhere = pl.BlockSpec(memory_space=pl.ANY)
    ends = [jax.ShapeDtypeStruct(s, BF) for s in shapes]
    act = jax.ShapeDtypeStruct((rows, depth), F32)
    block = (rows, depth)
    chunk_count = sum(s[0] for s in shapes)
    dma = lambda *n: pltpu.SemaphoreType.DMA(n)
    groups = (1, 2, 2, 2, 1)
    scratch = (
        [pltpu.VMEM(x.shape, x.dtype) for x in held]
        + [pltpu.VMEM(block, BF), pltpu.VMEM(block, F32)]
        + [pltpu.VMEM(s, BF) for s in shapes]
        + [pltpu.VMEM((shapes[i][0] - 2,) + shapes[i][1:], BF) for i in (1, 2, 4)]
        + [pltpu.VMEM(s, BF) for s in shapes]
        + [pltpu.VMEM((g,) + shapes[i][1:], BF) for g, i in zip(groups, (0, 1, 3, 4, 5))]
        + [
            pltpu.VMEM((max(half, q_width // 2, 128), total), BF),
            pltpu.VMEM((count - 1,) + block, BF),
            pltpu.VMEM((count - 1,) + block, BF),
            pltpu.VMEM((2, 2, half, ff), BF),
            pltpu.VMEM((2, ff, depth // 8), BF),
            pltpu.VMEM((2, half, q_width + 128), BF),
            pltpu.VMEM((total, depth), BF),
            pltpu.VMEM((count,) + block, BF),
            pltpu.VMEM((max(total, q_width), depth), BF),
            pltpu.VMEM((count, rows, q_width), BF),
            pltpu.VMEM((total, q_width + 128), BF),
            pltpu.VMEM((total, depth), BF),
            pltpu.VMEM((keys, 128), BF),
            pltpu.VMEM((keys, 128), F32),
            pltpu.VMEM((keys, 128), F32),
            pltpu.VMEM(kv_all.shape, BF),
            pltpu.VMEM((line,) + kv_all.shape[1:], BF),
            pltpu.VMEM((line,) + kv_all.shape[1:], BF),
            pltpu.VMEM((line - 1,) + kv_all.shape[1:], BF),
            pltpu.VMEM((2, 16, depth), F32),
            pltpu.VMEM((count, 16, depth), BF),
        ]
        + [dma(chunk_count)] * 12
        + [pltpu.SemaphoreType.REGULAR, dma(22), dma(2, 2)]
        + [dma(count - 1)] * 8
        + [dma(1)] * 2
        + [dma(line - 1)] * 2
        + [dma(count - 1)] * 2
    )
    out = pl.pallas_call(
        back_kernel,
        out_shape=ends + ends + [act, act],
        in_specs=[anywhere] * (len(held) + len(far)),
        out_specs=[anywhere] * 14,
        scratch_shapes=scratch,
        compiler_params=pltpu.CompilerParams(
            vmem_limit_bytes=63 * 1024 * 1024, has_side_effects=True
        ),
        name="back_pass",
    )(*held, *far)
    return out[:6], out[6:12], out[12], out[13]


def finish_kernel(
    own_down, own_gate, own_up, own_out, own_qkv, own_gain, sib_down, sib_gate, sib_up, sib_out, sib_qkv,
    outputs_in, input_grad_in, outputs, input_grad, down, gate, up, out, query, key, value, attn_gain, mlp_gain,
    low_rows, low_cols, high_rows, high_cols, kv, acts, gain_in, gain_high, load_s, store_s, side_s,
):
    f, k = lax.axis_index("fsdp"), lax.axis_index("core")
    plane = lax.axis_size("fsdp")
    half, ff = own_gate.shape[1], own_gate.shape[2]
    half_depth = own_down.shape[2]
    slab = 2 * half
    q_width = own_qkv.shape[2] - 128
    tasks = []
    for side, (d, o, g, u, q) in enumerate(
        ((own_down, own_out, own_gate, own_up, own_qkv), (sib_down, sib_out, sib_gate, sib_up, sib_qkv))
    ):
        rows_at = pl.ds(pl.multiple_of((k ^ side) * half, 8), half)
        cols_at = pl.ds(pl.multiple_of((k ^ side) * half_depth, 128), half_depth)
        for source, target in ((d, down), (o, out)):
            for i in range(source.shape[0]):
                size = source.shape[1]
                tasks.append((source.at[i], target.at[pl.ds(i * size, size), cols_at], 0))
        for source, target in ((g, gate), (u, up)):
            for j in range(plane):
                to = pl.ds(pl.multiple_of((f ^ j) * ff, 128), ff)
                tasks.append((source.at[j], target.at[rows_at, to], 1))
        for j in range(plane):
            to = pl.ds(pl.multiple_of((f ^ j) * q_width, 128), q_width)
            tasks.append((q.at[j, :, pl.ds(0, q_width)], query.at[rows_at, to], 1))
    slots = low_rows.shape[0]

    def window(buffer, n, shape):
        return buffer.at[n % slots, pl.ds(0, shape[0]), pl.ds(0, shape[1])]

    def load(n):
        source, _, kind = tasks[n]
        low = (low_rows, low_cols)[kind]
        return pltpu.make_async_copy(source, window(low, n, source.shape), load_s.at[n])

    def store(n):
        source, target, kind = tasks[n]
        high = (high_rows, high_cols)[kind]
        return pltpu.make_async_copy(window(high, n, source.shape), target, store_s.at[n])

    sides = [
        pltpu.make_async_copy(own_gain.at[0], gain_in, side_s.at[0]),
        pltpu.make_async_copy(own_qkv.at[:, :, pl.ds(q_width, 128)], kv.at[0], side_s.at[1]),
        pltpu.make_async_copy(sib_qkv.at[:, :, pl.ds(q_width, 128)], kv.at[1], side_s.at[2]),
        pltpu.make_async_copy(outputs_in, acts.at[0], side_s.at[3]),
        pltpu.make_async_copy(input_grad_in, acts.at[1], side_s.at[4]),
    ]
    for n in range(slots):
        load(n).start()
    for copy in sides:
        copy.start()
    for n in range(len(tasks)):
        source, _, kind = tasks[n]
        shape = source.shape
        low, high = ((low_rows, high_rows), (low_cols, high_cols))[kind]
        load(n).wait()
        if n >= slots:
            store(n - slots).wait()

        @pl.loop(0, shape[0] // 16)
        def _(i):
            at = pl.ds(pl.multiple_of(i * 16, 16), 16)
            high[n % slots, at, 0 : shape[1]] = low[n % slots, at, 0 : shape[1]].astype(F32)

        store(n).start()
        if n + slots < len(tasks):
            load(n + slots).start()
    for copy in sides:
        copy.wait()
    lasts = [
        pltpu.make_async_copy(acts.at[0], outputs, side_s.at[5]),
        pltpu.make_async_copy(acts.at[1], input_grad, side_s.at[6]),
    ]
    for copy in lasts:
        copy.start()
    mine = pl.ds(pl.multiple_of(f * slab, 128), slab)
    gain_high[...] = gain_in[...].astype(F32)
    attn_gain[...] = gain_high[0:1, mine]
    mlp_gain[...] = gain_high[1:2, mine]
    lane = lax.broadcasted_iota(jnp.int32, (half, 128), 1)
    for side in range(2):
        rows_at = pl.ds(pl.multiple_of((k ^ side) * half, 8), half)
        for pair in range(plane // 2):
            first = kv[side, f ^ (2 * pair)].astype(F32)
            second = kv[side, f ^ (2 * pair + 1)].astype(F32)
            at = slice(pair * 128, (pair + 1) * 128)
            key[rows_at, at] = jnp.where(lane < 64, first, pltpu.roll(second, 64, 1))
            value[rows_at, at] = jnp.where(lane < 64, pltpu.roll(first, 64, 1), second)
    for n in range(max(0, len(tasks) - slots), len(tasks)):
        store(n).wait()
    for copy in lasts:
        copy.wait()


def finish(owns, sibs, outputs, input_grad):
    plane = lax.axis_size("fsdp")
    down, gate, _, out, qkv, gain = (x.shape for x in owns)
    depth = 2 * down[2]
    slab = 2 * gate[1]
    q_width = qkv[2] - 128
    sds = jax.ShapeDtypeStruct
    shapes = [
        outputs.shape, input_grad.shape,
        (down[0] * down[1], depth), (slab, plane * gate[2]), (slab, plane * gate[2]), (out[0] * out[1], depth),
        (slab, plane * q_width), (slab, KV_HEADS * HEAD_DIM), (slab, KV_HEADS * HEAD_DIM), (1, slab), (1, slab),
    ]
    slots = 8
    tall = (slots, max(down[1], out[1]), down[2])
    wide = (slots, gate[1], max(gate[2], q_width))
    count = 2 * (down[0] + out[0] + 3 * plane)
    anywhere, local = pl.BlockSpec(memory_space=pl.ANY), pl.BlockSpec(memory_space=pltpu.VMEM)
    return pl.pallas_call(
        finish_kernel,
        out_shape=[sds(s, F32) for s in shapes],
        in_specs=[anywhere] * 13,
        out_specs=[anywhere] * 7 + [local] * 4,
        scratch_shapes=[
            pltpu.VMEM(tall, BF),
            pltpu.VMEM(wide, BF),
            pltpu.VMEM(tall, F32),
            pltpu.VMEM(wide, F32),
            pltpu.VMEM((2, plane, gate[1], 128), BF),
            pltpu.VMEM((2,) + outputs.shape, F32),
            pltpu.VMEM(gain[1:], BF),
            pltpu.VMEM(gain[1:], F32),
            pltpu.SemaphoreType.DMA((count,)),
            pltpu.SemaphoreType.DMA((count,)),
            pltpu.SemaphoreType.DMA((7,)),
        ],
        compiler_params=params(),
        name="finish",
    )(*owns, *sibs[:5], outputs, input_grad)


def body(
    tokens, cotangent, lengths, attn_gain, w_query, w_key, w_value, w_out, mlp_gain, w_gate, w_up, w_down
):
    seqs, rows, depth = tokens.shape
    count = lax.axis_size("fsdp")
    slab = depth // count
    x_own = tokens.reshape(rows, depth)
    (
        h1, queries, lse, attended, mixed, n2, limits, cosine, sine, kp, gain_one, gain_two, kv_all, branch, wqkv,
        gate_back, up_back, hidden, gate_own, gate_sib, up_own, up_sib,
    ) = front_pass(
        x_own, cotangent.reshape(rows, depth), lengths, attn_gain, mlp_gain,
        w_query, w_key, w_value, w_out, w_gate, w_up, w_down,
    )
    held = (
        limits, gate_back, up_back, hidden, mixed, x_own, gain_one, gain_two,
        attended, queries, lse, kv_all, kp, cosine, sine,
    )
    branch = branch.reshape(count * rows, depth)
    far = (branch, w_out, w_down, wqkv, h1, n2, gate_own, gate_sib, up_own, up_sib)
    owns, sibs, outputs, input_grad = back_pass(held, far)

    def whole(x):
        return x.reshape(4, -1, x.shape[2]) if x.shape[0] > 1 else x

    owns, sibs = [whole(x) for x in owns], [whole(x) for x in sibs]
    (
        outputs, input_grad, down_grad, gate_grad, up_grad, out_grad, query_grad, key_grad, value_grad, gain_a, gain_m
    ) = finish(owns, sibs, outputs, input_grad)
    return (
        outputs.reshape(seqs, rows, depth),
        input_grad.reshape(seqs, rows, depth),
        gain_a.reshape(slab),
        query_grad,
        key_grad,
        value_grad,
        out_grad,
        gain_m.reshape(slab),
        gate_grad,
        up_grad,
        down_grad,
    )


def solution(mesh):
    count, ctx = mesh.shape["fsdp"], mesh.shape["ctx"]
    split = Mesh(mesh.devices.reshape(count, ctx // 2, 2), ("fsdp", "z", "core"))
    act = P("fsdp", ("z", "core"), None)
    row, mat = P("fsdp"), P("fsdp", None)
    fast = count == 4 and count == KV_HEADS and ctx == 8
    return jax.shard_map(
        body if fast else body_plain,
        mesh=split,
        in_specs=(act, act, row, row, mat, mat, mat, mat, row, mat, mat, mat),
        out_specs=(act, act, row, mat, mat, mat, mat, row, mat, mat, mat),
        check_vma=False,
    )
```

```python
import functools

import jax
import jax.numpy as jnp
import numpy as np
from jax import lax
from jax.experimental import pallas as pl
from jax.experimental.pallas import tpu as pltpu
from jax.sharding import Mesh
from jax.sharding import PartitionSpec as P

HEADS = 32
KV_HEADS = 4
HEAD_DIM = 64
EPSILON = 1e-05
ROPE_BASE = 10000.0
MASKED = -1e30
FAR = 1 << 30
BF = jnp.bfloat16
F32 = jnp.float32
VMEM_BYTES = 56 * 1024 * 1024
LAGS = (0, 2, 4, 6)
AHEAD = (1, 4)
STEPS = (0, 1, 7, 12, 13, 14, 15, 16, 17, 18, 18, 20, 24, 24, 23, 28, 30)


def params(**kw):
    return pltpu.CompilerParams(vmem_limit_bytes=VMEM_BYTES, **kw)


def along_plane(value, step):
    count = lax.axis_size("fsdp")
    return lax.ppermute(value, "fsdp", [(i, i ^ step) for i in range(count)])


def to_sibling(value):
    return lax.ppermute(value, "core", [(0, 1), (1, 0)])


def along_line(value, shift):
    count = lax.axis_size("z")
    return lax.ppermute(
        value, "z", [(i, i + shift) for i in range(count) if 0 <= i + shift < count]
    )


def plane_bits():
    count = lax.axis_size("fsdp")
    return [1 << b for b in range(count.bit_length() - 1)]


def plane_gather(block):
    half = block.shape[0] // 2
    parts = []
    for which, bits in ((0, plane_bits()), (1, plane_bits()[::-1])):
        held = {0: block[which * half : (which + 1) * half]}
        for bit in bits:
            order = sorted(held)
            got = along_plane(jnp.stack([held[j] for j in order]), bit)
            for n, j in enumerate(order):
                held[j ^ bit] = got[n]
        parts.append(held)
    return [jnp.concatenate([parts[0][j], parts[1][j]]) for j in range(lax.axis_size("fsdp"))]


def plane_reduce(partial):
    half = partial.shape[1] // 2
    done = []
    for which, bits in ((0, plane_bits()[::-1]), (1, plane_bits())):
        held = {j: partial[j, which * half : (which + 1) * half] for j in range(partial.shape[0])}
        for bit in bits:
            going = [j for j in sorted(held) if j & bit]
            got = along_plane(jnp.stack([held[j].astype(BF) for j in going]), bit)
            for n, j in enumerate(going):
                held[j ^ bit] = held[j ^ bit].astype(F32) + got[n].astype(F32)
                del held[j]
        done.append(held[0])
    return jnp.concatenate(done)


def line_sum(value):
    count = lax.axis_size("z")
    place = lax.axis_index("z")
    half = count // 2
    for i in range(half - 1):
        got = lax.ppermute(value, "z", [(i, i + 1), (count - 1 - i, count - 2 - i)])
        value = value + got
    value = value + lax.ppermute(value, "z", [(half - 1, half), (half, half - 1)])
    for i in range(half - 2, -1, -1):
        got = lax.ppermute(value, "z", [(i + 1, i), (count - 2 - i, count - 1 - i)])
        outer = (place == i) | (place == count - 1 - i)
        value = jnp.where(outer, got, value)
    return value


def move_kernel(idx_ref, x_ref, o_ref):
    o_ref[...] = x_ref[...]


def pick_columns(x, index, count):
    rows, width = x.shape
    size = width // count
    spec = pltpu.PrefetchScalarGridSpec(
        num_scalar_prefetch=1,
        grid=(count,),
        in_specs=[pl.BlockSpec((rows, size), lambda b, idx: (0, idx[b]))],
        out_specs=pl.BlockSpec((rows, size), lambda b, idx: (0, b)),
    )
    return pl.pallas_call(
        move_kernel,
        grid_spec=spec,
        out_shape=jax.ShapeDtypeStruct(x.shape, x.dtype),
        compiler_params=params(),
        name="pick_columns",
    )(index, x)


def put_columns(x, index, count):
    rows, width = x.shape
    size = width // count
    spec = pltpu.PrefetchScalarGridSpec(
        num_scalar_prefetch=1,
        grid=(count,),
        in_specs=[pl.BlockSpec((rows, size), lambda b, idx: (0, b))],
        out_specs=pl.BlockSpec((rows, size), lambda b, idx: (0, idx[b])),
    )
    return pl.pallas_call(
        move_kernel,
        grid_spec=spec,
        out_shape=jax.ShapeDtypeStruct(x.shape, x.dtype),
        compiler_params=params(),
        name="put_columns",
    )(index, x)


def cut_blocks(weight, f, k, count, dtype=BF):
    rows, full = weight.shape
    width, half = full // count, rows // 2
    if width % 128:
        own = lax.dynamic_slice_in_dim(weight, k * half, half, 0).reshape(half, count, width)
        return jnp.stack(
            [lax.dynamic_index_in_dim(own, f ^ j, 1, keepdims=False) for j in range(count)]
        )
    spec = pltpu.PrefetchScalarGridSpec(
        num_scalar_prefetch=1,
        grid=(count,),
        in_specs=[pl.BlockSpec((half, width), lambda j, at: (at[1], at[0] ^ j))],
        out_specs=pl.BlockSpec((None, half, width), lambda j, at: (j, 0, 0)),
    )
    return pl.pallas_call(
        move_kernel,
        grid_spec=spec,
        out_shape=jax.ShapeDtypeStruct((count, half, width), weight.dtype),
        compiler_params=params(),
        name="cut_blocks",
    )(jnp.stack([f, k]), weight)


def join_kernel(at_ref, own_ref, sib_ref, o_ref):
    @pl.when(pl.program_id(0) == 0)
    def _():
        o_ref[...] = own_ref[...].astype(o_ref.dtype)

    @pl.when(pl.program_id(0) == 1)
    def _():
        o_ref[...] = sib_ref[...].astype(o_ref.dtype)


def join_rows(own, sib, f, k):
    count, half, width = own.shape
    if width % 128:
        halves = jnp.stack([own, sib])
        return jnp.concatenate(
            [
                jnp.concatenate(
                    [
                        lax.dynamic_index_in_dim(
                            lax.dynamic_index_in_dim(halves, k ^ h, 0, keepdims=False),
                            f ^ i,
                            0,
                            keepdims=False,
                        )
                        for i in range(count)
                    ],
                    axis=1,
                )
                for h in range(2)
            ],
            axis=0,
        ).astype(F32)
    spec = pltpu.PrefetchScalarGridSpec(
        num_scalar_prefetch=1,
        grid=(2, count),
        in_specs=[
            pl.BlockSpec(
                (None, half, width),
                lambda s, i, at: (at[0] ^ jnp.where(s == 0, i, count - 1), 0, 0),
            ),
            pl.BlockSpec(
                (None, half, width), lambda s, i, at: (at[0] ^ jnp.where(s == 1, i, 0), 0, 0)
            ),
        ],
        out_specs=pl.BlockSpec((half, width), lambda s, i, at: (at[1] ^ s, i)),
    )
    return pl.pallas_call(
        join_kernel,
        grid_spec=spec,
        out_shape=jax.ShapeDtypeStruct((2 * half, count * width), F32),
        compiler_params=params(),
        name="join_rows",
    )(jnp.stack([f, k]), own, sib)


def join_columns(own, sib, k):
    rows, half = own.shape
    count = 4
    size = rows // count
    spec = pltpu.PrefetchScalarGridSpec(
        num_scalar_prefetch=1,
        grid=(2, count),
        in_specs=[
            pl.BlockSpec((size, half), lambda s, i, at: (jnp.where(s == 0, i, count - 1), 0)),
            pl.BlockSpec((size, half), lambda s, i, at: (jnp.where(s == 1, i, 0), 0)),
        ],
        out_specs=pl.BlockSpec((size, half), lambda s, i, at: (i, at[0] ^ s)),
    )
    return pl.pallas_call(
        join_kernel,
        grid_spec=spec,
        out_shape=jax.ShapeDtypeStruct((rows, 2 * half), F32),
        compiler_params=params(),
        name="join_columns",
    )(k.reshape(1), own, sib)


def swap_halves(block):
    lane = lax.broadcasted_iota(jnp.int32, block.shape, 1)
    return jnp.where(lane % 64 < 32, pltpu.roll(block, 96, 1), pltpu.roll(block, 32, 1))


def qkv_kernel(idx_ref, x_ref, gain_ref, w_ref, cos_ref, sin_ref, h_ref, q_ref, kv_ref):
    blocks = idx_ref.shape[0]
    size = x_ref.shape[1] // blocks
    x = x_ref[...].astype(F32)
    inverse = lax.rsqrt(jnp.mean(x * x, axis=1, keepdims=True) + EPSILON)
    for b in range(blocks):
        at = pl.ds(pl.multiple_of(idx_ref[b] * size, 128), size)
        part = x_ref[:, at].astype(F32) * inverse * gain_ref[:, at]
        h_ref[:, b * size : (b + 1) * size] = part.astype(BF)
    out = jnp.dot(h_ref[...], w_ref[...], preferred_element_type=F32)
    cosine, sine = cos_ref[...], sin_ref[...]
    pairs = q_ref.shape[1] // 128
    for c in range(pairs):
        block = out[:, c * 128 : (c + 1) * 128]
        q_ref[:, c * 128 : (c + 1) * 128] = (block * cosine + swap_halves(block) * sine).astype(BF)
    block = out[:, pairs * 128 :]
    lane = lax.broadcasted_iota(jnp.int32, block.shape, 1)
    turned = block * cosine + swap_halves(block) * sine
    kv_ref[...] = jnp.where(lane < 64, turned, block).astype(BF)


def qkv_project(idx, x, gain, weight, cosine, sine, rows):
    total, depth = x.shape
    width = weight.shape[1]
    spec = pltpu.PrefetchScalarGridSpec(
        num_scalar_prefetch=1,
        grid=(total // rows,),
        in_specs=[
            pl.BlockSpec((rows, depth), lambda i, idx: (i, 0)),
            pl.BlockSpec((1, depth), lambda i, idx: (0, 0)),
            pl.BlockSpec((depth, width), lambda i, idx: (0, 0)),
            pl.BlockSpec((rows, 128), lambda i, idx: (0, 0)),
            pl.BlockSpec((rows, 128), lambda i, idx: (0, 0)),
        ],
        out_specs=[
            pl.BlockSpec((rows, depth), lambda i, idx: (i, 0)),
            pl.BlockSpec((rows, width - 128), lambda i, idx: (i, 0)),
            pl.BlockSpec((rows, 128), lambda i, idx: (i, 0)),
        ],
    )
    return pl.pallas_call(
        qkv_kernel,
        grid_spec=spec,
        out_shape=[
            jax.ShapeDtypeStruct((total, depth), BF),
            jax.ShapeDtypeStruct((total, width - 128), BF),
            jax.ShapeDtypeStruct((total, 128), BF),
        ],
        compiler_params=params(),
        cost_estimate=pl.CostEstimate(
            flops=2 * total * depth * width,
            bytes_accessed=4 * total * depth + 2 * depth * width + 2 * total * width,
            transcendentals=0,
        ),
        name="qkv_project",
    )(idx, x, gain, weight, cosine, sine)


def nt(a, b):
    return lax.dot_general(a, b, (((1,), (1,)), ((), ())), preferred_element_type=F32)


def tn(a, b):
    return lax.dot_general(a, b, (((0,), (0,)), ((), ())), preferred_element_type=F32)


def nn(a, b):
    return jnp.dot(a, b, preferred_element_type=F32)


def limits(at_ref, rows):
    j = pl.program_id(0)
    place = at_ref[0] - lax.broadcasted_iota(jnp.int32, (rows, 1), 0)
    return jnp.minimum(place, at_ref[1 + j] - 1)


def attend_kernel(at_ref, q_ref, kv_ref, kp_ref, o_ref, lse_ref, vk_ref):
    rows = q_ref.shape[0]
    keys = vk_ref.shape[0]
    kv = kv_ref[...].reshape(keys, 128)

    @pl.when(pl.program_id(1) == 0)
    def _():
        vk_ref[...] = pltpu.roll(kv.astype(F32), 64, 1).astype(BF)

    vk = vk_ref[...]
    allowed = kp_ref[...] <= limits(at_ref, rows)
    lane = lax.broadcasted_iota(jnp.int32, (rows, 128), 1)
    q = q_ref[...]
    zero = jnp.zeros_like(q)
    outs, logs = [], []
    for first in (True, False):
        mine = lane < 64 if first else lane >= 64
        scores = nt(jnp.where(mine, q, zero), kv if first else vk) * (HEAD_DIM**-0.5)
        scores = jnp.where(allowed, scores, MASKED)
        top = jnp.max(scores, axis=1, keepdims=True)
        weights = jnp.exp(scores - top)
        total = jnp.sum(weights, axis=1, keepdims=True)
        outs.append(nn(weights.astype(BF), vk if first else kv) / total)
        logs.append(jnp.broadcast_to(top + jnp.log(total), (rows, 128)))
    o_ref[...] = jnp.where(lane < 64, outs[0], outs[1]).astype(BF)
    lse_ref[...] = jnp.where(lane < 64, logs[0], logs[1])


def attend(at, q, kv, kp):
    chunks, seqs, rows, _ = kv.shape
    pairs = q.shape[2] // 128
    keys = chunks * rows
    spec = pltpu.PrefetchScalarGridSpec(
        num_scalar_prefetch=1,
        grid=(seqs, pairs),
        in_specs=[
            pl.BlockSpec((None, rows, 128), lambda j, p, at: (j, 0, p)),
            pl.BlockSpec((chunks, None, rows, 128), lambda j, p, at: (0, j, 0, 0)),
            pl.BlockSpec((1, keys), lambda j, p, at: (0, 0)),
        ],
        out_specs=[
            pl.BlockSpec((None, rows, 128), lambda j, p, at: (j, 0, p)),
            pl.BlockSpec((None, rows, 128), lambda j, p, at: (j, 0, p)),
        ],
        scratch_shapes=[pltpu.VMEM((keys, 128), BF)],
    )
    size = seqs * pairs * 2 * rows * keys
    return pl.pallas_call(
        attend_kernel,
        grid_spec=spec,
        out_shape=[
            jax.ShapeDtypeStruct(q.shape, BF),
            jax.ShapeDtypeStruct(q.shape, F32),
        ],
        compiler_params=params(),
        cost_estimate=pl.CostEstimate(
            flops=size * 4 * 128, bytes_accessed=4 << 20, transcendentals=size
        ),
        name="attend",
    )(at, q, kv, kp)


def attend_back_kernel(
    at_ref, q_ref, do_ref, lse_ref, kv_ref, kp_ref, cos_ref, sin_ref, dq_ref, dkv_ref, vk_ref, dk_ref, dv_ref
):
    rows = q_ref.shape[0]
    keys = vk_ref.shape[0]
    pair = pl.program_id(1)
    kv = kv_ref[...].reshape(keys, 128)

    @pl.when(pair == 0)
    def _():
        vk_ref[...] = pltpu.roll(kv.astype(F32), 64, 1).astype(BF)
        dk_ref[...] = jnp.zeros_like(dk_ref)
        dv_ref[...] = jnp.zeros_like(dv_ref)

    vk = vk_ref[...]
    allowed = kp_ref[...] <= limits(at_ref, rows)
    lane = lax.broadcasted_iota(jnp.int32, (rows, 128), 1)
    q, do = q_ref[...], do_ref[...]
    zero = jnp.zeros_like(q)
    parts = []
    for first in (True, False):
        mine = lane < 64 if first else lane >= 64
        keyed, valued = (kv, vk) if first else (vk, kv)
        q_own, do_own = jnp.where(mine, q, zero), jnp.where(mine, do, zero)
        scores = nt(q_own, keyed) * (HEAD_DIM**-0.5)
        log_total = lse_ref[:, 0:1] if first else lse_ref[:, 64:65]
        weights = jnp.where(allowed, jnp.exp(scores - log_total), 0.0)
        joint = weights * nt(do_own, valued)
        back = (joint - weights * jnp.sum(joint, axis=1, keepdims=True)).astype(BF)
        parts.append(nn(back, keyed))
        dk_ref[...] += tn(back, q_own)
        dv_ref[...] += tn(weights.astype(BF), do_own)
    turned = jnp.where(lane < 64, parts[0], parts[1]) * (HEAD_DIM**-0.5)
    dq_ref[...] = (turned * cos_ref[...] - swap_halves(turned) * sin_ref[...]).astype(BF)

    @pl.when(pair == pl.num_programs(1) - 1)
    def _():
        dk = dk_ref[...]
        dv = dv_ref[...]
        dk = (dk + pltpu.roll(dk, 64, 1)) * (HEAD_DIM**-0.5)
        dv = dv + pltpu.roll(dv, 64, 1)
        wide = lax.broadcasted_iota(jnp.int32, dk.shape, 1)
        dkv_ref[...] = jnp.where(wide < 64, dk, dv).astype(BF).reshape(dkv_ref.shape)


def attend_back(at, q, do, lse, kv, kp, cosine, sine):
    chunks, seqs, rows, _ = kv.shape
    pairs = q.shape[2] // 128
    keys = chunks * rows
    tall = pl.BlockSpec((None, rows, 128), lambda j, p, at: (j, 0, p))
    whole = pl.BlockSpec((chunks, None, rows, 128), lambda j, p, at: (0, j, 0, 0))
    flat = pl.BlockSpec((rows, 128), lambda j, p, at: (0, 0))
    spec = pltpu.PrefetchScalarGridSpec(
        num_scalar_prefetch=1,
        grid=(seqs, pairs),
        in_specs=[tall, tall, tall, whole, pl.BlockSpec((1, keys), lambda j, p, at: (0, 0)), flat, flat],
        out_specs=[tall, whole],
        scratch_shapes=[
            pltpu.VMEM((keys, 128), BF),
            pltpu.VMEM((keys, 128), F32),
            pltpu.VMEM((keys, 128), F32),
        ],
    )
    size = seqs * pairs * 2 * rows * keys
    return pl.pallas_call(
        attend_back_kernel,
        grid_spec=spec,
        out_shape=[
            jax.ShapeDtypeStruct(q.shape, BF),
            jax.ShapeDtypeStruct(kv.shape, BF),
        ],
        compiler_params=params(),
        cost_estimate=pl.CostEstimate(
            flops=size * 10 * 128, bytes_accessed=8 << 20, transcendentals=size
        ),
        name="attend_back",
    )(at, q, do, lse, kv, kp, cosine, sine)


def rms_backward(row_block, inverse, gain_vec, gradient):
    normed = row_block * inverse
    gain_grad = jnp.sum(gradient * normed, axis=0)
    scaled = gradient * gain_vec
    back = inverse * (scaled - normed * jnp.mean(scaled * normed, axis=1, keepdims=True))
    return (back, gain_grad)


def body_plain(
    tokens, cotangent, lengths, attn_gain, w_query, w_key, w_value, w_out, mlp_gain, w_gate, w_up, w_down
):
    seqs, rows, depth = tokens.shape
    count, line = lax.axis_size("fsdp"), lax.axis_size("z")
    f, z, k = lax.axis_index("fsdp"), lax.axis_index("z"), lax.axis_index("core")
    slot = rows * line * 2
    total = count * rows
    slab = depth // count
    half = slab // 2
    q_width = HEADS * HEAD_DIM // count
    shared = max(1, count // KV_HEADS)

    x_own = tokens.reshape(rows, depth)
    chunk = 2 * z + k
    first_pos = slot - 1 - chunk * rows

    length = lengths[0]
    words = jnp.zeros((slab,), F32).at[0].set((length // 64).astype(F32)).at[1].set((length % 64).astype(F32))
    note = jnp.stack([attn_gain, mlp_gain, words.astype(BF), jnp.zeros((slab,), BF)])
    notes = [note] + [along_plane(note, j) for j in range(1, count)]
    notes_abs = [lax.dynamic_index_in_dim(jnp.stack(notes), f ^ i, 0, keepdims=False) for i in range(count)]
    gain_one = jnp.concatenate([n[0] for n in notes_abs]).astype(F32).reshape(1, depth)
    gain_two = jnp.concatenate([n[1] for n in notes_abs]).astype(F32).reshape(1, depth)
    all_lengths = jnp.stack(
        [n[2, 0].astype(jnp.int32) * 64 + n[2, 1].astype(jnp.int32) for n in notes]
    )

    x_all = jnp.concatenate(plane_gather(x_own))

    wq = cut_blocks(w_query, f, k, count)
    key_cols = lax.dynamic_slice_in_dim(w_key, k * half, half, 0).reshape(half, KV_HEADS, HEAD_DIM)
    value_cols = lax.dynamic_slice_in_dim(w_value, k * half, half, 0).reshape(half, KV_HEADS, HEAD_DIM)

    def head_of(j):
        return (f ^ j) // shared

    wkv = jnp.stack(
        [
            jnp.concatenate(
                [
                    lax.dynamic_index_in_dim(key_cols, head_of(j), 1, keepdims=False),
                    lax.dynamic_index_in_dim(value_cols, head_of(j), 1, keepdims=False),
                ],
                axis=1,
            )
            for j in range(count)
        ]
    )
    wqkv = jnp.concatenate([wq, wkv], axis=2)
    wqkv_own = jnp.stack([wqkv[0]] + [along_plane(wqkv[j], j) for j in range(1, count)])
    wqkv_sib = to_sibling(wqkv_own)
    wqkv_all = jnp.concatenate([wqkv_own, wqkv_sib]).reshape(depth, q_width + 128)

    def fetch(weight):
        cut = cut_blocks(weight, f, k, count)
        width = cut.shape[2]
        own = jnp.stack([cut[0]] + [along_plane(cut[j], j) for j in range(1, count)])
        sib = to_sibling(own)
        return own.reshape(depth // 2, width), sib.reshape(depth // 2, width)

    gate_own, gate_sib = fetch(w_gate)
    up_own, up_sib = fetch(w_up)

    order = jnp.stack([(f ^ j) * 2 + (k ^ h) for h in range(2) for j in range(count)]).astype(jnp.int32)

    half_dim = HEAD_DIM // 2
    frequency = jnp.power(ROPE_BASE, jnp.arange(half_dim, dtype=F32) * (-2.0 / HEAD_DIM))
    positions = first_pos - jnp.arange(rows, dtype=jnp.int32)
    angles = positions.astype(F32)[:, None] * frequency[None, :]
    cos32, sin32 = jnp.cos(angles), jnp.sin(angles)
    cosine = jnp.concatenate([cos32] * 4, axis=1)
    sine = jnp.concatenate([-sin32, sin32, -sin32, sin32], axis=1)

    normed_one, queries, kv = qkv_project(order, x_all, gain_one, wqkv_all, cosine, sine, rows)
    queries = queries.reshape(count, rows, q_width)
    kv = kv.reshape(count, rows, 128)

    mine = [kv] + [along_line(kv, -s) for s in range(1, line)]
    mine = jnp.stack(mine)
    kv_all = jnp.concatenate([mine, to_sibling(mine)])
    places = []
    for h in range(2):
        for s in range(line):
            start = slot - 1 - (2 * (z + s) + (k ^ h)) * rows
            places.append(start - jnp.arange(rows, dtype=jnp.int32))
    kp = jnp.concatenate(places)
    kp = jnp.where(kp < 0, FAR, kp).reshape(1, -1)
    at = jnp.concatenate([first_pos.reshape(1), all_lengths]).astype(jnp.int32)

    attended, log_total = attend(at, queries, kv_all, kp)
    attended = attended.reshape(total, q_width)

    mixed_part = nn(attended, w_out).astype(BF).reshape(count, rows, depth)
    inputs = x_own.astype(F32)
    mixed = inputs + plane_reduce(mixed_part)
    inv_two = lax.rsqrt(jnp.mean(mixed * mixed, axis=1, keepdims=True) + EPSILON)
    normed_two_own = (mixed * inv_two * gain_two).astype(BF)
    normed_two = jnp.concatenate(plane_gather(normed_two_own))
    normed_two = pick_columns(normed_two, order, 2 * count)
    n2_own, n2_sib = normed_two[:, : depth // 2], normed_two[:, depth // 2 :]

    valid = (positions < length).astype(F32)[:, None]
    out_back = cotangent.reshape(rows, depth).astype(F32) * valid
    branch_own = out_back.astype(BF)
    branch = jnp.concatenate(plane_gather(branch_own))

    gate = nn(n2_own, gate_own) + nn(n2_sib, gate_sib)
    up = nn(n2_own, up_own) + nn(n2_sib, up_sib)
    sigmoid = jax.nn.sigmoid(gate)
    hidden = (gate * sigmoid * up).astype(BF)

    half_depth = depth // 2
    branch_mine = lax.dynamic_slice_in_dim(branch, k * half_depth, half_depth, 1)
    branch_other = lax.dynamic_slice_in_dim(branch, (1 - k) * half_depth, half_depth, 1)

    def pair_sum(own, other):
        return (own + to_sibling(other.astype(BF)).astype(F32)).astype(BF)

    def swap_slabs(own):
        return jnp.stack([own[0]] + [along_plane(own[j], j) for j in range(1, count)])

    down_half = line_sum(pair_sum(tn(hidden, branch_mine), tn(hidden, branch_other)))
    down_grad = join_columns(down_half, to_sibling(down_half), k)

    hidden_grad = nt(branch, w_down)
    gate_back = (hidden_grad * up * sigmoid * (1.0 + gate * (1.0 - sigmoid))).astype(BF)
    up_back = (hidden_grad * gate * sigmoid).astype(BF)

    def slab_grad(left_own, left_other, right):
        width = right.shape[1]
        own = pair_sum(tn(left_own, right), tn(left_other, right)).reshape(count, half, width)
        return line_sum(swap_slabs(own))

    gate_half = slab_grad(n2_own, n2_sib, gate_back)
    gate_grad = join_rows(gate_half, to_sibling(gate_half), f, k)
    up_half = slab_grad(n2_own, n2_sib, up_back)
    up_grad = join_rows(up_half, to_sibling(up_half), f, k)

    back_own = (nt(gate_back, gate_own) + nt(up_back, up_own)).astype(BF)
    back_sib = (nt(gate_back, gate_sib) + nt(up_back, up_sib)).astype(BF)
    normed_back = put_columns(jnp.concatenate([back_own, back_sib], axis=1), order, 2 * count)
    normed_back = plane_reduce(normed_back.reshape(count, rows, depth))

    out_part = nn(hidden, w_down).astype(BF).reshape(count, rows, depth)
    outputs = mixed + plane_reduce(out_part)

    mixed_back, gain_two_grad = rms_backward(mixed, inv_two, gain_two, normed_back)
    mixed_grad = out_back + mixed_back
    attn_back = jnp.concatenate(plane_gather(mixed_grad.astype(BF)))
    attended_grad = nt(attn_back, w_out).astype(BF).reshape(count, rows, q_width)

    back_mine = lax.dynamic_slice_in_dim(attn_back, k * half_depth, half_depth, 1)
    back_other = lax.dynamic_slice_in_dim(attn_back, (1 - k) * half_depth, half_depth, 1)
    out_half = line_sum(pair_sum(tn(attended, back_mine), tn(attended, back_other)))
    out_grad = join_columns(out_half, to_sibling(out_half), k)

    query_back, kv_part = attend_back(at, queries, attended_grad, log_total, kv_all, kp, cosine, sine)
    kv_mine = kv_part[:line].astype(F32) + to_sibling(kv_part[line:]).astype(F32)
    kv_back = kv_mine[0]
    for s in range(1, line):
        kv_back = kv_back + along_line(kv_mine[s].astype(BF), s).astype(F32)
    lead, trail, flat = kv_back[..., :32], kv_back[..., 32:64], kv_back[..., 64:]
    kv_back = jnp.concatenate(
        [lead * cos32 + trail * sin32, trail * cos32 - lead * sin32, flat], axis=-1
    ).astype(BF)
    qkv_back = jnp.concatenate(
        [query_back.reshape(total, q_width), kv_back.reshape(total, 128)], axis=1
    )

    normed_one_back = nt(qkv_back, wqkv_all).astype(BF)
    normed_one_back = put_columns(normed_one_back, order, 2 * count)
    normed_one_back = plane_reduce(normed_one_back.reshape(count, rows, depth))
    inv_one = lax.rsqrt(jnp.mean(inputs * inputs, axis=1, keepdims=True) + EPSILON)
    input_back, gain_one_grad = rms_backward(inputs, inv_one, gain_one, normed_one_back)
    input_grad = mixed_grad + input_back

    n1_own, n1_sib = normed_one[:, :half_depth], normed_one[:, half_depth:]
    qkv_own = pair_sum(tn(n1_own, qkv_back), tn(n1_sib, qkv_back)).reshape(count, half, q_width + 128)
    gains = jnp.stack([gain_one_grad, gain_two_grad]).reshape(2, count, slab)
    gains = jnp.stack(
        [lax.dynamic_index_in_dim(gains, f ^ j, 1, keepdims=False) for j in range(count)]
    ).astype(BF)
    gains = line_sum(swap_slabs(gains))
    qkv_half = line_sum(swap_slabs(qkv_own))
    gains = jnp.sum(gains.astype(F32), axis=0) + jnp.sum(to_sibling(gains).astype(F32), axis=0)
    qkv_other = to_sibling(qkv_half)
    query_grad = join_rows(qkv_half[:, :, :q_width], qkv_other[:, :, :q_width], f, k)
    halves = jnp.stack([qkv_half[:, :, q_width:], qkv_other[:, :, q_width:]])

    def by_head(lo, hi):
        both = [lax.dynamic_index_in_dim(halves, k ^ h, 0, keepdims=False) for h in range(2)]
        both = jnp.concatenate(both, axis=1).astype(F32)[:, :, lo:hi]
        cols = jnp.stack([lax.dynamic_index_in_dim(both, f ^ i, 0, keepdims=False) for i in range(count)])
        cols = cols.reshape(KV_HEADS, shared, slab, HEAD_DIM).sum(1)
        return jnp.transpose(cols, (1, 0, 2)).reshape(slab, KV_HEADS * HEAD_DIM)

    key_grad = by_head(0, 64)
    value_grad = by_head(64, 128)

    return (
        outputs.reshape(seqs, rows, depth),
        input_grad.reshape(seqs, rows, depth),
        gains[0],
        query_grad,
        key_grad,
        value_grad,
        out_grad,
        gains[1],
        gate_grad,
        up_grad,
        down_grad,
    )


def rotary_parts(slot, rows):
    lane = np.arange(128) % (HEAD_DIM // 2)
    frequency = ROPE_BASE ** (lane * (-2.0 / HEAD_DIM))
    starts = (slot - 1 - rows * np.arange(slot // rows))[:, None] * frequency[None, :]
    steps = np.arange(rows)[:, None] * frequency[None, :]
    return [jnp.asarray(t(a), F32) for a in (starts, steps) for t in (np.cos, np.sin)]


def front_kernel(
    length_ref, attn_gain, mlp_gain, start_cos, start_sin, step_cos, step_sin,
    tokens, cotangent, w_query, w_key, w_value, w_out, w_gate, w_up, w_down,
    h1_out, queries_out, lse_out, attended_out, mixed_out, n2_out, limits_out, cosine_out, sine_out, kp_out,
    gain_one_out, gain_two_out, kv_out, branch_out, wqkv_out, gate_back_out, up_back_out, hidden_out,
    gate_own_out, gate_sib_out, up_own_out, up_sib_out,
    h1, queries, lse, attended, mixed, n2, limits, cosine, sine, kp, gain_one, gain_two,
    gate_back, up_back, hidden, grad,
    notes, x_all, wqkv, keys_in, values_in, kv_give, gate_own, gate_sib, up_own, up_sib, down,
    kv_all, vk, w_o, part, landed, relay, relayed, n2_all, branch_all, cot_in,
    local_s, store_s, wx_s, wx_r, note_s, note_r, tok_s, tok_r, tof_s, tof_r, wq_s, wq_r, wk_s, wk_r, wp_s, wp_r, wkp_s, wkp_r,
    kz_s, kz_r, kp_s, kp_r, gt_s, gt_r, up_s, up_r, gz_s, gz_r, gs_s, gs_r, us_s, us_r,
    bt_s, bt_r, btf_s, btf_r, mx_s, mx_r, nt_s, nt_r, ntf_s, ntf_r,
):
    f, z, k = lax.axis_index("fsdp"), lax.axis_index("z"), lax.axis_index("core")
    plane, line = 4, 4
    rows, depth = tokens.shape
    total = plane * rows
    slab = depth // plane
    half = slab // 2
    hr = rows // 2
    q_width = w_out.shape[0]
    pairs = q_width // 128
    ff = w_down.shape[0]
    keys = vk.shape[0]
    slot = rows * line * 2
    even = z % 2 == 0
    across = z + 1 - 2 * (z % 2)
    peers = (1, 2, 3)
    first_pos = slot - 1 - (2 * z + k) * rows

    def remote(source, target, send, recv, where):
        return pltpu.make_async_remote_copy(
            src_ref=source,
            dst_ref=target,
            send_sem=send,
            recv_sem=recv,
            device_id=where,
            device_id_type=pl.DeviceIdType.MESH,
        )

    sib = {"core": 1 - k}

    def chip(j):
        return {"fsdp": f ^ j}

    def cols(weight, j, side, width):
        start = pl.multiple_of((f ^ j) * width, 128)
        return weight.at[pl.ds(pl.multiple_of((k ^ side) * half, 16), half), pl.ds(start, width)]

    class Gather:
        def __init__(self, source, target, send, recv, fsend, frecv):
            self.near = {
                j: remote(source, target.at[j], send.at[j - 1], recv.at[j - 1], chip(j)) for j in (1, 2)
            }
            self.far = {
                j: remote(
                    target.at[j, pl.ds((j - 1) * hr, hr), :],
                    target.at[3, pl.ds((j - 1) * hr, hr), :],
                    fsend.at[j - 1],
                    frecv.at[j - 1],
                    chip(3 - j),
                )
                for j in (1, 2)
            }

        def start(self):
            for j in (1, 2):
                self.near[j].start()

        def forward(self):
            for j in (1, 2):
                self.near[j].wait_recv()
                self.far[j].start()

        def arrive(self):
            for j in (1, 2):
                self.far[j].wait_recv()

        def close(self):
            for j in (1, 2):
                self.near[j].wait_send()
                self.far[j].wait_send()

    def note_send(j):
        return remote(notes.at[0], notes.at[j], note_s.at[j - 1], note_r.at[j - 1], chip(j))

    token_gather = Gather(tokens, x_all, tok_s, tok_r, tof_s, tof_r)
    branch_gather = Gather(branch_all.at[0], branch_all, bt_s, bt_r, btf_s, btf_r)
    n2_gather = Gather(n2_all.at[0], n2_all, nt_s, nt_r, ntf_s, ntf_r)

    def wq_send(j):
        target = wqkv.at[pl.ds(j * half, half), pl.ds(0, q_width)]
        return remote(cols(w_query, j, 0, q_width), target, wq_s.at[j - 1], wq_r.at[j - 1], chip(j))

    def wk_send(j):
        target = wqkv.at[pl.ds(j * half, half), pl.ds(q_width, 128)]
        return remote(kv_give.at[j], target, wk_s.at[j - 1], wk_r.at[j - 1], chip(j))

    def wp_send(j):
        source = wqkv.at[pl.ds(j * half, half), :]
        target = wqkv.at[pl.ds((plane + j) * half, half), :]
        return remote(source, target, wp_s.at[j - 1], wp_r.at[j - 1], sib)

    def w_across(j):
        block = wqkv.at[pl.ds(j * half, half), :]
        return remote(block, block, wx_s.at[j - 1], wx_r.at[j - 1], {"z": across})

    def kv_send(s):
        return remote(kv_all.at[0], kv_all.at[s], kz_s.at[s - 1], kz_r.at[s - 1], {"z": z - s})

    def kv_pair(s):
        return remote(kv_all.at[s], kv_all.at[line + s], kp_s.at[s], kp_r.at[s], sib)

    def gate_send(j):
        return remote(cols(w_gate, j, 0, ff), gate_own.at[j], gt_s.at[j - 1], gt_r.at[j - 1], chip(j))

    def up_send(j):
        return remote(cols(w_up, j, 0, ff), up_own.at[j], up_s.at[j - 1], up_r.at[j - 1], chip(j))

    def gate_across(j):
        return remote(gate_own.at[j], gate_own.at[j], gz_s.at[j - 1], gz_r.at[j - 1], {"z": across})

    def up_across(j):
        return remote(up_own.at[j], up_own.at[j], gz_s.at[j - 1], gz_r.at[j - 1], {"z": across})

    def by_parity(act_even, act_odd):
        @pl.when(even)
        def _():
            act_even()

        @pl.when(jnp.logical_not(even))
        def _():
            act_odd()

    def fetch_start():
        by_parity(
            lambda: [gate_send(j).start() for j in (3, 1, 2)], lambda: [up_send(j).start() for j in (3, 1, 2)]
        )

    def fetch_on(j):
        def gate_on():
            gate_send(j).wait_recv()
            gate_across(j).start()
            gate_pair(j).start()

        def up_on():
            up_send(j).wait_recv()
            up_across(j).start()
            up_pair(j).start()

        by_parity(gate_on, up_on)

    def cross_on(j):
        def up_on():
            up_across(j).wait_recv()
            up_pair(j).start()

        def gate_on():
            gate_across(j).wait_recv()
            gate_pair(j).start()

        by_parity(up_on, gate_on)

    def gate_pair(j):
        return remote(gate_own.at[j], gate_sib.at[j], gs_s.at[j - 1], gs_r.at[j - 1], sib)

    def up_pair(j):
        return remote(up_own.at[j], up_sib.at[j], us_s.at[j - 1], us_r.at[j - 1], sib)

    def span(which):
        return pl.ds(which * hr, hr)

    mix_first = {
        "one": remote(part.at[1, span(0), :], landed.at[0, span(0), :], mx_s.at[0], mx_r.at[0], chip(1)),
        "two": remote(part.at[2, span(1), :], landed.at[1, span(1), :], mx_s.at[1], mx_r.at[1], chip(2)),
        "far_one": remote(part.at[3, span(0), :], relay.at[0], mx_s.at[2], mx_r.at[2], chip(1)),
        "far_two": remote(part.at[3, span(1), :], relay.at[1], mx_s.at[3], mx_r.at[3], chip(2)),
        "late_two": remote(relayed.at[0], landed.at[1, span(0), :], mx_s.at[4], mx_r.at[4], chip(2)),
        "late_one": remote(relayed.at[1], landed.at[0, span(1), :], mx_s.at[5], mx_r.at[5], chip(1)),
    }

    local = [
        pltpu.make_async_copy(source, target, local_s.at[n])
        for n, (source, target) in enumerate(
            [
                (tokens, x_all.at[0]),
                (w_key, keys_in),
                (w_value, values_in),
                (cols(w_query, 0, 0, q_width), wqkv.at[pl.ds(0, half), pl.ds(0, q_width)]),
                (cols(w_query, 0, 1, q_width), wqkv.at[pl.ds(plane * half, half), pl.ds(0, q_width)]),
                (cotangent, cot_in),
                (w_out, w_o),
                (cols(w_gate, 0, 0, ff), gate_own.at[0]),
                (cols(w_gate, 0, 1, ff), gate_sib.at[0]),
                (cols(w_up, 0, 0, ff), up_own.at[0]),
                (cols(w_up, 0, 1, ff), up_sib.at[0]),
                (w_down, down),
            ]
        )
    ]

    stored = [
        (h1, h1_out), (queries, queries_out), (lse, lse_out), (attended, attended_out), (mixed, mixed_out),
        (n2, n2_out), (limits, limits_out), (cosine, cosine_out), (sine, sine_out), (kp, kp_out),
        (gain_one, gain_one_out), (gain_two, gain_two_out), (kv_all, kv_out), (branch_all, branch_out),
        (wqkv, wqkv_out), (gate_back, gate_back_out), (up_back, up_back_out), (hidden, hidden_out),
        (gate_own, gate_own_out), (gate_sib, gate_sib_out), (up_own, up_own_out), (up_sib, up_sib_out),
    ]

    def store(n):
        return pltpu.make_async_copy(*stored[n], store_s.at[n])

    length = length_ref[0]
    place = lax.broadcasted_iota(jnp.int32, (16, slab), 0)
    high, low = (length // 64).astype(F32), (length % 64).astype(F32)
    note = jnp.where(place == 0, attn_gain[...].astype(F32)[None, :], mlp_gain[...].astype(F32)[None, :])
    note = jnp.where(place == 2, high, jnp.where(place == 3, low, note))
    notes[0] = note.astype(BF)
    for j in peers:
        note_send(j).start()
    by_parity(lambda: wq_send(3).start(), lambda: [wq_send(j).start() for j in (1, 2)])
    token_gather.start()
    for copy in local:
        copy.start()

    local[1].wait()
    local[2].wait()

    def head_columns(j, side):
        at = pl.ds(pl.multiple_of((k ^ side) * half, 16), half)
        head = f ^ j
        width = KV_HEADS * HEAD_DIM
        key = pltpu.roll(keys_in[at, :].astype(F32), (width - head * 64) % width, 1)[:, :128]
        value = pltpu.roll(values_in[at, :].astype(F32), (width - head * 64 + 64) % width, 1)[:, :128]
        lane = lax.broadcasted_iota(jnp.int32, key.shape, 1)
        return jnp.where(lane < 64, key, value).astype(BF)

    for j in (3, 1, 2):
        kv_give[j] = head_columns(j, 0)
    by_parity(lambda: wk_send(3).start(), lambda: [wk_send(j).start() for j in (1, 2)])
    wqkv[0:half, q_width : q_width + 128] = head_columns(0, 0)
    wqkv[plane * half : (plane + 1) * half, q_width : q_width + 128] = head_columns(0, 1)

    chunk = pl.ds(2 * z + k, 1)
    cos_at, sin_at = start_cos[chunk, :], start_sin[chunk, :]
    lane = lax.broadcasted_iota(jnp.int32, (rows, 128), 1)
    cosine[...] = cos_at * step_cos[...] + sin_at * step_sin[...]
    turn = sin_at * step_cos[...] - cos_at * step_sin[...]
    sine[...] = jnp.where(lane % 64 < 32, -turn, turn)
    for h in range(2):
        for s in range(line):
            start = slot - 1 - (2 * (z + s) + (k ^ h)) * rows
            spot = start - lax.broadcasted_iota(jnp.int32, (8, rows), 1)
            spot = jnp.where(spot < 0, FAR, spot).astype(F32)
            kp[:, (h * line + s) * rows : (h * line + s + 1) * rows] = spot

    for s in range(1, line):

        @pl.when(z + s >= line)
        def _():
            kv_all[s] = jnp.zeros(kv_all.shape[1:], BF)
            kv_all[line + s] = jnp.zeros(kv_all.shape[1:], BF)

    local[5].wait()
    row_pos = (first_pos - lax.broadcasted_iota(jnp.int32, (rows, 1), 0)).astype(F32)
    valid = row_pos < jnp.full((rows, 1), length.astype(F32))
    branch_all[0] = jnp.where(valid, cot_in[...].astype(F32), 0.0).astype(BF)

    def projections_on(j):
        wq_send(j).wait_recv()
        wk_send(j).wait_recv()
        w_across(j).start()
        wp_send(j).start()

    by_parity(lambda: projections_on(3), lambda: [projections_on(j) for j in (1, 2)])
    token_gather.forward()
    fetch_start()

    for j in peers:
        note_send(j).wait_recv()
    for j in range(plane):
        at = pl.ds(pl.multiple_of((f ^ j) * slab, 128), slab)
        gain_one[:, at] = jnp.broadcast_to(notes[j, 0:1, :].astype(F32), (8, slab))
        gain_two[:, at] = jnp.broadcast_to(notes[j, 1:2, :].astype(F32), (8, slab))
        theirs = notes[j, 2:3, 0:1].astype(F32) * 64.0 + notes[j, 3:4, 0:1].astype(F32)
        limits[j] = jnp.broadcast_to(jnp.minimum(row_pos, theirs - 1.0), (rows, 128))

    def normalize(j, x_ref):
        @pl.loop(0, rows // 16)
        def _(i):
            at = pl.ds(pl.multiple_of(i * 16, 16), 16)
            x = x_ref[at, :].astype(F32)
            inverse = lax.rsqrt(jnp.mean(x * x, axis=1, keepdims=True) + EPSILON)
            to = pl.ds(pl.multiple_of(j * rows + i * 16, 16), 16)
            for h in range(2):
                for b in range(plane):
                    from_ = pl.ds(pl.multiple_of(((f ^ b) * 2 + (k ^ h)) * half, 128), half)
                    value = x_ref[at, from_].astype(F32) * inverse * gain_one[0:1, from_]
                    c = (h * plane + b) * half
                    h1[to, c : c + half] = value.astype(BF)

    local[0].wait()
    normalize(0, x_all.at[0])

    def projections_in(js):
        for j in js:
            w_across(j).wait_recv()
            wp_send(j).start()

    by_parity(lambda: projections_in((1, 2)), lambda: projections_in((3,)))

    @pl.loop(1, 3)
    def _(j):
        normalize(j, x_all.at[j])

    token_gather.arrive()
    normalize(3, x_all.at[3])
    local[3].wait()
    local[4].wait()
    for j in (1, 2, 3):
        wp_send(j).wait_recv()

    kv_cols = nn(h1[...], wqkv[:, q_width : q_width + 128])
    for j in range(plane):
        value = kv_cols[j * rows : (j + 1) * rows]
        turned = value * cosine[...] + swap_halves(value) * sine[...]
        kv_all[0, j] = jnp.where(lane < 64, turned, value).astype(BF)
    for s in range(1, line):

        @pl.when(z >= s)
        def _():
            kv_send(s).start()

    kv_pair(0).start()
    branch_gather.start()

    @pl.loop(0, pairs // 2)
    def _(p):
        at = pl.ds(pl.multiple_of(p * 256, 256), 256)
        out = nn(h1[...], wqkv[:, at])
        for j in range(plane):
            for c in range(2):
                value = out[j * rows : (j + 1) * rows, c * 128 : (c + 1) * 128]
                turned = value * cosine[...] + swap_halves(value) * sine[...]
                queries[j, :, pl.ds(pl.multiple_of(p * 256 + c * 128, 128), 128)] = turned.astype(BF)

    for s in range(1, line):

        @pl.when(z + s < line)
        def _():
            kv_send(s).wait_recv()
            kv_pair(s).start()

    fetch_on(1)
    fetch_on(2)
    kv_pair(0).wait_recv()
    for s in range(1, line):

        @pl.when(z + s < line)
        def _():
            kv_pair(s).wait_recv()

    local[6].wait()

    def by_columns(act):
        @pl.loop(0, ff // 256)
        def _(n):
            act(pl.ds(pl.multiple_of(n * 256, 256), 256))

        if ff % 256:
            act(pl.ds(ff // 256 * 256, ff % 256))

    def relay_on(far, late, which, j):
        mix_first[far].wait_recv()
        value = relay[which].astype(F32) + part[j, which * hr : (which + 1) * hr, :].astype(F32)
        relayed[which] = value.astype(BF)
        mix_first[late].start()

    @pl.loop(0, plane)
    def _(t):
        j = plane - 1 - t
        here = pl.ds(pl.multiple_of(j * rows, 16), rows)
        vk[...] = pltpu.roll(kv_all[:, j].reshape(keys, 128).astype(F32), 64, 1).astype(BF)
        limit = limits[j, :, 0:1]

        @pl.loop(0, pairs)
        def _(p):
            at = pl.ds(pl.multiple_of(p * 128, 128), 128)
            allowed = kp[0:1, :] <= limit
            q = queries[j, :, at]
            zero = jnp.zeros_like(q)
            outs, logs = [], []
            for first in (True, False):
                mine = lane < 64 if first else lane >= 64
                kv = kv_all[:, j].reshape(keys, 128)
                keyed, valued = (kv, vk[...]) if first else (vk[...], kv)
                scores = nt(jnp.where(mine, q, zero), keyed) * (HEAD_DIM**-0.5)
                scores = jnp.where(allowed, scores, MASKED)
                top = jnp.max(scores, axis=1, keepdims=True)
                weights = jnp.exp(scores - top)
                sums = jnp.sum(weights, axis=1, keepdims=True)
                outs.append(nn(weights.astype(BF), valued) / sums)
                logs.append(jnp.broadcast_to(top + jnp.log(sums), (rows, 128)))
            attended[here, at] = jnp.where(lane < 64, outs[0], outs[1]).astype(BF)
            lse[j, :, at] = jnp.where(lane < 64, logs[0], logs[1])

        part[j] = nn(attended[here, :], w_o[...]).astype(BF)

        @pl.when(t == 0)
        def _():
            mix_first["far_one"].start()
            mix_first["far_two"].start()
            branch_gather.forward()

        @pl.when(t == 1)
        def _():
            mix_first["two"].start()
            fetch_on(3)

        @pl.when(t == 2)
        def _():
            mix_first["one"].start()
            relay_on("far_one", "late_two", 0, 2)
            relay_on("far_two", "late_one", 1, 1)

    early_stores = [store(n) for n in range(12)]
    for n in (0, 1, 2, 3, 6, 7, 8, 9, 10, 11):
        early_stores[n].start()
    cross_on(1)
    cross_on(2)
    for name in ("one", "late_one", "two", "late_two"):
        mix_first[name].wait_recv()

    @pl.loop(0, rows // 16)
    def _(i):
        at = pl.ds(pl.multiple_of(i * 16, 16), 16)
        value = x_all[0, at, :].astype(F32) + part[0, at, :].astype(F32)
        value = value + landed[0, at, :].astype(F32) + landed[1, at, :].astype(F32)
        mixed[at, :] = value
        inverse = lax.rsqrt(jnp.mean(value * value, axis=1, keepdims=True) + EPSILON)
        n2_all[0, at, :] = (value * inverse * gain_two[0:1, :]).astype(BF)

    n2_gather.start()
    early_stores[4].start()

    def pack(j):
        @pl.loop(0, rows // 16)
        def _(i):
            at = pl.ds(pl.multiple_of(i * 16, 16), 16)
            to = pl.ds(pl.multiple_of(j * rows + i * 16, 16), 16)
            for h in range(2):
                for b in range(plane):
                    from_ = pl.ds(pl.multiple_of(((f ^ b) * 2 + (k ^ h)) * half, 128), half)
                    c = (h * plane + b) * half
                    n2[to, c : c + half] = n2_all[j, at, from_]

    pack(0)
    branch_gather.arrive()
    local[11].wait()

    def down_grad(at):
        grad[:, at] = nt(branch_all[...].reshape(total, depth), down[at, :])

    by_columns(down_grad)
    n2_gather.forward()

    @pl.loop(1, 3)
    def _(j):
        pack(j)

    cross_on(3)
    for n in range(7, 11):
        local[n].wait()
    for j in peers:
        gate_pair(j).wait_recv()
        up_pair(j).wait_recv()
    weight_stores = [store(n) for n in range(18, 22)]
    for copy in weight_stores:
        copy.start()
    n2_gather.arrive()

    pack(3)
    early_stores[5].start()
    later = [store(n) for n in range(12, 18)]
    for n in range(3):
        later[n].start()

    def feed(at):
        width = at.size
        n2_own, n2_sib = n2[:, 0 : depth // 2], n2[:, depth // 2 : depth]

        def through(own, other):
            first = nn(n2_own, own[:, :, at].reshape(depth // 2, width))
            return first + nn(n2_sib, other[:, :, at].reshape(depth // 2, width))

        gate = through(gate_own, gate_sib)
        up = through(up_own, up_sib)
        sigmoid = 1.0 / (1.0 + jnp.exp(-gate))
        hidden[:, at] = (gate * sigmoid * up).astype(BF)
        back = grad[:, at]
        gate_back[:, at] = (back * up * sigmoid * (1.0 + gate * (1.0 - sigmoid))).astype(BF)
        up_back[:, at] = (back * gate * sigmoid).astype(BF)

    by_columns(feed)
    for n in range(3, 6):
        later[n].start()
    for gather in (token_gather, branch_gather, n2_gather):
        gather.close()
    for copy in mix_first.values():
        copy.wait_send()
    for j in peers:
        note_send(j).wait_send()
        wp_send(j).wait_send()
        gate_pair(j).wait_send()
        up_pair(j).wait_send()
    projections = (wq_send, wk_send, w_across)
    by_parity(
        lambda: [c(3).wait_send() for c in projections],
        lambda: [c(j).wait_send() for j in (1, 2) for c in projections],
    )
    by_parity(
        lambda: [c(j).wait_send() for j in peers for c in (gate_send, gate_across)],
        lambda: [c(j).wait_send() for j in peers for c in (up_send, up_across)],
    )

    kv_pair(0).wait_send()
    for s in range(1, line):

        @pl.when(z >= s)
        def _():
            kv_send(s).wait_send()

        @pl.when(z + s < line)
        def _():
            kv_pair(s).wait_send()

    for copy in early_stores + later + weight_stores:
        copy.wait()


def front_pass(tokens, cotangent, lengths, attn_gain, mlp_gain, w_query, w_key, w_value, w_out, w_gate, w_up, w_down):
    rows, depth = tokens.shape
    plane, line = 4, 4
    total, slab = plane * rows, depth // plane
    half = slab // 2
    q_width = HEADS * HEAD_DIM // plane
    width = q_width + 128
    ff = w_down.shape[0]
    slot = rows * line * 2
    keys = slot
    act = (rows, depth)
    local = pl.BlockSpec(memory_space=pltpu.VMEM)
    anywhere = pl.BlockSpec(memory_space=pl.ANY)
    dma = lambda n: pltpu.SemaphoreType.DMA((n,))
    kv_shape = (2 * line, plane, rows, 128)
    sds = jax.ShapeDtypeStruct
    outs = [
        sds((total, depth), BF),
        sds((plane, rows, q_width), BF),
        sds((plane, rows, q_width), F32),
        sds((total, q_width), BF),
        sds(act, F32),
        sds((total, depth), BF),
        sds((plane, rows, 128), F32),
        sds((rows, 128), F32),
        sds((rows, 128), F32),
        sds((8, keys), F32),
        sds((8, depth), F32),
        sds((8, depth), F32),
        sds(kv_shape, BF),
        sds((plane,) + act, BF),
        sds((depth, width), BF),
        sds((total, ff), BF),
        sds((total, ff), BF),
        sds((total, ff), BF),
    ] + [sds((plane, half, ff), BF)] * 4
    held = [pltpu.VMEM(o.shape, o.dtype) for o in outs]
    held = held[:12] + held[15:18] + [pltpu.VMEM((total, ff), F32)]
    slabs = pltpu.VMEM((plane, half, ff), BF)
    scratch = held + [
        pltpu.VMEM((plane, 16, slab), BF),
        pltpu.VMEM((plane,) + act, BF),
        pltpu.VMEM((depth, width), BF),
        pltpu.VMEM(w_key.shape, BF),
        pltpu.VMEM(w_value.shape, BF),
        pltpu.VMEM((plane, half, 128), BF),
        slabs,
        slabs,
        slabs,
        slabs,
        pltpu.VMEM(w_down.shape, BF),
        pltpu.VMEM(kv_shape, BF),
        pltpu.VMEM((keys, 128), BF),
        pltpu.VMEM(w_out.shape, BF),
        pltpu.VMEM((plane,) + act, BF),
        pltpu.VMEM((2,) + act, BF),
        pltpu.VMEM((2, rows // 2, depth), BF),
        pltpu.VMEM((2, rows // 2, depth), BF),
        pltpu.VMEM((plane,) + act, BF),
        pltpu.VMEM((plane,) + act, BF),
        pltpu.VMEM(act, BF),
    ]
    sems = [12, 22, 3, 3, 3, 3, 2, 2, 2, 2, 3, 3, 3, 3, 3, 3, 1, 1, 3, 3, 4, 4, 3, 3, 3, 3, 3, 3, 3, 3, 3, 3]
    sems += [2, 2, 2, 2, 6, 6, 2, 2, 2, 2]
    return pl.pallas_call(
        front_kernel,
        out_shape=outs,
        in_specs=[pl.BlockSpec(memory_space=pltpu.SMEM)] + [local] * 6 + [anywhere] * 9,
        out_specs=[anywhere] * 22,
        scratch_shapes=scratch + [dma(n) for n in sems],
        compiler_params=pltpu.CompilerParams(
            vmem_limit_bytes=62 * 1024 * 1024, has_side_effects=True
        ),
        name="front_pass",
    )(
        lengths, attn_gain, mlp_gain, *rotary_parts(slot, rows),
        tokens, cotangent, w_query, w_key, w_value, w_out, w_gate, w_up, w_down,
    )


def add_into(target, other):
    @pl.loop(0, target.shape[0] // 16)
    def _(i):
        at = pl.ds(pl.multiple_of(i * 16, 16), 16)
        target[at, :] = (target[at, :].astype(F32) + other[at, :].astype(F32)).astype(BF)


def back_kernel(
    limits_in, gate_back_in, up_back_in, hidden_in, mixed_in, x_own_in, gain_one_in, gain_two_in,
    attended_in, queries_in, lse_in, kv_all_in, kp_in, cosine_in, sine_in,
    branch, w_out, w_down, wqkv, h1_hbm, n2_hbm, gate_own, gate_sib, up_own, up_sib,
    fin_down, fin_gate, fin_up, fin_out, fin_qkv, fin_gain,
    sib_down, sib_gate, sib_up, sib_out, sib_qkv, sib_gain,
    outputs, input_grad_out,
    limits, gate_back, up_back, hidden, mixed, x_own, gain_one, gain_two,
    attended, queries, lse, kv_all, kp, cosine, sine, branch_own, input_grad,
    src_down, src_gate, src_up, src_out, src_qkv, src_gain,
    swap_gate, swap_up, swap_qkv,
    end_down, end_gate, end_up, end_out, end_qkv, end_gain,
    give_down, give_gate, give_out, give_qkv, give_gain,
    turned, landed, landed_out, weights, down_blocks, qkv_blocks, part, da_all, wide, do_all, dqkv, left,
    vk, dk_sum, dv_sum, kv_part, kv_land, kv_mine, kv_line, gain_acc, gain_all,
    pair_s, pair_r, swap_s, swap_r, in_s, in_r, mid_s, mid_r, out_s, done_s, back_s, back_r, ready,
    local_s, weight_s, rs_s, rs_r, ro_s, ro_r, ag_s, ag_r, rq_s, rq_r, kp_s, kp_r, kz_s, kz_r, ga_s, ga_r,
):
    f, z, k = lax.axis_index("fsdp"), lax.axis_index("z"), lax.axis_index("core")
    plane, line = lax.axis_size("fsdp"), lax.axis_size("z")
    branch_flat = branch
    outer = (z == 0) | (z == line - 1)
    inner = jnp.logical_not(outer)
    inward = jnp.where(z < line // 2, z + 1, z - 1)
    outward = jnp.where(z < line // 2, z - 1, z + 1)
    rows, depth = mixed.shape
    total = plane * rows
    half_depth = depth // 2
    half = half_depth // plane
    q_width = attended.shape[1]
    pairs = q_width // 128
    peers = range(1, plane)

    kinds = {
        "down": (src_down, None, end_down, give_down, fin_down, sib_down),
        "gate": (src_gate, swap_gate, end_gate, give_gate, fin_gate, sib_gate),
        "up": (src_up, swap_up, end_up, give_gate, fin_up, sib_up),
        "out": (src_out, None, end_out, give_out, fin_out, sib_out),
        "qkv": (src_qkv, swap_qkv, end_qkv, give_qkv, fin_qkv, sib_qkv),
        "gain": (src_gain, None, end_gain, give_gain, fin_gain, sib_gain),
    }
    chunks = [(name, i) for name, kind in kinds.items() for i in range(kind[0].shape[0])]
    chunks.insert(len(chunks) - 5, chunks.pop())
    count = len(chunks)

    def group(c):
        return kinds[chunks[c][0]][3].shape[0]

    heads = [c for c in range(count) if chunks[c][1] % group(c) == 0]

    def remote(source, target, send, recv, where):
        return pltpu.make_async_remote_copy(
            src_ref=source,
            dst_ref=target,
            send_sem=send,
            recv_sem=recv,
            device_id=where,
            device_id_type=pl.DeviceIdType.MESH,
        )

    def swapped(c):
        name, i = chunks[c]
        return i // group(c) if kinds[name][1] is not None else 0

    def source(c):
        return part_of(c, 0)

    def part_of(c, which):
        name, i = chunks[c]
        return kinds[name][which].at[i]

    def given(c):
        return kinds[chunks[c][0]][3]

    def end(c):
        return part_of(c, 2)

    def pair_copy(c):
        start = given(c).at[chunks[c][1] % group(c)]
        return remote(start, source(c), pair_s.at[c], pair_r.at[c], {"core": 1 - k})

    def landing(c):
        name, i = chunks[c]
        return kinds[name][1].at[i - group(c)]

    def swap_copy(c):
        return remote(source(c), landing(c), swap_s.at[c], swap_r.at[c], {"fsdp": f ^ swapped(c)})

    def base(c):
        return landing(c) if swapped(c) else source(c)

    def in_copy(c):
        return remote(base(c), end(c), in_s.at[c], in_r.at[c], {"z": inward})

    def mid_copy(c):
        return remote(base(c), end(c), mid_s.at[c], mid_r.at[c], {"z": inward})

    def out_copy(c):
        return remote(end(c), end(c), out_s.at[c], mid_r.at[c], {"z": outward})

    def keep_copy(c):
        return pltpu.make_async_copy(end(c), part_of(c, 4), done_s.at[c])

    def back_copy(c):
        return remote(end(c), part_of(c, 5), back_s.at[c], back_r.at[c], {"core": 1 - k})

    def term(c, side, act):
        name, i = chunks[c]
        if name == "gain":
            act(slice(None), gain_all[...].astype(F32).sum(axis=0))
            return
        start = pl.multiple_of((k ^ side) * half_depth, 128)
        if name == "down":
            size, width = 128, half_depth
            turned[0:size, :] = hidden[:, i * size : (i + 1) * size].T
        elif name == "out":
            size, width = 2 * src_out.shape[1], half_depth
            turned[0:size, :] = attended[:, i * size // 2 : i * size // 2 + size].T
        else:
            size, width = half, source(c).shape[1]
            at = side * half_depth + i * (half // 2)
            turned[0:size, :] = left[:, at : at + half].T

        def block(first, span):
            if name == "down":
                right = wide[0:total, pl.ds(start + first, span)]
            elif name == "out":
                right = da_all[:, :, pl.ds(start + first, span)].reshape(total, span)
            else:
                right = {"gate": gate_back, "up": up_back, "qkv": dqkv}[name][:, pl.ds(first, span)]
            act(pl.ds(first, span), nn(turned[0:size, :], right))

        @pl.loop(0, width // 256)
        def _(n):
            block(pl.multiple_of(n * 256, 256), 256)

        if width % 256:
            block(width // 256 * 256, width % 256)

    def stage_give(c):
        slots = given(c)
        for n in [n for n in range(c) if given(n) is slots][-group(c) :]:
            pair_copy(n).wait_send()
        size = slots.shape[1]

        def act(lanes, value):
            for n in range(group(c)):
                slots[n, :, lanes] = value[n * size : (n + 1) * size].astype(BF)

        term(c, 1, act)
        for n in range(group(c)):
            pair_copy(c + n).start()

    def stage_pair(c):
        for n in range(group(c)):
            pair_copy(c + n).wait_recv()
        size = source(c).shape[0]

        def act(lanes, value):
            for n in range(group(c)):
                target = source(c + n)
                added = target[:, lanes].astype(F32) + value[n * size : (n + 1) * size]
                target[:, lanes] = added.astype(BF)

        term(c, 0, act)
        for n in range(group(c)):
            if swapped(c + n):
                swap_copy(c + n).start()

    def stage_in(c):
        if swapped(c):
            swap_copy(c).wait_recv()

        @pl.when(outer)
        def _():
            in_copy(c).start()

    def stage_mid(c):
        @pl.when(inner)
        def _():
            in_copy(c).wait_recv()
            add_into(base(c), end(c))
            pl.semaphore_signal(
                ready, inc=1, device_id={"z": inward}, device_id_type=pl.DeviceIdType.MESH
            )
            pl.semaphore_wait(ready, 1)
            mid_copy(c).start()

    def stage_out(c):
        @pl.when(inner)
        def _():
            mid_copy(c).wait_recv()
            add_into(end(c), base(c))
            out_copy(c).start()

    def stage_keep(c):
        @pl.when(outer)
        def _():
            out_copy(c).wait_recv()

        keep_copy(c).start()
        back_copy(c).start()

    def back_send(j):
        mine = part.at[pl.ds(j * rows, rows), :]
        return remote(mine, landed.at[j - 1], rs_s.at[j - 1], rs_r.at[j - 1], {"fsdp": f ^ j})

    def out_send(j):
        mine = part.at[pl.ds(j * rows, rows), :]
        return remote(mine, landed_out.at[j - 1], ro_s.at[j - 1], ro_r.at[j - 1], {"fsdp": f ^ j})

    def da_send(j):
        return remote(da_all.at[0], da_all.at[j], ag_s.at[j - 1], ag_r.at[j - 1], {"fsdp": f ^ j})

    def dh_send(j):
        mine = wide.at[pl.ds(j * rows, rows), :]
        return remote(mine, landed.at[j - 1], rq_s.at[j - 1], rq_r.at[j - 1], {"fsdp": f ^ j})

    def gain_send(j):
        return remote(gain_all.at[0], gain_all.at[j], ga_s.at[j - 1], ga_r.at[j - 1], {"fsdp": f ^ j})

    moves = {
        "branch": (branch_flat, wide.at[pl.ds(0, total), :]), "hidden": (hidden_in, hidden), "n2": (n2_hbm, left),
        "gate_back": (gate_back_in, gate_back), "up_back": (up_back_in, up_back), "mixed": (mixed_in, mixed),
        "branch_own": (branch_flat.at[pl.ds(0, rows), :], branch_own), "gain_two": (gain_two_in, gain_two),
        "queries": (queries_in, queries), "lse": (lse_in, lse), "kv_all": (kv_all_in, kv_all),
        "limits": (limits_in, limits), "kp": (kp_in, kp), "cosine": (cosine_in, cosine), "sine": (sine_in, sine),
        "attended": (attended_in, attended), "x_own": (x_own_in, x_own), "gain_one": (gain_one_in, gain_one),
        "w_out": (w_out, wide.at[pl.ds(0, w_out.shape[0]), :]), "h1": (h1_hbm, left),
        "outputs": (mixed, outputs), "input_grad": (input_grad, input_grad_out),
    }
    moves = {
        name: pltpu.make_async_copy(*ends, local_s.at[n]) for n, (name, ends) in enumerate(moves.items())
    }

    def weight_loads(h, j):
        pairs_of = ((gate_own, up_own), (gate_sib, up_sib))[h]
        return [
            pltpu.make_async_copy(w.at[j], weights.at[j % 2, n], weight_s.at[j % 2, n])
            for n, w in enumerate(pairs_of)
        ]

    def columns_of(h, j):
        return pl.ds(pl.multiple_of(((f ^ j) * 2 + (k ^ h)) * half, 128), half)

    def piece_back(h):
        @pl.loop(0, plane)
        def _(j):
            @pl.when(j + 1 < plane)
            def _():
                for copy in weight_loads(h, j + 1):
                    copy.start()

            for copy in weight_loads(h, j):
                copy.wait()
            value = nt(gate_back[...], weights[j % 2, 0]) + nt(up_back[...], weights[j % 2, 1])
            part[:, columns_of(h, j)] = value.astype(BF)

        if h == 0:
            for copy in weight_loads(1, 0):
                copy.start()
        if h == 1:
            for j in peers:
                back_send(j).start()

    def down_at(b):
        size = depth // 8
        return pl.ds(pl.multiple_of(b * size, size), size)

    def down_load(b):
        return pltpu.make_async_copy(w_down.at[:, down_at(b)], down_blocks.at[b % 2], weight_s.at[b % 2, 0])

    def piece_out(h):
        if h == 0:
            for j in peers:
                back_send(j).wait_send()
            down_load(0).start()

        @pl.loop(4 * h, 4 * h + 4)
        def _(b):
            @pl.when(b + 1 < 8)
            def _():
                down_load(b + 1).start()

            down_load(b).wait()
            part[:, down_at(b)] = nn(hidden[...], down_blocks[b % 2]).astype(BF)

        if h == 1:
            for j in peers:
                out_send(j).start()

    def dh_load(b):
        block = wqkv.at[pl.ds(pl.multiple_of(b * half, half), half), :]
        return pltpu.make_async_copy(block, qkv_blocks.at[b % 2], weight_s.at[b % 2, 0])

    def rms_back(gradient_of, x_ref, gain, acc, write):
        acc[...] = jnp.zeros_like(acc)

        @pl.loop(0, rows // 16)
        def _(i):
            at = pl.ds(pl.multiple_of(i * 16, 16), 16)
            gradient = gradient_of(at)
            x = x_ref[at, :].astype(F32)
            inverse = lax.rsqrt(jnp.mean(x * x, axis=1, keepdims=True) + EPSILON)
            normed = x * inverse
            acc[...] += gradient * normed
            scaled = gradient * gain[0:1, :]
            write(at, inverse * (scaled - normed * jnp.mean(scaled * normed, axis=1, keepdims=True)))

    def piece_mixed():
        for name in ("mixed", "branch_own", "gain_two"):
            moves[name].wait()
        for j in peers:
            back_send(j).wait_recv()

        def gradient_of(at):
            value = part[at, :].astype(F32)
            for j in peers:
                value = value + landed[j - 1, at, :].astype(F32)
            return value

        def write(at, value):
            value = value + branch_own[at, :].astype(F32)
            input_grad[at, :] = value
            da_all[0, at, :] = value.astype(BF)

        rms_back(gradient_of, mixed, gain_two, gain_acc.at[1], write)
        for j in peers:
            da_send(j).start()

    def piece_do():
        moves["w_out"].wait()
        for j in peers:
            da_send(j).wait_recv()

        @pl.loop(0, plane)
        def _(j):
            do_all[j] = nt(da_all[j], wide[0 : w_out.shape[0], :]).astype(BF)

    def piece_attend(j):
        here = pl.ds(pl.multiple_of(j * rows, 16), rows)
        vk[...] = pltpu.roll(kv_all[:, j].reshape(vk.shape).astype(F32), 64, 1).astype(BF)
        dk_sum[...] = jnp.zeros_like(dk_sum)
        dv_sum[...] = jnp.zeros_like(dv_sum)
        limit = limits[j, :, 0:1]
        lane = lax.broadcasted_iota(jnp.int32, (rows, 128), 1)

        @pl.loop(0, pairs)
        def _(p):
            at = pl.ds(pl.multiple_of(p * 128, 128), 128)
            allowed = kp[0:1, :] <= limit
            q, do = queries[j, :, at], do_all[j, :, at]
            logs = lse[j, :, at]
            zero = jnp.zeros_like(q)
            parts = []
            for first in (True, False):
                mine = lane < 64 if first else lane >= 64
                kv = kv_all[:, j].reshape(vk.shape)
                keyed, valued = (kv, vk[...]) if first else (vk[...], kv)
                q_own, do_own = jnp.where(mine, q, zero), jnp.where(mine, do, zero)
                scores = nt(q_own, keyed) * (HEAD_DIM**-0.5)
                log_total = logs[:, 0:1] if first else logs[:, 64:65]
                weights = jnp.where(allowed, jnp.exp(scores - log_total), 0.0)
                joint = weights * nt(do_own, valued)
                back = (joint - weights * jnp.sum(joint, axis=1, keepdims=True)).astype(BF)
                parts.append(nn(back, keyed))
                dk_sum[...] += tn(back, q_own)
                dv_sum[...] += tn(weights.astype(BF), do_own)
            rotated = jnp.where(lane < 64, parts[0], parts[1]) * (HEAD_DIM**-0.5)
            rotated = rotated * cosine[...] - swap_halves(rotated) * sine[...]
            dqkv[here, at] = rotated.astype(BF)

        dk = dk_sum[...]
        dv = dv_sum[...]
        dk = (dk + pltpu.roll(dk, 64, 1)) * (HEAD_DIM**-0.5)
        dv = dv + pltpu.roll(dv, 64, 1)
        wide_lane = lax.broadcasted_iota(jnp.int32, dk.shape, 1)
        packed = jnp.where(wide_lane < 64, dk, dv).astype(BF)
        kv_part[:, j] = packed.reshape(kv_part.shape[0], rows, 128)

    kv_pair = remote(kv_part.at[pl.ds(line, line)], kv_land, kp_s.at[0], kp_r.at[0], {"core": 1 - k})

    def kv_send(s):
        return remote(kv_mine.at[s], kv_line.at[s - 1], kz_s.at[s - 1], kz_r.at[s - 1], {"z": z + s})

    def piece_kv_line():
        kv_pair.wait_recv()
        for s in range(line):
            kv_mine[s] = (kv_part[s].astype(F32) + kv_land[s].astype(F32)).astype(BF)
        for s in range(1, line):

            @pl.when(z + s < line)
            def _():
                kv_send(s).start()

    def piece_kv_sum():
        for s in range(1, line):

            @pl.when(z >= s)
            def _():
                kv_send(s).wait_recv()
                kv_mine[0] = (kv_mine[0].astype(F32) + kv_line[s - 1].astype(F32)).astype(BF)

        lane = lax.broadcasted_iota(jnp.int32, (rows, 128), 1)
        for j in range(plane):
            value = kv_mine[0, j].astype(F32)
            rotated = value * cosine[...] - swap_halves(value) * sine[...]
            value = jnp.where(lane < 64, rotated, value).astype(BF)
            dqkv[j * rows : (j + 1) * rows, q_width : q_width + 128] = value

    def piece_dh():
        dh_load(0).start()

        @pl.loop(0, 2 * plane)
        def _(b):
            @pl.when(b + 1 < 2 * plane)
            def _():
                dh_load(b + 1).start()

            dh_load(b).wait()
            wide[0:total, columns_of(b // plane, b % plane)] = nt(dqkv[...], qkv_blocks[b % 2]).astype(BF)

        for j in peers:
            dh_send(j).start()

    def piece_input():
        for name in ("x_own", "gain_one"):
            moves[name].wait()
        for j in peers:
            dh_send(j).wait_recv()

        def gradient_of(at):
            value = wide[at, :].astype(F32)
            for j in peers:
                value = value + landed[j - 1, at, :].astype(F32)
            return value

        def write(at, value):
            input_grad[at, :] = input_grad[at, :] + value

        rms_back(gradient_of, x_own, gain_one, gain_acc.at[0], write)
        moves["input_grad"].start()
        place = lax.broadcasted_iota(jnp.int32, (16, depth), 0)
        one = jnp.sum(gain_acc[0], axis=0, keepdims=True)
        two = jnp.sum(gain_acc[1], axis=0, keepdims=True)
        gain_all[0] = jnp.where(place == 0, one, jnp.where(place == 1, two, 0.0)).astype(BF)
        for j in peers:
            gain_send(j).start()

    def piece_outputs():
        for j in peers:
            out_send(j).wait_recv()

        @pl.loop(0, rows // 16)
        def _(i):
            at = pl.ds(pl.multiple_of(i * 16, 16), 16)
            value = mixed[at, :] + part[at, :].astype(F32)
            for j in peers:
                value = value + landed_out[j - 1, at, :].astype(F32)
            mixed[at, :] = value

        moves["outputs"].start()

    def piece_gain():
        for j in peers:
            gain_send(j).wait_recv()

    in_lag, mid_lag, out_lag, keep_lag = LAGS
    events = []

    def give_tick(c):
        return c - (AHEAD[1] if kinds[chunks[c][0]][1] is not None else AHEAD[0])

    for c in heads:
        events.append((give_tick(c), 4.5, stage_give, c))
        events.append((give_tick(c) + 1, 1, stage_pair, c))
    for c in range(count):
        events.append((c + in_lag, 2, stage_in, c))
        events.append((c + mid_lag, 3, stage_mid, c))
        events.append((c + out_lag, 4, stage_out, c))
        events.append((c + keep_lag, 5, stage_keep, c))
    steps = (
        (piece_back, 0), (piece_back, 1), piece_mixed, piece_do, (piece_out, 0), (piece_out, 1), (piece_attend, 0),
        (piece_attend, 1), (piece_attend, 2), (piece_attend, 3), kv_pair.start, piece_kv_line, piece_kv_sum, piece_dh, piece_outputs, piece_input, piece_gain,
    )
    for n, (step, tick) in enumerate(zip(steps, STEPS)):
        act, which = step if isinstance(step, tuple) else (step, None)
        events.append((tick, 6 + n, act, which))

    def head_of(name, which):
        return [c for c in heads if chunks[c][0] == name][which]

    def wait_for(*names):
        def act():
            for name in names:
                moves[name].wait()

        return act

    events.append((give_tick(head_of("down", 0)), -1, wait_for("branch", "hidden"), None))
    first = min(STEPS[0], give_tick(head_of("gate", 0)))
    events.append((first, 5.2, wait_for("n2", "gate_back", "up_back"), None))
    events.append((give_tick(head_of("down", -1)) + 1, 31, moves["w_out"].start, None))
    events.append((give_tick(head_of("up", -1)) + 1, 31, moves["h1"].start, None))
    events.append((give_tick(head_of("qkv", 0)), -1, moves["h1"].wait, None))
    events.append((give_tick(head_of("out", 0)), -1, moves["attended"].wait, None))
    attending = ("queries", "lse", "kv_all", "limits", "kp", "cosine", "sine")
    events.append((STEPS[6], 5.5, wait_for(*attending), None))
    events.sort(key=lambda e: e[:2])

    for name, move in moves.items():
        if name not in ("w_out", "h1", "outputs", "input_grad"):
            move.start()
    for copy in weight_loads(0, 0):
        copy.start()
    for _, _, act, which in events:
        act() if which is None else act(which)

    for c in range(count):
        if not [n for n in heads if n > c and given(n) is given(c)]:
            pair_copy(c).wait_send()
        if swapped(c):
            swap_copy(c).wait_send()
        keep_copy(c).wait()
        back_copy(c).wait_send()
        back_copy(c).wait_recv()

        @pl.when(outer)
        def _():
            in_copy(c).wait_send()

        @pl.when(inner)
        def _():
            mid_copy(c).wait_send()
            out_copy(c).wait_send()

    moves["outputs"].wait()
    moves["input_grad"].wait()
    for j in peers:
        out_send(j).wait_send()
        da_send(j).wait_send()
        dh_send(j).wait_send()
        gain_send(j).wait_send()
    kv_pair.wait_send()
    for s in range(1, line):

        @pl.when(z + s < line)
        def _():
            kv_send(s).wait_send()


def back_pass(held, far):
    count, line = lax.axis_size("fsdp"), lax.axis_size("z")
    mixed, attended, kv_all, hidden = held[4], held[8], held[11], held[3]
    rows, depth = mixed.shape
    total, half_depth = count * rows, depth // 2
    half = half_depth // count
    q_width = attended.shape[1]
    ff = hidden.shape[1]
    keys = kv_all.shape[0] * rows
    slabs = (2 * count, half // 2, ff)
    shapes = [
        (ff // 128, 128, half_depth),
        slabs,
        slabs,
        (4, q_width // 4, half_depth),
        (2 * count, half // 2, q_width + 128),
        (1, 16, depth),
    ]
    anywhere = pl.BlockSpec(memory_space=pl.ANY)
    ends = [jax.ShapeDtypeStruct(s, BF) for s in shapes]
    act = jax.ShapeDtypeStruct((rows, depth), F32)
    block = (rows, depth)
    chunk_count = sum(s[0] for s in shapes)
    dma = lambda *n: pltpu.SemaphoreType.DMA(n)
    groups = (1, 2, 2, 2, 1)
    scratch = (
        [pltpu.VMEM(x.shape, x.dtype) for x in held]
        + [pltpu.VMEM(block, BF), pltpu.VMEM(block, F32)]
        + [pltpu.VMEM(s, BF) for s in shapes]
        + [pltpu.VMEM((shapes[i][0] - 2,) + shapes[i][1:], BF) for i in (1, 2, 4)]
        + [pltpu.VMEM(s, BF) for s in shapes]
        + [pltpu.VMEM((g,) + shapes[i][1:], BF) for g, i in zip(groups, (0, 1, 3, 4, 5))]
        + [
            pltpu.VMEM((max(half, q_width // 2, 128), total), BF),
            pltpu.VMEM((count - 1,) + block, BF),
            pltpu.VMEM((count - 1,) + block, BF),
            pltpu.VMEM((2, 2, half, ff), BF),
            pltpu.VMEM((2, ff, depth // 8), BF),
            pltpu.VMEM((2, half, q_width + 128), BF),
            pltpu.VMEM((total, depth), BF),
            pltpu.VMEM((count,) + block, BF),
            pltpu.VMEM((max(total, q_width), depth), BF),
            pltpu.VMEM((count, rows, q_width), BF),
            pltpu.VMEM((total, q_width + 128), BF),
            pltpu.VMEM((total, depth), BF),
            pltpu.VMEM((keys, 128), BF),
            pltpu.VMEM((keys, 128), F32),
            pltpu.VMEM((keys, 128), F32),
            pltpu.VMEM(kv_all.shape, BF),
            pltpu.VMEM((line,) + kv_all.shape[1:], BF),
            pltpu.VMEM((line,) + kv_all.shape[1:], BF),
            pltpu.VMEM((line - 1,) + kv_all.shape[1:], BF),
            pltpu.VMEM((2, 16, depth), F32),
            pltpu.VMEM((count, 16, depth), BF),
        ]
        + [dma(chunk_count)] * 12
        + [pltpu.SemaphoreType.REGULAR, dma(22), dma(2, 2)]
        + [dma(count - 1)] * 8
        + [dma(1)] * 2
        + [dma(line - 1)] * 2
        + [dma(count - 1)] * 2
    )
    out = pl.pallas_call(
        back_kernel,
        out_shape=ends + ends + [act, act],
        in_specs=[anywhere] * (len(held) + len(far)),
        out_specs=[anywhere] * 14,
        scratch_shapes=scratch,
        compiler_params=pltpu.CompilerParams(
            vmem_limit_bytes=63 * 1024 * 1024, has_side_effects=True
        ),
        name="back_pass",
    )(*held, *far)
    return out[:6], out[6:12], out[12], out[13]


def finish_kernel(
    own_down, own_gate, own_up, own_out, own_qkv, own_gain, sib_down, sib_gate, sib_up, sib_out, sib_qkv,
    outputs_in, input_grad_in, outputs, input_grad, down, gate, up, out, query, key, value, attn_gain, mlp_gain,
    low_rows, low_cols, high_rows, high_cols, kv, acts, gain_in, gain_high, load_s, store_s, side_s,
):
    f, k = lax.axis_index("fsdp"), lax.axis_index("core")
    plane = lax.axis_size("fsdp")
    half, ff = own_gate.shape[1], own_gate.shape[2]
    half_depth = own_down.shape[2]
    slab = 2 * half
    q_width = own_qkv.shape[2] - 128
    tasks = []
    for side, (d, o, g, u, q) in enumerate(
        ((own_down, own_out, own_gate, own_up, own_qkv), (sib_down, sib_out, sib_gate, sib_up, sib_qkv))
    ):
        rows_at = pl.ds(pl.multiple_of((k ^ side) * half, 8), half)
        cols_at = pl.ds(pl.multiple_of((k ^ side) * half_depth, 128), half_depth)
        for source, target in ((d, down), (o, out)):
            for i in range(source.shape[0]):
                size = source.shape[1]
                tasks.append((source.at[i], target.at[pl.ds(i * size, size), cols_at], 0))
        for source, target in ((g, gate), (u, up)):
            for j in range(plane):
                to = pl.ds(pl.multiple_of((f ^ j) * ff, 128), ff)
                tasks.append((source.at[j], target.at[rows_at, to], 1))
        for j in range(plane):
            to = pl.ds(pl.multiple_of((f ^ j) * q_width, 128), q_width)
            tasks.append((q.at[j, :, pl.ds(0, q_width)], query.at[rows_at, to], 1))
    slots = low_rows.shape[0]

    def window(buffer, n, shape):
        return buffer.at[n % slots, pl.ds(0, shape[0]), pl.ds(0, shape[1])]

    def load(n):
        source, _, kind = tasks[n]
        low = (low_rows, low_cols)[kind]
        return pltpu.make_async_copy(source, window(low, n, source.shape), load_s.at[n])

    def store(n):
        source, target, kind = tasks[n]
        high = (high_rows, high_cols)[kind]
        return pltpu.make_async_copy(window(high, n, source.shape), target, store_s.at[n])

    sides = [
        pltpu.make_async_copy(own_gain.at[0], gain_in, side_s.at[0]),
        pltpu.make_async_copy(own_qkv.at[:, :, pl.ds(q_width, 128)], kv.at[0], side_s.at[1]),
        pltpu.make_async_copy(sib_qkv.at[:, :, pl.ds(q_width, 128)], kv.at[1], side_s.at[2]),
        pltpu.make_async_copy(outputs_in, acts.at[0], side_s.at[3]),
        pltpu.make_async_copy(input_grad_in, acts.at[1], side_s.at[4]),
    ]
    for n in range(slots):
        load(n).start()
    for copy in sides:
        copy.start()
    for n in range(len(tasks)):
        source, _, kind = tasks[n]
        shape = source.shape
        low, high = ((low_rows, high_rows), (low_cols, high_cols))[kind]
        load(n).wait()
        if n >= slots:
            store(n - slots).wait()

        @pl.loop(0, shape[0] // 16)
        def _(i):
            at = pl.ds(pl.multiple_of(i * 16, 16), 16)
            high[n % slots, at, 0 : shape[1]] = low[n % slots, at, 0 : shape[1]].astype(F32)

        store(n).start()
        if n + slots < len(tasks):
            load(n + slots).start()
    for copy in sides:
        copy.wait()
    lasts = [
        pltpu.make_async_copy(acts.at[0], outputs, side_s.at[5]),
        pltpu.make_async_copy(acts.at[1], input_grad, side_s.at[6]),
    ]
    for copy in lasts:
        copy.start()
    mine = pl.ds(pl.multiple_of(f * slab, 128), slab)
    gain_high[...] = gain_in[...].astype(F32)
    attn_gain[...] = gain_high[0:1, mine]
    mlp_gain[...] = gain_high[1:2, mine]
    lane = lax.broadcasted_iota(jnp.int32, (half, 128), 1)
    for side in range(2):
        rows_at = pl.ds(pl.multiple_of((k ^ side) * half, 8), half)
        for pair in range(plane // 2):
            first = kv[side, f ^ (2 * pair)].astype(F32)
            second = kv[side, f ^ (2 * pair + 1)].astype(F32)
            at = slice(pair * 128, (pair + 1) * 128)
            key[rows_at, at] = jnp.where(lane < 64, first, pltpu.roll(second, 64, 1))
            value[rows_at, at] = jnp.where(lane < 64, pltpu.roll(first, 64, 1), second)
    for n in range(max(0, len(tasks) - slots), len(tasks)):
        store(n).wait()
    for copy in lasts:
        copy.wait()


def finish(owns, sibs, outputs, input_grad):
    plane = lax.axis_size("fsdp")
    down, gate, _, out, qkv, gain = (x.shape for x in owns)
    depth = 2 * down[2]
    slab = 2 * gate[1]
    q_width = qkv[2] - 128
    sds = jax.ShapeDtypeStruct
    shapes = [
        outputs.shape, input_grad.shape,
        (down[0] * down[1], depth), (slab, plane * gate[2]), (slab, plane * gate[2]), (out[0] * out[1], depth),
        (slab, plane * q_width), (slab, KV_HEADS * HEAD_DIM), (slab, KV_HEADS * HEAD_DIM), (1, slab), (1, slab),
    ]
    slots = 8
    tall = (slots, max(down[1], out[1]), down[2])
    wide = (slots, gate[1], max(gate[2], q_width))
    count = 2 * (down[0] + out[0] + 3 * plane)
    anywhere, local = pl.BlockSpec(memory_space=pl.ANY), pl.BlockSpec(memory_space=pltpu.VMEM)
    return pl.pallas_call(
        finish_kernel,
        out_shape=[sds(s, F32) for s in shapes],
        in_specs=[anywhere] * 13,
        out_specs=[anywhere] * 7 + [local] * 4,
        scratch_shapes=[
            pltpu.VMEM(tall, BF),
            pltpu.VMEM(wide, BF),
            pltpu.VMEM(tall, F32),
            pltpu.VMEM(wide, F32),
            pltpu.VMEM((2, plane, gate[1], 128), BF),
            pltpu.VMEM((2,) + outputs.shape, F32),
            pltpu.VMEM(gain[1:], BF),
            pltpu.VMEM(gain[1:], F32),
            pltpu.SemaphoreType.DMA((count,)),
            pltpu.SemaphoreType.DMA((count,)),
            pltpu.SemaphoreType.DMA((7,)),
        ],
        compiler_params=params(),
        name="finish",
    )(*owns, *sibs[:5], outputs, input_grad)


def body(
    tokens, cotangent, lengths, attn_gain, w_query, w_key, w_value, w_out, mlp_gain, w_gate, w_up, w_down
):
    seqs, rows, depth = tokens.shape
    count = lax.axis_size("fsdp")
    slab = depth // count
    x_own = tokens.reshape(rows, depth)
    (
        h1, queries, lse, attended, mixed, n2, limits, cosine, sine, kp, gain_one, gain_two, kv_all, branch, wqkv,
        gate_back, up_back, hidden, gate_own, gate_sib, up_own, up_sib,
    ) = front_pass(
        x_own, cotangent.reshape(rows, depth), lengths, attn_gain, mlp_gain,
        w_query, w_key, w_value, w_out, w_gate, w_up, w_down,
    )
    held = (
        limits, gate_back, up_back, hidden, mixed, x_own, gain_one, gain_two,
        attended, queries, lse, kv_all, kp, cosine, sine,
    )
    branch = branch.reshape(count * rows, depth)
    far = (branch, w_out, w_down, wqkv, h1, n2, gate_own, gate_sib, up_own, up_sib)
    owns, sibs, outputs, input_grad = back_pass(held, far)

    def whole(x):
        return x.reshape(4, -1, x.shape[2]) if x.shape[0] > 1 else x

    owns, sibs = [whole(x) for x in owns], [whole(x) for x in sibs]
    (
        outputs, input_grad, down_grad, gate_grad, up_grad, out_grad, query_grad, key_grad, value_grad, gain_a, gain_m
    ) = finish(owns, sibs, outputs, input_grad)
    return (
        outputs.reshape(seqs, rows, depth),
        input_grad.reshape(seqs, rows, depth),
        gain_a.reshape(slab),
        query_grad,
        key_grad,
        value_grad,
        out_grad,
        gain_m.reshape(slab),
        gate_grad,
        up_grad,
        down_grad,
    )


def solution(mesh):
    count, ctx = mesh.shape["fsdp"], mesh.shape["ctx"]
    split = Mesh(mesh.devices.reshape(count, ctx // 2, 2), ("fsdp", "z", "core"))
    act = P("fsdp", ("z", "core"), None)
    row, mat = P("fsdp"), P("fsdp", None)
    fast = count == 4 and count == KV_HEADS and ctx == 8
    return jax.shard_map(
        body if fast else body_plain,
        mesh=split,
        in_specs=(act, act, row, row, mat, mat, mat, mat, row, mat, mat, mat),
        out_specs=(act, act, row, mat, mat, mat, mat, row, mat, mat, mat),
        check_vma=False,
    )
```
